32 devices in a mesh: dp: 4 (over z), span: 2 (over core), tensor: 4 (over y, x).
Axes of the slice: x: 2, y: 2, z: 4, core: 2. Of those that a mesh axis runs over, the one named last changes fastest.
Arguments:
- layer_input: bfloat16 [2, 16, 512, 768], P('span', 'dp', 'tensor'), may hold values from -6 to 6
- skip_tokens: bfloat16 [2, 16, 512, 768], P('span', 'dp', 'tensor'), may hold values from -6 to 6
- backbone_cotangent: bfloat16 [2, 16, 512, 768], P('span', 'dp', 'tensor'), may hold values from -6 to 6
- head_cotangent: bfloat16 [2, 16, 512, 768], P('span', 'dp', 'tensor'), may hold values from -6 to 6
- segment_lengths: int32 [2, 16, 4], P('span', 'dp'), may hold values from 1 to 174, 464 in all within a row
- pair_index: int32 [64], replicated, may hold values from 0 to 63, each once
- w_heads: bfloat16 [2, 3, 768, 768], P(None, None, None, 'tensor'), may hold values from -0.21875 to 0.21875
- heads_bias: bfloat16 [2, 2, 768], P(None, None, 'tensor'), may hold values from -1.75 to 1.75
- w_project: bfloat16 [2, 768, 768], P(None, 'tensor'), may hold values from -0.875 to 0.875
- project_bias: bfloat16 [2, 768], replicated, may hold values from -1.75 to 1.75
- norm_gain: bfloat16 [2, 2, 768], replicated, may hold values from 0.5 to 1.5
- norm_shift: bfloat16 [2, 2, 768], replicated, may hold values from -1.75 to 1.75
- w_expand: bfloat16 [2, 768, 3072], P(None, None, 'tensor'), may hold values from -0.21875 to 0.21875
- expand_bias: bfloat16 [2, 3072], P(None, 'tensor'), may hold values from -3 to 3
- w_shrink: bfloat16 [2, 3072, 768], P(None, 'tensor'), may hold values from -0.109375 to 0.109375
- shrink_bias: bfloat16 [2, 768], replicated, may hold values from -1.75 to 1.75
Outputs:
- backbone_out: bfloat16 [2, 16, 512, 768], P('span', 'dp', 'tensor')
- head_out: bfloat16 [2, 16, 512, 768], P('span', 'dp', 'tensor')
- span_loss: float32 [], replicated
- grad_input: bfloat16 [2, 16, 512, 768], P('span', 'dp', 'tensor')
- grad_skip: bfloat16 [2, 16, 512, 768], P('span', 'dp', 'tensor')
- grad_heads: float32 [2, 3, 768, 768], P(None, None, None, 'tensor')
- grad_heads_bias: float32 [2, 2, 768], P(None, None, 'tensor')
- grad_project: float32 [2, 768, 768], P(None, 'tensor')
- grad_project_bias: float32 [2, 768], replicated
- grad_gain: float32 [2, 2, 768], replicated
- grad_shift: float32 [2, 2, 768], replicated
- grad_expand: float32 [2, 768, 3072], P(None, None, 'tensor')
- grad_expand_bias: float32 [2, 3072], P(None, 'tensor')
- grad_shrink: float32 [2, 3072, 768], P(None, 'tensor')
- grad_shrink_bias: float32 [2, 768], replicated
The draws below stay inside these ranges and needn't reach their ends.
Inputs may be any that keep to these rules, and one draw needn't show every extreme that they name: `segment_lengths`: each row holds 4 spans whose lengths add up to 464, the longest being 174; the rest of the row is padding. `pair_index`: each value occurs exactly once.
All inputs are finite; a program needn't handle non-finite values.
Results may differ from the reference program's by a relative error of at most 0.015.
The reference program's roundings to bfloat16 on the way count: a program that leaves them out, or rounds other values in their place, can miss the bound.
Values may be sent and summed in bfloat16 or wider, within the bound.
A program may use at most 192 MiB of HBM per device.

```python
import math
import jax
import jax.numpy as jnp
import numpy as np
from jax import lax

D = 768
HEADS = 12
HEAD_DIM = 64
FF = 3072
LEN = 512
SEGS = 4
ROWS = 16
NCLS = 64
FILLED = 464
MOST_SEG = 174


def shard_levels(own_key, shape, split, smallest, high):
    loudness = 1.0
    for dim, blocks in split:
        steps = jax.random.uniform(jax.random.fold_in(jax.random.fold_in(own_key, 6), dim), (blocks,), jnp.float32, smallest / len(split), high / len(split))
        loudness = loudness * jnp.repeat(jnp.exp(steps), shape[dim] // blocks).reshape((-1,) + (1,) * (len(shape) - 1 - dim))
    return loudness


def profile(number_of, total, limit, skew):
    loads = [(1 << 20) // math.isqrt(grade ** skew) + 1 for grade in range(2, number_of + 1)]
    surplus, given = total - limit - (number_of - 1), [1] * (number_of - 1)
    while surplus > 0:
        candidates = [i for i in range(number_of - 1) if given[i] < limit]
        pool, remaining = sum([loads[i] for i in candidates]), surplus
        for i in candidates:
            addition = min(limit - given[i], max(1, remaining * loads[i] // pool), surplus)
            given[i] = given[i] + addition
            surplus = surplus - addition
    return np.array([limit] + given)


def ragged_sizes(rng, count, total, most, skew):
    if count == 2:
        one = jax.random.randint(rng, (), max(1, total - most), min(most, total - 1) + 1)
        return jnp.stack([one, total - one])
    tallies = jnp.asarray(profile(count, total, most, skew), jnp.int32)
    twos = (count - 1) // 2
    giver, receiver = tallies[1:1 + 2 * twos:2], tallies[2:2 + 2 * twos:2]
    slack = jnp.minimum(giver - 1, most - receiver)
    moved = jax.random.randint(jax.random.fold_in(rng, 1), (twos,), 0, 1 << 20) % (slack + 1)
    tallies = tallies.at[1:1 + 2 * twos:2].set(giver - moved).at[2:2 + 2 * twos:2].set(receiver + moved)
    return tallies[jax.random.permutation(jax.random.fold_in(rng, 2), count)]


def gaussian(rng, extent, scale, limit, shards=(), kind=jnp.bfloat16):
    factor_of = shard_levels(rng, extent, shards, -0.22, 0.18) if shards else 1.0
    drawn = jax.random.normal(rng, extent, jnp.float32) * scale * factor_of
    return jnp.minimum(jnp.maximum(drawn, -limit), limit).astype(kind)


def setup_inputs(seed: int = 0) -> dict:
    seeds = jax.random.split(jax.random.key(seed), 17)
    return {
        "layer_input": gaussian(seeds[0], (2, ROWS, LEN, D), 1.0, 6.0, ((0, 2), (1, 4), (2, 4))),
        "skip_tokens": gaussian(seeds[1], (2, ROWS, LEN, D), 1.0, 6.0, ((0, 2), (1, 4), (2, 4))),
        "backbone_cotangent": gaussian(seeds[2], (2, ROWS, LEN, D), 1.0, 6.0, ((0, 2), (1, 4), (2, 4))),
        "head_cotangent": gaussian(seeds[3], (2, ROWS, LEN, D), 1.0, 6.0, ((0, 2), (1, 4), (2, 4))),
        "segment_lengths": jax.vmap(lambda own: ragged_sizes(own, SEGS, FILLED, MOST_SEG, 1))(jax.random.split(seeds[4], 2 * ROWS)).reshape((2, ROWS, SEGS)).astype(jnp.int32),
        "pair_index": jax.random.permutation(seeds[5], NCLS).astype(jnp.int32),
        "w_heads": gaussian(seeds[6], (2, 3, D, D), D ** -0.5, 0.21875, ((3, 4),)),
        "heads_bias": gaussian(seeds[7], (2, 2, D), 0.3, 1.75, ((2, 4),)),
        "w_project": gaussian(seeds[8], (2, D, D), (D // 16) ** -0.5, 0.875, ((1, 4),)),
        "project_bias": gaussian(seeds[9], (2, D), 0.3, 1.75),
        "norm_gain": jnp.clip(1.0 + 0.1 * jax.random.normal(seeds[10], (2, 2, D), jnp.float32), 0.5, 1.5).astype(jnp.bfloat16),
        "norm_shift": gaussian(seeds[11], (2, 2, D), 0.3, 1.75),
        "w_expand": gaussian(seeds[12], (2, D, FF), D ** -0.5, 0.21875, ((2, 4),)),
        "expand_bias": gaussian(seeds[13], (2, FF), 0.5, 3.0, ((1, 4),)),
        "w_shrink": gaussian(seeds[14], (2, FF, D), FF ** -0.5, 0.109375, ((1, 4),)),
        "shrink_bias": gaussian(seeds[15], (2, D), 0.3, 1.75),
    }


@jax.custom_vjp
def low(v):
    return lax.optimization_barrier(v.astype(jnp.bfloat16)).astype(jnp.float32)

@jax.custom_vjp
def low_back(v):
    return v

def low_keep(v):
    return (low(v), None)

def low_pass(kept, grad):
    return (grad,)

def back_keep(v):
    return (v, None)

def back_low(kept, grad):
    return (low(grad),)
low.defvjp(low_keep, low_pass)
low_back.defvjp(back_keep, back_low)
EPSILON = 1e-12
LOSS_WEIGHT = 8.0
HIGHEST = lax.Precision.HIGHEST

def both_ways(values):
    return low(low_back(values))

def normalize(values, norm_scale, norm_offset):
    centred = values - lax.optimization_barrier(jnp.mean(values, axis=-1, keepdims=True))
    spread = lax.optimization_barrier(jnp.mean(centred * centred, axis=-1, keepdims=True))
    return centred * lax.rsqrt(spread + EPSILON) * norm_scale + norm_offset

def layer_rows(pieces, weights):
    hidden, segment = pieces
    w_heads, heads_bias, w_project, project_bias, norm_gain, norm_shift, w_expand, expand_bias, w_shrink, shrink_bias = weights
    row_count = hidden.shape[0]
    projected = jnp.einsum('rtd,cde->crte', low(hidden), w_heads, precision=HIGHEST)
    queries = both_ways(projected[0] + heads_bias[0]).reshape(row_count, LEN, HEADS, HEAD_DIM)
    key_rows = both_ways(projected[1]).reshape(row_count, LEN, HEADS, HEAD_DIM)
    value_rows = both_ways(projected[2] + heads_bias[1]).reshape(row_count, LEN, HEADS, HEAD_DIM)
    scores = low_back(jnp.einsum('rqhd,rkhd->rhqk', queries, key_rows, precision=HIGHEST) * 0.125)
    same_span = segment[:, None, :, None] == segment[:, None, None, :]
    scores = jnp.where(same_span, scores, -1e+30)
    attention = low(jax.nn.softmax(scores, axis=-1))
    mixture = jnp.einsum('rhqk,rkhd->rqhd', attention, value_rows, precision=HIGHEST)
    mixture = both_ways(mixture.reshape(row_count, LEN, D))
    attended = low_back(jnp.einsum('rtd,de->rte', mixture, w_project, precision=HIGHEST)) + project_bias
    first_norm = normalize(hidden + attended, norm_gain[0], norm_shift[0])
    expanded = low_back(jnp.einsum('rtd,df->rtf', low(first_norm), w_expand, precision=HIGHEST)) + expand_bias
    activated = low(jax.nn.gelu(expanded, approximate=False))
    shrunk = low_back(jnp.einsum('rtf,fd->rtd', activated, w_shrink, precision=HIGHEST)) + shrink_bias
    return normalize(first_norm + shrunk, norm_gain[1], norm_shift[1])

def layer(hidden, segment, weights):
    row_count = hidden.shape[0]
    group_size = math.gcd(row_count, 8)

    def one_group(pieces):
        return layer_rows(pieces, weights)
    shaped = (hidden.reshape(row_count // group_size, group_size, LEN, D), segment.reshape(row_count // group_size, group_size, LEN))
    return lax.map(jax.checkpoint(one_group), shaped).reshape(row_count, LEN, D)

def reference(layer_input, skip_tokens, backbone_cotangent, head_cotangent, segment_lengths, pair_index, w_heads, heads_bias, w_project, project_bias, norm_gain, norm_shift, w_expand, expand_bias, w_shrink, shrink_bias):
    row_count = 2 * ROWS
    starts = (jnp.cumsum(segment_lengths, axis=-1) - segment_lengths).astype(jnp.int32)
    row_length = lax.optimization_barrier(jnp.sum(segment_lengths, axis=-1)).astype(jnp.int32)
    places = jnp.arange(LEN, dtype=jnp.int32)
    counted = (lax.optimization_barrier(jnp.sum((places[None, None, :, None] >= starts[:, :, None, :]).astype(jnp.int32), axis=-1)) - 1).astype(jnp.int32)
    valid_rows = places[None, None, :] < row_length[:, :, None]
    segment = jnp.where(valid_rows, counted, SEGS).astype(jnp.int32).reshape(row_count, LEN)
    picker = (starts[:, :, :, None] == places[None, None, None, :]).astype(jnp.float32)
    first_mark = lax.optimization_barrier(jnp.sum(picker, axis=2))[..., None] > 0
    valid_mask = valid_rows[..., None].astype(jnp.float32)
    backbone_seed = backbone_cotangent.astype(jnp.float32) * valid_mask
    head_seed = head_cotangent.astype(jnp.float32) * valid_mask
    target = (pair_index[:, None] == jnp.arange(NCLS, dtype=jnp.int32)[None, :]).astype(jnp.float32)
    floats = tuple((member.astype(jnp.float32) for member in (layer_input, skip_tokens, w_heads, heads_bias, w_project, project_bias, norm_gain, norm_shift, w_expand, expand_bias, w_shrink, shrink_bias)))

    def forward(inputs, skip_rows, w_heads, heads_bias, w_project, project_bias, norm_gain, norm_shift, w_expand, expand_bias, w_shrink, shrink_bias):

        def run_layer(hidden, layer_index):
            weights = (w_heads[layer_index], heads_bias[layer_index], w_project[layer_index], project_bias[layer_index], norm_gain[layer_index], norm_shift[layer_index], w_expand[layer_index], expand_bias[layer_index], w_shrink[layer_index], shrink_bias[layer_index])
            return layer(hidden.reshape(row_count, LEN, D), segment, weights).reshape(2, ROWS, LEN, D)
        backbone = run_layer(inputs, 0)
        chosen = jnp.einsum('srgp,srpd->srgd', picker, backbone, precision=HIGHEST)
        anchor_rows = low(chosen.reshape(2, NCLS, D))
        head_rows = run_layer(jnp.where(first_mark, backbone, skip_rows), 1)
        logits = jnp.dot(anchor_rows[0], anchor_rows[1].T, precision=HIGHEST) / math.sqrt(D)
        rowloss = jnp.sum(jax.nn.logsumexp(logits, axis=1)) + jnp.sum(jax.nn.logsumexp(logits, axis=0)) - 2.0 * jnp.sum(target * logits)
        backbone_out = backbone * valid_mask
        head_out = head_rows * valid_mask
        objective = jnp.sum(backbone_out * backbone_seed) + jnp.sum(head_out * head_seed) + LOSS_WEIGHT * rowloss
        return (objective, (backbone_out, head_out, rowloss / (2 * NCLS)))
    objective, pullback, outputs = jax.vjp(forward, *floats, has_aux=True)
    gradients = pullback(jnp.ones_like(objective))
    backbone_out, head_out, span_loss = outputs
    return (backbone_out.astype(jnp.bfloat16), head_out.astype(jnp.bfloat16), span_loss, gradients[0].astype(jnp.bfloat16), gradients[1].astype(jnp.bfloat16), gradients[2], gradients[3], gradients[4], gradients[5], gradients[6], gradients[7], gradients[8], gradients[9], gradients[10], gradients[11])
```

```python
import math

import jax
import jax.numpy as jnp
from jax import lax
from jax.sharding import PartitionSpec as P

HEAD_DIM = 64
EPSILON = 1e-12
LOSS_WEIGHT = 8.0
HIGHEST = lax.Precision.HIGHEST
MASKED = -1e30
BF = jnp.bfloat16
F32 = jnp.float32
BOTH = ("span", "tensor")


def mm(a, b, ca, cb):
    return lax.dot_general(a, b, (((ca,), (cb,)), ((), ())), preferred_element_type=F32)


def normal_parts(values):
    centred = values - jnp.mean(values, axis=-1, keepdims=True)
    spread = jnp.mean(centred * centred, axis=-1, keepdims=True)
    scale = lax.rsqrt(spread + EPSILON)
    return centred * scale, scale


def normal_back(upward, normed, scale, gain):
    weighted = upward * gain
    first = jnp.mean(weighted, axis=-1, keepdims=True)
    second = jnp.mean(weighted * normed, axis=-1, keepdims=True)
    return (weighted - first - normed * second) * scale


def split_heads(values):
    return values.reshape(values.shape[0], values.shape[1] // HEAD_DIM, HEAD_DIM)


def attend_forward(queries, keys, values, same):
    scores = (
        jnp.einsum("qhd,khd->hqk", split_heads(queries), split_heads(keys), preferred_element_type=F32)
        * 0.125
    )
    scores = jnp.where(same[None], scores, MASKED)
    maximum = jnp.max(scores, axis=-1, keepdims=True)
    raised = jnp.exp(scores - maximum)
    total = jnp.sum(raised, axis=-1, keepdims=True)
    attention = (raised / total).astype(BF)
    mixture = jnp.einsum("hqk,khd->qhd", attention, split_heads(values), preferred_element_type=F32)
    return mixture.reshape(queries.shape).astype(BF), maximum + jnp.log(total)


def attend_backward(queries, keys, values, same, upward, log_total):
    qh, kh, vh, uh = (split_heads(m) for m in (queries, keys, values, upward))
    scores = jnp.einsum("qhd,khd->hqk", qh, kh, preferred_element_type=F32) * 0.125
    scores = jnp.where(same[None], scores, MASKED)
    attention = jnp.exp(scores - log_total)
    grad_weights = jnp.einsum("qhd,khd->hqk", uh, vh, preferred_element_type=F32)
    inner = jnp.sum(attention * grad_weights, axis=-1, keepdims=True)
    grad_scores = (attention * (grad_weights - inner)).astype(BF)
    dq = jnp.einsum("hqk,khd->qhd", grad_scores, kh, preferred_element_type=F32) * 0.125
    dk = jnp.einsum("hqk,qhd->khd", grad_scores, qh, preferred_element_type=F32) * 0.125
    dv = jnp.einsum("hqk,qhd->khd", attention.astype(BF), uh, preferred_element_type=F32)
    return tuple(m.reshape(queries.shape).astype(BF) for m in (dq, dk, dv))


def gelu_parts(hidden):
    phi = 0.5 * (1.0 + lax.erf(hidden * math.sqrt(0.5)))
    slope = phi + hidden * jnp.exp(-0.5 * hidden * hidden) * (1.0 / math.sqrt(2.0 * math.pi))
    return hidden * phi, slope


def layer_forward(x, same, attn_w, ffn_w, vec):
    wq, wk, wv, wp = attn_w
    we, ws = ffn_w
    xb = x.astype(BF)
    q = (mm(xb, wq, 1, 1) + vec["qb"]).astype(BF)
    k = mm(xb, wk, 1, 1).astype(BF)
    v = (mm(xb, wv, 1, 1) + vec["vb"]).astype(BF)
    o, lse = attend_forward(q, k, v, same)
    z1 = x + mm(o, wp, 1, 0) + vec["pb"]
    n1, r1 = normal_parts(z1)
    y = n1 * vec["g0"] + vec["s0"]
    yb = y.astype(BF)
    hid = jnp.einsum("qd,tdf->tqf", yb, we, preferred_element_type=F32) + vec["eb"][:, None, :]
    act, slope = gelu_parts(hid)
    act = act.astype(BF)
    z2 = y + jnp.einsum("tqf,tfd->qd", act, ws, preferred_element_type=F32) + vec["sb"]
    n2, r2 = normal_parts(z2)
    out = n2 * vec["g1"] + vec["s1"]
    return out, (xb, q, k, v, o, lse, n1, r1, yb, act, slope.astype(BF), n2, r2)


def layer_backward(dout, same, attn_w, ffn_w, vec, kept):
    wq, wk, wv, wp = attn_w
    we, ws = ffn_w
    xb, q, k, v, o, lse, n1, r1, yb, act, slope, n2, r2 = kept
    dz2 = normal_back(dout, n2, r2, vec["g1"])
    dgain1 = jnp.sum(dout * n2, axis=0)
    dshift1 = jnp.sum(dout, axis=0)
    dsb = jnp.sum(dz2, axis=0)
    dzb = dz2.astype(BF)
    dws = jnp.einsum("tqf,qd->tfd", act, dzb, preferred_element_type=F32).astype(BF)
    dact = jnp.einsum("qd,tfd->tqf", dzb, ws, preferred_element_type=F32)
    dhid = dact * slope.astype(F32)
    deb = jnp.sum(dhid, axis=1)
    dhb = dhid.astype(BF)
    dwe = jnp.einsum("qd,tqf->tdf", yb, dhb, preferred_element_type=F32).astype(BF)
    dy = dz2 + jnp.einsum("tqf,tdf->qd", dhb, we, preferred_element_type=F32)
    dz1 = normal_back(dy, n1, r1, vec["g0"])
    dgain0 = jnp.sum(dy * n1, axis=0)
    dshift0 = jnp.sum(dy, axis=0)
    dpb = jnp.sum(dz1, axis=0)
    da = dz1.astype(BF)
    dwp = mm(o, da, 0, 0).astype(BF)
    do = mm(da, wp, 1, 1).astype(BF)
    dq, dk, dv = attend_backward(q, k, v, same, do, lse)
    dwq = mm(dq, xb, 0, 0).astype(BF)
    dwk = mm(dk, xb, 0, 0).astype(BF)
    dwv = mm(dv, xb, 0, 0).astype(BF)
    dqb = jnp.sum(dq.astype(F32), axis=0)
    dvb = jnp.sum(dv.astype(F32), axis=0)
    dx = dz1 + mm(dq, wq, 1, 0) + mm(dk, wk, 1, 0) + mm(dv, wv, 1, 0)
    small = {
        "qb": dqb, "vb": dvb, "pb": dpb, "g0": dgain0, "g1": dgain1,
        "s0": dshift0, "s1": dshift1, "sb": dsb, "eb": deb.reshape(-1),
    }
    return dx, (dwq, dwk, dwv, dwp), (dwe, dws), small


SMALL = ("qb", "vb", "pb", "g0", "g1", "s0", "s1", "sb", "eb")


def to_rows(values):
    return lax.all_to_all(values, "tensor", split_axis=0, concat_axis=1, tiled=True)[0]


def to_places(values):
    return lax.all_to_all(values[None], "tensor", split_axis=1, concat_axis=0, tiled=True)


def shards(
    layer_input, skip_tokens, backbone_cotangent, head_cotangent, segment_lengths, pair_index,
    w_heads, heads_bias, w_project, project_bias, norm_gain, norm_shift,
    w_expand, expand_bias, w_shrink, shrink_bias,
):
    side = lax.axis_index("span")
    mine = lax.axis_index("tensor")
    tensor_count = lax.axis_size("tensor")
    width = layer_input.shape[-1]
    head_cols = w_heads.shape[-1]
    ff_cols = w_expand.shape[-1]

    def gather_attn(l):
        heads = jnp.swapaxes(w_heads[l], 1, 2)
        zero = jnp.stack([heads[0], heads[1]])
        one = jnp.stack([heads[2], w_project[l]])
        got = lax.all_gather(jnp.where(side == 0, zero, one), BOTH, axis=0, tiled=False)
        got = got.reshape(2, tensor_count, 2, head_cols, width)
        return tuple(
            got[i, :, j].reshape(tensor_count * head_cols, width) for i in range(2) for j in range(2)
        )

    def gather_ffn(l):
        got = lax.all_gather(
            jnp.where(side == 0, w_expand[l], w_shrink[l]), BOTH, axis=0, tiled=False
        )
        got = got.reshape(2, tensor_count, width, ff_cols)
        return got[0], got[1]

    small_in = jnp.concatenate([heads_bias.reshape(-1), expand_bias.reshape(-1)])
    small_got = lax.all_gather(small_in, "tensor", axis=0, tiled=False).astype(F32)
    hb_all = jnp.transpose(small_got[:, : 4 * head_cols].reshape(tensor_count, 2, 2, head_cols), (1, 2, 0, 3))
    hb_all = hb_all.reshape(2, 2, tensor_count * head_cols)
    eb_all = jnp.transpose(small_got[:, 4 * head_cols :].reshape(tensor_count, 2, ff_cols), (1, 0, 2))

    def vectors(l):
        return {
            "qb": hb_all[l, 0], "vb": hb_all[l, 1], "pb": project_bias[l].astype(F32),
            "g0": norm_gain[l, 0].astype(F32), "g1": norm_gain[l, 1].astype(F32),
            "s0": norm_shift[l, 0].astype(F32), "s1": norm_shift[l, 1].astype(F32),
            "sb": shrink_bias[l].astype(F32), "eb": eb_all[l],
        }

    attn_w0 = gather_attn(0)
    ffn_w0 = gather_ffn(0)
    attn_w1 = gather_attn(1)
    ffn_w1 = gather_ffn(1)

    x = to_rows(layer_input[0])
    skip = to_rows(skip_tokens[0])
    backbone_cot = to_rows(backbone_cotangent[0])
    head_cot = to_rows(head_cotangent[0])
    tokens = x.shape[0]

    lengths = lax.dynamic_index_in_dim(segment_lengths[0], mine, 0, keepdims=False)
    span_count = lengths.shape[0]
    starts = jnp.cumsum(lengths) - lengths
    row_length = jnp.sum(lengths)
    places = jnp.arange(tokens, dtype=jnp.int32)
    counted = jnp.sum((places[:, None] >= starts[None, :]).astype(jnp.int32), axis=-1) - 1
    segment = jnp.where(places < row_length, counted, span_count)
    same = segment[:, None] == segment[None, :]
    valid = (places < row_length).astype(F32)[:, None]
    picker = (starts[:, None] == places[None, :]).astype(F32)
    first = jnp.sum(picker, axis=0)[:, None] > 0

    vec0, vec1 = vectors(0), vectors(1)
    backbone, kept0 = layer_forward(x.astype(F32), same, attn_w0, ffn_w0, vec0)
    cls = mm(picker.astype(BF), backbone.astype(BF), 1, 0).astype(BF)
    anchors = lax.all_gather(cls, ("dp", "span", "tensor"), axis=0, tiled=False)
    dp_count = lax.axis_size("dp")
    pair_count = lax.axis_size("span")
    anchors = anchors.reshape(dp_count, pair_count, tensor_count * span_count, width)
    anchors = jnp.swapaxes(anchors, 0, 1).reshape(pair_count, dp_count * tensor_count * span_count, width)

    head_in = jnp.where(first, backbone, skip.astype(F32))
    head, kept1 = layer_forward(head_in, same, attn_w1, ffn_w1, vec1)

    vector_count = anchors.shape[1]
    root = math.sqrt(width)
    logits = mm(anchors[0], anchors[1], 1, 1) / root
    columns = jnp.arange(vector_count, dtype=jnp.int32)
    target = (pair_index[:, None] == columns[None, :]).astype(F32)
    lse_rows = jax.nn.logsumexp(logits, axis=1)
    lse_cols = jax.nn.logsumexp(logits, axis=0)
    dlogits = LOSS_WEIGHT * (
        jnp.exp(logits - lse_rows[:, None]) + jnp.exp(logits - lse_cols[None, :]) - 2.0 * target
    )
    span_loss = (jnp.sum(lse_rows) + jnp.sum(lse_cols) - 2.0 * jnp.sum(target * logits)) / (
        2 * vector_count
    )
    own = (lax.axis_index("dp") * tensor_count + mine) * span_count
    wanted = jnp.where(side == 0, dlogits, dlogits.T)
    wanted = lax.dynamic_slice(wanted, (own, 0), (span_count, vector_count))
    other = lax.dynamic_index_in_dim(anchors, 1 - side, 0, keepdims=False).astype(F32)
    dcls = jnp.dot(wanted, other, precision=HIGHEST) / root

    du, dattn1, dffn1, small1 = layer_backward(
        head_cot.astype(F32) * valid, same, attn_w1, ffn_w1, vec1, kept1
    )
    grad_skip = jnp.where(first, 0.0, du).astype(BF)
    seed = backbone_cot.astype(F32) * valid + jnp.where(first, du, 0.0)
    seed = seed + jnp.dot(picker.T, dcls, precision=HIGHEST)
    dx, dattn0, dffn0, small0 = layer_backward(seed, same, attn_w0, ffn_w0, vec0, kept0)

    def reduce_attn(grads):
        packed = jnp.stack([g.reshape(tensor_count, head_cols, width) for g in grads])
        packed = packed.reshape(2, 2, tensor_count, head_cols, width)
        packed = jnp.swapaxes(packed, 1, 2).reshape(2 * tensor_count, 2, head_cols, width)
        part = lax.psum_scatter(packed, BOTH, scatter_dimension=0, tiled=False)
        part = lax.psum(part, "dp")
        got = lax.all_gather(part, "span", axis=0, tiled=False).astype(F32)
        heads = jnp.stack([got[0, 0], got[0, 1], got[1, 0]])
        return jnp.swapaxes(heads, 1, 2), got[1, 1]

    def reduce_ffn(grads):
        packed = jnp.stack(grads).reshape(2 * tensor_count, width, ff_cols)
        part = lax.psum_scatter(packed, BOTH, scatter_dimension=0, tiled=False)
        part = lax.psum(part, "dp")
        got = lax.all_gather(part, "span", axis=0, tiled=False).astype(F32)
        return got[0], got[1]

    ge1, gs1 = reduce_ffn(dffn1)
    gh1, gp1 = reduce_attn(dattn1)
    ge0, gs0 = reduce_ffn(dffn0)
    gh0, gp0 = reduce_attn(dattn0)

    flat = jnp.concatenate([small[k] for small in (small0, small1) for k in SMALL])
    flat = lax.psum(flat, ("dp", "span", "tensor"))
    sizes = [small0[k].shape[0] for k in SMALL] * 2
    cuts = []
    at = 0
    for size in sizes:
        cuts.append(flat[at : at + size])
        at += size
    s0 = dict(zip(SMALL, cuts[: len(SMALL)]))
    s1 = dict(zip(SMALL, cuts[len(SMALL) :]))

    def local(values, size):
        return lax.dynamic_slice(values, (mine * size,), (size,))

    hb = jnp.stack(
        [jnp.stack([local(s["qb"], head_cols), local(s["vb"], head_cols)]) for s in (s0, s1)]
    )
    eb = jnp.stack([local(s["eb"], ff_cols) for s in (s0, s1)])
    return (
        to_places((backbone * valid).astype(BF))[None],
        to_places((head * valid).astype(BF))[None],
        span_loss,
        to_places(dx.astype(BF))[None],
        to_places(grad_skip)[None],
        jnp.stack([gh0, gh1]),
        hb,
        jnp.stack([gp0, gp1]),
        jnp.stack([s0["pb"], s1["pb"]]),
        jnp.stack([jnp.stack([s["g0"], s["g1"]]) for s in (s0, s1)]),
        jnp.stack([jnp.stack([s["s0"], s["s1"]]) for s in (s0, s1)]),
        jnp.stack([ge0, ge1]),
        eb,
        jnp.stack([gs0, gs1]),
        jnp.stack([s0["sb"], s1["sb"]]),
    )


def solution(mesh):
    rows = P("span", "dp", "tensor", None)
    in_specs = (
        rows, rows, rows, rows, P("span", "dp", None), P(),
        P(None, None, None, "tensor"), P(None, None, "tensor"), P(None, "tensor", None),
        P(), P(), P(), P(None, None, "tensor"), P(None, "tensor"), P(None, "tensor", None), P(),
    )
    out_specs = (
        rows, rows, P(), rows, rows,
        P(None, None, None, "tensor"), P(None, None, "tensor"), P(None, "tensor", None),
        P(), P(), P(), P(None, None, "tensor"), P(None, "tensor"), P(None, "tensor", None), P(),
    )
    return jax.shard_map(shards, mesh=mesh, in_specs=in_specs, out_specs=out_specs, check_vma=False)
```

```python
import math

import jax
import jax.numpy as jnp
from jax import lax
from jax.experimental import pallas as pl
from jax.experimental.pallas import tpu as pltpu
from jax.sharding import PartitionSpec as P

HEAD_DIM = 64
EPSILON = 1e-12
LOSS_WEIGHT = 8.0
HIGHEST = lax.Precision.HIGHEST
MASKED = -1e30
BF = jnp.bfloat16
F32 = jnp.float32
PLANE = ("span", "tensor")
MESH = pl.DeviceIdType.MESH
TENSORS = 4
MAIN, DIAG, SWAP = "main", "diag", "swap"


def mm(a, b, ca, cb):
    return lax.dot_general(a, b, (((ca,), (cb,)), ((), ())), preferred_element_type=F32)


def normal_parts(values):
    centred = values - jnp.mean(values, axis=-1, keepdims=True)
    spread = jnp.mean(centred * centred, axis=-1, keepdims=True)
    scale = lax.rsqrt(spread + EPSILON)
    return centred * scale, scale


def normal_back(upward, normed, scale, gain):
    weighted = upward * gain
    first = jnp.mean(weighted, axis=-1, keepdims=True)
    second = jnp.mean(weighted * normed, axis=-1, keepdims=True)
    return (weighted - first - normed * second) * scale


def gelu_parts(hidden):
    phi = 0.5 * (1.0 + lax.erf(hidden * math.sqrt(0.5)))
    slope = phi + hidden * jnp.exp(-0.5 * hidden * hidden) * (1.0 / math.sqrt(2.0 * math.pi))
    return hidden * phi, slope


def to_rows(values):
    return lax.all_to_all(values, "tensor", split_axis=0, concat_axis=1, tiled=True)[0]


def to_places(values):
    return lax.all_to_all(values[None], "tensor", split_axis=1, concat_axis=0, tiled=True)


def plane_pairs(kind):
    pairs = []
    for side in range(2):
        for t in range(TENSORS):
            if kind == SWAP:
                target = (1 - side, t)
            elif kind == MAIN:
                target = (side, t ^ (1 + side))
            else:
                target = (side, t ^ (2 - side))
            pairs.append((side * TENSORS + t, target[0] * TENSORS + target[1]))
    return pairs


def send(values, kind):
    return lax.ppermute(values, PLANE, plane_pairs(kind))


def plus(*terms):
    total = terms[0].astype(F32)
    for term in terms[1:]:
        total = total + term.astype(F32)
    return total.astype(BF)


def gather_part(part, side):
    half = part.shape[0] // 2
    got = send(part, MAIN)
    piece = lax.dynamic_slice(got, (side * half, 0), (half, part.shape[1]))
    across = send(piece, DIAG)
    other = send(got, SWAP)
    rest = send(across, SWAP)
    lower = jnp.where(side == 0, across, rest)
    upper = jnp.where(side == 0, rest, across)
    return [part, got, other, jnp.concatenate([lower, upper], axis=0)], across


def sum_over_dp(values):
    count = lax.axis_size("dp")
    place = lax.axis_index("dp")
    width = values.shape[1]
    bits = []
    bit = 1
    while bit < count:
        pairs = [(d, d ^ bit) for d in range(count)]
        half = values.shape[0] // 2
        up = (place // bit) % 2
        away = lax.dynamic_slice(values, ((1 - up) * half, 0), (half, width))
        kept = lax.dynamic_slice(values, (up * half, 0), (half, width))
        values = plus(kept, lax.ppermute(away, "dp", pairs))
        bits.append((pairs, up))
        bit *= 2
    for pairs, up in reversed(bits):
        got = lax.ppermute(values, "dp", pairs)
        values = jnp.concatenate(
            [jnp.where(up == 0, values, got), jnp.where(up == 0, got, values)], axis=0
        )
    return values


def reduce_part(own, rest):
    outgoing = jnp.stack([own[2], rest[2], rest[3], rest[0]])
    got = send(outgoing, SWAP)
    main_rest = plus(rest[1], got[0])
    main_own = plus(own[1], got[1])
    across = plus(own[3], got[2])
    mine = plus(own[0], got[3])
    from_rest = send(main_rest, MAIN)
    main_own = plus(main_own, send(across, DIAG))
    from_own = send(main_own, MAIN)
    return plus(mine, from_own, send(from_rest, SWAP))


def finish_part(mine, side):
    mine = sum_over_dp(mine)
    other = send(mine, SWAP)
    low = jnp.where(side == 0, mine, other).astype(F32)
    high = jnp.where(side == 0, other, mine).astype(F32)
    return low, high


Q_ROWS = 128


def attend_forward_kernel(qkv_ref, down_ref, across_ref, o_ref, lse_ref):
    tokens, width = o_ref.shape

    def step(i, carry):
        rows = pl.ds(pl.multiple_of(i * Q_ROWS, Q_ROWS), Q_ROWS)
        same = down_ref[rows, :] == across_ref[...]
        for h in range(width // HEAD_DIM):
            at = h * HEAD_DIM
            q = qkv_ref[rows, at : at + HEAD_DIM]
            k = qkv_ref[:, width + at : width + at + HEAD_DIM]
            v = qkv_ref[:, 2 * width + at : 2 * width + at + HEAD_DIM]
            s = mm(q, k, 1, 1) * 0.125
            s = jnp.where(same, s, MASKED)
            top = jnp.max(s, axis=-1, keepdims=True)
            raised = jnp.exp(s - top)
            total = jnp.sum(raised, axis=-1, keepdims=True)
            weights = (raised * (1.0 / total)).astype(BF)
            o_ref[rows, at : at + HEAD_DIM] = mm(weights, v, 1, 0).astype(BF)
            lse_ref[rows, h : h + 1] = top + jnp.log(total)
        return carry

    lax.fori_loop(0, tokens // Q_ROWS, step, 0)


def attend_backward_kernel(qkv_ref, do_ref, lse_ref, down_ref, across_ref, d_ref, dk_ref, dv_ref):
    tokens, width = do_ref.shape
    dk_ref[...] = jnp.zeros_like(dk_ref)
    dv_ref[...] = jnp.zeros_like(dv_ref)

    def step(i, carry):
        rows = pl.ds(pl.multiple_of(i * Q_ROWS, Q_ROWS), Q_ROWS)
        same = down_ref[rows, :] == across_ref[...]
        for h in range(width // HEAD_DIM):
            at = h * HEAD_DIM
            q = qkv_ref[rows, at : at + HEAD_DIM]
            k = qkv_ref[:, width + at : width + at + HEAD_DIM]
            v = qkv_ref[:, 2 * width + at : 2 * width + at + HEAD_DIM]
            up = do_ref[rows, at : at + HEAD_DIM]
            s = mm(q, k, 1, 1) * 0.125
            s = jnp.where(same, s, MASKED)
            pr = jnp.exp(s - lse_ref[rows, h : h + 1])
            dp = mm(up, v, 1, 1)
            inner = jnp.sum(pr * dp, axis=-1, keepdims=True)
            ds = (pr * (dp - inner)).astype(BF)
            d_ref[rows, at : at + HEAD_DIM] = (mm(ds, k, 1, 0) * 0.125).astype(BF)
            dk_ref[:, at : at + HEAD_DIM] += mm(ds, q, 0, 0)
            dv_ref[:, at : at + HEAD_DIM] += mm(pr.astype(BF), up, 0, 0)
        return carry

    lax.fori_loop(0, tokens // Q_ROWS, step, 0)
    d_ref[:, width : 2 * width] = (dk_ref[...] * 0.125).astype(BF)
    d_ref[:, 2 * width :] = dv_ref[...].astype(BF)


def attend_cost(tokens, width, products):
    heads = width // HEAD_DIM
    return pl.CostEstimate(
        flops=2 * products * tokens * tokens * width,
        bytes_accessed=2 * 8 * tokens * width,
        transcendentals=heads * tokens * tokens,
    )


def attend_forward(qkv, down, across):
    tokens = qkv.shape[0]
    width = qkv.shape[1] // 3
    return pl.pallas_call(
        attend_forward_kernel,
        name="attend_forward",
        out_shape=(
            jax.ShapeDtypeStruct((tokens, width), BF),
            jax.ShapeDtypeStruct((tokens, width // HEAD_DIM), F32),
        ),
        compiler_params=pltpu.CompilerParams(vmem_limit_bytes=24 << 20),
        cost_estimate=attend_cost(tokens, width, 2),
    )(qkv, down, across)


def attend_backward(qkv, do, lse, down, across):
    tokens, width = do.shape
    return pl.pallas_call(
        attend_backward_kernel,
        name="attend_backward",
        out_shape=jax.ShapeDtypeStruct(qkv.shape, BF),
        scratch_shapes=[pltpu.VMEM((tokens, width), F32), pltpu.VMEM((tokens, width), F32)],
        compiler_params=pltpu.CompilerParams(vmem_limit_bytes=24 << 20),
        cost_estimate=attend_cost(tokens, width, 5),
    )(qkv, do, lse, down, across)


def anchors_kernel(dps, planes, x_ref, out_ref, near_send, near_recv, far_send, far_recv, own_sem):
    dp = lax.axis_index("dp")
    me = lax.axis_index("span") * TENSORS + lax.axis_index("tensor")

    def near(k):
        peer = lax.rem(me + k, planes)
        return {"span": peer // TENSORS, "tensor": lax.rem(peer, TENSORS)}

    def far(k):
        return {"dp": lax.rem(dp + k, dps)}

    barrier = pltpu.get_barrier_semaphore()
    for k in range(1, planes):
        pl.semaphore_signal(barrier, inc=1, device_id=near(k), device_id_type=MESH)
    for k in range(1, dps):
        pl.semaphore_signal(barrier, inc=1, device_id=far(k), device_id_type=MESH)
    pl.semaphore_wait(barrier, planes + dps - 2)

    own = pltpu.make_async_copy(x_ref, out_ref.at[dp, me], own_sem)
    own.start()

    def near_copy(k):
        return pltpu.make_async_remote_copy(
            src_ref=x_ref, dst_ref=out_ref.at[dp, me], send_sem=near_send.at[k],
            recv_sem=near_recv.at[k], device_id=near(k), device_id_type=MESH,
        )

    def far_copy(k):
        return pltpu.make_async_remote_copy(
            src_ref=out_ref.at[dp], dst_ref=out_ref.at[dp], send_sem=far_send.at[k],
            recv_sem=far_recv.at[k], device_id=far(k), device_id_type=MESH,
        )

    for k in range(1, planes):
        near_copy(k).start()
    own.wait()
    for k in range(1, planes):
        near_copy(k).wait()
    for k in range(1, dps):
        far_copy(k).start()
    for k in range(1, dps):
        far_copy(k).wait()


def gather_anchors(values):
    dps = lax.axis_size("dp")
    planes = lax.axis_size("span") * lax.axis_size("tensor")
    dma = pltpu.SemaphoreType.DMA
    vmem = pl.BlockSpec(memory_space=pltpu.VMEM)

    def body(*refs):
        anchors_kernel(dps, planes, *refs)

    return pl.pallas_call(
        body,
        name="gather_anchors",
        out_shape=jax.ShapeDtypeStruct((dps, planes) + values.shape, values.dtype),
        in_specs=[vmem],
        out_specs=vmem,
        scratch_shapes=[dma((planes,)), dma((planes,)), dma((dps,)), dma((dps,)), dma],
        compiler_params=pltpu.CompilerParams(collective_id=0, has_side_effects=True),
    )(values)


def total_kernel(
    dps, planes, x_ref, out_ref, parts, sums, one_send, one_recv, two_send, two_recv, three_send, three_recv
):
    dp = lax.axis_index("dp")
    me = lax.axis_index("span") * TENSORS + lax.axis_index("tensor")

    def near_peer(k):
        return lax.rem(me + k, planes)

    def near(k):
        peer = near_peer(k)
        return {"span": peer // TENSORS, "tensor": lax.rem(peer, TENSORS)}

    def far(k):
        return {"dp": lax.rem(dp + k, dps)}

    barrier = pltpu.get_barrier_semaphore()
    for k in range(1, planes):
        pl.semaphore_signal(barrier, inc=1, device_id=near(k), device_id_type=MESH)
    for k in range(1, dps):
        pl.semaphore_signal(barrier, inc=1, device_id=far(k), device_id_type=MESH)
    pl.semaphore_wait(barrier, planes + dps - 2)

    def one(k):
        return pltpu.make_async_remote_copy(
            src_ref=x_ref.at[near_peer(k)], dst_ref=parts.at[k], send_sem=one_send.at[k],
            recv_sem=one_recv.at[k], device_id=near(k), device_id_type=MESH,
        )

    def two(k):
        return pltpu.make_async_remote_copy(
            src_ref=sums.at[dp], dst_ref=sums.at[dp], send_sem=two_send.at[k],
            recv_sem=two_recv.at[k], device_id=far(k), device_id_type=MESH,
        )

    def three(k):
        return pltpu.make_async_remote_copy(
            src_ref=out_ref.at[me], dst_ref=out_ref.at[me], send_sem=three_send.at[k],
            recv_sem=three_recv.at[k], device_id=near(k), device_id_type=MESH,
        )

    for k in range(1, planes):
        one(k).start()
    for k in range(1, planes):
        one(k).wait()
    total = x_ref[me]
    for k in range(1, planes):
        total = total + parts[k]
    sums[dp] = total
    for k in range(1, dps):
        two(k).start()
    for k in range(1, dps):
        two(k).wait()
    total = sums[0]
    for k in range(1, dps):
        total = total + sums[k]
    out_ref[me] = total
    for k in range(1, planes):
        three(k).start()
    for k in range(1, planes):
        three(k).wait()


def total_over_all(flat):
    dps = lax.axis_size("dp")
    planes = lax.axis_size("span") * lax.axis_size("tensor")
    lanes = 128
    unit = planes * 8 * lanes
    size = flat.shape[0]
    padded = -(-size // unit) * unit
    flat = jnp.pad(flat, (0, padded - size)).reshape(planes, padded // (planes * lanes), lanes)
    dma = pltpu.SemaphoreType.DMA
    vmem = pl.BlockSpec(memory_space=pltpu.VMEM)

    def body(*refs):
        total_kernel(dps, planes, *refs)

    out = pl.pallas_call(
        body,
        name="total_over_all",
        out_shape=jax.ShapeDtypeStruct(flat.shape, F32),
        in_specs=[vmem],
        out_specs=vmem,
        scratch_shapes=[
            pltpu.VMEM(flat.shape, F32),
            pltpu.VMEM((dps,) + flat.shape[1:], F32),
            dma((planes,)), dma((planes,)), dma((dps,)), dma((dps,)), dma((planes,)), dma((planes,)),
        ],
        compiler_params=pltpu.CompilerParams(collective_id=1, has_side_effects=True),
    )(flat)
    return out.reshape(-1)[:size]


def layer_forward(x, seg, attn_w, ffn_w, vec):
    down, across = seg
    xb = x.astype(BF)
    cols = vec["heads"][0].shape[0]
    qkv, o, lse = [], [], []
    z1 = x + vec["pb"]
    for w, bias in zip(attn_w, vec["heads"]):
        qkv.append((mm(xb, w[:cols], 1, 1) + bias).astype(BF))
        mixed, total = attend_forward(qkv[-1], down, across)
        o.append(mixed)
        lse.append(total)
        z1 = z1 + mm(mixed, w[cols : cols + cols // 3], 1, 0)
    n1, r1 = normal_parts(z1)
    y = n1 * vec["g0"] + vec["s0"]
    yb = y.astype(BF)
    width = x.shape[1]
    act, slope = [], []
    z2 = y + vec["sb"]
    for w, bias in zip(ffn_w, vec["eb"]):
        hid = mm(yb, w[:width], 1, 0) + bias
        a, b = gelu_parts(hid)
        act.append(a.astype(BF))
        slope.append(b.astype(BF))
        z2 = z2 + mm(act[-1], w[width:], 1, 0)
    n2, r2 = normal_parts(z2)
    out = n2 * vec["g1"] + vec["s1"]
    return out, (xb, qkv, o, lse, n1, r1, yb, act, slope, n2, r2)


def halves(values, side):
    half = values.shape[1] // 2
    rows = values.shape[0]
    own = lax.dynamic_slice(values, (0, side * half), (rows, half))
    rest = lax.dynamic_slice(values, (0, (1 - side) * half), (rows, half))
    return own, rest


def ffn_backward(dout, ffn_w, vec, kept, side):
    xb, qkv, o, lse, n1, r1, yb, act, slope, n2, r2 = kept
    width = yb.shape[1]
    dz2 = normal_back(dout, n2, r2, vec["g1"])
    dgain1 = jnp.sum(dout * n2, axis=0)
    dshift1 = jnp.sum(dout, axis=0)
    dsb = jnp.sum(dz2, axis=0)
    dzb = dz2.astype(BF)
    yb_halves = halves(yb, side)
    parts = ([], [])
    dy = dz2
    deb = []
    for w, a, b in zip(ffn_w, act, slope):
        dhid = mm(dzb, w[width:], 1, 1) * b.astype(F32)
        deb.append(jnp.sum(dhid, axis=0))
        dhb = dhid.astype(BF)
        dy = dy + mm(dhb, w[:width], 1, 1)
        for part, y_half, a_half in zip(parts, yb_halves, halves(a, side)):
            part.append((mm(y_half, dhb, 0, 0).astype(BF), mm(a_half, dzb, 0, 0).astype(BF)))
    return dy, parts, {"g1": dgain1, "s1": dshift1, "sb": dsb, "eb": jnp.stack(deb)}


def attn_backward(dy, seg, attn_w, vec, kept, side):
    xb, qkv, o, lse, n1, r1, yb, act, slope, n2, r2 = kept
    down, across = seg
    cols = vec["heads"][0].shape[0]
    dz1 = normal_back(dy, n1, r1, vec["g0"])
    dgain0 = jnp.sum(dy * n1, axis=0)
    dshift0 = jnp.sum(dy, axis=0)
    dpb = jnp.sum(dz1, axis=0)
    da = dz1.astype(BF)
    x_halves = halves(xb, side)
    da_halves = halves(da, side)
    parts = ([], [])
    dhead = []
    dx = dz1
    for w, qkv_j, o_j, lse_j in zip(attn_w, qkv, o, lse):
        do = mm(da, w[cols : cols + cols // 3], 1, 1).astype(BF)
        d = attend_backward(qkv_j, do, lse_j, down, across)
        dx = dx + mm(d, w[:cols], 1, 0)
        dhead.append(jnp.sum(d.astype(F32), axis=0))
        for part, x_half, da_half in zip(parts, x_halves, da_halves):
            top = mm(d, x_half, 0, 0).astype(BF)
            low = mm(o_j, da_half, 0, 0).astype(BF)
            part.append((top, low))
    small = {"g0": dgain0, "s0": dshift0, "pb": dpb, "heads": jnp.stack(dhead)}
    return dx, parts, small


def pack_ffn(parts):
    return [[jnp.concatenate([e, s], axis=0) for e, s in part] for part in parts]


def pack_attn(parts):
    packed = []
    for part in parts:
        rows = []
        for top, low in part:
            whole = jnp.concatenate([top, low], axis=0)
            half = whole.shape[0] // 2
            rows.append(jnp.concatenate([whole[:half], whole[half:]], axis=1))
        packed.append(rows)
    return packed


def unpack_ffn(low, high):
    rows = low.shape[0] // 2
    expand = jnp.concatenate([low[:rows], high[:rows]], axis=0)
    shrink = jnp.concatenate([low[rows:], high[rows:]], axis=0)
    return expand, shrink


def unpack_attn(low, high):
    half = low.shape[1] // 2
    upper = jnp.concatenate([low[:, :half], high[:, :half]], axis=1)
    lower = jnp.concatenate([low[:, half:], high[:, half:]], axis=1)
    cols = low.shape[0] // 2
    heads = jnp.stack([upper[:cols], upper[cols:], lower[:cols]])
    return jnp.swapaxes(heads, 1, 2), lower[cols:]


VECTORS = ("pb", "g0", "g1", "s0", "s1", "sb")


def shards(
    layer_input, skip_tokens, backbone_cotangent, head_cotangent, segment_lengths, pair_index,
    w_heads, heads_bias, w_project, project_bias, norm_gain, norm_shift,
    w_expand, expand_bias, w_shrink, shrink_bias,
):
    side = lax.axis_index("span")
    mine = lax.axis_index("tensor")
    width = layer_input.shape[-1]
    head_cols = w_heads.shape[-1]
    ff_cols = w_expand.shape[-1]

    def attn_rows(l):
        heads = jnp.swapaxes(w_heads[l], 1, 2).reshape(3 * head_cols, width)
        return jnp.concatenate([heads, w_project[l]], axis=0)

    def ffn_rows(l):
        return jnp.concatenate([w_expand[l], w_shrink[l]], axis=0)

    bias_rows = jnp.concatenate([heads_bias.reshape(1, 4 * head_cols), expand_bias], axis=0)
    bias_rows = jnp.pad(bias_rows, ((0, 32 - bias_rows.shape[0]), (0, 0)))
    attn_rows_count = 4 * head_cols

    attn_w0, mark = gather_part(jnp.concatenate([attn_rows(0), bias_rows], axis=0), side)
    x = to_rows(layer_input[0])
    payload, mark = lax.optimization_barrier((ffn_rows(0), mark))
    ffn_w0, mark = gather_part(payload, side)
    payload, mark = lax.optimization_barrier(
        (jnp.concatenate([attn_rows(1), ffn_rows(1)], axis=0), mark)
    )
    w1, mark = gather_part(payload, side)
    attn_w1 = [w[:attn_rows_count] for w in w1]
    ffn_w1 = [w[attn_rows_count:] for w in w1]

    skip = to_rows(skip_tokens[0])
    backbone_cot = to_rows(backbone_cotangent[0])
    head_cot = to_rows(head_cotangent[0])
    tokens = x.shape[0]

    biases = [w[attn_rows_count : attn_rows_count + 3].astype(F32) for w in attn_w0]

    def vectors(l):
        heads = []
        for b in biases:
            own = b[0].reshape(2, 2, head_cols)[l]
            heads.append(jnp.concatenate([own[0], jnp.zeros_like(own[0]), own[1]]))
        return {
            "heads": heads, "eb": [b[1 + l] for b in biases], "pb": project_bias[l].astype(F32),
            "g0": norm_gain[l, 0].astype(F32), "g1": norm_gain[l, 1].astype(F32),
            "s0": norm_shift[l, 0].astype(F32), "s1": norm_shift[l, 1].astype(F32),
            "sb": shrink_bias[l].astype(F32),
        }

    lengths = lax.dynamic_index_in_dim(segment_lengths[0], mine, 0, keepdims=False)
    span_count = lengths.shape[0]
    starts = jnp.cumsum(lengths) - lengths
    row_length = jnp.sum(lengths)
    places = jnp.arange(tokens, dtype=jnp.int32)
    counted = jnp.sum((places[:, None] >= starts[None, :]).astype(jnp.int32), axis=-1) - 1
    segment = jnp.where(places < row_length, counted, span_count)
    seg = (segment[:, None], segment[None, :])
    valid = (places < row_length).astype(F32)[:, None]
    picker = (starts[:, None] == places[None, :]).astype(F32)
    first = jnp.sum(picker, axis=0)[:, None] > 0

    vec0, vec1 = vectors(0), vectors(1)
    backbone, kept0 = layer_forward(x.astype(F32), seg, attn_w0, ffn_w0, vec0)
    cls = mm(picker.astype(BF), backbone.astype(BF), 1, 0).astype(BF)
    anchors = gather_anchors(cls)
    dp_count = lax.axis_size("dp")
    pair_count = lax.axis_size("span")
    vector_count = dp_count * TENSORS * span_count
    anchors = anchors.reshape(dp_count, pair_count, TENSORS * span_count, width)
    anchors = jnp.swapaxes(anchors, 0, 1).reshape(pair_count, vector_count, width)

    head_in = jnp.where(first, backbone, skip.astype(F32))
    head, kept1 = layer_forward(head_in, seg, attn_w1, ffn_w1, vec1)

    root = math.sqrt(width)
    logits = mm(anchors[0], anchors[1], 1, 1) / root
    columns = jnp.arange(vector_count, dtype=jnp.int32)
    target = (pair_index[:, None] == columns[None, :]).astype(F32)
    lse_rows = jax.nn.logsumexp(logits, axis=1)
    lse_cols = jax.nn.logsumexp(logits, axis=0)
    dlogits = LOSS_WEIGHT * (
        jnp.exp(logits - lse_rows[:, None]) + jnp.exp(logits - lse_cols[None, :]) - 2.0 * target
    )
    span_loss = (jnp.sum(lse_rows) + jnp.sum(lse_cols) - 2.0 * jnp.sum(target * logits)) / (
        2 * vector_count
    )
    own = (lax.axis_index("dp") * TENSORS + mine) * span_count
    wanted = jnp.where(side == 0, dlogits, dlogits.T)
    wanted = lax.dynamic_slice(wanted, (own, 0), (span_count, vector_count))
    other = lax.dynamic_index_in_dim(anchors, 1 - side, 0, keepdims=False).astype(F32)
    dcls = jnp.dot(wanted, other, precision=HIGHEST) / root

    dy1, ffn_parts1, small1 = ffn_backward(head_cot.astype(F32) * valid, ffn_w1, vec1, kept1, side)
    du, attn_parts1, more1 = attn_backward(dy1, seg, attn_w1, vec1, kept1, side)
    small1.update(more1)
    grad_skip = jnp.where(first, 0.0, du).astype(BF)
    attn_packed = pack_attn(attn_parts1)
    ffn_packed = pack_ffn(ffn_parts1)
    packed1 = [
        [jnp.concatenate([a, f], axis=0) for a, f in zip(a_part, f_part)]
        for a_part, f_part in zip(attn_packed, ffn_packed)
    ]
    sum1 = reduce_part(*packed1)

    seed = backbone_cot.astype(F32) * valid + jnp.where(first, du, 0.0)
    seed = seed + jnp.dot(picker.T, dcls, precision=HIGHEST)
    dy0, ffn_parts0, small0 = ffn_backward(seed, ffn_w0, vec0, kept0, side)
    ffn_sum0 = reduce_part(*pack_ffn(ffn_parts0))
    dx, attn_parts0, more0 = attn_backward(dy0, seg, attn_w0, vec0, kept0, side)
    small0.update(more0)
    attn_sum0 = reduce_part(*pack_attn(attn_parts0))

    order = jnp.where(
        side == 0,
        jnp.stack([mine, mine ^ 1, mine ^ 2, mine ^ 3]),
        jnp.stack([mine, mine ^ 2, mine ^ 1, mine ^ 3]),
    )
    chosen = (order[None, :] == jnp.arange(TENSORS, dtype=order.dtype)[:, None]).astype(F32)

    def placed(values):
        return jnp.sum(chosen[:, :, None] * values[None], axis=1)

    flat = []
    for small in (small0, small1):
        flat += [small[k] for k in VECTORS]
        flat += [placed(small["heads"]).reshape(-1), placed(small["eb"]).reshape(-1)]
    sizes = [f.shape[0] for f in flat]
    total = total_over_all(jnp.concatenate(flat))
    cuts = []
    at = 0
    for size in sizes:
        cuts.append(total[at : at + size])
        at += size
    count = len(VECTORS) + 2
    sums = [dict(zip(VECTORS + ("heads", "eb"), cuts[l * count : (l + 1) * count])) for l in range(2)]

    def local(values):
        size = values.shape[0] // TENSORS
        return lax.dynamic_slice(values, (mine * size,), (size,))

    hb, eb = [], []
    for s in sums:
        h = local(s["heads"]).reshape(3, head_cols)
        hb.append(jnp.stack([h[0], h[2]]))
        eb.append(local(s["eb"]))

    low1, high1 = finish_part(sum1, side)
    half_rows = attn_rows_count // 2
    gh1, gp1 = unpack_attn(low1[:half_rows], high1[:half_rows])
    ge1, gs1 = unpack_ffn(low1[half_rows:], high1[half_rows:])
    ge0, gs0 = unpack_ffn(*finish_part(ffn_sum0, side))
    gh0, gp0 = unpack_attn(*finish_part(attn_sum0, side))

    return (
        to_places((backbone * valid).astype(BF))[None],
        to_places((head * valid).astype(BF))[None],
        span_loss,
        to_places(dx.astype(BF))[None],
        to_places(grad_skip)[None],
        jnp.stack([gh0, gh1]),
        jnp.stack(hb),
        jnp.stack([gp0, gp1]),
        jnp.stack([s["pb"] for s in sums]),
        jnp.stack([jnp.stack([s["g0"], s["g1"]]) for s in sums]),
        jnp.stack([jnp.stack([s["s0"], s["s1"]]) for s in sums]),
        jnp.stack([ge0, ge1]),
        jnp.stack(eb),
        jnp.stack([gs0, gs1]),
        jnp.stack([s["sb"] for s in sums]),
    )


def solution(mesh):
    rows = P("span", "dp", "tensor", None)
    in_specs = (
        rows, rows, rows, rows, P("span", "dp", None), P(),
        P(None, None, None, "tensor"), P(None, None, "tensor"), P(None, "tensor", None),
        P(), P(), P(), P(None, None, "tensor"), P(None, "tensor"), P(None, "tensor", None), P(),
    )
    out_specs = (
        rows, rows, P(), rows, rows,
        P(None, None, None, "tensor"), P(None, None, "tensor"), P(None, "tensor", None),
        P(), P(), P(), P(None, None, "tensor"), P(None, "tensor"), P(None, "tensor", None), P(),
    )
    return jax.shard_map(shards, mesh=mesh, in_specs=in_specs, out_specs=out_specs, check_vma=False)
```

```python
import math

import jax
import jax.numpy as jnp
from jax import lax
from jax.experimental import pallas as pl
from jax.experimental.pallas import tpu as pltpu
from jax.sharding import PartitionSpec as P

HEAD_DIM = 64
EPSILON = 1e-12
LOSS_WEIGHT = 8.0
HIGHEST = lax.Precision.HIGHEST
MASKED = -1e30
BF = jnp.bfloat16
F32 = jnp.float32
PLANE = ("span", "tensor")
MESH = pl.DeviceIdType.MESH
TENSORS = 4
MAIN, DIAG, SWAP = "main", "diag", "swap"


def mm(a, b, ca, cb):
    return lax.dot_general(a, b, (((ca,), (cb,)), ((), ())), preferred_element_type=F32)


def normal_parts(values):
    centred = values - jnp.mean(values, axis=-1, keepdims=True)
    spread = jnp.mean(centred * centred, axis=-1, keepdims=True)
    scale = lax.rsqrt(spread + EPSILON)
    return centred * scale, scale


def normal_back(upward, normed, scale, gain):
    weighted = upward * gain
    first = jnp.mean(weighted, axis=-1, keepdims=True)
    second = jnp.mean(weighted * normed, axis=-1, keepdims=True)
    return (weighted - first - normed * second) * scale


def gelu_parts(hidden):
    phi = 0.5 * (1.0 + lax.erf(hidden * math.sqrt(0.5)))
    slope = phi + hidden * jnp.exp(-0.5 * hidden * hidden) * (1.0 / math.sqrt(2.0 * math.pi))
    return hidden * phi, slope


def plane_pairs(kind):
    pairs = []
    for side in range(2):
        for t in range(TENSORS):
            if kind == SWAP:
                target = (1 - side, t)
            elif kind == MAIN:
                target = (side, t ^ (1 + side))
            else:
                target = (side, t ^ (2 - side))
            pairs.append((side * TENSORS + t, target[0] * TENSORS + target[1]))
    return pairs


def send(values, kind):
    return lax.ppermute(values, PLANE, plane_pairs(kind))


def plus(*terms):
    total = terms[0].astype(F32)
    for term in terms[1:]:
        total = total + term.astype(F32)
    return total.astype(BF)


def pick(side, zero, one):
    return jnp.where(side == 0, zero, one)


def tie(*values):
    return lax.optimization_barrier(values)


def gather_part(first, second, side):
    got_first, got_second = send(first, MAIN), send(second, MAIN)
    across = send(pick(side, got_first, got_second), DIAG)
    other_first, other_second = send(got_first, SWAP), send(got_second, SWAP)
    rest = send(across, SWAP)
    blocks = [
        (first, second), (got_first, got_second), (other_first, other_second),
        (pick(side, across, rest), pick(side, rest, across)),
    ]
    return blocks, across


def reduce_outgoing(blocks, side):
    return (
        blocks[2][0], blocks[2][1], pick(side, blocks[3][1], blocks[3][0]), pick(side, blocks[0][1], blocks[0][0])
    )


def reduce_swapped(blocks, outgoing, side):
    got = [send(o, SWAP) for o in outgoing]
    first = plus(blocks[1][0], got[0])
    second = plus(blocks[1][1], got[1])
    main_rest = pick(side, second, first)
    main_own = pick(side, first, second)
    across = plus(pick(side, blocks[3][0], blocks[3][1]), got[2])
    mine = plus(pick(side, blocks[0][0], blocks[0][1]), got[3])
    return main_rest, main_own, across, mine


def reduce_across(main_own, across):
    return plus(main_own, send(across, DIAG))


def finish_part(mine, side):
    other = send(mine, SWAP)
    return pick(side, mine, other).astype(F32), pick(side, other, mine).astype(F32)


Q_ROWS = 128


def attend_forward_kernel(qk_ref, v_ref, down_ref, across_ref, o_ref, lse_ref):
    tokens, width = o_ref.shape

    def step(i, carry):
        rows = pl.ds(pl.multiple_of(i * Q_ROWS, Q_ROWS), Q_ROWS)
        same = down_ref[rows, :] == across_ref[...]
        for h in range(width // HEAD_DIM):
            at = h * HEAD_DIM
            q = qk_ref[rows, at : at + HEAD_DIM]
            k = qk_ref[:, width + at : width + at + HEAD_DIM]
            v = v_ref[:, at : at + HEAD_DIM]
            s = mm(q, k, 1, 1) * 0.125
            s = jnp.where(same, s, MASKED)
            top = jnp.max(s, axis=-1, keepdims=True)
            raised = jnp.exp(s - top)
            total = jnp.sum(raised, axis=-1, keepdims=True)
            weights = (raised * (1.0 / total)).astype(BF)
            o_ref[rows, at : at + HEAD_DIM] = mm(weights, v, 1, 0).astype(BF)
            lse_ref[rows, h : h + 1] = top + jnp.log(total)
        return carry

    lax.fori_loop(0, tokens // Q_ROWS, step, 0)


def attend_backward_kernel(
    qk_ref, v_ref, do_ref, lse_ref, down_ref, across_ref, dqk_ref, dv_out_ref, dk_ref, dv_ref
):
    tokens, width = do_ref.shape
    dk_ref[...] = jnp.zeros_like(dk_ref)
    dv_ref[...] = jnp.zeros_like(dv_ref)

    def step(i, carry):
        rows = pl.ds(pl.multiple_of(i * Q_ROWS, Q_ROWS), Q_ROWS)
        same = down_ref[rows, :] == across_ref[...]
        for h in range(width // HEAD_DIM):
            at = h * HEAD_DIM
            q = qk_ref[rows, at : at + HEAD_DIM]
            k = qk_ref[:, width + at : width + at + HEAD_DIM]
            v = v_ref[:, at : at + HEAD_DIM]
            up = do_ref[rows, at : at + HEAD_DIM]
            s = mm(q, k, 1, 1) * 0.125
            s = jnp.where(same, s, MASKED)
            pr = jnp.exp(s - lse_ref[rows, h : h + 1])
            dp = mm(up, v, 1, 1)
            inner = jnp.sum(pr * dp, axis=-1, keepdims=True)
            ds = (pr * (dp - inner)).astype(BF)
            dqk_ref[rows, at : at + HEAD_DIM] = (mm(ds, k, 1, 0) * 0.125).astype(BF)
            dk_ref[:, at : at + HEAD_DIM] += mm(ds, q, 0, 0)
            dv_ref[:, at : at + HEAD_DIM] += mm(pr.astype(BF), up, 0, 0)
        return carry

    lax.fori_loop(0, tokens // Q_ROWS, step, 0)
    dqk_ref[:, width:] = (dk_ref[...] * 0.125).astype(BF)
    dv_out_ref[...] = dv_ref[...].astype(BF)


def attend_cost(tokens, width, products):
    heads = width // HEAD_DIM
    return pl.CostEstimate(
        flops=2 * products * tokens * tokens * width,
        bytes_accessed=2 * 8 * tokens * width,
        transcendentals=heads * tokens * tokens,
    )


def attend_forward(qk, v, down, across):
    tokens, width = v.shape
    return pl.pallas_call(
        attend_forward_kernel,
        name="attend_forward",
        out_shape=(
            jax.ShapeDtypeStruct((tokens, width), BF),
            jax.ShapeDtypeStruct((tokens, width // HEAD_DIM), F32),
        ),
        compiler_params=pltpu.CompilerParams(vmem_limit_bytes=24 << 20),
        cost_estimate=attend_cost(tokens, width, 2),
    )(qk, v, down, across)


def attend_backward(qk, v, do, lse, down, across):
    tokens, width = do.shape
    return pl.pallas_call(
        attend_backward_kernel,
        name="attend_backward",
        out_shape=(jax.ShapeDtypeStruct(qk.shape, BF), jax.ShapeDtypeStruct(v.shape, BF)),
        scratch_shapes=[pltpu.VMEM((tokens, width), F32), pltpu.VMEM((tokens, width), F32)],
        compiler_params=pltpu.CompilerParams(vmem_limit_bytes=24 << 20),
        cost_estimate=attend_cost(tokens, width, 5),
    )(qk, v, do, lse, down, across)


def anchors_kernel(dps, planes, x_ref, out_ref, near_send, near_recv, far_send, far_recv, own_sem):
    dp = lax.axis_index("dp")
    me = lax.axis_index("span") * TENSORS + lax.axis_index("tensor")

    def near(k):
        peer = lax.rem(me + k, planes)
        return {"span": peer // TENSORS, "tensor": lax.rem(peer, TENSORS)}

    def far(k):
        return {"dp": lax.rem(dp + k, dps)}

    barrier = pltpu.get_barrier_semaphore()
    for k in range(1, planes):
        pl.semaphore_signal(barrier, inc=1, device_id=near(k), device_id_type=MESH)
    for k in range(1, dps):
        pl.semaphore_signal(barrier, inc=1, device_id=far(k), device_id_type=MESH)
    pl.semaphore_wait(barrier, planes + dps - 2)

    own = pltpu.make_async_copy(x_ref, out_ref.at[dp, me], own_sem)
    own.start()

    def near_copy(k):
        return pltpu.make_async_remote_copy(
            src_ref=x_ref, dst_ref=out_ref.at[dp, me], send_sem=near_send.at[k],
            recv_sem=near_recv.at[k], device_id=near(k), device_id_type=MESH,
        )

    def far_copy(k):
        return pltpu.make_async_remote_copy(
            src_ref=out_ref.at[dp], dst_ref=out_ref.at[dp], send_sem=far_send.at[k],
            recv_sem=far_recv.at[k], device_id=far(k), device_id_type=MESH,
        )

    for k in range(1, planes):
        near_copy(k).start()
    own.wait()
    for k in range(1, planes):
        near_copy(k).wait()
    for k in range(1, dps):
        far_copy(k).start()
    for k in range(1, dps):
        far_copy(k).wait()


def gather_anchors(values):
    dps = lax.axis_size("dp")
    planes = lax.axis_size("span") * lax.axis_size("tensor")
    dma = pltpu.SemaphoreType.DMA
    vmem = pl.BlockSpec(memory_space=pltpu.VMEM)

    def body(*refs):
        anchors_kernel(dps, planes, *refs)

    return pl.pallas_call(
        body,
        name="gather_anchors",
        out_shape=jax.ShapeDtypeStruct((dps, planes) + values.shape, values.dtype),
        in_specs=[vmem],
        out_specs=vmem,
        scratch_shapes=[dma((planes,)), dma((planes,)), dma((dps,)), dma((dps,)), dma],
        compiler_params=pltpu.CompilerParams(collective_id=0, has_side_effects=True),
    )(values)


VECTORS = ("pb", "g0", "g1", "s0", "s1", "sb")
ROWS_PER_CHUNK = 4
CHUNKS_PER_LAYER = 4
FAR_LANE = 256


def total_kernel(dps, planes, inputs, out_ref, x_ref, parts, sums, sems):
    one_send, one_recv, two_send, two_recv, three_send, three_recv = sems
    dp = lax.axis_index("dp")
    side = lax.axis_index("span")
    tensor = lax.axis_index("tensor")
    me = side * TENSORS + tensor
    flip_one = tensor + 1 - 2 * lax.rem(tensor, 2)
    flip_two = tensor + 2 - 4 * (tensor // 2)
    order = (
        tensor, flip_one + side * (flip_two - flip_one), flip_two + side * (flip_one - flip_two),
        TENSORS - 1 - tensor,
    )

    x_ref[...] = jnp.zeros_like(x_ref)
    for l, (vectors, eb, dq, dv) in enumerate(inputs):
        base = l * CHUNKS_PER_LAYER
        for j in range(TENSORS):
            row = pl.ds(order[j], 1)
            cols = dq[j].shape[1]
            x_ref[base, row, :] = eb[j][...]
            x_ref[base + 1, row, :cols] = dq[j][...]
            x_ref[base + 1, row, FAR_LANE : FAR_LANE + cols] = dv[j][...]
        for i, vector in enumerate(vectors):
            at = 2 * ROWS_PER_CHUNK + i
            x_ref[base + at // ROWS_PER_CHUNK, pl.ds(at % ROWS_PER_CHUNK, 1), :] = vector[...]

    def near_peer(k):
        return lax.rem(me + k, planes)

    def near(k):
        peer = near_peer(k)
        return {"span": peer // TENSORS, "tensor": lax.rem(peer, TENSORS)}

    def far(k):
        return {"dp": lax.rem(dp + k, dps)}

    barrier = pltpu.get_barrier_semaphore()
    for k in range(1, planes):
        pl.semaphore_signal(barrier, inc=1, device_id=near(k), device_id_type=MESH)
    for k in range(1, dps):
        pl.semaphore_signal(barrier, inc=1, device_id=far(k), device_id_type=MESH)
    pl.semaphore_wait(barrier, planes + dps - 2)

    def one(k):
        return pltpu.make_async_remote_copy(
            src_ref=x_ref.at[near_peer(k)], dst_ref=parts.at[k], send_sem=one_send.at[k],
            recv_sem=one_recv.at[k], device_id=near(k), device_id_type=MESH,
        )

    def two(k):
        return pltpu.make_async_remote_copy(
            src_ref=sums.at[dp], dst_ref=sums.at[dp], send_sem=two_send.at[k],
            recv_sem=two_recv.at[k], device_id=far(k), device_id_type=MESH,
        )

    def three(k):
        return pltpu.make_async_remote_copy(
            src_ref=out_ref.at[me], dst_ref=out_ref.at[me], send_sem=three_send.at[k],
            recv_sem=three_recv.at[k], device_id=near(k), device_id_type=MESH,
        )

    for k in range(1, planes):
        one(k).start()
    for k in range(1, planes):
        one(k).wait()
    total = x_ref[me]
    for k in range(1, planes):
        total = total + parts[k]
    sums[dp] = total
    for k in range(1, dps):
        two(k).start()
    for k in range(1, dps):
        two(k).wait()
    total = sums[0]
    for k in range(1, dps):
        total = total + sums[k]
    out_ref[me] = total
    for k in range(1, planes):
        three(k).start()
    for k in range(1, planes):
        three(k).wait()


def total_over_all(layers):
    dps = lax.axis_size("dp")
    planes = lax.axis_size("span") * lax.axis_size("tensor")
    flat, tree = jax.tree.flatten(layers)
    width = layers[0][0][0].shape[1]
    shape = (planes, ROWS_PER_CHUNK, width)
    dma = pltpu.SemaphoreType.DMA
    vmem = pl.BlockSpec(memory_space=pltpu.VMEM)

    def body(*refs):
        inputs = jax.tree.unflatten(tree, refs[: len(flat)])
        out_ref, x_ref, parts, sums = refs[len(flat) : len(flat) + 4]
        total_kernel(dps, planes, inputs, out_ref, x_ref, parts, sums, refs[len(flat) + 4 :])

    return pl.pallas_call(
        body,
        name="total_over_all",
        out_shape=jax.ShapeDtypeStruct(shape, F32),
        in_specs=[vmem] * len(flat),
        out_specs=vmem,
        scratch_shapes=[
            pltpu.VMEM(shape, F32),
            pltpu.VMEM(shape, F32),
            pltpu.VMEM((dps,) + shape[1:], F32),
            dma((planes,)), dma((planes,)), dma((dps,)), dma((dps,)), dma((planes,)), dma((planes,)),
        ],
        compiler_params=pltpu.CompilerParams(collective_id=1, has_side_effects=True),
    )(*flat)


def to_rows(values):
    return lax.all_to_all(values, "tensor", split_axis=0, concat_axis=0, tiled=True).reshape(
        -1, values.shape[-1]
    )


def to_places(values):
    blocks = values.reshape(TENSORS, -1, values.shape[-1])
    return lax.all_to_all(blocks, "tensor", split_axis=0, concat_axis=0, tiled=True)


def layer_forward(x, seg, attn_w, ffn_w, vec):
    down, across = seg
    xb = x.astype(BF)
    cols = vec["qb"][0].shape[0]
    q_k, v, o, lse = [], [], [], []
    z1 = x + vec["pb"]
    for (first, second), qb, vb in zip(attn_w, vec["qb"], vec["vb"]):
        bias = jnp.concatenate([qb, jnp.zeros_like(qb)])
        q_k.append((mm(xb, first[: 2 * cols], 1, 1) + bias).astype(BF))
        v.append((mm(xb, second[:cols], 1, 1) + vb).astype(BF))
        mixed, total = attend_forward(q_k[-1], v[-1], down, across)
        o.append(mixed)
        lse.append(total)
        z1 = z1 + mm(mixed, second[cols : 2 * cols], 1, 0)
    n1, r1 = normal_parts(z1)
    y = n1 * vec["g0"] + vec["s0"]
    yb = y.astype(BF)
    act, slope = [], []
    z2 = y + vec["sb"]
    for (first, second), bias in zip(ffn_w, vec["eb"]):
        a, b = gelu_parts(mm(yb, first, 1, 0) + bias)
        act.append(a.astype(BF))
        slope.append(b.astype(BF))
        z2 = z2 + mm(act[-1], second, 1, 0)
    n2, r2 = normal_parts(z2)
    out = n2 * vec["g1"] + vec["s1"]
    return out, (xb, q_k, v, o, lse, n1, r1, yb, act, slope, n2, r2)


def total_rows(values):
    return jnp.sum(values.astype(F32), axis=0, keepdims=True)


def ffn_backward(dout, ffn_w, vec, kept, hook):
    xb, q_k, v, o, lse, n1, r1, yb, act, slope, n2, r2 = kept
    dz2 = normal_back(dout, n2, r2, vec["g1"])
    small = {"g1": total_rows(dout * n2), "s1": total_rows(dout), "sb": total_rows(dz2), "eb": []}
    dz2 = hook("seeded", dz2)
    dzb = dz2.astype(BF)
    dy = dz2
    hidden = []
    for (first, second), b in zip(ffn_w, slope):
        dhid = mm(dzb, second, 1, 1) * b.astype(F32)
        small["eb"].append(total_rows(dhid))
        hidden.append(dhid.astype(BF))
        dy = dy + mm(hidden[-1], first, 1, 1)
    dy = hook("hidden", dy)
    blocks = [(mm(yb, h, 0, 0).astype(BF), mm(a, dzb, 0, 0).astype(BF)) for h, a in zip(hidden, act)]
    return dy, blocks, small


def attn_backward(dy, seg, attn_w, vec, kept, hook):
    xb, q_k, v, o, lse, n1, r1, yb, act, slope, n2, r2 = kept
    down, across = seg
    cols = vec["qb"][0].shape[0]
    dz1 = normal_back(dy, n1, r1, vec["g0"])
    small = {"g0": total_rows(dy * n1), "s0": total_rows(dy), "pb": total_rows(dz1), "dq": [], "dv": []}
    dz1 = hook("normed", dz1)
    da = dz1.astype(BF)
    dx = dz1
    grads = []
    for j, (first, second) in enumerate(attn_w):
        do = mm(da, second[cols : 2 * cols], 1, 1).astype(BF)
        dqk, dv = attend_backward(q_k[j], v[j], do, lse[j], down, across)
        dx = dx + mm(dqk, first[: 2 * cols], 1, 0) + mm(dv, second[:cols], 1, 0)
        small["dq"].append(total_rows(dqk[:, :cols]))
        small["dv"].append(total_rows(dv))
        grads.append((dqk, dv))
        if j == 2:
            da, dx = hook("three", (da, dx))
    blocks = [
        (
            mm(dqk, xb, 0, 0).astype(BF),
            jnp.concatenate([mm(dv, xb, 0, 0), mm(o_j, da, 0, 0)], axis=0).astype(BF),
        )
        for (dqk, dv), o_j in zip(grads, o)
    ]
    return dx, blocks, small


def attn_unpack(first, second):
    cols = first.shape[0] // 2
    heads = jnp.stack([first[:cols], first[cols:], second[:cols]])
    return jnp.swapaxes(heads, 1, 2), second[cols:]


class Reduction:
    def __init__(self, side):
        self.side = side

    def start(self, value, blocks):
        self.blocks = blocks
        value, *self.outgoing = tie(value, *reduce_outgoing(blocks, self.side))
        return value

    def swapped(self, value):
        value, self.main_rest, self.main_own, self.across, self.mine = tie(
            value, *reduce_swapped(self.blocks, self.outgoing, self.side)
        )
        self.from_rest = send(self.main_rest, MAIN)
        return value

    def crossed(self, value):
        value, self.main_own = tie(value, reduce_across(self.main_own, self.across))
        self.from_own = send(self.main_own, MAIN)
        self.from_peer = send(self.from_rest, SWAP)
        return value

    def summed(self, value):
        value, self.total = tie(value, plus(self.mine, self.from_own, self.from_peer))
        return value


def shards(
    layer_input, skip_tokens, backbone_cotangent, head_cotangent, segment_lengths, pair_index,
    w_heads, heads_bias, w_project, project_bias, norm_gain, norm_shift,
    w_expand, expand_bias, w_shrink, shrink_bias,
):
    side = lax.axis_index("span")
    mine = lax.axis_index("tensor")
    width = layer_input.shape[-1]
    head_cols = w_heads.shape[-1]
    ff_cols = w_expand.shape[-1]

    extra = 16
    bias_rows = jnp.concatenate([heads_bias.reshape(1, 4 * head_cols), expand_bias], axis=0)
    bias_rows = jnp.pad(bias_rows, ((0, extra - bias_rows.shape[0]), (0, 0)))

    def attn_rows(l):
        heads = jnp.swapaxes(w_heads[l], 1, 2)
        first = heads[:2].reshape(2 * head_cols, width)
        return first, jnp.concatenate([heads[2], w_project[l]], axis=0)

    first, second = attn_rows(0)
    first = jnp.concatenate([first, bias_rows], axis=0)
    second = jnp.pad(second, ((0, extra), (0, 0)))
    attn_w0, mark = gather_part(first, second, side)
    x = to_rows(layer_input[0])
    first, second, mark = tie(w_expand[0], w_shrink[0], mark)
    ffn_w0, mark = gather_part(first, second, side)
    first, second, mark = tie(*attn_rows(1), mark)
    attn_w1, mark = gather_part(first, second, side)
    later_skip, mark = tie(skip_tokens[0], mark)
    skip = to_rows(later_skip)
    first, second, mark = tie(w_expand[1], w_shrink[1], mark)
    ffn_w1, mark = gather_part(first, second, side)
    later_head, later_backbone, mark = tie(head_cotangent[0], backbone_cotangent[0], mark)
    head_cot = to_rows(later_head)
    backbone_cot = to_rows(later_backbone)
    tokens = x.shape[0]

    biases = [first[2 * head_cols : 2 * head_cols + 3].astype(F32) for first, second in attn_w0]

    def vectors(l):
        heads = [b[0].reshape(2, 2, head_cols)[l] for b in biases]
        return {
            "qb": [h[0] for h in heads], "vb": [h[1] for h in heads],
            "eb": [b[1 + l] for b in biases], "pb": project_bias[l].astype(F32),
            "g0": norm_gain[l, 0].astype(F32), "g1": norm_gain[l, 1].astype(F32),
            "s0": norm_shift[l, 0].astype(F32), "s1": norm_shift[l, 1].astype(F32),
            "sb": shrink_bias[l].astype(F32),
        }

    lengths = lax.dynamic_index_in_dim(segment_lengths[0], mine, 0, keepdims=False)
    span_count = lengths.shape[0]
    starts = jnp.cumsum(lengths) - lengths
    row_length = jnp.sum(lengths)
    places = jnp.arange(tokens, dtype=jnp.int32)
    counted = jnp.sum((places[:, None] >= starts[None, :]).astype(jnp.int32), axis=-1) - 1
    segment = jnp.where(places < row_length, counted, span_count)
    seg = (segment[:, None], segment[None, :])
    valid = (places < row_length).astype(F32)[:, None]
    picker = (starts[:, None] == places[None, :]).astype(F32)
    first_place = jnp.sum(picker, axis=0)[:, None] > 0

    vec0, vec1 = vectors(0), vectors(1)
    backbone, kept0 = layer_forward(x.astype(F32), seg, attn_w0, ffn_w0, vec0)
    cls = mm(picker.astype(BF), backbone.astype(BF), 1, 0).astype(BF)
    anchors = gather_anchors(cls)
    dp_count = lax.axis_size("dp")
    pair_count = lax.axis_size("span")
    vector_count = dp_count * TENSORS * span_count
    anchors = anchors.reshape(dp_count, pair_count, TENSORS * span_count, width)
    anchors = jnp.swapaxes(anchors, 0, 1).reshape(pair_count, vector_count, width)

    head_in = jnp.where(first_place, backbone, skip.astype(F32))
    head, kept1 = layer_forward(head_in, seg, attn_w1, ffn_w1, vec1)

    root = math.sqrt(width)
    logits = mm(anchors[0], anchors[1], 1, 1) / root
    columns = jnp.arange(vector_count, dtype=jnp.int32)
    target = (pair_index[:, None] == columns[None, :]).astype(F32)
    lse_rows = jax.nn.logsumexp(logits, axis=1)
    lse_cols = jax.nn.logsumexp(logits, axis=0)
    dlogits = LOSS_WEIGHT * (
        jnp.exp(logits - lse_rows[:, None]) + jnp.exp(logits - lse_cols[None, :]) - 2.0 * target
    )
    span_loss = (jnp.sum(lse_rows) + jnp.sum(lse_cols) - 2.0 * jnp.sum(target * logits)) / (
        2 * vector_count
    )
    own = (lax.axis_index("dp") * TENSORS + mine) * span_count
    wanted = jnp.where(side == 0, dlogits, dlogits.T)
    wanted = lax.dynamic_slice(wanted, (own, 0), (span_count, vector_count))
    other = lax.dynamic_index_in_dim(anchors, 1 - side, 0, keepdims=False).astype(F32)
    dcls = jnp.dot(wanted, other, precision=HIGHEST) / root

    ffn1, attn1, ffn0, attn0 = (Reduction(side) for _ in range(4))

    def plain(name, value):
        return value

    dy, blocks, small1 = ffn_backward(head_cot.astype(F32) * valid, ffn_w1, vec1, kept1, plain)
    dy = ffn1.start(dy, blocks)

    def during_attn1(name, value):
        if name == "normed":
            return ffn1.swapped(value)
        return ffn1.crossed(value)

    du, blocks, more = attn_backward(dy, seg, attn_w1, vec1, kept1, during_attn1)
    small1.update(more)
    du = attn1.start(du, blocks)
    du = ffn1.summed(du)
    grad_skip = jnp.where(first_place, 0.0, du).astype(BF)

    seed = backbone_cot.astype(F32) * valid + jnp.where(first_place, du, 0.0)
    seed = seed + jnp.dot(picker.T, dcls, precision=HIGHEST)

    def during_ffn0(name, value):
        if name == "seeded":
            return attn1.swapped(value)
        return attn1.crossed(value)

    dy, blocks, small0 = ffn_backward(seed, ffn_w0, vec0, kept0, during_ffn0)
    dy = ffn0.start(dy, blocks)
    dy = attn1.summed(dy)
    ffn_total1, attn_total1 = lax.psum((ffn1.total, attn1.total), "dp")

    def during_attn0(name, value):
        if name == "normed":
            return ffn0.swapped(value)
        return ffn0.crossed(value)

    dx, blocks, more = attn_backward(dy, seg, attn_w0, vec0, kept0, during_attn0)
    small0.update(more)
    dx = attn0.start(dx, blocks)
    dx = ffn0.summed(dx)
    ffn_total0, ffn_total1, attn_total1 = tie(ffn0.total, ffn_total1, attn_total1)
    ffn_total0 = lax.psum(ffn_total0, "dp")

    rows0, rows1 = (
        ([small[k] for k in VECTORS], small["eb"], small["dq"], small["dv"]) for small in (small0, small1)
    )
    last = attn0.swapped(rows0[0][0])
    rows0[0][0] = last
    total = total_over_all((rows0, rows1))
    total = attn0.crossed(total)
    total = attn0.summed(total)
    attn_total0, ffn_total0 = tie(attn0.total, ffn_total0)
    attn_total0 = lax.psum(attn_total0, "dp")

    hb, eb, vector_sums = [], [], []
    for l in range(2):
        base = l * CHUNKS_PER_LAYER
        own = lax.dynamic_slice(total[base : base + 2], (0, mine, 0), (2, 1, width))[:, 0]
        eb.append(own[0])
        hb.append(jnp.stack([own[1, :head_cols], own[1, FAR_LANE : FAR_LANE + head_cols]]))
        rows = total[base + 2 : base + CHUNKS_PER_LAYER].reshape(-1, width)
        vector_sums.append({k: rows[i] for i, k in enumerate(VECTORS)})
    sums = vector_sums

    ge1, gs1 = finish_part(ffn_total1, side)
    gh1, gp1 = attn_unpack(*finish_part(attn_total1, side))
    ge0, gs0 = finish_part(ffn_total0, side)
    gh0, gp0 = attn_unpack(*finish_part(attn_total0, side))

    return (
        to_places((backbone * valid).astype(BF))[None],
        to_places((head * valid).astype(BF))[None],
        span_loss,
        to_places(dx.astype(BF))[None],
        to_places(grad_skip)[None],
        jnp.stack([gh0, gh1]),
        jnp.stack(hb),
        jnp.stack([gp0, gp1]),
        jnp.stack([s["pb"] for s in sums]),
        jnp.stack([jnp.stack([s["g0"], s["g1"]]) for s in sums]),
        jnp.stack([jnp.stack([s["s0"], s["s1"]]) for s in sums]),
        jnp.stack([ge0, ge1]),
        jnp.stack(eb),
        jnp.stack([gs0, gs1]),
        jnp.stack([s["sb"] for s in sums]),
    )


def solution(mesh):
    rows = P("span", "dp", "tensor", None)
    in_specs = (
        rows, rows, rows, rows, P("span", "dp", None), P(),
        P(None, None, None, "tensor"), P(None, None, "tensor"), P(None, "tensor", None),
        P(), P(), P(), P(None, None, "tensor"), P(None, "tensor"), P(None, "tensor", None), P(),
    )
    out_specs = (
        rows, rows, P(), rows, rows,
        P(None, None, None, "tensor"), P(None, None, "tensor"), P(None, "tensor", None),
        P(), P(), P(), P(None, None, "tensor"), P(None, "tensor"), P(None, "tensor", None), P(),
    )
    return jax.shard_map(shards, mesh=mesh, in_specs=in_specs, out_specs=out_specs, check_vma=False)
```

```python
import math

import jax
import jax.numpy as jnp
from jax import lax
from jax.experimental import pallas as pl
from jax.experimental.pallas import tpu as pltpu
from jax.sharding import PartitionSpec as P

HEAD_DIM = 64
EPSILON = 1e-12
LOSS_WEIGHT = 8.0
HIGHEST = lax.Precision.HIGHEST
MASKED = -1e30
BF = jnp.bfloat16
F32 = jnp.float32
PLANE = ("span", "tensor")
MESH = pl.DeviceIdType.MESH
TENSORS = 4
MAIN, DIAG, SWAP = "main", "diag", "swap"


def mm(a, b, ca, cb):
    return lax.dot_general(a, b, (((ca,), (cb,)), ((), ())), preferred_element_type=F32)


def normal_parts(values):
    centred = values - jnp.mean(values, axis=-1, keepdims=True)
    spread = jnp.mean(centred * centred, axis=-1, keepdims=True)
    scale = lax.rsqrt(spread + EPSILON)
    return centred * scale, scale


def normal_back(upward, normed, scale, gain):
    weighted = upward * gain
    first = jnp.mean(weighted, axis=-1, keepdims=True)
    second = jnp.mean(weighted * normed, axis=-1, keepdims=True)
    return (weighted - first - normed * second) * scale


def gelu_parts(hidden):
    phi = 0.5 * (1.0 + lax.erf(hidden * math.sqrt(0.5)))
    slope = phi + hidden * jnp.exp(-0.5 * hidden * hidden) * (1.0 / math.sqrt(2.0 * math.pi))
    return hidden * phi, slope


def plane_pairs(kind):
    pairs = []
    for side in range(2):
        for t in range(TENSORS):
            if kind == SWAP:
                target = (1 - side, t)
            elif kind == MAIN:
                target = (side, t ^ (1 + side))
            else:
                target = (side, t ^ (2 - side))
            pairs.append((side * TENSORS + t, target[0] * TENSORS + target[1]))
    return pairs


def send(values, kind):
    return lax.ppermute(values, PLANE, plane_pairs(kind))


def plus(*terms):
    total = terms[0].astype(F32)
    for term in terms[1:]:
        total = total + term.astype(F32)
    return total.astype(BF)


def pick(side, zero, one):
    return jnp.where(side == 0, zero, one)


def tie(*values):
    return lax.optimization_barrier(values)


def gather_part(first, second, side):
    got_first, got_second = send(first, MAIN), send(second, MAIN)
    across = send(pick(side, got_first, got_second), DIAG)
    other_first, other_second = send(got_first, SWAP), send(got_second, SWAP)
    rest = send(across, SWAP)
    blocks = [
        (first, second), (got_first, got_second), (other_first, other_second),
        (pick(side, across, rest), pick(side, rest, across)),
    ]
    return blocks, across


def reduce_outgoing(blocks, side):
    return (
        blocks[2][0], blocks[2][1], pick(side, blocks[3][1], blocks[3][0]), pick(side, blocks[0][1], blocks[0][0])
    )


def reduce_swapped(blocks, outgoing, side):
    got = [send(o, SWAP) for o in outgoing]
    first = plus(blocks[1][0], got[0])
    second = plus(blocks[1][1], got[1])
    main_rest = pick(side, second, first)
    main_own = pick(side, first, second)
    across = plus(pick(side, blocks[3][0], blocks[3][1]), got[2])
    mine = plus(pick(side, blocks[0][0], blocks[0][1]), got[3])
    return main_rest, main_own, across, mine


def reduce_across(main_own, across):
    return plus(main_own, send(across, DIAG))


def finish_part(mine, side):
    other = send(mine, SWAP)
    return pick(side, mine, other).astype(F32), pick(side, other, mine).astype(F32)


Q_ROWS = 128


def attend_forward_kernel(
    layer, x_ref, first_ref, second_ref, bias_ref, z_ref, down_ref, across_ref,
    q_ref, k_ref, v_ref, o_ref, lse_ref, out_ref
):
    tokens, width = q_ref.shape
    at = 2 * layer * width
    x = x_ref[...]
    q_ref[...] = (mm(x, first_ref[:width, :], 1, 1) + bias_ref[:, at : at + width]).astype(BF)
    k_ref[...] = mm(x, first_ref[width : 2 * width, :], 1, 1).astype(BF)
    v_ref[...] = (mm(x, second_ref[:width, :], 1, 1) + bias_ref[:, at + width : at + 2 * width]).astype(BF)

    def step(i, carry):
        rows = pl.ds(pl.multiple_of(i * Q_ROWS, Q_ROWS), Q_ROWS)
        same = down_ref[rows, :] == across_ref[...]
        for h in range(width // HEAD_DIM):
            head = slice(h * HEAD_DIM, (h + 1) * HEAD_DIM)
            s = mm(q_ref[rows, head], k_ref[:, head], 1, 1) * 0.125
            s = jnp.where(same, s, MASKED)
            top = jnp.max(s, axis=-1, keepdims=True)
            raised = jnp.exp(s - top)
            total = jnp.sum(raised, axis=-1, keepdims=True)
            weights = (raised * (1.0 / total)).astype(BF)
            o_ref[rows, head] = mm(weights, v_ref[:, head], 1, 0).astype(BF)
            lse_ref[rows, h : h + 1] = top + jnp.log(total)
        out_ref[rows, :] = z_ref[rows, :] + mm(o_ref[rows, :], second_ref[width : 2 * width, :], 1, 0)
        return carry

    lax.fori_loop(0, tokens // Q_ROWS, step, 0)


def attend_backward_kernel(
    da_ref, x_ref, first_ref, second_ref, q_ref, k_ref, v_ref, o_ref, lse_ref, dx_ref, down_ref, across_ref,
    dfirst_ref, dsecond_ref, sums_ref, out_ref, do_ref, dq_ref, dk_ref, dv_ref
):
    tokens, width = q_ref.shape
    da = da_ref[...]
    do_ref[...] = mm(da, second_ref[width : 2 * width, :], 1, 1).astype(BF)
    dk_ref[...] = jnp.zeros_like(dk_ref)
    dv_ref[...] = jnp.zeros_like(dv_ref)

    def step(i, carry):
        rows = pl.ds(pl.multiple_of(i * Q_ROWS, Q_ROWS), Q_ROWS)
        same = down_ref[rows, :] == across_ref[...]
        for h in range(width // HEAD_DIM):
            head = slice(h * HEAD_DIM, (h + 1) * HEAD_DIM)
            q, k, up = q_ref[rows, head], k_ref[:, head], do_ref[rows, head]
            s = mm(q, k, 1, 1) * 0.125
            s = jnp.where(same, s, MASKED)
            pr = jnp.exp(s - lse_ref[rows, h : h + 1])
            dp = mm(up, v_ref[:, head], 1, 1)
            inner = jnp.sum(pr * dp, axis=-1, keepdims=True)
            ds = (pr * (dp - inner)).astype(BF)
            dq_ref[rows, head] = (mm(ds, k, 1, 0) * 0.125).astype(BF)
            dk_ref[:, head] += mm(ds, q, 0, 0)
            dv_ref[:, head] += mm(pr.astype(BF), up, 0, 0)
        return carry

    lax.fori_loop(0, tokens // Q_ROWS, step, 0)
    x = x_ref[...]
    dq = dq_ref[...]
    dk = (dk_ref[...] * 0.125).astype(BF)
    dv = dv_ref[...].astype(BF)
    out_ref[...] = (
        dx_ref[...]
        + mm(dq, first_ref[:width, :], 1, 0)
        + mm(dk, first_ref[width : 2 * width, :], 1, 0)
        + mm(dv, second_ref[:width, :], 1, 0)
    )
    dfirst_ref[:width, :] = mm(dq, x, 0, 0).astype(BF)
    dfirst_ref[width:, :] = mm(dk, x, 0, 0).astype(BF)
    dsecond_ref[:width, :] = mm(dv, x, 0, 0).astype(BF)
    dsecond_ref[width:, :] = mm(o_ref[...], da, 0, 0).astype(BF)
    sums_ref[:, :width] = jnp.sum(dq.astype(F32), axis=0, keepdims=True)
    sums_ref[:, width:] = jnp.sum(dv.astype(F32), axis=0, keepdims=True)


def attend_cost(tokens, width, model, products, mats):
    heads = width // HEAD_DIM
    return pl.CostEstimate(
        flops=2 * tokens * width * (products * tokens + mats * model),
        bytes_accessed=8 << 20,
        transcendentals=heads * tokens * tokens,
    )


def attend_forward(layer, cols, x, first, second, bias, z, seg):
    tokens, model = x.shape
    narrow = jax.ShapeDtypeStruct((tokens, cols), BF)

    def body(*refs):
        attend_forward_kernel(layer, *refs)

    return pl.pallas_call(
        body,
        name="attend_forward",
        out_shape=(
            narrow, narrow, narrow, narrow,
            jax.ShapeDtypeStruct((tokens, cols // HEAD_DIM), F32),
            jax.ShapeDtypeStruct(z.shape, F32),
        ),
        compiler_params=pltpu.CompilerParams(vmem_limit_bytes=24 << 20),
        cost_estimate=attend_cost(tokens, cols, model, 2, 4),
    )(x, first, second, bias, z, *seg)


def attend_backward(cols, da, x, first, second, kept, dx, seg):
    tokens, model = x.shape
    return pl.pallas_call(
        attend_backward_kernel,
        name="attend_backward",
        out_shape=(
            jax.ShapeDtypeStruct((2 * cols, model), BF),
            jax.ShapeDtypeStruct((2 * cols, model), BF),
            jax.ShapeDtypeStruct((1, 2 * cols), F32),
            jax.ShapeDtypeStruct(dx.shape, F32),
        ),
        scratch_shapes=[
            pltpu.VMEM((tokens, cols), BF), pltpu.VMEM((tokens, cols), BF),
            pltpu.VMEM((tokens, cols), F32), pltpu.VMEM((tokens, cols), F32),
        ],
        compiler_params=pltpu.CompilerParams(vmem_limit_bytes=24 << 20),
        cost_estimate=attend_cost(tokens, cols, model, 5, 8),
    )(da, x, first, second, *kept, dx, *seg)


def anchors_kernel(dps, planes, x_ref, out_ref, near_send, near_recv, far_send, far_recv, own_sem):
    dp = lax.axis_index("dp")
    me = lax.axis_index("span") * TENSORS + lax.axis_index("tensor")

    def near(k):
        peer = lax.rem(me + k, planes)
        return {"span": peer // TENSORS, "tensor": lax.rem(peer, TENSORS)}

    def far(k):
        return {"dp": lax.rem(dp + k, dps)}

    barrier = pltpu.get_barrier_semaphore()
    for k in range(1, planes):
        pl.semaphore_signal(barrier, inc=1, device_id=near(k), device_id_type=MESH)
    for k in range(1, dps):
        pl.semaphore_signal(barrier, inc=1, device_id=far(k), device_id_type=MESH)
    pl.semaphore_wait(barrier, planes + dps - 2)

    own = pltpu.make_async_copy(x_ref, out_ref.at[dp, me], own_sem)
    own.start()

    def near_copy(k):
        return pltpu.make_async_remote_copy(
            src_ref=x_ref, dst_ref=out_ref.at[dp, me], send_sem=near_send.at[k],
            recv_sem=near_recv.at[k], device_id=near(k), device_id_type=MESH,
        )

    def far_copy(k):
        return pltpu.make_async_remote_copy(
            src_ref=out_ref.at[dp], dst_ref=out_ref.at[dp], send_sem=far_send.at[k],
            recv_sem=far_recv.at[k], device_id=far(k), device_id_type=MESH,
        )

    for k in range(1, planes):
        near_copy(k).start()
    own.wait()
    for k in range(1, planes):
        near_copy(k).wait()
    for k in range(1, dps):
        far_copy(k).start()
    for k in range(1, dps):
        far_copy(k).wait()


def gather_anchors(values):
    dps = lax.axis_size("dp")
    planes = lax.axis_size("span") * lax.axis_size("tensor")
    dma = pltpu.SemaphoreType.DMA
    vmem = pl.BlockSpec(memory_space=pltpu.VMEM)

    def body(*refs):
        anchors_kernel(dps, planes, *refs)

    return pl.pallas_call(
        body,
        name="gather_anchors",
        out_shape=jax.ShapeDtypeStruct((dps, planes) + values.shape, values.dtype),
        in_specs=[vmem],
        out_specs=vmem,
        scratch_shapes=[dma((planes,)), dma((planes,)), dma((dps,)), dma((dps,)), dma],
        compiler_params=pltpu.CompilerParams(collective_id=0, has_side_effects=True),
    )(values)


VECTORS = ("pb", "g0", "g1", "s0", "s1", "sb")
ROWS_PER_CHUNK = 4
CHUNKS_PER_LAYER = 4


def block_order(side, tensor):
    flip_one = tensor + 1 - 2 * lax.rem(tensor, 2)
    flip_two = tensor + 2 - 4 * (tensor // 2)
    swing = side * (flip_two - flip_one)
    return tensor, flip_one + swing, flip_two - swing, TENSORS - 1 - tensor


def total_kernel(dps, planes, rows_ref, heads, out_ref, x_ref, parts, sums, sems):
    one_send, one_recv, two_send, two_recv, three_send, three_recv = sems
    dp = lax.axis_index("dp")
    side = lax.axis_index("span")
    tensor = lax.axis_index("tensor")
    me = side * TENSORS + tensor
    order = block_order(side, tensor)
    x_ref[...] = rows_ref[...]
    for l in range(2):
        for j in range(TENSORS):
            columns = heads[l][j].shape[1]
            x_ref[l * CHUNKS_PER_LAYER + 1, pl.ds(order[j], 1), :columns] = heads[l][j][...]

    def near_peer(k):
        return lax.rem(me + k, planes)

    def near(k):
        peer = near_peer(k)
        return {"span": peer // TENSORS, "tensor": lax.rem(peer, TENSORS)}

    def far(k):
        return {"dp": lax.rem(dp + k, dps)}

    barrier = pltpu.get_barrier_semaphore()
    for k in range(1, planes):
        pl.semaphore_signal(barrier, inc=1, device_id=near(k), device_id_type=MESH)
    for k in range(1, dps):
        pl.semaphore_signal(barrier, inc=1, device_id=far(k), device_id_type=MESH)
    pl.semaphore_wait(barrier, planes + dps - 2)

    def one(k):
        return pltpu.make_async_remote_copy(
            src_ref=x_ref.at[near_peer(k)], dst_ref=parts.at[k], send_sem=one_send.at[k],
            recv_sem=one_recv.at[k], device_id=near(k), device_id_type=MESH,
        )

    def two(k):
        return pltpu.make_async_remote_copy(
            src_ref=sums.at[dp], dst_ref=sums.at[dp], send_sem=two_send.at[k],
            recv_sem=two_recv.at[k], device_id=far(k), device_id_type=MESH,
        )

    def three(k):
        return pltpu.make_async_remote_copy(
            src_ref=out_ref.at[me], dst_ref=out_ref.at[me], send_sem=three_send.at[k],
            recv_sem=three_recv.at[k], device_id=near(k), device_id_type=MESH,
        )

    for k in range(1, planes):
        one(k).start()
    for k in range(1, planes):
        one(k).wait()
    total = x_ref[me]
    for k in range(1, planes):
        total = total + parts[k]
    sums[dp] = total
    for k in range(1, dps):
        two(k).start()
    for k in range(1, dps):
        two(k).wait()
    total = sums[0]
    for k in range(1, dps):
        total = total + sums[k]
    out_ref[me] = total
    for k in range(1, planes):
        three(k).start()
    for k in range(1, planes):
        three(k).wait()


def total_over_all(rows, heads):
    dps = lax.axis_size("dp")
    planes = lax.axis_size("span") * lax.axis_size("tensor")
    flat, tree = jax.tree.flatten(heads)
    shape = rows.shape
    dma = pltpu.SemaphoreType.DMA
    vmem = pl.BlockSpec(memory_space=pltpu.VMEM)

    def body(rows_ref, *refs):
        inputs = jax.tree.unflatten(tree, refs[: len(flat)])
        out_ref, x_ref, parts, sums = refs[len(flat) : len(flat) + 4]
        total_kernel(dps, planes, rows_ref, inputs, out_ref, x_ref, parts, sums, refs[len(flat) + 4 :])

    return pl.pallas_call(
        body,
        name="total_over_all",
        out_shape=jax.ShapeDtypeStruct(shape, F32),
        in_specs=[vmem] * (1 + len(flat)),
        out_specs=vmem,
        scratch_shapes=[
            pltpu.VMEM(shape, F32),
            pltpu.VMEM(shape, F32),
            pltpu.VMEM((dps,) + shape[1:], F32),
            dma((planes,)), dma((planes,)), dma((dps,)), dma((dps,)), dma((planes,)), dma((planes,)),
        ],
        compiler_params=pltpu.CompilerParams(collective_id=1, has_side_effects=True),
    )(rows, *flat)


def to_rows(values):
    return lax.all_to_all(values, "tensor", split_axis=0, concat_axis=0, tiled=True).reshape(
        -1, values.shape[-1]
    )


def to_places(values):
    blocks = values.reshape(TENSORS, -1, values.shape[-1])
    return lax.all_to_all(blocks, "tensor", split_axis=0, concat_axis=0, tiled=True)


def layer_forward(l, x, seg, attn_w, ffn_w, vec):
    xb = x.astype(BF)
    kept = []
    z1 = x + vec["pb"]
    for (first, second), bias in zip(attn_w, vec["heads"]):
        *saved, z1 = attend_forward(l, vec["cols"], xb, first, second, bias, z1, seg)
        kept.append(saved)
    n1, r1 = normal_parts(z1)
    y = n1 * vec["g0"] + vec["s0"]
    yb = y.astype(BF)
    act, slope = [], []
    z2 = y + vec["sb"]
    for (first, second), bias in zip(ffn_w, vec["eb"]):
        a, b = gelu_parts(mm(yb, first, 1, 0) + bias)
        act.append(a.astype(BF))
        slope.append(b.astype(BF))
        z2 = z2 + mm(act[-1], second, 1, 0)
    n2, r2 = normal_parts(z2)
    out = n2 * vec["g1"] + vec["s1"]
    return out, (xb, kept, n1, r1, yb, act, slope, n2, r2)


def total_rows(values):
    return jnp.sum(values, axis=0)


def ffn_backward(dout, ffn_w, vec, kept, hook):
    xb, saved, n1, r1, yb, act, slope, n2, r2 = kept
    dz2 = normal_back(dout, n2, r2, vec["g1"])
    small = {"g1": total_rows(dout * n2), "s1": total_rows(dout), "sb": total_rows(dz2), "eb": []}
    dz2 = hook("seeded", dz2)
    dzb = dz2.astype(BF)
    dy = dz2
    hidden = []
    for (first, second), b in zip(ffn_w, slope):
        dhid = mm(dzb, second, 1, 1) * b.astype(F32)
        small["eb"].append(total_rows(dhid))
        hidden.append(dhid.astype(BF))
        dy = dy + mm(hidden[-1], first, 1, 1)
    dy = hook("hidden", dy)
    blocks = [(mm(yb, h, 0, 0).astype(BF), mm(a, dzb, 0, 0).astype(BF)) for h, a in zip(hidden, act)]
    return dy, blocks, small


def attn_backward(dy, seg, attn_w, vec, kept, hook):
    xb, saved, n1, r1, yb, act, slope, n2, r2 = kept
    dz1 = normal_back(dy, n1, r1, vec["g0"])
    small = {"g0": total_rows(dy * n1), "s0": total_rows(dy), "pb": total_rows(dz1), "heads": []}
    dz1 = hook("normed", dz1)
    da = dz1.astype(BF)
    dx = dz1
    blocks = []
    for j, (first, second) in enumerate(attn_w):
        dfirst, dsecond, sums, dx = attend_backward(vec["cols"], da, xb, first, second, saved[j], dx, seg)
        small["heads"].append(sums)
        blocks.append((dfirst, dsecond))
        if j == 2:
            da, dx = hook("three", (da, dx))
    return dx, blocks, small


def attn_unpack(first, second):
    cols = first.shape[0] // 2
    heads = jnp.stack([first[:cols], first[cols:], second[:cols]])
    return jnp.swapaxes(heads, 1, 2), second[cols:]


class Reduction:
    def __init__(self, side):
        self.side = side

    def start(self, value, blocks):
        self.blocks = blocks
        value, *self.outgoing = tie(value, *reduce_outgoing(blocks, self.side))
        return value

    def swapped(self, value):
        value, self.main_rest, self.main_own, self.across, self.mine = tie(
            value, *reduce_swapped(self.blocks, self.outgoing, self.side)
        )
        self.from_rest = send(self.main_rest, MAIN)
        return value

    def crossed(self, value):
        value, self.main_own = tie(value, reduce_across(self.main_own, self.across))
        self.from_own = send(self.main_own, MAIN)
        self.from_peer = send(self.from_rest, SWAP)
        return value

    def summed(self, value):
        value, self.total = tie(value, plus(self.mine, self.from_own, self.from_peer))
        return value


def shards(
    layer_input, skip_tokens, backbone_cotangent, head_cotangent, segment_lengths, pair_index,
    w_heads, heads_bias, w_project, project_bias, norm_gain, norm_shift,
    w_expand, expand_bias, w_shrink, shrink_bias,
):
    side = lax.axis_index("span")
    mine = lax.axis_index("tensor")
    width = layer_input.shape[-1]
    head_cols = w_heads.shape[-1]
    ff_cols = w_expand.shape[-1]

    extra = 16
    bias_rows = jnp.concatenate([heads_bias.reshape(1, 4 * head_cols), expand_bias], axis=0)
    bias_rows = jnp.pad(bias_rows, ((0, extra - bias_rows.shape[0]), (0, 0)))

    def attn_rows(l):
        heads = jnp.swapaxes(w_heads[l], 1, 2)
        first = heads[:2].reshape(2 * head_cols, width)
        return first, jnp.concatenate([heads[2], w_project[l]], axis=0)

    first, second = attn_rows(0)
    first = jnp.concatenate([first, bias_rows], axis=0)
    second = jnp.pad(second, ((0, extra), (0, 0)))
    attn_w0, mark = gather_part(first, second, side)
    x = to_rows(layer_input[0])
    expand, shrink, first = tie(w_expand[0], w_shrink[0], first)
    ffn_w0, mark = gather_part(expand, shrink, side)
    first, second, expand = tie(*attn_rows(1), expand)
    attn_w1, attn_mark = gather_part(first, second, side)
    expand, shrink, first = tie(w_expand[1], w_shrink[1], first)
    ffn_w1, ffn_mark = gather_part(expand, shrink, side)
    later_skip, mark = tie(skip_tokens[0], mark)
    skip = to_rows(later_skip)
    mark = attn_mark
    later_head, later_backbone, mark = tie(head_cotangent[0], backbone_cotangent[0], mark)
    head_cot = to_rows(later_head)
    backbone_cot = to_rows(later_backbone)
    tokens = x.shape[0]

    biases = [first[2 * head_cols : 2 * head_cols + 3].astype(F32) for first, second in attn_w0]

    def vectors(l):
        return {
            "cols": head_cols, "heads": [b[:1] for b in biases],
            "eb": [b[1 + l] for b in biases], "pb": project_bias[l].astype(F32),
            "g0": norm_gain[l, 0].astype(F32), "g1": norm_gain[l, 1].astype(F32),
            "s0": norm_shift[l, 0].astype(F32), "s1": norm_shift[l, 1].astype(F32),
            "sb": shrink_bias[l].astype(F32),
        }

    lengths = lax.dynamic_index_in_dim(segment_lengths[0], mine, 0, keepdims=False)
    span_count = lengths.shape[0]
    starts = jnp.cumsum(lengths) - lengths
    row_length = jnp.sum(lengths)
    places = jnp.arange(tokens, dtype=jnp.int32)
    counted = jnp.sum((places[:, None] >= starts[None, :]).astype(jnp.int32), axis=-1) - 1
    segment = jnp.where(places < row_length, counted, span_count)
    seg = (segment[:, None], segment[None, :])
    valid = (places < row_length).astype(F32)[:, None]
    picker = (starts[:, None] == places[None, :]).astype(F32)
    first_place = jnp.sum(picker, axis=0)[:, None] > 0

    vec0, vec1 = vectors(0), vectors(1)
    backbone, kept0 = layer_forward(0, x.astype(F32), seg, attn_w0, ffn_w0, vec0)
    cls = mm(picker.astype(BF), backbone.astype(BF), 1, 0).astype(BF)
    anchors = gather_anchors(cls)
    dp_count = lax.axis_size("dp")
    pair_count = lax.axis_size("span")
    vector_count = dp_count * TENSORS * span_count
    anchors = anchors.reshape(dp_count, pair_count, TENSORS * span_count, width)
    anchors = jnp.swapaxes(anchors, 0, 1).reshape(pair_count, vector_count, width)

    head_in = jnp.where(first_place, backbone, skip.astype(F32))
    head, kept1 = layer_forward(1, head_in, seg, attn_w1, ffn_w1, vec1)

    root = math.sqrt(width)
    logits = mm(anchors[0], anchors[1], 1, 1) / root
    columns = jnp.arange(vector_count, dtype=jnp.int32)
    target = (pair_index[:, None] == columns[None, :]).astype(F32)
    lse_rows = jax.nn.logsumexp(logits, axis=1)
    lse_cols = jax.nn.logsumexp(logits, axis=0)
    dlogits = LOSS_WEIGHT * (
        jnp.exp(logits - lse_rows[:, None]) + jnp.exp(logits - lse_cols[None, :]) - 2.0 * target
    )
    span_loss = (jnp.sum(lse_rows) + jnp.sum(lse_cols) - 2.0 * jnp.sum(target * logits)) / (
        2 * vector_count
    )
    own = (lax.axis_index("dp") * TENSORS + mine) * span_count
    wanted = jnp.where(side == 0, dlogits, dlogits.T)
    wanted = lax.dynamic_slice(wanted, (own, 0), (span_count, vector_count))
    other = lax.dynamic_index_in_dim(anchors, 1 - side, 0, keepdims=False).astype(F32)
    dcls = jnp.dot(wanted, other, precision=HIGHEST) / root

    ffn1, attn1, ffn0, attn0 = (Reduction(side) for _ in range(4))

    def plain(name, value):
        return value

    dy, blocks, small1 = ffn_backward(head_cot.astype(F32) * valid, ffn_w1, vec1, kept1, plain)
    dy = ffn1.start(dy, blocks)

    def during_attn1(name, value):
        if name == "normed":
            return ffn1.swapped(value)
        return ffn1.crossed(value)

    du, blocks, more = attn_backward(dy, seg, attn_w1, vec1, kept1, during_attn1)
    small1.update(more)
    du = attn1.start(du, blocks)
    du = ffn1.summed(du)
    grad_skip = jnp.where(first_place, 0.0, du).astype(BF)

    seed = backbone_cot.astype(F32) * valid + jnp.where(first_place, du, 0.0)
    seed = seed + jnp.dot(picker.T, dcls, precision=HIGHEST)

    def during_ffn0(name, value):
        if name == "seeded":
            return attn1.swapped(value)
        return attn1.crossed(value)

    dy, blocks, small0 = ffn_backward(seed, ffn_w0, vec0, kept0, during_ffn0)
    dy = ffn0.start(dy, blocks)
    dy = attn1.summed(dy)
    ffn_total1, attn_total1 = lax.psum((ffn1.total, attn1.total), "dp")

    def during_attn0(name, value):
        if name == "normed":
            return ffn0.swapped(value)
        return ffn0.crossed(value)

    dx, blocks, more = attn_backward(dy, seg, attn_w0, vec0, kept0, during_attn0)
    small0.update(more)
    dx = attn0.start(dx, blocks)
    dx = ffn0.summed(dx)
    late, ffn_total1, attn_total1 = tie(ffn0.total, ffn_total1, attn_total1)
    ffn_total0 = lax.psum(late, "dp")

    order = block_order(side, mine)
    place = lax.broadcasted_iota(jnp.int32, (2 * CHUNKS_PER_LAYER * ROWS_PER_CHUNK, 1), 0)
    rows = jnp.zeros((place.shape[0], width), F32)
    for l, small in enumerate((small0, small1)):
        base = l * CHUNKS_PER_LAYER * ROWS_PER_CHUNK
        for j in range(TENSORS):
            rows = rows + jnp.where(place == base + order[j], small["eb"][j][None], 0.0)
        for i, k in enumerate(VECTORS):
            rows = rows + jnp.where(place == base + 2 * ROWS_PER_CHUNK + i, small[k][None], 0.0)
    rows, mark = tie(rows.reshape(2 * CHUNKS_PER_LAYER, ROWS_PER_CHUNK, width), ffn0.total)
    rows = attn0.swapped(rows)
    total = total_over_all(rows, (small0["heads"], small1["heads"]))
    total = attn0.crossed(total)
    total = attn0.summed(total)
    attn_total0, ffn_total0 = tie(attn0.total, ffn_total0)
    attn_total0 = lax.psum(attn_total0, "dp")

    hb, eb, vector_sums = [], [], []
    for l in range(2):
        base = l * CHUNKS_PER_LAYER
        own = lax.dynamic_slice(total[base : base + 2], (0, mine, 0), (2, 1, width))[:, 0]
        eb.append(own[0])
        hb.append(jnp.stack([own[1, :head_cols], own[1, head_cols : 2 * head_cols]]))
        rows = total[base + 2 : base + CHUNKS_PER_LAYER].reshape(-1, width)
        vector_sums.append({k: rows[i] for i, k in enumerate(VECTORS)})
    sums = vector_sums

    ge1, gs1 = finish_part(ffn_total1, side)
    gh1, gp1 = attn_unpack(*finish_part(attn_total1, side))
    ge0, gs0 = finish_part(ffn_total0, side)
    gh0, gp0 = attn_unpack(*finish_part(attn_total0, side))

    return (
        to_places((backbone * valid).astype(BF))[None],
        to_places((head * valid).astype(BF))[None],
        span_loss,
        to_places(dx.astype(BF))[None],
        to_places(grad_skip)[None],
        jnp.stack([gh0, gh1]),
        jnp.stack(hb),
        jnp.stack([gp0, gp1]),
        jnp.stack([s["pb"] for s in sums]),
        jnp.stack([jnp.stack([s["g0"], s["g1"]]) for s in sums]),
        jnp.stack([jnp.stack([s["s0"], s["s1"]]) for s in sums]),
        jnp.stack([ge0, ge1]),
        jnp.stack(eb),
        jnp.stack([gs0, gs1]),
        jnp.stack([s["sb"] for s in sums]),
    )


def solution(mesh):
    rows = P("span", "dp", "tensor", None)
    in_specs = (
        rows, rows, rows, rows, P("span", "dp", None), P(),
        P(None, None, None, "tensor"), P(None, None, "tensor"), P(None, "tensor", None),
        P(), P(), P(), P(None, None, "tensor"), P(None, "tensor"), P(None, "tensor", None), P(),
    )
    out_specs = (
        rows, rows, P(), rows, rows,
        P(None, None, None, "tensor"), P(None, None, "tensor"), P(None, "tensor", None),
        P(), P(), P(), P(None, None, "tensor"), P(None, "tensor"), P(None, "tensor", None), P(),
    )
    return jax.shard_map(shards, mesh=mesh, in_specs=in_specs, out_specs=out_specs, check_vma=False)
```

```python
import math

import jax
import jax.numpy as jnp
from jax import lax
from jax.experimental import pallas as pl
from jax.experimental.pallas import tpu as pltpu
from jax.sharding import PartitionSpec as P

HEAD_DIM = 64
EPSILON = 1e-12
LOSS_WEIGHT = 8.0
HIGHEST = lax.Precision.HIGHEST
MASKED = -1e30
BF = jnp.bfloat16
F32 = jnp.float32
PLANE = ("span", "tensor")
MESH = pl.DeviceIdType.MESH
TENSORS = 4
MAIN, DIAG, SWAP = "main", "diag", "swap"


def mm(a, b, ca, cb):
    return lax.dot_general(a, b, (((ca,), (cb,)), ((), ())), preferred_element_type=F32)


def normal_parts(values):
    centred = values - jnp.mean(values, axis=-1, keepdims=True)
    spread = jnp.mean(centred * centred, axis=-1, keepdims=True)
    scale = lax.rsqrt(spread + EPSILON)
    return centred * scale, scale


def normal_back(upward, normed, scale, gain):
    weighted = upward * gain
    first = jnp.mean(weighted, axis=-1, keepdims=True)
    second = jnp.mean(weighted * normed, axis=-1, keepdims=True)
    return (weighted - first - normed * second) * scale


def gelu_parts(hidden):
    phi = 0.5 * (1.0 + lax.erf(hidden * math.sqrt(0.5)))
    slope = phi + hidden * jnp.exp(-0.5 * hidden * hidden) * (1.0 / math.sqrt(2.0 * math.pi))
    return hidden * phi, slope


def plane_pairs(kind):
    pairs = []
    for side in range(2):
        for t in range(TENSORS):
            if kind == SWAP:
                target = (1 - side, t)
            elif kind == MAIN:
                target = (side, t ^ (1 + side))
            else:
                target = (side, t ^ (2 - side))
            pairs.append((side * TENSORS + t, target[0] * TENSORS + target[1]))
    return pairs


def send(values, kind):
    return lax.ppermute(values, PLANE, plane_pairs(kind))


def plus(*terms):
    total = terms[0].astype(F32)
    for term in terms[1:]:
        total = total + term.astype(F32)
    return total.astype(BF)


def pick(side, zero, one):
    return jnp.where(side == 0, zero, one)


def tie(*values):
    return lax.optimization_barrier(values)


def gather_part(first, second, side):
    got_first, got_second = send(first, MAIN), send(second, MAIN)
    across = send(pick(side, got_first, got_second), DIAG)
    other_first, other_second = send(got_first, SWAP), send(got_second, SWAP)
    rest = send(across, SWAP)
    blocks = [
        (first, second), (got_first, got_second), (other_first, other_second),
        (pick(side, across, rest), pick(side, rest, across)),
    ]
    return blocks, across


def reduce_outgoing(blocks):
    return blocks[2][0], blocks[2][1], blocks[3][1], blocks[0][1]


def reduce_swapped(blocks, outgoing):
    got = [send(o, SWAP) for o in outgoing]
    return (
        plus(blocks[1][1], got[0]), plus(blocks[1][0], got[1]), plus(blocks[3][0], got[2]), plus(blocks[0][0], got[3])
    )


def reduce_across(main_own, across):
    return plus(main_own, send(across, DIAG))


def finish_part(mine, side):
    other = send(mine, SWAP)
    return pick(side, mine, other).astype(F32), pick(side, other, mine).astype(F32)


Q_ROWS = 128


def attend_forward_kernel(
    layer, x_ref, first_ref, second_ref, bias_ref, z_ref, down_ref, across_ref,
    q_ref, k_ref, v_ref, o_ref, lse_ref, out_ref
):
    tokens, width = q_ref.shape
    at = 2 * layer * width
    x = x_ref[...]
    q_ref[...] = (mm(x, first_ref[:width, :], 1, 1) + bias_ref[:, at : at + width]).astype(BF)
    k_ref[...] = mm(x, first_ref[width : 2 * width, :], 1, 1).astype(BF)
    v_ref[...] = (mm(x, second_ref[:width, :], 1, 1) + bias_ref[:, at + width : at + 2 * width]).astype(BF)

    def step(i, carry):
        rows = pl.ds(pl.multiple_of(i * Q_ROWS, Q_ROWS), Q_ROWS)
        same = down_ref[rows, :] == across_ref[...]
        for h in range(width // HEAD_DIM):
            head = slice(h * HEAD_DIM, (h + 1) * HEAD_DIM)
            s = mm(q_ref[rows, head], k_ref[:, head], 1, 1) * 0.125
            s = jnp.where(same, s, MASKED)
            top = jnp.max(s, axis=-1, keepdims=True)
            raised = jnp.exp(s - top)
            total = jnp.sum(raised, axis=-1, keepdims=True)
            weights = (raised * (1.0 / total)).astype(BF)
            o_ref[rows, head] = mm(weights, v_ref[:, head], 1, 0).astype(BF)
            lse_ref[rows, h : h + 1] = top + jnp.log(total)
        out_ref[rows, :] = z_ref[rows, :] + mm(o_ref[rows, :], second_ref[width : 2 * width, :], 1, 0)
        return carry

    lax.fori_loop(0, tokens // Q_ROWS, step, 0)


def attend_backward_kernel(
    da_ref, x_ref, first_ref, second_ref, q_ref, k_ref, v_ref, o_ref, lse_ref, dx_ref, down_ref, across_ref,
    own_ref, rest_ref, sums_ref, out_ref, do_ref, dq_ref, dk_ref, dv_ref
):
    tokens, width = q_ref.shape
    da = da_ref[...]
    do_ref[...] = mm(da, second_ref[width : 2 * width, :], 1, 1).astype(BF)
    dk_ref[...] = jnp.zeros_like(dk_ref)
    dv_ref[...] = jnp.zeros_like(dv_ref)

    def step(i, carry):
        rows = pl.ds(pl.multiple_of(i * Q_ROWS, Q_ROWS), Q_ROWS)
        same = down_ref[rows, :] == across_ref[...]
        for h in range(width // HEAD_DIM):
            head = slice(h * HEAD_DIM, (h + 1) * HEAD_DIM)
            q, k, up = q_ref[rows, head], k_ref[:, head], do_ref[rows, head]
            s = mm(q, k, 1, 1) * 0.125
            s = jnp.where(same, s, MASKED)
            pr = jnp.exp(s - lse_ref[rows, h : h + 1])
            dp = mm(up, v_ref[:, head], 1, 1)
            inner = jnp.sum(pr * dp, axis=-1, keepdims=True)
            ds = (pr * (dp - inner)).astype(BF)
            dq_ref[rows, head] = (mm(ds, k, 1, 0) * 0.125).astype(BF)
            dk_ref[:, head] += mm(ds, q, 0, 0)
            dv_ref[:, head] += mm(pr.astype(BF), up, 0, 0)
        return carry

    lax.fori_loop(0, tokens // Q_ROWS, step, 0)
    x = x_ref[...]
    dq = dq_ref[...]
    dk = (dk_ref[...] * 0.125).astype(BF)
    dv = dv_ref[...].astype(BF)
    out_ref[...] = (
        dx_ref[...]
        + mm(dq, first_ref[:width, :], 1, 0)
        + mm(dk, first_ref[width : 2 * width, :], 1, 0)
        + mm(dv, second_ref[:width, :], 1, 0)
    )
    side = lax.axis_index("span")
    store_both(
        side, own_ref, rest_ref, slice(0, width), mm(dq, x, 0, 0).astype(BF), mm(dv, x, 0, 0).astype(BF)
    )
    store_both(
        side, own_ref, rest_ref, slice(width, 2 * width),
        mm(dk, x, 0, 0).astype(BF), mm(o_ref[...], da, 0, 0).astype(BF),
    )
    sums_ref[:, :width] = jnp.sum(dq.astype(F32), axis=0, keepdims=True)
    sums_ref[:, width:] = jnp.sum(dv.astype(F32), axis=0, keepdims=True)


def small_cost():
    return pl.CostEstimate(flops=1 << 20, bytes_accessed=1 << 10, transcendentals=0)


def kernel_params():
    return pltpu.CompilerParams(vmem_limit_bytes=24 << 20)


def store_both(side, own_ref, rest_ref, rows, first, second):
    @pl.when(side == 0)
    def _():
        own_ref[rows, :] = first
        rest_ref[rows, :] = second

    @pl.when(side != 0)
    def _():
        own_ref[rows, :] = second
        rest_ref[rows, :] = first


def ffn_backward_kernel(
    dz_ref, y_ref, act_ref, slope_ref, first_ref, second_ref, dy_ref, own_ref, rest_ref, sums_ref, out_ref, dh_ref
):
    tokens, model = dz_ref.shape
    side = lax.axis_index("span")
    sums_ref[...] = jnp.zeros_like(sums_ref)

    def data(i, carry):
        rows = pl.ds(pl.multiple_of(i * Q_ROWS, Q_ROWS), Q_ROWS)
        dhid = mm(dz_ref[rows, :], second_ref[...], 1, 1) * slope_ref[rows, :].astype(F32)
        sums_ref[...] += jnp.sum(dhid, axis=0, keepdims=True)
        dhb = dhid.astype(BF)
        dh_ref[rows, :] = dhb
        out_ref[rows, :] = dy_ref[rows, :] + mm(dhb, first_ref[...], 1, 1)
        return carry

    def weights(i, carry):
        rows = pl.ds(pl.multiple_of(i * Q_ROWS, Q_ROWS), Q_ROWS)
        first = mm(y_ref[:, rows], dh_ref[...], 0, 0).astype(BF)
        second = mm(act_ref[:, rows], dz_ref[...], 0, 0).astype(BF)
        store_both(side, own_ref, rest_ref, rows, first, second)
        return carry

    lax.fori_loop(0, tokens // Q_ROWS, data, 0)
    lax.fori_loop(0, model // Q_ROWS, weights, 0)


def ffn_block_backward(dzb, yb, act, slope, first, second, dy):
    return pl.pallas_call(
        ffn_backward_kernel,
        name="ffn_backward",
        out_shape=(
            jax.ShapeDtypeStruct(first.shape, BF),
            jax.ShapeDtypeStruct(first.shape, BF),
            jax.ShapeDtypeStruct((1, act.shape[1]), F32),
            jax.ShapeDtypeStruct(dy.shape, F32),
        ),
        scratch_shapes=[pltpu.VMEM(act.shape, BF)],
        compiler_params=kernel_params(),
        cost_estimate=small_cost(),
    )(dzb, yb, act, slope, first, second, dy)


def attend_forward(layer, cols, x, first, second, bias, z, seg):
    tokens, model = x.shape
    narrow = jax.ShapeDtypeStruct((tokens, cols), BF)

    def body(*refs):
        attend_forward_kernel(layer, *refs)

    return pl.pallas_call(
        body,
        name="attend_forward",
        out_shape=(
            narrow, narrow, narrow, narrow,
            jax.ShapeDtypeStruct((tokens, cols // HEAD_DIM), F32),
            jax.ShapeDtypeStruct(z.shape, F32),
        ),
        compiler_params=kernel_params(),
        cost_estimate=small_cost(),
    )(x, first, second, bias, z, *seg)


def attend_backward(cols, da, x, first, second, kept, dx, seg):
    tokens, model = x.shape
    return pl.pallas_call(
        attend_backward_kernel,
        name="attend_backward",
        out_shape=(
            jax.ShapeDtypeStruct((2 * cols, model), BF),
            jax.ShapeDtypeStruct((2 * cols, model), BF),
            jax.ShapeDtypeStruct((1, 2 * cols), F32),
            jax.ShapeDtypeStruct(dx.shape, F32),
        ),
        scratch_shapes=[
            pltpu.VMEM((tokens, cols), BF), pltpu.VMEM((tokens, cols), BF),
            pltpu.VMEM((tokens, cols), F32), pltpu.VMEM((tokens, cols), F32),
        ],
        compiler_params=kernel_params(),
        cost_estimate=small_cost(),
    )(da, x, first, second, *kept, dx, *seg)


def anchors_kernel(dps, planes, x_ref, out_ref, near_send, near_recv, far_send, far_recv, own_sem):
    dp = lax.axis_index("dp")
    me = lax.axis_index("span") * TENSORS + lax.axis_index("tensor")

    def near(k):
        peer = lax.rem(me + k, planes)
        return {"span": peer // TENSORS, "tensor": lax.rem(peer, TENSORS)}

    def far(k):
        return {"dp": lax.rem(dp + k, dps)}

    barrier = pltpu.get_barrier_semaphore()
    for k in range(1, planes):
        pl.semaphore_signal(barrier, inc=1, device_id=near(k), device_id_type=MESH)
    for k in range(1, dps):
        pl.semaphore_signal(barrier, inc=1, device_id=far(k), device_id_type=MESH)
    pl.semaphore_wait(barrier, planes + dps - 2)

    own = pltpu.make_async_copy(x_ref, out_ref.at[dp, me], own_sem)
    own.start()

    def near_copy(k):
        return pltpu.make_async_remote_copy(
            src_ref=x_ref, dst_ref=out_ref.at[dp, me], send_sem=near_send.at[k],
            recv_sem=near_recv.at[k], device_id=near(k), device_id_type=MESH,
        )

    def far_copy(k):
        return pltpu.make_async_remote_copy(
            src_ref=out_ref.at[dp], dst_ref=out_ref.at[dp], send_sem=far_send.at[k],
            recv_sem=far_recv.at[k], device_id=far(k), device_id_type=MESH,
        )

    for k in range(1, planes):
        near_copy(k).start()
    own.wait()
    for k in range(1, planes):
        near_copy(k).wait()
    for k in range(1, dps):
        far_copy(k).start()
    for k in range(1, dps):
        far_copy(k).wait()


def gather_anchors(values):
    dps = lax.axis_size("dp")
    planes = lax.axis_size("span") * lax.axis_size("tensor")
    dma = pltpu.SemaphoreType.DMA
    vmem = pl.BlockSpec(memory_space=pltpu.VMEM)

    def body(*refs):
        anchors_kernel(dps, planes, *refs)

    return pl.pallas_call(
        body,
        name="gather_anchors",
        out_shape=jax.ShapeDtypeStruct((dps, planes) + values.shape, values.dtype),
        in_specs=[vmem],
        out_specs=vmem,
        scratch_shapes=[dma((planes,)), dma((planes,)), dma((dps,)), dma((dps,)), dma],
        compiler_params=pltpu.CompilerParams(collective_id=0, has_side_effects=True),
    )(values)


VECTORS = ("pb", "g0", "g1", "s0", "s1", "sb")
ROWS_PER_CHUNK = 4
CHUNKS_PER_LAYER = 4


def block_order(side, tensor):
    flip_one = tensor + 1 - 2 * lax.rem(tensor, 2)
    flip_two = tensor + 2 - 4 * (tensor // 2)
    swing = side * (flip_two - flip_one)
    return tensor, flip_one + swing, flip_two - swing, TENSORS - 1 - tensor


def total_kernel(dps, planes, rows_ref, blocks, out_ref, x_ref, parts, sums, sems):
    one_send, one_recv, two_send, two_recv, three_send, three_recv = sems
    dp = lax.axis_index("dp")
    side = lax.axis_index("span")
    tensor = lax.axis_index("tensor")
    me = side * TENSORS + tensor
    order = block_order(side, tensor)
    x_ref[...] = rows_ref[...]
    for l in range(2):
        for j in range(TENSORS):
            for k in range(2):
                columns = blocks[l][k][j].shape[1]
                x_ref[l * CHUNKS_PER_LAYER + k, pl.ds(order[j], 1), :columns] = blocks[l][k][j][...]

    def near_peer(k):
        return lax.rem(me + k, planes)

    def near(k):
        peer = near_peer(k)
        return {"span": peer // TENSORS, "tensor": lax.rem(peer, TENSORS)}

    def far(k):
        return {"dp": lax.rem(dp + k, dps)}

    barrier = pltpu.get_barrier_semaphore()
    for k in range(1, planes):
        pl.semaphore_signal(barrier, inc=1, device_id=near(k), device_id_type=MESH)
    for k in range(1, dps):
        pl.semaphore_signal(barrier, inc=1, device_id=far(k), device_id_type=MESH)
    pl.semaphore_wait(barrier, planes + dps - 2)

    def one(k):
        return pltpu.make_async_remote_copy(
            src_ref=x_ref.at[near_peer(k)], dst_ref=parts.at[k], send_sem=one_send.at[k],
            recv_sem=one_recv.at[k], device_id=near(k), device_id_type=MESH,
        )

    def two(k):
        return pltpu.make_async_remote_copy(
            src_ref=sums.at[dp], dst_ref=sums.at[dp], send_sem=two_send.at[k],
            recv_sem=two_recv.at[k], device_id=far(k), device_id_type=MESH,
        )

    def three(k):
        return pltpu.make_async_remote_copy(
            src_ref=out_ref.at[me], dst_ref=out_ref.at[me], send_sem=three_send.at[k],
            recv_sem=three_recv.at[k], device_id=near(k), device_id_type=MESH,
        )

    for k in range(1, planes):
        one(k).start()
    for k in range(1, planes):
        one(k).wait()
    total = x_ref[me]
    for k in range(1, planes):
        total = total + parts[k]
    sums[dp] = total
    for k in range(1, dps):
        two(k).start()
    for k in range(1, dps):
        two(k).wait()
    total = sums[0]
    for k in range(1, dps):
        total = total + sums[k]
    out_ref[me] = total
    for k in range(1, planes):
        three(k).start()
    for k in range(1, planes):
        three(k).wait()


def total_over_all(rows, blocks):
    dps = lax.axis_size("dp")
    planes = lax.axis_size("span") * lax.axis_size("tensor")
    flat, tree = jax.tree.flatten(blocks)
    shape = rows.shape
    dma = pltpu.SemaphoreType.DMA
    vmem = pl.BlockSpec(memory_space=pltpu.VMEM)

    def body(rows_ref, *refs):
        inputs = jax.tree.unflatten(tree, refs[: len(flat)])
        out_ref, x_ref, parts, sums = refs[len(flat) : len(flat) + 4]
        total_kernel(dps, planes, rows_ref, inputs, out_ref, x_ref, parts, sums, refs[len(flat) + 4 :])

    return pl.pallas_call(
        body,
        name="total_over_all",
        out_shape=jax.ShapeDtypeStruct(shape, F32),
        in_specs=[vmem] * (1 + len(flat)),
        out_specs=vmem,
        scratch_shapes=[
            pltpu.VMEM(shape, F32),
            pltpu.VMEM(shape, F32),
            pltpu.VMEM((dps,) + shape[1:], F32),
            dma((planes,)), dma((planes,)), dma((dps,)), dma((dps,)), dma((planes,)), dma((planes,)),
        ],
        compiler_params=pltpu.CompilerParams(collective_id=1, has_side_effects=True),
    )(rows, *flat)


def to_rows(values):
    return lax.all_to_all(values, "tensor", split_axis=0, concat_axis=0, tiled=True).reshape(
        -1, values.shape[-1]
    )


def to_places(values):
    blocks = values.reshape(TENSORS, -1, values.shape[-1])
    return lax.all_to_all(blocks, "tensor", split_axis=0, concat_axis=0, tiled=True)


def layer_forward(l, x, seg, attn_w, ffn_w, vec, hook):
    xb = x.astype(BF)
    kept = []
    z1 = x + vec["pb"]
    for j, ((first, second), bias) in enumerate(zip(attn_w, vec["heads"])):
        *saved, z1 = attend_forward(l, vec["cols"], xb, first, second, bias, z1, seg)
        kept.append(saved)
        z1 = hook(j, z1)
    n1, r1 = normal_parts(z1)
    y = n1 * vec["g0"] + vec["s0"]
    yb = y.astype(BF)
    act, slope = [], []
    z2 = y + vec["sb"]
    for (first, second), bias in zip(ffn_w, vec["eb"]):
        a, b = gelu_parts(mm(yb, first, 1, 0) + bias)
        act.append(a.astype(BF))
        slope.append(b.astype(BF))
        z2 = z2 + mm(act[-1], second, 1, 0)
    n2, r2 = normal_parts(z2)
    out = n2 * vec["g1"] + vec["s1"]
    return out, (xb, kept, n1, r1, yb, act, slope, n2, r2)


def total_rows(values):
    return jnp.sum(values, axis=0)


def ffn_backward(dout, ffn_w, vec, kept, hook):
    xb, saved, n1, r1, yb, act, slope, n2, r2 = kept
    dz2 = normal_back(dout, n2, r2, vec["g1"])
    small = {"g1": total_rows(dout * n2), "s1": total_rows(dout), "sb": total_rows(dz2), "eb": []}
    dz2 = hook("seeded", dz2)
    dzb = dz2.astype(BF)
    dy = dz2
    blocks = []
    for j, (first, second) in enumerate(ffn_w):
        own, rest, sums, dy = ffn_block_backward(dzb, yb, act[j], slope[j], first, second, dy)
        small["eb"].append(sums)
        blocks.append((own, rest))
        if j == 2:
            dzb, dy = hook("three", (dzb, dy))
    return dy, blocks, small


def attn_backward(dy, seg, attn_w, vec, kept, hook):
    xb, saved, n1, r1, yb, act, slope, n2, r2 = kept
    dz1 = normal_back(dy, n1, r1, vec["g0"])
    small = {"g0": total_rows(dy * n1), "s0": total_rows(dy), "pb": total_rows(dz1), "heads": []}
    dz1 = hook("normed", dz1)
    da = dz1.astype(BF)
    dx = dz1
    blocks = []
    for j, (first, second) in enumerate(attn_w):
        dfirst, dsecond, sums, dx = attend_backward(vec["cols"], da, xb, first, second, saved[j], dx, seg)
        small["heads"].append(sums)
        blocks.append((dfirst, dsecond))
        if j == 2:
            da, dx = hook("three", (da, dx))
    return dx, blocks, small


def attn_unpack(first, second):
    cols = first.shape[0] // 2
    heads = jnp.stack([first[:cols], first[cols:], second[:cols]])
    return jnp.swapaxes(heads, 1, 2), second[cols:]


class Reduction:
    def start(self, value, blocks):
        self.blocks = blocks
        value, *self.outgoing = tie(value, *reduce_outgoing(blocks))
        return value

    def swapped(self, value):
        value, self.main_rest, self.main_own, self.across, self.mine = tie(
            value, *reduce_swapped(self.blocks, self.outgoing)
        )
        self.from_rest = send(self.main_rest, MAIN)
        return value

    def crossed(self, value):
        value, self.main_own = tie(value, reduce_across(self.main_own, self.across))
        self.from_own = send(self.main_own, MAIN)
        self.from_peer = send(self.from_rest, SWAP)
        return value

    def summed(self, value):
        value, self.total = tie(value, plus(self.mine, self.from_own, self.from_peer))
        return value


def shards(
    layer_input, skip_tokens, backbone_cotangent, head_cotangent, segment_lengths, pair_index,
    w_heads, heads_bias, w_project, project_bias, norm_gain, norm_shift,
    w_expand, expand_bias, w_shrink, shrink_bias,
):
    side = lax.axis_index("span")
    mine = lax.axis_index("tensor")
    width = layer_input.shape[-1]
    head_cols = w_heads.shape[-1]
    ff_cols = w_expand.shape[-1]

    extra = 16
    bias_rows = jnp.concatenate([heads_bias.reshape(1, 4 * head_cols), expand_bias], axis=0)
    bias_rows = jnp.pad(bias_rows, ((0, extra - bias_rows.shape[0]), (0, 0)))

    def attn_rows(l):
        heads = jnp.swapaxes(w_heads[l], 1, 2)
        first = heads[:2].reshape(2 * head_cols, width)
        return first, jnp.concatenate([heads[2], w_project[l]], axis=0)

    first, second = attn_rows(0)
    first = jnp.concatenate([first, bias_rows], axis=0)
    second = jnp.pad(second, ((0, extra), (0, 0)))
    attn_w0, mark = gather_part(first, second, side)
    x = to_rows(layer_input[0])
    expand, shrink, first = tie(w_expand[0], w_shrink[0], first)
    ffn_w0, mark = gather_part(expand, shrink, side)
    later = {}

    def during_forward0(j, value):
        if j == 1:
            first, second, value = tie(*attn_rows(1), value)
            later["attn"], mark = gather_part(first, second, side)
        if j == 3:
            first, second, skip, value = tie(w_expand[1], w_shrink[1], skip_tokens[0], value)
            later["ffn"], mark = gather_part(first, second, side)
            later["skip"] = to_rows(skip)
        return value

    def plain(name, value):
        return value

    tokens = x.shape[0]

    biases = [first[2 * head_cols : 2 * head_cols + 3].astype(F32) for first, second in attn_w0]

    def vectors(l):
        return {
            "cols": head_cols, "heads": [b[:1] for b in biases],
            "eb": [b[1 + l] for b in biases], "pb": project_bias[l].astype(F32),
            "g0": norm_gain[l, 0].astype(F32), "g1": norm_gain[l, 1].astype(F32),
            "s0": norm_shift[l, 0].astype(F32), "s1": norm_shift[l, 1].astype(F32),
            "sb": shrink_bias[l].astype(F32),
        }

    lengths = lax.dynamic_index_in_dim(segment_lengths[0], mine, 0, keepdims=False)
    span_count = lengths.shape[0]
    starts = jnp.cumsum(lengths) - lengths
    row_length = jnp.sum(lengths)
    places = jnp.arange(tokens, dtype=jnp.int32)
    counted = jnp.sum((places[:, None] >= starts[None, :]).astype(jnp.int32), axis=-1) - 1
    segment = jnp.where(places < row_length, counted, span_count)
    seg = (segment[:, None], segment[None, :])
    valid = (places < row_length).astype(F32)[:, None]
    picker = (starts[:, None] == places[None, :]).astype(F32)
    first_place = jnp.sum(picker, axis=0)[:, None] > 0

    vec0, vec1 = vectors(0), vectors(1)
    backbone, kept0 = layer_forward(0, x.astype(F32), seg, attn_w0, ffn_w0, vec0, during_forward0)
    attn_w1, ffn_w1, skip = later["attn"], later["ffn"], later["skip"]
    later_head, later_backbone, backbone = tie(head_cotangent[0], backbone_cotangent[0], backbone)
    head_cot = to_rows(later_head)
    backbone_cot = to_rows(later_backbone)
    cls = mm(picker.astype(BF), backbone.astype(BF), 1, 0).astype(BF)
    anchors = gather_anchors(cls)
    dp_count = lax.axis_size("dp")
    pair_count = lax.axis_size("span")
    vector_count = dp_count * TENSORS * span_count
    anchors = anchors.reshape(dp_count, pair_count, TENSORS * span_count, width)
    anchors = jnp.swapaxes(anchors, 0, 1).reshape(pair_count, vector_count, width)

    head_in = jnp.where(first_place, backbone, skip.astype(F32))
    head, kept1 = layer_forward(1, head_in, seg, attn_w1, ffn_w1, vec1, plain)

    root = math.sqrt(width)
    logits = mm(anchors[0], anchors[1], 1, 1) / root
    columns = jnp.arange(vector_count, dtype=jnp.int32)
    target = (pair_index[:, None] == columns[None, :]).astype(F32)
    lse_rows = jax.nn.logsumexp(logits, axis=1)
    lse_cols = jax.nn.logsumexp(logits, axis=0)
    dlogits = LOSS_WEIGHT * (
        jnp.exp(logits - lse_rows[:, None]) + jnp.exp(logits - lse_cols[None, :]) - 2.0 * target
    )
    span_loss = (jnp.sum(lse_rows) + jnp.sum(lse_cols) - 2.0 * jnp.sum(target * logits)) / (
        2 * vector_count
    )
    own = (lax.axis_index("dp") * TENSORS + mine) * span_count
    wanted = jnp.where(side == 0, dlogits, dlogits.T)
    wanted = lax.dynamic_slice(wanted, (own, 0), (span_count, vector_count))
    other = lax.dynamic_index_in_dim(anchors, 1 - side, 0, keepdims=False).astype(F32)
    dcls = jnp.dot(wanted, other, precision=HIGHEST) / root

    ffn1, attn1, ffn0, attn0 = (Reduction() for _ in range(4))

    dy, blocks, small1 = ffn_backward(head_cot.astype(F32) * valid, ffn_w1, vec1, kept1, plain)
    dy = ffn1.start(dy, blocks)

    def during_attn1(name, value):
        if name == "normed":
            return ffn1.swapped(value)
        return ffn1.crossed(value)

    du, blocks, more = attn_backward(dy, seg, attn_w1, vec1, kept1, during_attn1)
    small1.update(more)
    du = attn1.start(du, blocks)
    du = ffn1.summed(du)
    ffn_total1 = lax.psum(ffn1.total, "dp")
    grad_skip = jnp.where(first_place, 0.0, du).astype(BF)

    seed = backbone_cot.astype(F32) * valid + jnp.where(first_place, du, 0.0)
    seed = seed + jnp.dot(picker.T, dcls, precision=HIGHEST)

    def during_ffn0(name, value):
        if name == "seeded":
            return attn1.swapped(value)
        return attn1.crossed(value)

    dy, blocks, small0 = ffn_backward(seed, ffn_w0, vec0, kept0, during_ffn0)
    dy = ffn0.start(dy, blocks)
    dy = attn1.summed(dy)

    def during_attn0(name, value):
        if name == "normed":
            return ffn0.swapped(value)
        return ffn0.crossed(value)

    dy, ffn_total1, attn_total1 = tie(dy, ffn_total1, attn1.total)
    attn_total1 = lax.psum(attn_total1, "dp")

    dx, blocks, more = attn_backward(dy, seg, attn_w0, vec0, kept0, during_attn0)
    small0.update(more)
    dx = attn0.start(dx, blocks)
    dx = ffn0.summed(dx)
    dx, late, attn_total1 = tie(dx, ffn0.total, attn_total1)
    ffn_total0 = lax.psum(late, "dp")

    place = lax.broadcasted_iota(jnp.int32, (2 * CHUNKS_PER_LAYER * ROWS_PER_CHUNK, 1), 0)
    rows = jnp.zeros((place.shape[0], width), F32)
    for l, small in enumerate((small0, small1)):
        base = l * CHUNKS_PER_LAYER * ROWS_PER_CHUNK
        for i, k in enumerate(VECTORS):
            rows = rows + jnp.where(place == base + 2 * ROWS_PER_CHUNK + i, small[k][None], 0.0)
    rows, mark = tie(rows.reshape(2 * CHUNKS_PER_LAYER, ROWS_PER_CHUNK, width), late)
    rows = attn0.swapped(rows)
    total = total_over_all(rows, [(small["eb"], small["heads"]) for small in (small0, small1)])
    total = attn0.crossed(total)
    total = attn0.summed(total)
    attn_total0, ffn_total0 = tie(attn0.total, ffn_total0)
    attn_total0 = lax.psum(attn_total0, "dp")

    hb, eb, vector_sums = [], [], []
    for l in range(2):
        base = l * CHUNKS_PER_LAYER
        own = lax.dynamic_slice(total[base : base + 2], (0, mine, 0), (2, 1, width))[:, 0]
        eb.append(own[0])
        hb.append(jnp.stack([own[1, :head_cols], own[1, head_cols : 2 * head_cols]]))
        rows = total[base + 2 : base + CHUNKS_PER_LAYER].reshape(-1, width)
        vector_sums.append({k: rows[i] for i, k in enumerate(VECTORS)})
    sums = vector_sums

    ge1, gs1 = finish_part(ffn_total1, side)
    gh1, gp1 = attn_unpack(*finish_part(attn_total1, side))
    ge0, gs0 = finish_part(ffn_total0, side)
    gh0, gp0 = attn_unpack(*finish_part(attn_total0, side))

    return (
        to_places((backbone * valid).astype(BF))[None],
        to_places((head * valid).astype(BF))[None],
        span_loss,
        to_places(dx.astype(BF))[None],
        to_places(grad_skip)[None],
        jnp.stack([gh0, gh1]),
        jnp.stack(hb),
        jnp.stack([gp0, gp1]),
        jnp.stack([s["pb"] for s in sums]),
        jnp.stack([jnp.stack([s["g0"], s["g1"]]) for s in sums]),
        jnp.stack([jnp.stack([s["s0"], s["s1"]]) for s in sums]),
        jnp.stack([ge0, ge1]),
        jnp.stack(eb),
        jnp.stack([gs0, gs1]),
        jnp.stack([s["sb"] for s in sums]),
    )


def solution(mesh):
    rows = P("span", "dp", "tensor", None)
    in_specs = (
        rows, rows, rows, rows, P("span", "dp", None), P(),
        P(None, None, None, "tensor"), P(None, None, "tensor"), P(None, "tensor", None),
        P(), P(), P(), P(None, None, "tensor"), P(None, "tensor"), P(None, "tensor", None), P(),
    )
    out_specs = (
        rows, rows, P(), rows, rows,
        P(None, None, None, "tensor"), P(None, None, "tensor"), P(None, "tensor", None),
        P(), P(), P(), P(None, None, "tensor"), P(None, "tensor"), P(None, "tensor", None), P(),
    )
    return jax.shard_map(shards, mesh=mesh, in_specs=in_specs, out_specs=out_specs, check_vma=False)
```

```python
import math

import jax
import jax.numpy as jnp
from jax import lax
from jax.experimental import pallas as pl
from jax.experimental.pallas import tpu as pltpu
from jax.sharding import PartitionSpec as P

HEAD_DIM = 64
EPSILON = 1e-12
LOSS_WEIGHT = 8.0
HIGHEST = lax.Precision.HIGHEST
MASKED = -1e30
BF = jnp.bfloat16
F32 = jnp.float32
PLANE = ("span", "tensor")
MESH = pl.DeviceIdType.MESH
TENSORS = 4
MAIN, DIAG, SWAP = "main", "diag", "swap"


def mm(a, b, ca, cb):
    return lax.dot_general(a, b, (((ca,), (cb,)), ((), ())), preferred_element_type=F32)


def normal_parts(values):
    centred = values - jnp.mean(values, axis=-1, keepdims=True)
    spread = jnp.mean(centred * centred, axis=-1, keepdims=True)
    scale = lax.rsqrt(spread + EPSILON)
    return centred * scale, scale


def normal_back(upward, normed, scale, gain):
    weighted = upward * gain
    first = jnp.mean(weighted, axis=-1, keepdims=True)
    second = jnp.mean(weighted * normed, axis=-1, keepdims=True)
    return (weighted - first - normed * second) * scale


def gelu_parts(hidden):
    phi = 0.5 * (1.0 + lax.erf(hidden * math.sqrt(0.5)))
    slope = phi + hidden * jnp.exp(-0.5 * hidden * hidden) * (1.0 / math.sqrt(2.0 * math.pi))
    return hidden * phi, slope


def plane_pairs(kind):
    pairs = []
    for side in range(2):
        for t in range(TENSORS):
            if kind == SWAP:
                target = (1 - side, t)
            elif kind == MAIN:
                target = (side, t ^ (1 + side))
            else:
                target = (side, t ^ (2 - side))
            pairs.append((side * TENSORS + t, target[0] * TENSORS + target[1]))
    return pairs


def send(values, kind):
    return lax.ppermute(values, PLANE, plane_pairs(kind))


def plus(*terms):
    total = terms[0].astype(F32)
    for term in terms[1:]:
        total = total + term.astype(F32)
    return total.astype(BF)


def pick(side, zero, one):
    return jnp.where(side == 0, zero, one)


def tie(*values):
    return lax.optimization_barrier(values)


class Gathering:
    def __init__(self, side):
        self.side = side

    def start(self, value, first, second):
        value, first, second = tie(value, first, second)
        self.got = (send(first, MAIN), send(second, MAIN))
        self.blocks = [(first, second)]
        return value

    def arrived(self, value):
        value, *got = tie(value, *self.got)
        self.across = send(pick(self.side, *got), DIAG)
        self.blocks += [tuple(got), tuple(send(g, SWAP) for g in got)]
        return value

    def crossed(self, value):
        value, across = tie(value, self.across)
        rest = send(across, SWAP)
        self.blocks.append((pick(self.side, across, rest), pick(self.side, rest, across)))
        return value


def reduce_outgoing(blocks):
    return blocks[2][0], blocks[2][1], blocks[3][1], blocks[0][1]


def reduce_swapped(blocks, outgoing):
    got = [send(o, SWAP) for o in outgoing]
    return (
        plus(blocks[1][1], got[0]), plus(blocks[1][0], got[1]), plus(blocks[3][0], got[2]), plus(blocks[0][0], got[3])
    )


def reduce_across(main_own, across):
    return plus(main_own, send(across, DIAG))


def finish_part(mine, side):
    other = send(mine, SWAP)
    return pick(side, mine, other).astype(F32), pick(side, other, mine).astype(F32)


Q_ROWS = 128


def attend_forward_kernel(
    layer, x_ref, first_ref, second_ref, bias_ref, z_ref, down_ref, across_ref,
    q_ref, k_ref, v_ref, o_ref, lse_ref, out_ref
):
    tokens, width = q_ref.shape
    at = 2 * layer * width
    x = x_ref[...]
    q_ref[...] = (mm(x, first_ref[:width, :], 1, 1) + bias_ref[:, at : at + width]).astype(BF)
    k_ref[...] = mm(x, first_ref[width : 2 * width, :], 1, 1).astype(BF)
    v_ref[...] = (mm(x, second_ref[:width, :], 1, 1) + bias_ref[:, at + width : at + 2 * width]).astype(BF)

    def step(i, carry):
        rows = pl.ds(pl.multiple_of(i * Q_ROWS, Q_ROWS), Q_ROWS)
        same = down_ref[rows, :] == across_ref[...]
        for h in range(width // HEAD_DIM):
            head = slice(h * HEAD_DIM, (h + 1) * HEAD_DIM)
            s = mm(q_ref[rows, head], k_ref[:, head], 1, 1) * 0.125
            s = jnp.where(same, s, MASKED)
            top = jnp.max(s, axis=-1, keepdims=True)
            raised = jnp.exp(s - top)
            total = jnp.sum(raised, axis=-1, keepdims=True)
            weights = (raised * (1.0 / total)).astype(BF)
            o_ref[rows, head] = mm(weights, v_ref[:, head], 1, 0).astype(BF)
            lse_ref[rows, h : h + 1] = top + jnp.log(total)
        out_ref[rows, :] = z_ref[rows, :] + mm(o_ref[rows, :], second_ref[width : 2 * width, :], 1, 0)
        return carry

    lax.fori_loop(0, tokens // Q_ROWS, step, 0)


def attend_backward_kernel(
    da_ref, x_ref, first_ref, second_ref, q_ref, k_ref, v_ref, o_ref, lse_ref, dx_ref, down_ref, across_ref,
    own_ref, rest_ref, sums_ref, out_ref, do_ref, dq_ref, dk_ref, dv_ref
):
    tokens, width = q_ref.shape
    da = da_ref[...]
    do_ref[...] = mm(da, second_ref[width : 2 * width, :], 1, 1).astype(BF)
    dk_ref[...] = jnp.zeros_like(dk_ref)
    dv_ref[...] = jnp.zeros_like(dv_ref)

    def step(i, carry):
        rows = pl.ds(pl.multiple_of(i * Q_ROWS, Q_ROWS), Q_ROWS)
        same = down_ref[rows, :] == across_ref[...]
        for h in range(width // HEAD_DIM):
            head = slice(h * HEAD_DIM, (h + 1) * HEAD_DIM)
            q, k, up = q_ref[rows, head], k_ref[:, head], do_ref[rows, head]
            s = mm(q, k, 1, 1) * 0.125
            s = jnp.where(same, s, MASKED)
            pr = jnp.exp(s - lse_ref[rows, h : h + 1])
            dp = mm(up, v_ref[:, head], 1, 1)
            inner = jnp.sum(pr * dp, axis=-1, keepdims=True)
            ds = (pr * (dp - inner)).astype(BF)
            dq_ref[rows, head] = (mm(ds, k, 1, 0) * 0.125).astype(BF)
            dk_ref[:, head] += mm(ds, q, 0, 0)
            dv_ref[:, head] += mm(pr.astype(BF), up, 0, 0)
        return carry

    lax.fori_loop(0, tokens // Q_ROWS, step, 0)
    x = x_ref[...]
    dq = dq_ref[...]
    dk = (dk_ref[...] * 0.125).astype(BF)
    dv = dv_ref[...].astype(BF)
    out_ref[...] = (
        dx_ref[...]
        + mm(dq, first_ref[:width, :], 1, 0)
        + mm(dk, first_ref[width : 2 * width, :], 1, 0)
        + mm(dv, second_ref[:width, :], 1, 0)
    )
    side = lax.axis_index("span")
    store_both(
        side, own_ref, rest_ref, slice(0, width), mm(dq, x, 0, 0).astype(BF), mm(dv, x, 0, 0).astype(BF)
    )
    store_both(
        side, own_ref, rest_ref, slice(width, 2 * width),
        mm(dk, x, 0, 0).astype(BF), mm(o_ref[...], da, 0, 0).astype(BF),
    )
    sums_ref[:, :width] = jnp.sum(dq.astype(F32), axis=0, keepdims=True)
    sums_ref[:, width:] = jnp.sum(dv.astype(F32), axis=0, keepdims=True)


def small_cost():
    return pl.CostEstimate(flops=1 << 20, bytes_accessed=1 << 10, transcendentals=0)


def kernel_params():
    return pltpu.CompilerParams(vmem_limit_bytes=24 << 20)


def store_both(side, own_ref, rest_ref, rows, first, second):
    @pl.when(side == 0)
    def _():
        own_ref[rows, :] = first
        rest_ref[rows, :] = second

    @pl.when(side != 0)
    def _():
        own_ref[rows, :] = second
        rest_ref[rows, :] = first


def ffn_backward_kernel(
    dz_ref, y_ref, act_ref, slope_ref, first_ref, second_ref, dy_ref, own_ref, rest_ref, sums_ref, out_ref, dh_ref
):
    tokens, model = dz_ref.shape
    side = lax.axis_index("span")
    sums_ref[...] = jnp.zeros_like(sums_ref)

    def data(i, carry):
        rows = pl.ds(pl.multiple_of(i * Q_ROWS, Q_ROWS), Q_ROWS)
        dhid = mm(dz_ref[rows, :], second_ref[...], 1, 1) * slope_ref[rows, :].astype(F32)
        sums_ref[...] += jnp.sum(dhid, axis=0, keepdims=True)
        dhb = dhid.astype(BF)
        dh_ref[rows, :] = dhb
        out_ref[rows, :] = dy_ref[rows, :] + mm(dhb, first_ref[...], 1, 1)
        return carry

    def weights(i, carry):
        rows = pl.ds(pl.multiple_of(i * Q_ROWS, Q_ROWS), Q_ROWS)
        first = mm(y_ref[:, rows], dh_ref[...], 0, 0).astype(BF)
        second = mm(act_ref[:, rows], dz_ref[...], 0, 0).astype(BF)
        store_both(side, own_ref, rest_ref, rows, first, second)
        return carry

    lax.fori_loop(0, tokens // Q_ROWS, data, 0)
    lax.fori_loop(0, model // Q_ROWS, weights, 0)


def ffn_block_backward(dzb, yb, act, slope, first, second, dy):
    return pl.pallas_call(
        ffn_backward_kernel,
        name="ffn_backward",
        out_shape=(
            jax.ShapeDtypeStruct(first.shape, BF),
            jax.ShapeDtypeStruct(first.shape, BF),
            jax.ShapeDtypeStruct((1, act.shape[1]), F32),
            jax.ShapeDtypeStruct(dy.shape, F32),
        ),
        scratch_shapes=[pltpu.VMEM(act.shape, BF)],
        compiler_params=kernel_params(),
        cost_estimate=small_cost(),
    )(dzb, yb, act, slope, first, second, dy)


def attend_forward(layer, cols, x, first, second, bias, z, seg):
    tokens, model = x.shape
    narrow = jax.ShapeDtypeStruct((tokens, cols), BF)

    def body(*refs):
        attend_forward_kernel(layer, *refs)

    return pl.pallas_call(
        body,
        name="attend_forward",
        out_shape=(
            narrow, narrow, narrow, narrow,
            jax.ShapeDtypeStruct((tokens, cols // HEAD_DIM), F32),
            jax.ShapeDtypeStruct(z.shape, F32),
        ),
        compiler_params=kernel_params(),
        cost_estimate=small_cost(),
    )(x, first, second, bias, z, *seg)


def attend_backward(cols, da, x, first, second, kept, dx, seg):
    tokens, model = x.shape
    return pl.pallas_call(
        attend_backward_kernel,
        name="attend_backward",
        out_shape=(
            jax.ShapeDtypeStruct((2 * cols, model), BF),
            jax.ShapeDtypeStruct((2 * cols, model), BF),
            jax.ShapeDtypeStruct((1, 2 * cols), F32),
            jax.ShapeDtypeStruct(dx.shape, F32),
        ),
        scratch_shapes=[
            pltpu.VMEM((tokens, cols), BF), pltpu.VMEM((tokens, cols), BF),
            pltpu.VMEM((tokens, cols), F32), pltpu.VMEM((tokens, cols), F32),
        ],
        compiler_params=kernel_params(),
        cost_estimate=small_cost(),
    )(da, x, first, second, *kept, dx, *seg)


def anchors_kernel(dps, planes, x_ref, out_ref, near_send, near_recv, far_send, far_recv, own_sem):
    dp = lax.axis_index("dp")
    me = lax.axis_index("span") * TENSORS + lax.axis_index("tensor")

    def near(k):
        peer = lax.rem(me + k, planes)
        return {"span": peer // TENSORS, "tensor": lax.rem(peer, TENSORS)}

    def far(k):
        return {"dp": lax.rem(dp + k, dps)}

    barrier = pltpu.get_barrier_semaphore()
    for k in range(1, planes):
        pl.semaphore_signal(barrier, inc=1, device_id=near(k), device_id_type=MESH)
    for k in range(1, dps):
        pl.semaphore_signal(barrier, inc=1, device_id=far(k), device_id_type=MESH)
    pl.semaphore_wait(barrier, planes + dps - 2)

    own = pltpu.make_async_copy(x_ref, out_ref.at[dp, me], own_sem)
    own.start()

    def near_copy(k):
        return pltpu.make_async_remote_copy(
            src_ref=x_ref, dst_ref=out_ref.at[dp, me], send_sem=near_send.at[k],
            recv_sem=near_recv.at[k], device_id=near(k), device_id_type=MESH,
        )

    def far_copy(k):
        return pltpu.make_async_remote_copy(
            src_ref=out_ref.at[dp], dst_ref=out_ref.at[dp], send_sem=far_send.at[k],
            recv_sem=far_recv.at[k], device_id=far(k), device_id_type=MESH,
        )

    for k in range(1, planes):
        near_copy(k).start()
    own.wait()
    for k in range(1, planes):
        near_copy(k).wait()
    for k in range(1, dps):
        far_copy(k).start()
    for k in range(1, dps):
        far_copy(k).wait()


def gather_anchors(values):
    dps = lax.axis_size("dp")
    planes = lax.axis_size("span") * lax.axis_size("tensor")
    dma = pltpu.SemaphoreType.DMA
    vmem = pl.BlockSpec(memory_space=pltpu.VMEM)

    def body(*refs):
        anchors_kernel(dps, planes, *refs)

    return pl.pallas_call(
        body,
        name="gather_anchors",
        out_shape=jax.ShapeDtypeStruct((dps, planes) + values.shape, values.dtype),
        in_specs=[vmem],
        out_specs=vmem,
        scratch_shapes=[dma((planes,)), dma((planes,)), dma((dps,)), dma((dps,)), dma],
        compiler_params=pltpu.CompilerParams(collective_id=0, has_side_effects=True),
    )(values)


VECTORS = ("pb", "g0", "g1", "s0", "s1", "sb")
ROWS_PER_CHUNK = 4
CHUNKS_PER_LAYER = 4


def block_order(side, tensor):
    flip_one = tensor + 1 - 2 * lax.rem(tensor, 2)
    flip_two = tensor + 2 - 4 * (tensor // 2)
    swing = side * (flip_two - flip_one)
    return tensor, flip_one + swing, flip_two - swing, TENSORS - 1 - tensor


def total_kernel(dps, planes, rows_ref, blocks, out_ref, x_ref, parts, sums, sems):
    one_send, one_recv, two_send, two_recv, three_send, three_recv = sems
    dp = lax.axis_index("dp")
    side = lax.axis_index("span")
    tensor = lax.axis_index("tensor")
    me = side * TENSORS + tensor
    order = block_order(side, tensor)
    x_ref[...] = rows_ref[...]
    for l in range(2):
        for j in range(TENSORS):
            for k in range(2):
                columns = blocks[l][k][j].shape[1]
                x_ref[l * CHUNKS_PER_LAYER + k, pl.ds(order[j], 1), :columns] = blocks[l][k][j][...]

    def near_peer(k):
        return lax.rem(me + k, planes)

    def near(k):
        peer = near_peer(k)
        return {"span": peer // TENSORS, "tensor": lax.rem(peer, TENSORS)}

    def far(k):
        return {"dp": lax.rem(dp + k, dps)}

    barrier = pltpu.get_barrier_semaphore()
    for k in range(1, planes):
        pl.semaphore_signal(barrier, inc=1, device_id=near(k), device_id_type=MESH)
    for k in range(1, dps):
        pl.semaphore_signal(barrier, inc=1, device_id=far(k), device_id_type=MESH)
    pl.semaphore_wait(barrier, planes + dps - 2)

    def one(k):
        return pltpu.make_async_remote_copy(
            src_ref=x_ref.at[near_peer(k)], dst_ref=parts.at[k], send_sem=one_send.at[k],
            recv_sem=one_recv.at[k], device_id=near(k), device_id_type=MESH,
        )

    def two(k):
        return pltpu.make_async_remote_copy(
            src_ref=sums.at[dp], dst_ref=sums.at[dp], send_sem=two_send.at[k],
            recv_sem=two_recv.at[k], device_id=far(k), device_id_type=MESH,
        )

    def three(k):
        return pltpu.make_async_remote_copy(
            src_ref=out_ref.at[me], dst_ref=out_ref.at[me], send_sem=three_send.at[k],
            recv_sem=three_recv.at[k], device_id=near(k), device_id_type=MESH,
        )

    for k in range(1, planes):
        one(k).start()
    for k in range(1, planes):
        one(k).wait()
    total = x_ref[me]
    for k in range(1, planes):
        total = total + parts[k]
    sums[dp] = total
    for k in range(1, dps):
        two(k).start()
    for k in range(1, dps):
        two(k).wait()
    total = sums[0]
    for k in range(1, dps):
        total = total + sums[k]
    out_ref[me] = total
    for k in range(1, planes):
        three(k).start()
    for k in range(1, planes):
        three(k).wait()


def total_over_all(rows, blocks):
    dps = lax.axis_size("dp")
    planes = lax.axis_size("span") * lax.axis_size("tensor")
    flat, tree = jax.tree.flatten(blocks)
    shape = rows.shape
    dma = pltpu.SemaphoreType.DMA
    vmem = pl.BlockSpec(memory_space=pltpu.VMEM)

    def body(rows_ref, *refs):
        inputs = jax.tree.unflatten(tree, refs[: len(flat)])
        out_ref, x_ref, parts, sums = refs[len(flat) : len(flat) + 4]
        total_kernel(dps, planes, rows_ref, inputs, out_ref, x_ref, parts, sums, refs[len(flat) + 4 :])

    return pl.pallas_call(
        body,
        name="total_over_all",
        out_shape=jax.ShapeDtypeStruct(shape, F32),
        in_specs=[vmem] * (1 + len(flat)),
        out_specs=vmem,
        scratch_shapes=[
            pltpu.VMEM(shape, F32),
            pltpu.VMEM(shape, F32),
            pltpu.VMEM((dps,) + shape[1:], F32),
            dma((planes,)), dma((planes,)), dma((dps,)), dma((dps,)), dma((planes,)), dma((planes,)),
        ],
        compiler_params=pltpu.CompilerParams(collective_id=1, has_side_effects=True),
    )(rows, *flat)


def to_rows(values):
    return lax.all_to_all(values, "tensor", split_axis=0, concat_axis=0, tiled=True).reshape(
        -1, values.shape[-1]
    )


def to_places(values):
    blocks = values.reshape(TENSORS, -1, values.shape[-1])
    return lax.all_to_all(blocks, "tensor", split_axis=0, concat_axis=0, tiled=True)


def layer_forward(l, x, seg, attn, ffn, vec, hook):
    xb = x.astype(BF)
    kept = []
    z1 = x + vec["pb"]
    for j in range(TENSORS):
        first, second = attn.blocks[j]
        *saved, z1 = attend_forward(l, vec["cols"], xb, first, second, vec["heads"](j), z1, seg)
        kept.append(saved)
        z1 = hook("attn", j, z1)
    n1, r1 = normal_parts(z1)
    y = n1 * vec["g0"] + vec["s0"]
    yb = y.astype(BF)
    act, slope = [], []
    z2 = y + vec["sb"]
    for j in range(TENSORS):
        first, second = ffn.blocks[j]
        a, b = gelu_parts(mm(yb, first, 1, 0) + vec["eb"](j))
        act.append(a.astype(BF))
        slope.append(b.astype(BF))
        z2 = z2 + mm(act[-1], second, 1, 0)
        z2 = hook("ffn", j, z2)
    n2, r2 = normal_parts(z2)
    out = n2 * vec["g1"] + vec["s1"]
    return out, (xb, kept, n1, r1, yb, act, slope, n2, r2)


def total_rows(values):
    return jnp.sum(values, axis=0)


def ffn_backward(dout, ffn_w, vec, kept, hook):
    xb, saved, n1, r1, yb, act, slope, n2, r2 = kept
    dz2 = normal_back(dout, n2, r2, vec["g1"])
    small = {"g1": total_rows(dout * n2), "s1": total_rows(dout), "sb": total_rows(dz2), "eb": []}
    dz2 = hook("seeded", dz2)
    dzb = dz2.astype(BF)
    dy = dz2
    blocks = []
    for j, (first, second) in enumerate(ffn_w):
        own, rest, sums, dy = ffn_block_backward(dzb, yb, act[j], slope[j], first, second, dy)
        small["eb"].append(sums)
        blocks.append((own, rest))
        if j == 2:
            dzb, dy = hook("three", (dzb, dy))
    return dy, blocks, small


def attn_backward(dy, seg, attn_w, vec, kept, hook):
    xb, saved, n1, r1, yb, act, slope, n2, r2 = kept
    dz1 = normal_back(dy, n1, r1, vec["g0"])
    small = {"g0": total_rows(dy * n1), "s0": total_rows(dy), "pb": total_rows(dz1), "heads": []}
    dz1 = hook("normed", dz1)
    da = dz1.astype(BF)
    dx = dz1
    blocks = []
    for j, (first, second) in enumerate(attn_w):
        dfirst, dsecond, sums, dx = attend_backward(vec["cols"], da, xb, first, second, saved[j], dx, seg)
        small["heads"].append(sums)
        blocks.append((dfirst, dsecond))
        if j == 2:
            da, dx = hook("three", (da, dx))
    return dx, blocks, small


def attn_unpack(first, second):
    cols = first.shape[0] // 2
    heads = jnp.stack([first[:cols], first[cols:], second[:cols]])
    return jnp.swapaxes(heads, 1, 2), second[cols:]


class Reduction:
    def start(self, value, blocks):
        self.blocks = blocks
        value, *self.outgoing = tie(value, *reduce_outgoing(blocks))
        return value

    def swapped(self, value):
        value, self.main_rest, self.main_own, self.across, self.mine = tie(
            value, *reduce_swapped(self.blocks, self.outgoing)
        )
        self.from_rest = send(self.main_rest, MAIN)
        return value

    def crossed(self, value):
        value, self.main_own = tie(value, reduce_across(self.main_own, self.across))
        self.from_own = send(self.main_own, MAIN)
        self.from_peer = send(self.from_rest, SWAP)
        return value

    def summed(self, value):
        value, self.total = tie(value, plus(self.mine, self.from_own, self.from_peer))
        return value


def shards(
    layer_input, skip_tokens, backbone_cotangent, head_cotangent, segment_lengths, pair_index,
    w_heads, heads_bias, w_project, project_bias, norm_gain, norm_shift,
    w_expand, expand_bias, w_shrink, shrink_bias,
):
    side = lax.axis_index("span")
    mine = lax.axis_index("tensor")
    width = layer_input.shape[-1]
    head_cols = w_heads.shape[-1]
    ff_cols = w_expand.shape[-1]

    extra = 16
    bias_rows = jnp.concatenate([heads_bias.reshape(1, 4 * head_cols), expand_bias], axis=0)
    bias_rows = jnp.pad(bias_rows, ((0, extra - bias_rows.shape[0]), (0, 0)))

    def attn_rows(l):
        heads = jnp.swapaxes(w_heads[l], 1, 2)
        first = heads[:2].reshape(2 * head_cols, width)
        return first, jnp.concatenate([heads[2], w_project[l]], axis=0)

    first, second = attn_rows(0)
    first = jnp.concatenate([first, bias_rows], axis=0)
    second = jnp.pad(second, ((0, extra), (0, 0)))
    gather_attn0, gather_ffn0, gather_attn1, gather_ffn1 = (Gathering(side) for _ in range(4))
    x = to_rows(layer_input[0])
    mark = gather_attn0.start(layer_input[0, 0, 0], first, second)
    mark = gather_ffn0.start(mark, w_expand[0], w_shrink[0])
    later = {}

    def during_forward0(kind, j, value):
        if kind == "attn":
            if j == 0:
                value = gather_attn0.arrived(value)
            if j == 1:
                value = gather_attn1.start(value, *attn_rows(1))
            if j == 2:
                value = gather_attn0.crossed(value)
            if j == 3:
                value = gather_ffn0.arrived(value)
                value = gather_ffn1.start(value, w_expand[1], w_shrink[1])
        else:
            if j == 0:
                skip, value = tie(skip_tokens[0], value)
                later["skip"] = to_rows(skip)
            if j == 1:
                value = gather_attn1.arrived(value)
            if j == 2:
                value = gather_ffn0.crossed(value)
        return value

    def during_forward1(kind, j, value):
        if kind == "attn":
            if j == 0:
                head_cot, value = tie(head_cotangent[0], value)
                later["head"] = to_rows(head_cot)
            if j == 1:
                value = gather_attn1.crossed(value)
            if j == 2:
                value, later["backbone_out"] = tie(value, later["backbone_out"])
            if j == 3:
                value = gather_ffn1.arrived(value)
        else:
            if j == 0:
                backbone_cot, value = tie(backbone_cotangent[0], value)
                later["backbone"] = to_rows(backbone_cot)
            if j == 2:
                value = gather_ffn1.crossed(value)
        return value

    tokens = x.shape[0]

    def bias_row(j, i):
        first, second = gather_attn0.blocks[j]
        return first[2 * head_cols + i : 2 * head_cols + i + 1].astype(F32)

    def vectors(l):
        return {
            "cols": head_cols, "heads": lambda j: bias_row(j, 0),
            "eb": lambda j: bias_row(j, 1 + l), "pb": project_bias[l].astype(F32),
            "g0": norm_gain[l, 0].astype(F32), "g1": norm_gain[l, 1].astype(F32),
            "s0": norm_shift[l, 0].astype(F32), "s1": norm_shift[l, 1].astype(F32),
            "sb": shrink_bias[l].astype(F32),
        }

    lengths = lax.dynamic_index_in_dim(segment_lengths[0], mine, 0, keepdims=False)
    span_count = lengths.shape[0]
    starts = jnp.cumsum(lengths) - lengths
    row_length = jnp.sum(lengths)
    places = jnp.arange(tokens, dtype=jnp.int32)
    counted = jnp.sum((places[:, None] >= starts[None, :]).astype(jnp.int32), axis=-1) - 1
    segment = jnp.where(places < row_length, counted, span_count)
    seg = (segment[:, None], segment[None, :])
    valid = (places < row_length).astype(F32)[:, None]
    picker = (starts[:, None] == places[None, :]).astype(F32)
    first_place = jnp.sum(picker, axis=0)[:, None] > 0

    vec0, vec1 = vectors(0), vectors(1)
    backbone, kept0 = layer_forward(0, x.astype(F32), seg, gather_attn0, gather_ffn0, vec0, during_forward0)
    attn_w0, ffn_w0 = gather_attn0.blocks, gather_ffn0.blocks
    later["backbone_out"] = to_places((backbone * valid).astype(BF))
    cls = mm(picker.astype(BF), backbone.astype(BF), 1, 0).astype(BF)
    anchors = gather_anchors(cls)
    dp_count = lax.axis_size("dp")
    pair_count = lax.axis_size("span")
    vector_count = dp_count * TENSORS * span_count
    anchors = anchors.reshape(dp_count, pair_count, TENSORS * span_count, width)
    anchors = jnp.swapaxes(anchors, 0, 1).reshape(pair_count, vector_count, width)

    head_in = jnp.where(first_place, backbone, later["skip"].astype(F32))
    head, kept1 = layer_forward(1, head_in, seg, gather_attn1, gather_ffn1, vec1, during_forward1)
    attn_w1, ffn_w1 = gather_attn1.blocks, gather_ffn1.blocks
    head_cot, backbone_cot = later["head"], later["backbone"]
    head_out = to_places((head * valid).astype(BF))

    root = math.sqrt(width)
    logits = mm(anchors[0], anchors[1], 1, 1) / root
    columns = jnp.arange(vector_count, dtype=jnp.int32)
    target = (pair_index[:, None] == columns[None, :]).astype(F32)
    lse_rows = jax.nn.logsumexp(logits, axis=1)
    lse_cols = jax.nn.logsumexp(logits, axis=0)
    dlogits = LOSS_WEIGHT * (
        jnp.exp(logits - lse_rows[:, None]) + jnp.exp(logits - lse_cols[None, :]) - 2.0 * target
    )
    span_loss = (jnp.sum(lse_rows) + jnp.sum(lse_cols) - 2.0 * jnp.sum(target * logits)) / (
        2 * vector_count
    )
    own = (lax.axis_index("dp") * TENSORS + mine) * span_count
    wanted = jnp.where(side == 0, dlogits, dlogits.T)
    wanted = lax.dynamic_slice(wanted, (own, 0), (span_count, vector_count))
    other = lax.dynamic_index_in_dim(anchors, 1 - side, 0, keepdims=False).astype(F32)
    dcls = jnp.dot(wanted, other, precision=HIGHEST) / root

    def plain(name, value):
        return value

    ffn1, attn1, ffn0, attn0 = (Reduction() for _ in range(4))

    dy, blocks, small1 = ffn_backward(head_cot.astype(F32) * valid, ffn_w1, vec1, kept1, plain)
    dy, head_out = tie(dy, head_out)
    dy = ffn1.start(dy, blocks)

    def during_attn1(name, value):
        if name == "normed":
            return ffn1.swapped(value)
        return ffn1.crossed(value)

    du, blocks, more = attn_backward(dy, seg, attn_w1, vec1, kept1, during_attn1)
    small1.update(more)
    du = attn1.start(du, blocks)
    du = ffn1.summed(du)
    ffn_total1 = lax.psum(ffn1.total, "dp")
    grad_skip = to_places(jnp.where(first_place, 0.0, du).astype(BF))

    seed = backbone_cot.astype(F32) * valid + jnp.where(first_place, du, 0.0)
    seed = seed + jnp.dot(picker.T, dcls, precision=HIGHEST)

    def during_ffn0(name, value):
        if name == "seeded":
            return attn1.swapped(value)
        return attn1.crossed(value)

    dy, blocks, small0 = ffn_backward(seed, ffn_w0, vec0, kept0, during_ffn0)
    dy, grad_skip = tie(dy, grad_skip)
    dy = ffn0.start(dy, blocks)
    dy = attn1.summed(dy)

    def during_attn0(name, value):
        if name == "normed":
            return ffn0.swapped(value)
        return ffn0.crossed(value)

    dy, ffn_total1, attn_total1 = tie(dy, ffn_total1, attn1.total)
    attn_total1 = lax.psum(attn_total1, "dp")

    dx, blocks, more = attn_backward(dy, seg, attn_w0, vec0, kept0, during_attn0)
    small0.update(more)
    dx = attn0.start(dx, blocks)
    dx = ffn0.summed(dx)
    dx, late, attn_total1 = tie(dx, ffn0.total, attn_total1)
    ffn_total0 = lax.psum(late, "dp")

    place = lax.broadcasted_iota(jnp.int32, (2 * CHUNKS_PER_LAYER * ROWS_PER_CHUNK, 1), 0)
    rows = jnp.zeros((place.shape[0], width), F32)
    for l, small in enumerate((small0, small1)):
        base = l * CHUNKS_PER_LAYER * ROWS_PER_CHUNK
        for i, k in enumerate(VECTORS):
            rows = rows + jnp.where(place == base + 2 * ROWS_PER_CHUNK + i, small[k][None], 0.0)
    rows, mark = tie(rows.reshape(2 * CHUNKS_PER_LAYER, ROWS_PER_CHUNK, width), late)
    rows = attn0.swapped(rows)
    total = total_over_all(rows, [(small["eb"], small["heads"]) for small in (small0, small1)])
    total = attn0.crossed(total)
    total = attn0.summed(total)
    attn_total0, ffn_total0 = tie(attn0.total, ffn_total0)
    attn_total0 = lax.psum(attn_total0, "dp")

    hb, eb, vector_sums = [], [], []
    for l in range(2):
        base = l * CHUNKS_PER_LAYER
        own = lax.dynamic_slice(total[base : base + 2], (0, mine, 0), (2, 1, width))[:, 0]
        eb.append(own[0])
        hb.append(jnp.stack([own[1, :head_cols], own[1, head_cols : 2 * head_cols]]))
        rows = total[base + 2 : base + CHUNKS_PER_LAYER].reshape(-1, width)
        vector_sums.append({k: rows[i] for i, k in enumerate(VECTORS)})
    sums = vector_sums

    ge1, gs1 = finish_part(ffn_total1, side)
    gh1, gp1 = attn_unpack(*finish_part(attn_total1, side))
    ge0, gs0 = finish_part(ffn_total0, side)
    gh0, gp0 = attn_unpack(*finish_part(attn_total0, side))

    return (
        later["backbone_out"][None],
        head_out[None],
        span_loss,
        to_places(dx.astype(BF))[None],
        grad_skip[None],
        jnp.stack([gh0, gh1]),
        jnp.stack(hb),
        jnp.stack([gp0, gp1]),
        jnp.stack([s["pb"] for s in sums]),
        jnp.stack([jnp.stack([s["g0"], s["g1"]]) for s in sums]),
        jnp.stack([jnp.stack([s["s0"], s["s1"]]) for s in sums]),
        jnp.stack([ge0, ge1]),
        jnp.stack(eb),
        jnp.stack([gs0, gs1]),
        jnp.stack([s["sb"] for s in sums]),
    )


def solution(mesh):
    rows = P("span", "dp", "tensor", None)
    in_specs = (
        rows, rows, rows, rows, P("span", "dp", None), P(),
        P(None, None, None, "tensor"), P(None, None, "tensor"), P(None, "tensor", None),
        P(), P(), P(), P(None, None, "tensor"), P(None, "tensor"), P(None, "tensor", None), P(),
    )
    out_specs = (
        rows, rows, P(), rows, rows,
        P(None, None, None, "tensor"), P(None, None, "tensor"), P(None, "tensor", None),
        P(), P(), P(), P(None, None, "tensor"), P(None, "tensor"), P(None, "tensor", None), P(),
    )
    return jax.shard_map(shards, mesh=mesh, in_specs=in_specs, out_specs=out_specs, check_vma=False)
```

```python
import math

import jax
import jax.numpy as jnp
from jax import lax
from jax.experimental import pallas as pl
from jax.experimental.pallas import tpu as pltpu
from jax.sharding import PartitionSpec as P

HEAD_DIM = 64
EPSILON = 1e-12
LOSS_WEIGHT = 8.0
HIGHEST = lax.Precision.HIGHEST
MASKED = -1e30
BF = jnp.bfloat16
F32 = jnp.float32
PLANE = ("span", "tensor")
MESH = pl.DeviceIdType.MESH
TENSORS = 4
MAIN, DIAG, SWAP = "main", "diag", "swap"


def mm(a, b, ca, cb):
    return lax.dot_general(a, b, (((ca,), (cb,)), ((), ())), preferred_element_type=F32)


def normal_parts(values):
    centred = values - jnp.mean(values, axis=-1, keepdims=True)
    spread = jnp.mean(centred * centred, axis=-1, keepdims=True)
    scale = lax.rsqrt(spread + EPSILON)
    return centred * scale, scale


def normal_back(upward, normed, scale, gain):
    weighted = upward * gain
    first = jnp.mean(weighted, axis=-1, keepdims=True)
    second = jnp.mean(weighted * normed, axis=-1, keepdims=True)
    return (weighted - first - normed * second) * scale


def gelu_parts(hidden):
    phi = 0.5 * (1.0 + lax.erf(hidden * math.sqrt(0.5)))
    slope = phi + hidden * jnp.exp(-0.5 * hidden * hidden) * (1.0 / math.sqrt(2.0 * math.pi))
    return hidden * phi, slope


def plane_pairs(kind):
    pairs = []
    for side in range(2):
        for t in range(TENSORS):
            if kind == SWAP:
                target = (1 - side, t)
            elif kind == MAIN:
                target = (side, t ^ (1 + side))
            else:
                target = (side, t ^ (2 - side))
            pairs.append((side * TENSORS + t, target[0] * TENSORS + target[1]))
    return pairs


def send(values, kind):
    return lax.ppermute(values, PLANE, plane_pairs(kind))


def plus(*terms):
    total = terms[0].astype(F32)
    for term in terms[1:]:
        total = total + term.astype(F32)
    return total.astype(BF)


def pick(side, zero, one):
    return jnp.where(side == 0, zero, one)


def tie(*values):
    return lax.optimization_barrier(values)


class Gathering:
    def __init__(self, side):
        self.side = side

    def start(self, value, first, second):
        value, first, second = tie(value, first, second)
        self.got = (send(first, MAIN), send(second, MAIN))
        self.blocks = [(first, second)]
        return value

    def arrived(self, value):
        value, *got = tie(value, *self.got)
        self.across = send(pick(self.side, *got), DIAG)
        self.blocks += [tuple(got), tuple(send(g, SWAP) for g in got)]
        return value

    def crossed(self, value):
        value, across = tie(value, self.across)
        rest = send(across, SWAP)
        self.blocks.append((pick(self.side, across, rest), pick(self.side, rest, across)))
        return value


def reduce_outgoing(blocks):
    return blocks[2][0], blocks[2][1], blocks[3][1], blocks[0][1]


def reduce_swapped(blocks, outgoing):
    got = [send(o, SWAP) for o in outgoing]
    return (
        plus(blocks[1][1], got[0]), plus(blocks[1][0], got[1]), plus(blocks[3][0], got[2]), plus(blocks[0][0], got[3])
    )


def reduce_across(main_own, across):
    return plus(main_own, send(across, DIAG))


def in_order(side, own, other):
    return pick(side, own, other).astype(F32), pick(side, other, own).astype(F32)


Q_ROWS = 128


def attend_forward_kernel(
    layer, x_ref, first_ref, second_ref, bias_ref, z_ref, down_ref, across_ref,
    q_ref, k_ref, v_ref, o_ref, lse_ref, out_ref
):
    tokens, width = q_ref.shape
    at = 2 * layer * width
    x = x_ref[...]
    q_ref[...] = (mm(x, first_ref[:width, :], 1, 1) + bias_ref[:, at : at + width]).astype(BF)
    k_ref[...] = mm(x, first_ref[width : 2 * width, :], 1, 1).astype(BF)
    v_ref[...] = (mm(x, second_ref[:width, :], 1, 1) + bias_ref[:, at + width : at + 2 * width]).astype(BF)

    def step(i, carry):
        rows = pl.ds(pl.multiple_of(i * Q_ROWS, Q_ROWS), Q_ROWS)
        same = down_ref[rows, :] == across_ref[...]
        for h in range(width // HEAD_DIM):
            head = slice(h * HEAD_DIM, (h + 1) * HEAD_DIM)
            s = mm(q_ref[rows, head], k_ref[:, head], 1, 1) * 0.125
            s = jnp.where(same, s, MASKED)
            top = jnp.max(s, axis=-1, keepdims=True)
            raised = jnp.exp(s - top)
            total = jnp.sum(raised, axis=-1, keepdims=True)
            weights = (raised * (1.0 / total)).astype(BF)
            o_ref[rows, head] = mm(weights, v_ref[:, head], 1, 0).astype(BF)
            lse_ref[rows, h : h + 1] = top + jnp.log(total)
        out_ref[rows, :] = z_ref[rows, :] + mm(o_ref[rows, :], second_ref[width : 2 * width, :], 1, 0)
        return carry

    lax.fori_loop(0, tokens // Q_ROWS, step, 0)


def attend_backward_kernel(
    da_ref, x_ref, first_ref, second_ref, q_ref, k_ref, v_ref, o_ref, lse_ref, dx_ref, down_ref, across_ref,
    own_ref, rest_ref, sums_ref, out_ref, do_ref, dq_ref, dk_ref, dv_ref
):
    tokens, width = q_ref.shape
    da = da_ref[...]
    do_ref[...] = mm(da, second_ref[width : 2 * width, :], 1, 1).astype(BF)
    dk_ref[...] = jnp.zeros_like(dk_ref)
    dv_ref[...] = jnp.zeros_like(dv_ref)

    def step(i, carry):
        rows = pl.ds(pl.multiple_of(i * Q_ROWS, Q_ROWS), Q_ROWS)
        same = down_ref[rows, :] == across_ref[...]
        for h in range(width // HEAD_DIM):
            head = slice(h * HEAD_DIM, (h + 1) * HEAD_DIM)
            q, k, up = q_ref[rows, head], k_ref[:, head], do_ref[rows, head]
            s = mm(q, k, 1, 1) * 0.125
            s = jnp.where(same, s, MASKED)
            pr = jnp.exp(s - lse_ref[rows, h : h + 1])
            dp = mm(up, v_ref[:, head], 1, 1)
            inner = jnp.sum(pr * dp, axis=-1, keepdims=True)
            ds = (pr * (dp - inner)).astype(BF)
            dq_ref[rows, head] = (mm(ds, k, 1, 0) * 0.125).astype(BF)
            dk_ref[:, head] += mm(ds, q, 0, 0)
            dv_ref[:, head] += mm(pr.astype(BF), up, 0, 0)
        return carry

    lax.fori_loop(0, tokens // Q_ROWS, step, 0)
    x = x_ref[...]
    dq = dq_ref[...]
    dk = (dk_ref[...] * 0.125).astype(BF)
    dv = dv_ref[...].astype(BF)
    out_ref[...] = (
        dx_ref[...]
        + mm(dq, first_ref[:width, :], 1, 0)
        + mm(dk, first_ref[width : 2 * width, :], 1, 0)
        + mm(dv, second_ref[:width, :], 1, 0)
    )
    side = lax.axis_index("span")
    store_both(
        side, own_ref, rest_ref, slice(0, width), mm(dq, x, 0, 0).astype(BF), mm(dv, x, 0, 0).astype(BF)
    )
    store_both(
        side, own_ref, rest_ref, slice(width, 2 * width),
        mm(dk, x, 0, 0).astype(BF), mm(o_ref[...], da, 0, 0).astype(BF),
    )
    sums_ref[:, :width] = jnp.sum(dq.astype(F32), axis=0, keepdims=True)
    sums_ref[:, width:] = jnp.sum(dv.astype(F32), axis=0, keepdims=True)


def small_cost():
    return pl.CostEstimate(flops=1 << 20, bytes_accessed=1 << 10, transcendentals=0)


def kernel_params():
    return pltpu.CompilerParams(vmem_limit_bytes=24 << 20)


def store_both(side, own_ref, rest_ref, rows, first, second):
    @pl.when(side == 0)
    def _():
        own_ref[rows, :] = first
        rest_ref[rows, :] = second

    @pl.when(side != 0)
    def _():
        own_ref[rows, :] = second
        rest_ref[rows, :] = first


def ffn_backward_kernel(
    dz_ref, y_ref, act_ref, slope_ref, first_ref, second_ref, dy_ref, own_ref, rest_ref, sums_ref, out_ref, dh_ref
):
    tokens, model = dz_ref.shape
    side = lax.axis_index("span")
    sums_ref[...] = jnp.zeros_like(sums_ref)

    def data(i, carry):
        rows = pl.ds(pl.multiple_of(i * Q_ROWS, Q_ROWS), Q_ROWS)
        dhid = mm(dz_ref[rows, :], second_ref[...], 1, 1) * slope_ref[rows, :].astype(F32)
        sums_ref[...] += jnp.sum(dhid, axis=0, keepdims=True)
        dhb = dhid.astype(BF)
        dh_ref[rows, :] = dhb
        out_ref[rows, :] = dy_ref[rows, :] + mm(dhb, first_ref[...], 1, 1)
        return carry

    def weights(i, carry):
        rows = pl.ds(pl.multiple_of(i * Q_ROWS, Q_ROWS), Q_ROWS)
        first = mm(y_ref[:, rows], dh_ref[...], 0, 0).astype(BF)
        second = mm(act_ref[:, rows], dz_ref[...], 0, 0).astype(BF)
        store_both(side, own_ref, rest_ref, rows, first, second)
        return carry

    lax.fori_loop(0, tokens // Q_ROWS, data, 0)
    lax.fori_loop(0, model // Q_ROWS, weights, 0)


def ffn_block_backward(dzb, yb, act, slope, first, second, dy):
    return pl.pallas_call(
        ffn_backward_kernel,
        name="ffn_backward",
        out_shape=(
            jax.ShapeDtypeStruct(first.shape, BF),
            jax.ShapeDtypeStruct(first.shape, BF),
            jax.ShapeDtypeStruct((1, act.shape[1]), F32),
            jax.ShapeDtypeStruct(dy.shape, F32),
        ),
        scratch_shapes=[pltpu.VMEM(act.shape, BF)],
        compiler_params=kernel_params(),
        cost_estimate=small_cost(),
    )(dzb, yb, act, slope, first, second, dy)


def attend_forward(layer, cols, x, first, second, bias, z, seg):
    tokens, model = x.shape
    narrow = jax.ShapeDtypeStruct((tokens, cols), BF)

    def body(*refs):
        attend_forward_kernel(layer, *refs)

    return pl.pallas_call(
        body,
        name="attend_forward",
        out_shape=(
            narrow, narrow, narrow, narrow,
            jax.ShapeDtypeStruct((tokens, cols // HEAD_DIM), F32),
            jax.ShapeDtypeStruct(z.shape, F32),
        ),
        compiler_params=kernel_params(),
        cost_estimate=small_cost(),
    )(x, first, second, bias, z, *seg)


def attend_backward(cols, da, x, first, second, kept, dx, seg):
    tokens, model = x.shape
    return pl.pallas_call(
        attend_backward_kernel,
        name="attend_backward",
        out_shape=(
            jax.ShapeDtypeStruct((2 * cols, model), BF),
            jax.ShapeDtypeStruct((2 * cols, model), BF),
            jax.ShapeDtypeStruct((1, 2 * cols), F32),
            jax.ShapeDtypeStruct(dx.shape, F32),
        ),
        scratch_shapes=[
            pltpu.VMEM((tokens, cols), BF), pltpu.VMEM((tokens, cols), BF),
            pltpu.VMEM((tokens, cols), F32), pltpu.VMEM((tokens, cols), F32),
        ],
        compiler_params=kernel_params(),
        cost_estimate=small_cost(),
    )(da, x, first, second, *kept, dx, *seg)


def anchors_kernel(dps, planes, x_ref, out_ref, near_send, near_recv, far_send, far_recv, own_sem):
    dp = lax.axis_index("dp")
    me = lax.axis_index("span") * TENSORS + lax.axis_index("tensor")

    def near(k):
        peer = lax.rem(me + k, planes)
        return {"span": peer // TENSORS, "tensor": lax.rem(peer, TENSORS)}

    def far(k):
        return {"dp": lax.rem(dp + k, dps)}

    barrier = pltpu.get_barrier_semaphore()
    for k in range(1, planes):
        pl.semaphore_signal(barrier, inc=1, device_id=near(k), device_id_type=MESH)
    for k in range(1, dps):
        pl.semaphore_signal(barrier, inc=1, device_id=far(k), device_id_type=MESH)
    pl.semaphore_wait(barrier, planes + dps - 2)

    own = pltpu.make_async_copy(x_ref, out_ref.at[dp, me], own_sem)
    own.start()

    def near_copy(k):
        return pltpu.make_async_remote_copy(
            src_ref=x_ref, dst_ref=out_ref.at[dp, me], send_sem=near_send.at[k],
            recv_sem=near_recv.at[k], device_id=near(k), device_id_type=MESH,
        )

    def far_copy(k):
        return pltpu.make_async_remote_copy(
            src_ref=out_ref.at[dp], dst_ref=out_ref.at[dp], send_sem=far_send.at[k],
            recv_sem=far_recv.at[k], device_id=far(k), device_id_type=MESH,
        )

    for k in range(1, planes):
        near_copy(k).start()
    own.wait()
    for k in range(1, planes):
        near_copy(k).wait()
    for k in range(1, dps):
        far_copy(k).start()
    for k in range(1, dps):
        far_copy(k).wait()


def gather_anchors(values):
    dps = lax.axis_size("dp")
    planes = lax.axis_size("span") * lax.axis_size("tensor")
    dma = pltpu.SemaphoreType.DMA
    vmem = pl.BlockSpec(memory_space=pltpu.VMEM)

    def body(*refs):
        anchors_kernel(dps, planes, *refs)

    return pl.pallas_call(
        body,
        name="gather_anchors",
        out_shape=jax.ShapeDtypeStruct((dps, planes) + values.shape, values.dtype),
        in_specs=[vmem],
        out_specs=vmem,
        scratch_shapes=[dma((planes,)), dma((planes,)), dma((dps,)), dma((dps,)), dma],
        compiler_params=pltpu.CompilerParams(collective_id=0, has_side_effects=True),
    )(values)


VECTORS = ("pb", "g0", "g1", "s0", "s1", "sb")
ROWS_PER_CHUNK = 4
CHUNKS_PER_LAYER = 4


def block_order(side, tensor):
    flip_one = tensor + 1 - 2 * lax.rem(tensor, 2)
    flip_two = tensor + 2 - 4 * (tensor // 2)
    swing = side * (flip_two - flip_one)
    return tensor, flip_one + swing, flip_two - swing, TENSORS - 1 - tensor


def remote(src, dst, sems, i, device):
    return pltpu.make_async_remote_copy(
        src_ref=src, dst_ref=dst, send_sem=sems.at[0, i], recv_sem=sems.at[1, i],
        device_id=device, device_id_type=MESH,
    )


def last_kernel(dps, planes, ffn_ref, own, rest, rows_ref, blocks, outs, scratch):
    ffn_own, ffn_other, attn_own, attn_other, out_ref = outs
    (
        swapped, main_rest, main_own, across, mine, got_rest, got_own, got_across, got_peer, total_ref,
        ffn_parts, attn_parts, x_ref, parts, sums,
        swap_sems, plane_sems, ffn_one, ffn_two, attn_one, attn_two, one_sems, two_sems, three_sems,
    ) = scratch
    dp = lax.axis_index("dp")
    side = lax.axis_index("span")
    tensor = lax.axis_index("tensor")
    me = side * TENSORS + tensor
    order = block_order(side, tensor)
    x_ref[...] = rows_ref[...]
    for l in range(2):
        for j in range(TENSORS):
            for k in range(2):
                columns = blocks[l][k][j].shape[1]
                x_ref[l * CHUNKS_PER_LAYER + k, pl.ds(order[j], 1), :columns] = blocks[l][k][j][...]

    def near_peer(k):
        return lax.rem(me + k, planes)

    def near(k):
        peer = near_peer(k)
        return {"span": peer // TENSORS, "tensor": lax.rem(peer, TENSORS)}

    def far_peer(k):
        return lax.rem(dp + k, dps)

    def far(k):
        return {"dp": far_peer(k)}

    peer_core, main_peer, diag_peer = {"span": 1 - side}, {"tensor": order[1]}, {"tensor": order[2]}
    nears, fars = range(1, planes), range(1, dps)

    barrier = pltpu.get_barrier_semaphore()
    for k in nears:
        pl.semaphore_signal(barrier, inc=1, device_id=near(k), device_id_type=MESH)
    for k in fars:
        pl.semaphore_signal(barrier, inc=1, device_id=far(k), device_id_type=MESH)
    pl.semaphore_wait(barrier, planes + dps - 2)

    swaps = [
        remote(src, swapped.at[i], swap_sems, i, peer_core)
        for i, src in enumerate((own[2], rest[2], rest[3], rest[0]))
    ]
    for copy in swaps:
        copy.start()
    ones = [remote(x_ref.at[near_peer(k)], parts.at[k], one_sems, k, near(k)) for k in nears]
    for copy in ones:
        copy.start()
    ffn_ones = [remote(ffn_ref.at[far_peer(k)], ffn_parts.at[k], ffn_one, k, far(k)) for k in fars]
    for copy in ffn_ones:
        copy.start()

    for copy in swaps:
        copy.wait()
    across[...] = plus(own[3][...], swapped[2])
    main_rest[...] = plus(rest[1][...], swapped[0])
    send_across = remote(across, got_across, plane_sems, 0, diag_peer)
    send_across.start()
    send_rest = remote(main_rest, got_rest, plane_sems, 1, main_peer)
    send_rest.start()
    mine[...] = plus(own[0][...], swapped[3])
    for copy in ones:
        copy.wait()
    total = x_ref[me]
    for k in nears:
        total = total + parts[k]
    sums[dp] = total
    twos = [remote(sums.at[dp], sums.at[dp], two_sems, k, far(k)) for k in fars]
    for copy in twos:
        copy.start()

    send_across.wait()
    main_own[...] = plus(own[1][...], swapped[1], got_across[...])
    send_own = remote(main_own, got_own, plane_sems, 2, main_peer)
    send_own.start()
    send_rest.wait()
    send_peer = remote(got_rest, got_peer, swap_sems, 4, peer_core)
    send_peer.start()
    send_peer.wait()
    send_own.wait()
    total_ref[...] = plus(mine[...], got_own[...], got_peer[...])
    attn_ones = [remote(total_ref.at[far_peer(k)], attn_parts.at[k], attn_one, k, far(k)) for k in fars]
    for copy in attn_ones:
        copy.start()

    for copy in ffn_ones:
        copy.wait()
    ffn_own[dp] = plus(ffn_ref[dp], *[ffn_parts[k] for k in fars])
    ffn_twos = [remote(ffn_own.at[dp], ffn_own.at[dp], ffn_two, k, far(k)) for k in fars]
    for copy in ffn_twos:
        copy.start()

    for copy in twos:
        copy.wait()
    total = sums[0]
    for k in fars:
        total = total + sums[k]
    out_ref[me] = total
    threes = [remote(out_ref.at[me], out_ref.at[me], three_sems, k, near(k)) for k in nears]
    for copy in threes:
        copy.start()

    for copy in attn_ones:
        copy.wait()
    attn_own[dp] = plus(total_ref[dp], *[attn_parts[k] for k in fars])
    attn_twos = [remote(attn_own.at[dp], attn_own.at[dp], attn_two, k, far(k)) for k in fars]
    for copy in attn_twos:
        copy.start()

    for copy in ffn_twos:
        copy.wait()
    swap_ffn = remote(ffn_own, ffn_other, swap_sems, 5, peer_core)
    swap_ffn.start()
    for copy in attn_twos:
        copy.wait()
    swap_attn = remote(attn_own, attn_other, swap_sems, 6, peer_core)
    swap_attn.start()
    for copy in threes:
        copy.wait()
    swap_ffn.wait()
    swap_attn.wait()


def last_sums(ffn_total, attn_blocks, rows, blocks):
    dps = lax.axis_size("dp")
    planes = lax.axis_size("span") * lax.axis_size("tensor")
    flat, tree = jax.tree.flatten(blocks)

    def by_dp(values):
        return values.reshape(dps, values.shape[0] // dps, values.shape[1])

    ffn_total = by_dp(ffn_total)
    own = [by_dp(o) for o, r in attn_blocks]
    rest = [by_dp(r) for o, r in attn_blocks]
    dma = pltpu.SemaphoreType.DMA
    vmem = pl.BlockSpec(memory_space=pltpu.VMEM)
    attn, ffn = own[0].shape, ffn_total.shape

    def body(ffn_ref, *refs):
        own_refs, rest_refs, rows_ref = refs[:TENSORS], refs[TENSORS : 2 * TENSORS], refs[2 * TENSORS]
        refs = refs[2 * TENSORS + 1 :]
        inputs = jax.tree.unflatten(tree, refs[: len(flat)])
        outs, scratch = refs[len(flat) : len(flat) + 5], refs[len(flat) + 5 :]
        last_kernel(dps, planes, ffn_ref, own_refs, rest_refs, rows_ref, inputs, outs, scratch)

    outs = pl.pallas_call(
        body,
        name="last_sums",
        out_shape=tuple(jax.ShapeDtypeStruct(shape, BF) for shape in (ffn, ffn, attn, attn))
        + (jax.ShapeDtypeStruct(rows.shape, F32),),
        in_specs=[vmem] * (2 + 2 * TENSORS + len(flat)),
        out_specs=(vmem,) * 5,
        scratch_shapes=[pltpu.VMEM((TENSORS,) + attn, BF)]
        + [pltpu.VMEM(attn, BF)] * 9
        + [pltpu.VMEM(ffn, BF), pltpu.VMEM(attn, BF)]
        + [pltpu.VMEM(rows.shape, F32), pltpu.VMEM(rows.shape, F32), pltpu.VMEM((dps,) + rows.shape[1:], F32)]
        + [dma((2, 7)), dma((2, 3))]
        + [dma((2, dps))] * 4
        + [dma((2, planes)), dma((2, dps)), dma((2, planes))],
        compiler_params=pltpu.CompilerParams(
            collective_id=1, has_side_effects=True, vmem_limit_bytes=36 << 20
        ),
    )(ffn_total, *own, *rest, rows, *flat)
    whole = [o.reshape(-1, o.shape[-1]) for o in outs[:4]]
    return (*whole, outs[4])


def to_rows(values):
    return lax.all_to_all(values, "tensor", split_axis=0, concat_axis=0, tiled=True).reshape(
        -1, values.shape[-1]
    )


def to_places(values):
    blocks = values.reshape(TENSORS, -1, values.shape[-1])
    return lax.all_to_all(blocks, "tensor", split_axis=0, concat_axis=0, tiled=True)


def layer_forward(l, x, seg, attn, ffn, vec, hook):
    xb = x.astype(BF)
    kept = []
    z1 = x + vec["pb"]
    for j in range(TENSORS):
        first, second = attn.blocks[j]
        *saved, z1 = attend_forward(l, vec["cols"], xb, first, second, vec["heads"](j), z1, seg)
        kept.append(saved)
        z1 = hook("attn", j, z1)
    n1, r1 = normal_parts(z1)
    y = n1 * vec["g0"] + vec["s0"]
    yb = y.astype(BF)
    act, slope = [], []
    z2 = y + vec["sb"]
    for j in range(TENSORS):
        first, second = ffn.blocks[j]
        a, b = gelu_parts(mm(yb, first, 1, 0) + vec["eb"](j))
        act.append(a.astype(BF))
        slope.append(b.astype(BF))
        z2 = z2 + mm(act[-1], second, 1, 0)
        z2 = hook("ffn", j, z2)
    n2, r2 = normal_parts(z2)
    out = n2 * vec["g1"] + vec["s1"]
    return out, (xb, kept, n1, r1, yb, act, slope, n2, r2)


def total_rows(values):
    return jnp.sum(values, axis=0)


def ffn_backward(dout, ffn_w, vec, kept, hook):
    xb, saved, n1, r1, yb, act, slope, n2, r2 = kept
    dz2 = normal_back(dout, n2, r2, vec["g1"])
    small = {"g1": total_rows(dout * n2), "s1": total_rows(dout), "sb": total_rows(dz2), "eb": []}
    dz2 = hook("seeded", dz2)
    dzb = dz2.astype(BF)
    dy = dz2
    blocks = []
    for j, (first, second) in enumerate(ffn_w):
        own, rest, sums, dy = ffn_block_backward(dzb, yb, act[j], slope[j], first, second, dy)
        small["eb"].append(sums)
        blocks.append((own, rest))
        if j == 2:
            dzb, dy = hook("three", (dzb, dy))
    return dy, blocks, small


def attn_backward(dy, seg, attn_w, vec, kept, hook):
    xb, saved, n1, r1, yb, act, slope, n2, r2 = kept
    dz1 = normal_back(dy, n1, r1, vec["g0"])
    small = {"g0": total_rows(dy * n1), "s0": total_rows(dy), "pb": total_rows(dz1), "heads": []}
    dz1 = hook("normed", dz1)
    da = dz1.astype(BF)
    dx = dz1
    blocks = []
    for j, (first, second) in enumerate(attn_w):
        dfirst, dsecond, sums, dx = attend_backward(vec["cols"], da, xb, first, second, saved[j], dx, seg)
        small["heads"].append(sums)
        blocks.append((dfirst, dsecond))
        if j == 2:
            da, dx = hook("three", (da, dx))
    return dx, blocks, small


def attn_unpack(first, second):
    cols = first.shape[0] // 2
    heads = jnp.stack([first[:cols], first[cols:], second[:cols]])
    return jnp.swapaxes(heads, 1, 2), second[cols:]


class Reduction:
    def start(self, value, blocks):
        self.blocks = blocks
        value, *self.outgoing = tie(value, *reduce_outgoing(blocks))
        return value

    def swapped(self, value):
        value, self.main_rest, self.main_own, self.across, self.mine = tie(
            value, *reduce_swapped(self.blocks, self.outgoing)
        )
        self.from_rest = send(self.main_rest, MAIN)
        return value

    def crossed(self, value):
        value, self.main_own = tie(value, reduce_across(self.main_own, self.across))
        self.from_own = send(self.main_own, MAIN)
        self.from_peer = send(self.from_rest, SWAP)
        return value

    def summed(self, value):
        value, self.total = tie(value, plus(self.mine, self.from_own, self.from_peer))
        return value


def shards(
    layer_input, skip_tokens, backbone_cotangent, head_cotangent, segment_lengths, pair_index,
    w_heads, heads_bias, w_project, project_bias, norm_gain, norm_shift,
    w_expand, expand_bias, w_shrink, shrink_bias,
):
    side = lax.axis_index("span")
    mine = lax.axis_index("tensor")
    width = layer_input.shape[-1]
    head_cols = w_heads.shape[-1]
    ff_cols = w_expand.shape[-1]

    extra = 16
    bias_rows = jnp.concatenate([heads_bias.reshape(1, 4 * head_cols), expand_bias], axis=0)
    bias_rows = jnp.pad(bias_rows, ((0, extra - bias_rows.shape[0]), (0, 0)))

    def attn_rows(l):
        heads = jnp.swapaxes(w_heads[l], 1, 2)
        first = heads[:2].reshape(2 * head_cols, width)
        return first, jnp.concatenate([heads[2], w_project[l]], axis=0)

    first, second = attn_rows(0)
    first = jnp.concatenate([first, bias_rows], axis=0)
    second = jnp.pad(second, ((0, extra), (0, 0)))
    gather_attn0, gather_ffn0, gather_attn1, gather_ffn1 = (Gathering(side) for _ in range(4))
    x = to_rows(layer_input[0])
    mark = gather_attn0.start(layer_input[0, 0, 0], first, second)
    mark = gather_ffn0.start(mark, w_expand[0], w_shrink[0])
    later = {}

    def during_forward0(kind, j, value):
        if kind == "attn":
            if j == 0:
                value = gather_attn0.arrived(value)
            if j == 1:
                value = gather_attn1.start(value, *attn_rows(1))
            if j == 2:
                value = gather_attn0.crossed(value)
            if j == 3:
                value = gather_ffn0.arrived(value)
                value = gather_ffn1.start(value, w_expand[1], w_shrink[1])
        else:
            if j == 0:
                skip, value = tie(skip_tokens[0], value)
                later["skip"] = to_rows(skip)
            if j == 1:
                value = gather_attn1.arrived(value)
            if j == 2:
                value = gather_ffn0.crossed(value)
        return value

    def during_forward1(kind, j, value):
        if kind == "attn":
            if j == 0:
                head_cot, value = tie(head_cotangent[0], value)
                later["head"] = to_rows(head_cot)
            if j == 1:
                value = gather_attn1.crossed(value)
            if j == 2:
                value, later["backbone_out"] = tie(value, later["backbone_out"])
            if j == 3:
                value = gather_ffn1.arrived(value)
        else:
            if j == 0:
                backbone_cot, value = tie(backbone_cotangent[0], value)
                later["backbone"] = to_rows(backbone_cot)
            if j == 2:
                value = gather_ffn1.crossed(value)
        return value

    tokens = x.shape[0]

    def bias_row(j, i):
        first, second = gather_attn0.blocks[j]
        return first[2 * head_cols + i : 2 * head_cols + i + 1].astype(F32)

    def vectors(l):
        return {
            "cols": head_cols, "heads": lambda j: bias_row(j, 0),
            "eb": lambda j: bias_row(j, 1 + l), "pb": project_bias[l].astype(F32),
            "g0": norm_gain[l, 0].astype(F32), "g1": norm_gain[l, 1].astype(F32),
            "s0": norm_shift[l, 0].astype(F32), "s1": norm_shift[l, 1].astype(F32),
            "sb": shrink_bias[l].astype(F32),
        }

    lengths = lax.dynamic_index_in_dim(segment_lengths[0], mine, 0, keepdims=False)
    span_count = lengths.shape[0]
    starts = jnp.cumsum(lengths) - lengths
    row_length = jnp.sum(lengths)
    places = jnp.arange(tokens, dtype=jnp.int32)
    counted = jnp.sum((places[:, None] >= starts[None, :]).astype(jnp.int32), axis=-1) - 1
    segment = jnp.where(places < row_length, counted, span_count)
    seg = (segment[:, None], segment[None, :])
    valid = (places < row_length).astype(F32)[:, None]
    picker = (starts[:, None] == places[None, :]).astype(F32)
    first_place = jnp.sum(picker, axis=0)[:, None] > 0

    vec0, vec1 = vectors(0), vectors(1)
    backbone, kept0 = layer_forward(0, x.astype(F32), seg, gather_attn0, gather_ffn0, vec0, during_forward0)
    attn_w0, ffn_w0 = gather_attn0.blocks, gather_ffn0.blocks
    later["backbone_out"] = to_places((backbone * valid).astype(BF))
    cls = mm(picker.astype(BF), backbone.astype(BF), 1, 0).astype(BF)
    anchors = gather_anchors(cls)
    dp_count = lax.axis_size("dp")
    pair_count = lax.axis_size("span")
    vector_count = dp_count * TENSORS * span_count
    anchors = anchors.reshape(dp_count, pair_count, TENSORS * span_count, width)
    anchors = jnp.swapaxes(anchors, 0, 1).reshape(pair_count, vector_count, width)

    head_in = jnp.where(first_place, backbone, later["skip"].astype(F32))
    head, kept1 = layer_forward(1, head_in, seg, gather_attn1, gather_ffn1, vec1, during_forward1)
    attn_w1, ffn_w1 = gather_attn1.blocks, gather_ffn1.blocks
    head_cot, backbone_cot = later["head"], later["backbone"]
    head_out = to_places((head * valid).astype(BF))

    root = math.sqrt(width)
    logits = mm(anchors[0], anchors[1], 1, 1) / root
    columns = jnp.arange(vector_count, dtype=jnp.int32)
    target = (pair_index[:, None] == columns[None, :]).astype(F32)
    lse_rows = jax.nn.logsumexp(logits, axis=1)
    lse_cols = jax.nn.logsumexp(logits, axis=0)
    dlogits = LOSS_WEIGHT * (
        jnp.exp(logits - lse_rows[:, None]) + jnp.exp(logits - lse_cols[None, :]) - 2.0 * target
    )
    span_loss = (jnp.sum(lse_rows) + jnp.sum(lse_cols) - 2.0 * jnp.sum(target * logits)) / (
        2 * vector_count
    )
    own = (lax.axis_index("dp") * TENSORS + mine) * span_count
    wanted = jnp.where(side == 0, dlogits, dlogits.T)
    wanted = lax.dynamic_slice(wanted, (own, 0), (span_count, vector_count))
    other = lax.dynamic_index_in_dim(anchors, 1 - side, 0, keepdims=False).astype(F32)
    dcls = jnp.dot(wanted, other, precision=HIGHEST) / root

    def plain(name, value):
        return value

    ffn1, attn1, ffn0 = (Reduction() for _ in range(3))

    dy, blocks, small1 = ffn_backward(head_cot.astype(F32) * valid, ffn_w1, vec1, kept1, plain)
    dy, head_out = tie(dy, head_out)
    dy = ffn1.start(dy, blocks)

    def during_attn1(name, value):
        if name == "normed":
            return ffn1.swapped(value)
        return ffn1.crossed(value)

    du, blocks, more = attn_backward(dy, seg, attn_w1, vec1, kept1, during_attn1)
    small1.update(more)
    du = attn1.start(du, blocks)
    du = ffn1.summed(du)
    ffn_total1 = lax.psum(ffn1.total, "dp")
    grad_skip = to_places(jnp.where(first_place, 0.0, du).astype(BF))

    seed = backbone_cot.astype(F32) * valid + jnp.where(first_place, du, 0.0)
    seed = seed + jnp.dot(picker.T, dcls, precision=HIGHEST)

    def during_ffn0(name, value):
        if name == "seeded":
            return attn1.swapped(value)
        return attn1.crossed(value)

    dy, blocks, small0 = ffn_backward(seed, ffn_w0, vec0, kept0, during_ffn0)
    dy, grad_skip = tie(dy, grad_skip)
    dy = ffn0.start(dy, blocks)
    dy = attn1.summed(dy)

    dy, ffn_total1, late = tie(dy, ffn_total1, attn1.total)
    attn_total1 = lax.psum(late, "dp")
    finished = {}

    def during_attn0(name, value):
        if name == "normed":
            return ffn0.swapped(value)
        value = ffn0.crossed(value)
        value, finished["attn"] = tie(value, attn_total1)
        return value

    dx, attn_blocks, more = attn_backward(dy, seg, attn_w0, vec0, kept0, during_attn0)
    small0.update(more)
    attn_total1 = finished["attn"]
    grad_input = to_places(dx.astype(BF))

    place = lax.broadcasted_iota(jnp.int32, (2 * CHUNKS_PER_LAYER * ROWS_PER_CHUNK, 1), 0)
    rows = jnp.zeros((place.shape[0], width), F32)
    for l, small in enumerate((small0, small1)):
        base = l * CHUNKS_PER_LAYER * ROWS_PER_CHUNK
        for i, k in enumerate(VECTORS):
            rows = rows + jnp.where(place == base + 2 * ROWS_PER_CHUNK + i, small[k][None], 0.0)
    rows = ffn0.summed(rows.reshape(2 * CHUNKS_PER_LAYER, ROWS_PER_CHUNK, width))
    ffn_total1, attn_total1 = tie(ffn_total1, attn_total1)
    other_ffn1, other_attn1 = send(ffn_total1, SWAP), send(attn_total1, SWAP)
    rows, other_ffn1, other_attn1 = tie(rows, other_ffn1, other_attn1)
    ffn_own, ffn_other, attn_own, attn_other, total = last_sums(
        ffn0.total, attn_blocks, rows, [(small["eb"], small["heads"]) for small in (small0, small1)]
    )

    hb, eb, vector_sums = [], [], []
    for l in range(2):
        base = l * CHUNKS_PER_LAYER
        own = lax.dynamic_slice(total[base : base + 2], (0, mine, 0), (2, 1, width))[:, 0]
        eb.append(own[0])
        hb.append(jnp.stack([own[1, :head_cols], own[1, head_cols : 2 * head_cols]]))
        rows = total[base + 2 : base + CHUNKS_PER_LAYER].reshape(-1, width)
        vector_sums.append({k: rows[i] for i, k in enumerate(VECTORS)})
    sums = vector_sums

    ge1, gs1 = in_order(side, ffn_total1, other_ffn1)
    gh1, gp1 = attn_unpack(*in_order(side, attn_total1, other_attn1))
    ge0, gs0 = in_order(side, ffn_own, ffn_other)
    gh0, gp0 = attn_unpack(*in_order(side, attn_own, attn_other))

    return (
        later["backbone_out"][None],
        head_out[None],
        span_loss,
        grad_input[None],
        grad_skip[None],
        jnp.stack([gh0, gh1]),
        jnp.stack(hb),
        jnp.stack([gp0, gp1]),
        jnp.stack([s["pb"] for s in sums]),
        jnp.stack([jnp.stack([s["g0"], s["g1"]]) for s in sums]),
        jnp.stack([jnp.stack([s["s0"], s["s1"]]) for s in sums]),
        jnp.stack([ge0, ge1]),
        jnp.stack(eb),
        jnp.stack([gs0, gs1]),
        jnp.stack([s["sb"] for s in sums]),
    )


def solution(mesh):
    rows = P("span", "dp", "tensor", None)
    in_specs = (
        rows, rows, rows, rows, P("span", "dp", None), P(),
        P(None, None, None, "tensor"), P(None, None, "tensor"), P(None, "tensor", None),
        P(), P(), P(), P(None, None, "tensor"), P(None, "tensor"), P(None, "tensor", None), P(),
    )
    out_specs = (
        rows, rows, P(), rows, rows,
        P(None, None, None, "tensor"), P(None, None, "tensor"), P(None, "tensor", None),
        P(), P(), P(), P(None, None, "tensor"), P(None, "tensor"), P(None, "tensor", None), P(),
    )
    return jax.shard_map(shards, mesh=mesh, in_specs=in_specs, out_specs=out_specs, check_vma=False)
```

```python
import math

import jax
import jax.numpy as jnp
from jax import lax
from jax.experimental import pallas as pl
from jax.experimental.pallas import tpu as pltpu
from jax.sharding import PartitionSpec as P

HEAD_DIM = 64
EPSILON = 1e-12
LOSS_WEIGHT = 8.0
HIGHEST = lax.Precision.HIGHEST
MASKED = -1e30
BF = jnp.bfloat16
F32 = jnp.float32
PLANE = ("span", "tensor")
MESH = pl.DeviceIdType.MESH
TENSORS = 4
MAIN, DIAG, SWAP = "main", "diag", "swap"


def mm(a, b, ca, cb):
    return lax.dot_general(a, b, (((ca,), (cb,)), ((), ())), preferred_element_type=F32)


def normal_parts(values):
    centred = values - jnp.mean(values, axis=-1, keepdims=True)
    spread = jnp.mean(centred * centred, axis=-1, keepdims=True)
    scale = lax.rsqrt(spread + EPSILON)
    return centred * scale, scale


def normal_back(upward, normed, scale, gain):
    weighted = upward * gain
    first = jnp.mean(weighted, axis=-1, keepdims=True)
    second = jnp.mean(weighted * normed, axis=-1, keepdims=True)
    return (weighted - first - normed * second) * scale


def gelu_parts(hidden):
    phi = 0.5 * (1.0 + lax.erf(hidden * math.sqrt(0.5)))
    slope = phi + hidden * jnp.exp(-0.5 * hidden * hidden) * (1.0 / math.sqrt(2.0 * math.pi))
    return hidden * phi, slope


def plane_pairs(kind):
    pairs = []
    for side in range(2):
        for t in range(TENSORS):
            if kind == SWAP:
                target = (1 - side, t)
            elif kind == MAIN:
                target = (side, t ^ (1 + side))
            else:
                target = (side, t ^ (2 - side))
            pairs.append((side * TENSORS + t, target[0] * TENSORS + target[1]))
    return pairs


def send(values, kind):
    return lax.ppermute(values, PLANE, plane_pairs(kind))


def plus(*terms):
    total = terms[0].astype(F32)
    for term in terms[1:]:
        total = total + term.astype(F32)
    return total.astype(BF)


def pick(side, zero, one):
    return jnp.where(side == 0, zero, one)


def tie(*values):
    return lax.optimization_barrier(values)


class Gathering:
    def __init__(self, side):
        self.side = side

    def start(self, value, first, second):
        value, first, second = tie(value, first, second)
        self.got = (send(first, MAIN), send(second, MAIN))
        self.blocks = [(first, second)]
        return value

    def arrived(self, value):
        value, *got = tie(value, *self.got)
        self.across = send(pick(self.side, *got), DIAG)
        self.blocks += [tuple(got), tuple(send(g, SWAP) for g in got)]
        return value

    def crossed(self, value):
        value, across = tie(value, self.across)
        rest = send(across, SWAP)
        self.blocks.append((pick(self.side, across, rest), pick(self.side, rest, across)))
        return value


def reduce_outgoing(blocks):
    return blocks[2][0], blocks[2][1], blocks[3][1], blocks[0][1]


def reduce_swapped(blocks, outgoing):
    got = [send(o, SWAP) for o in outgoing]
    return (
        plus(blocks[1][1], got[0]), plus(blocks[1][0], got[1]), plus(blocks[3][0], got[2]), plus(blocks[0][0], got[3])
    )


def reduce_across(main_own, across):
    return plus(main_own, send(across, DIAG))


def in_order(side, own, other):
    return pick(side, own, other).astype(F32), pick(side, other, own).astype(F32)


Q_ROWS = 128


def attend_forward_kernel(
    layer, x_ref, first_ref, second_ref, bias_ref, z_ref, down_ref, across_ref,
    q_ref, k_ref, v_ref, o_ref, lse_ref, out_ref
):
    tokens, width = q_ref.shape
    at = 2 * layer * width
    x = x_ref[...]
    q_ref[...] = (mm(x, first_ref[:width, :], 1, 1) + bias_ref[:, at : at + width]).astype(BF)
    k_ref[...] = mm(x, first_ref[width : 2 * width, :], 1, 1).astype(BF)
    v_ref[...] = (mm(x, second_ref[:width, :], 1, 1) + bias_ref[:, at + width : at + 2 * width]).astype(BF)

    def step(i, carry):
        rows = pl.ds(pl.multiple_of(i * Q_ROWS, Q_ROWS), Q_ROWS)
        same = down_ref[rows, :] == across_ref[...]
        for h in range(width // HEAD_DIM):
            head = slice(h * HEAD_DIM, (h + 1) * HEAD_DIM)
            s = mm(q_ref[rows, head], k_ref[:, head], 1, 1) * 0.125
            s = jnp.where(same, s, MASKED)
            top = jnp.max(s, axis=-1, keepdims=True)
            raised = jnp.exp(s - top)
            total = jnp.sum(raised, axis=-1, keepdims=True)
            weights = (raised * (1.0 / total)).astype(BF)
            o_ref[rows, head] = mm(weights, v_ref[:, head], 1, 0).astype(BF)
            lse_ref[rows, h : h + 1] = top + jnp.log(total)
        out_ref[rows, :] = z_ref[rows, :] + mm(o_ref[rows, :], second_ref[width : 2 * width, :], 1, 0)
        return carry

    lax.fori_loop(0, tokens // Q_ROWS, step, 0)


def attend_backward_kernel(
    da_ref, x_ref, first_ref, second_ref, q_ref, k_ref, v_ref, o_ref, lse_ref, dx_ref, down_ref, across_ref,
    own_ref, rest_ref, sums_ref, out_ref, do_ref, dq_ref, dk_ref, dv_ref
):
    tokens, width = q_ref.shape
    da = da_ref[...]
    do_ref[...] = mm(da, second_ref[width : 2 * width, :], 1, 1).astype(BF)
    dk_ref[...] = jnp.zeros_like(dk_ref)
    dv_ref[...] = jnp.zeros_like(dv_ref)

    def step(i, carry):
        rows = pl.ds(pl.multiple_of(i * Q_ROWS, Q_ROWS), Q_ROWS)
        same = down_ref[rows, :] == across_ref[...]
        for h in range(width // HEAD_DIM):
            head = slice(h * HEAD_DIM, (h + 1) * HEAD_DIM)
            q, k, up = q_ref[rows, head], k_ref[:, head], do_ref[rows, head]
            s = mm(q, k, 1, 1) * 0.125
            s = jnp.where(same, s, MASKED)
            pr = jnp.exp(s - lse_ref[rows, h : h + 1])
            dp = mm(up, v_ref[:, head], 1, 1)
            inner = jnp.sum(pr * dp, axis=-1, keepdims=True)
            ds = (pr * (dp - inner)).astype(BF)
            dq_ref[rows, head] = (mm(ds, k, 1, 0) * 0.125).astype(BF)
            dk_ref[:, head] += mm(ds, q, 0, 0)
            dv_ref[:, head] += mm(pr.astype(BF), up, 0, 0)
        return carry

    lax.fori_loop(0, tokens // Q_ROWS, step, 0)
    x = x_ref[...]
    dq = dq_ref[...]
    dk = (dk_ref[...] * 0.125).astype(BF)
    dv = dv_ref[...].astype(BF)
    out_ref[...] = (
        dx_ref[...]
        + mm(dq, first_ref[:width, :], 1, 0)
        + mm(dk, first_ref[width : 2 * width, :], 1, 0)
        + mm(dv, second_ref[:width, :], 1, 0)
    )
    side = lax.axis_index("span")
    store_both(
        side, own_ref, rest_ref, slice(0, width), mm(dq, x, 0, 0).astype(BF), mm(dv, x, 0, 0).astype(BF)
    )
    store_both(
        side, own_ref, rest_ref, slice(width, 2 * width),
        mm(dk, x, 0, 0).astype(BF), mm(o_ref[...], da, 0, 0).astype(BF),
    )
    sums_ref[:, :width] = jnp.sum(dq.astype(F32), axis=0, keepdims=True)
    sums_ref[:, width:] = jnp.sum(dv.astype(F32), axis=0, keepdims=True)


def small_cost():
    return pl.CostEstimate(flops=1 << 20, bytes_accessed=1 << 10, transcendentals=0)


def kernel_params():
    return pltpu.CompilerParams(vmem_limit_bytes=24 << 20)


def store_both(side, own_ref, rest_ref, rows, first, second):
    @pl.when(side == 0)
    def _():
        own_ref[rows, :] = first
        rest_ref[rows, :] = second

    @pl.when(side != 0)
    def _():
        own_ref[rows, :] = second
        rest_ref[rows, :] = first


def ffn_backward_kernel(
    dz_ref, y_ref, act_ref, slope_ref, first_ref, second_ref, dy_ref, own_ref, rest_ref, sums_ref, out_ref, dh_ref
):
    tokens, model = dz_ref.shape
    side = lax.axis_index("span")
    sums_ref[...] = jnp.zeros_like(sums_ref)

    def data(i, carry):
        rows = pl.ds(pl.multiple_of(i * Q_ROWS, Q_ROWS), Q_ROWS)
        dhid = mm(dz_ref[rows, :], second_ref[...], 1, 1) * slope_ref[rows, :].astype(F32)
        sums_ref[...] += jnp.sum(dhid, axis=0, keepdims=True)
        dhb = dhid.astype(BF)
        dh_ref[rows, :] = dhb
        out_ref[rows, :] = dy_ref[rows, :] + mm(dhb, first_ref[...], 1, 1)
        return carry

    def weights(i, carry):
        rows = pl.ds(pl.multiple_of(i * Q_ROWS, Q_ROWS), Q_ROWS)
        first = mm(y_ref[:, rows], dh_ref[...], 0, 0).astype(BF)
        second = mm(act_ref[:, rows], dz_ref[...], 0, 0).astype(BF)
        store_both(side, own_ref, rest_ref, rows, first, second)
        return carry

    lax.fori_loop(0, tokens // Q_ROWS, data, 0)
    lax.fori_loop(0, model // Q_ROWS, weights, 0)


def ffn_block_backward(dzb, yb, act, slope, first, second, dy):
    return pl.pallas_call(
        ffn_backward_kernel,
        name="ffn_backward",
        out_shape=(
            jax.ShapeDtypeStruct(first.shape, BF),
            jax.ShapeDtypeStruct(first.shape, BF),
            jax.ShapeDtypeStruct((1, act.shape[1]), F32),
            jax.ShapeDtypeStruct(dy.shape, F32),
        ),
        scratch_shapes=[pltpu.VMEM(act.shape, BF)],
        compiler_params=kernel_params(),
        cost_estimate=small_cost(),
    )(dzb, yb, act, slope, first, second, dy)


def attend_forward(layer, cols, x, first, second, bias, z, seg):
    tokens, model = x.shape
    narrow = jax.ShapeDtypeStruct((tokens, cols), BF)

    def body(*refs):
        attend_forward_kernel(layer, *refs)

    return pl.pallas_call(
        body,
        name="attend_forward",
        out_shape=(
            narrow, narrow, narrow, narrow,
            jax.ShapeDtypeStruct((tokens, cols // HEAD_DIM), F32),
            jax.ShapeDtypeStruct(z.shape, F32),
        ),
        compiler_params=kernel_params(),
        cost_estimate=small_cost(),
    )(x, first, second, bias, z, *seg)


def attend_backward(cols, da, x, first, second, kept, dx, seg):
    tokens, model = x.shape
    return pl.pallas_call(
        attend_backward_kernel,
        name="attend_backward",
        out_shape=(
            jax.ShapeDtypeStruct((2 * cols, model), BF),
            jax.ShapeDtypeStruct((2 * cols, model), BF),
            jax.ShapeDtypeStruct((1, 2 * cols), F32),
            jax.ShapeDtypeStruct(dx.shape, F32),
        ),
        scratch_shapes=[
            pltpu.VMEM((tokens, cols), BF), pltpu.VMEM((tokens, cols), BF),
            pltpu.VMEM((tokens, cols), F32), pltpu.VMEM((tokens, cols), F32),
        ],
        compiler_params=kernel_params(),
        cost_estimate=small_cost(),
    )(da, x, first, second, *kept, dx, *seg)


def anchors_kernel(dps, planes, x_ref, out_ref, near_send, near_recv, far_send, far_recv, own_sem):
    dp = lax.axis_index("dp")
    me = lax.axis_index("span") * TENSORS + lax.axis_index("tensor")

    def near(k):
        peer = lax.rem(me + k, planes)
        return {"span": peer // TENSORS, "tensor": lax.rem(peer, TENSORS)}

    def far(k):
        return {"dp": lax.rem(dp + k, dps)}

    barrier = pltpu.get_barrier_semaphore()
    for k in range(1, planes):
        pl.semaphore_signal(barrier, inc=1, device_id=near(k), device_id_type=MESH)
    for k in range(1, dps):
        pl.semaphore_signal(barrier, inc=1, device_id=far(k), device_id_type=MESH)
    pl.semaphore_wait(barrier, planes + dps - 2)

    own = pltpu.make_async_copy(x_ref, out_ref.at[dp, me], own_sem)
    own.start()

    def near_copy(k):
        return pltpu.make_async_remote_copy(
            src_ref=x_ref, dst_ref=out_ref.at[dp, me], send_sem=near_send.at[k],
            recv_sem=near_recv.at[k], device_id=near(k), device_id_type=MESH,
        )

    def far_copy(k):
        return pltpu.make_async_remote_copy(
            src_ref=out_ref.at[dp], dst_ref=out_ref.at[dp], send_sem=far_send.at[k],
            recv_sem=far_recv.at[k], device_id=far(k), device_id_type=MESH,
        )

    for k in range(1, planes):
        near_copy(k).start()
    own.wait()
    for k in range(1, planes):
        near_copy(k).wait()
    for k in range(1, dps):
        far_copy(k).start()
    for k in range(1, dps):
        far_copy(k).wait()


def gather_anchors(values):
    dps = lax.axis_size("dp")
    planes = lax.axis_size("span") * lax.axis_size("tensor")
    dma = pltpu.SemaphoreType.DMA
    vmem = pl.BlockSpec(memory_space=pltpu.VMEM)

    def body(*refs):
        anchors_kernel(dps, planes, *refs)

    return pl.pallas_call(
        body,
        name="gather_anchors",
        out_shape=jax.ShapeDtypeStruct((dps, planes) + values.shape, values.dtype),
        in_specs=[vmem],
        out_specs=vmem,
        scratch_shapes=[dma((planes,)), dma((planes,)), dma((dps,)), dma((dps,)), dma],
        compiler_params=pltpu.CompilerParams(collective_id=0, has_side_effects=True),
    )(values)


VECTORS = ("pb", "g0", "g1", "s0", "s1", "sb")
ROWS_PER_CHUNK = 4
CHUNKS_PER_LAYER = 4


def block_order(side, tensor):
    flip_one = tensor + 1 - 2 * lax.rem(tensor, 2)
    flip_two = tensor + 2 - 4 * (tensor // 2)
    swing = side * (flip_two - flip_one)
    return tensor, flip_one + swing, flip_two - swing, TENSORS - 1 - tensor


def remote(src, dst, sems, i, device):
    return pltpu.make_async_remote_copy(
        src_ref=src, dst_ref=dst, send_sem=sems.at[0, i], recv_sem=sems.at[1, i],
        device_id=device, device_id_type=MESH,
    )


class Halving:
    def __init__(self, dps, dp, src, result, scratch, sums, sems):
        self.src, self.result, self.scratch, self.sums, self.sems = src, result, scratch, sums, sems
        self.steps = []
        base, size, bit = 0, dps, 1
        while bit < dps:
            size = size // 2
            up = lax.rem(dp // bit, 2)
            self.steps.append((base + (1 - up) * size, base + up * size, size, {"dp": dp + bit * (1 - 2 * up)}))
            base = base + up * size
            bit *= 2

    def current(self, s):
        return self.src if s == 0 else self.sums

    def down(self, s):
        away, kept, size, partner = self.steps[s]
        room = self.scratch.at[pl.ds(self.steps_room(s), size)]
        return remote(self.current(s).at[pl.ds(away, size)], room, self.sems, s, partner)

    def steps_room(self, s):
        return sum(step[2] for step in self.steps[:s])

    def add(self, s):
        self.down(s).wait()
        away, kept, size, partner = self.steps[s]
        came = self.scratch[pl.ds(self.steps_room(s), size)]
        into = self.result if s == len(self.steps) - 1 else self.sums
        into[pl.ds(kept, size)] = plus(self.current(s)[pl.ds(kept, size)], came)

    def up(self, s):
        away, kept, size, partner = self.steps[s]
        part = self.result.at[pl.ds(kept, size)]
        return remote(part, part, self.sems, len(self.steps) + s, partner)


def last_kernel(dps, planes, ffn_ref, own, rest, rows_ref, blocks, outs, scratch):
    ffn_own, ffn_other, attn_own, attn_other, out_ref = outs
    (
        swapped, main_rest, main_own, across, mine, got_rest, got_own, got_across, got_peer, total_ref,
        ffn_room, attn_room, ffn_sums, attn_sums, x_ref, parts, sums,
        swap_sems, plane_sems, ffn_sems, attn_sems, one_sems, two_sems, three_sems,
    ) = scratch
    dp = lax.axis_index("dp")
    side = lax.axis_index("span")
    tensor = lax.axis_index("tensor")
    me = side * TENSORS + tensor
    order = block_order(side, tensor)
    x_ref[...] = rows_ref[...]
    for l in range(2):
        for j in range(TENSORS):
            for k in range(2):
                columns = blocks[l][k][j].shape[1]
                x_ref[l * CHUNKS_PER_LAYER + k, pl.ds(order[j], 1), :columns] = blocks[l][k][j][...]

    def near_peer(k):
        return lax.rem(me + k, planes)

    def near(k):
        peer = near_peer(k)
        return {"span": peer // TENSORS, "tensor": lax.rem(peer, TENSORS)}

    def far_peer(k):
        return lax.rem(dp + k, dps)

    def far(k):
        return {"dp": far_peer(k)}

    peer_core, main_peer, diag_peer = {"span": 1 - side}, {"tensor": order[1]}, {"tensor": order[2]}
    nears, fars = range(1, planes), range(1, dps)

    barrier = pltpu.get_barrier_semaphore()
    for k in nears:
        pl.semaphore_signal(barrier, inc=1, device_id=near(k), device_id_type=MESH)
    for k in fars:
        pl.semaphore_signal(barrier, inc=1, device_id=far(k), device_id_type=MESH)
    pl.semaphore_wait(barrier, planes + dps - 2)

    swaps = [
        remote(src, swapped.at[i], swap_sems, i, peer_core)
        for i, src in enumerate((own[2], rest[2], rest[3], rest[0]))
    ]
    for copy in swaps:
        copy.start()
    ones = [remote(x_ref.at[near_peer(k)], parts.at[k], one_sems, k, near(k)) for k in nears]
    for copy in ones:
        copy.start()
    ffn_chunks = [
        Halving(dps, dp, ffn_ref.at[c], ffn_own.at[c], ffn_room.at[c], ffn_sums.at[c], ffn_sems.at[c])
        for c in range(ffn_ref.shape[0])
    ]
    attn_chunks = [
        Halving(dps, dp, total_ref.at[c], attn_own.at[c], attn_room.at[c], attn_sums.at[c], attn_sems.at[c])
        for c in range(total_ref.shape[0])
    ]
    stages = range(len(ffn_chunks[0].steps))
    last = len(stages) - 1

    def down_from(chunks, s):
        for chunk in chunks:
            chunk.down(s).start()

    def down_to_end(chunks, s):
        for chunk in chunks:
            chunk.add(s)
            (chunk.down(s + 1) if s < last else chunk.up(last)).start()

    def up_next(chunks, s):
        for chunk in chunks:
            chunk.up(s).wait()
            if s > 0:
                chunk.up(s - 1).start()

    down_from(ffn_chunks, 0)

    for copy in swaps:
        copy.wait()
    across[...] = plus(own[3][...], swapped[2])
    main_rest[...] = plus(rest[1][...], swapped[0])
    send_across = remote(across, got_across, plane_sems, 0, diag_peer)
    send_across.start()
    send_rest = remote(main_rest, got_rest, plane_sems, 1, main_peer)
    send_rest.start()
    mine[...] = plus(own[0][...], swapped[3])
    for copy in ones:
        copy.wait()
    total = x_ref[me]
    for k in nears:
        total = total + parts[k]
    sums[dp] = total
    twos = [remote(sums.at[dp], sums.at[dp], two_sems, k, far(k)) for k in fars]
    for copy in twos:
        copy.start()

    down_to_end(ffn_chunks, 0)
    send_across.wait()
    main_own[...] = plus(own[1][...], swapped[1], got_across[...])
    send_own = remote(main_own, got_own, plane_sems, 2, main_peer)
    send_own.start()
    for s in stages[1:]:
        down_to_end(ffn_chunks, s)
    send_rest.wait()
    send_peer = remote(got_rest, got_peer, swap_sems, 4, peer_core)
    send_peer.start()
    send_peer.wait()
    send_own.wait()
    total_ref[...] = plus(mine[...], got_own[...], got_peer[...])
    down_from(attn_chunks, 0)

    for copy in twos:
        copy.wait()
    total = sums[0]
    for k in fars:
        total = total + sums[k]
    out_ref[me] = total
    threes = [remote(out_ref.at[me], out_ref.at[me], three_sems, k, near(k)) for k in nears]
    for copy in threes:
        copy.start()

    for s in reversed(stages[1:]):
        up_next(ffn_chunks, s)
    for s in stages:
        down_to_end(attn_chunks, s)
    up_next(ffn_chunks, 0)
    swap_ffn = remote(ffn_own, ffn_other, swap_sems, 5, peer_core)
    swap_ffn.start()
    for s in reversed(stages):
        up_next(attn_chunks, s)
    swap_attn = remote(attn_own, attn_other, swap_sems, 6, peer_core)
    swap_attn.start()
    for copy in threes:
        copy.wait()
    swap_ffn.wait()
    swap_attn.wait()


def last_sums(ffn_total, attn_blocks, rows, blocks):
    dps = lax.axis_size("dp")
    planes = lax.axis_size("span") * lax.axis_size("tensor")
    flat, tree = jax.tree.flatten(blocks)

    def by_dp(values):
        rows = values.shape[0]
        chunks = 2 if rows % (32 * dps) == 0 else 1
        return values.reshape(chunks, dps, rows // (chunks * dps), values.shape[1])

    ffn_total = by_dp(ffn_total)
    own = [by_dp(o) for o, r in attn_blocks]
    rest = [by_dp(r) for o, r in attn_blocks]
    dma = pltpu.SemaphoreType.DMA
    vmem = pl.BlockSpec(memory_space=pltpu.VMEM)
    attn, ffn = own[0].shape, ffn_total.shape

    def body(ffn_ref, *refs):
        own_refs, rest_refs, rows_ref = refs[:TENSORS], refs[TENSORS : 2 * TENSORS], refs[2 * TENSORS]
        refs = refs[2 * TENSORS + 1 :]
        inputs = jax.tree.unflatten(tree, refs[: len(flat)])
        outs, scratch = refs[len(flat) : len(flat) + 5], refs[len(flat) + 5 :]
        last_kernel(dps, planes, ffn_ref, own_refs, rest_refs, rows_ref, inputs, outs, scratch)

    outs = pl.pallas_call(
        body,
        name="last_sums",
        out_shape=tuple(jax.ShapeDtypeStruct(shape, BF) for shape in (ffn, ffn, attn, attn))
        + (jax.ShapeDtypeStruct(rows.shape, F32),),
        in_specs=[vmem] * (2 + 2 * TENSORS + len(flat)),
        out_specs=(vmem,) * 5,
        scratch_shapes=[pltpu.VMEM((TENSORS,) + attn, BF)]
        + [pltpu.VMEM(attn, BF)] * 9
        + [pltpu.VMEM(ffn, BF), pltpu.VMEM(attn, BF)] * 2
        + [pltpu.VMEM(rows.shape, F32), pltpu.VMEM(rows.shape, F32), pltpu.VMEM((dps,) + rows.shape[1:], F32)]
        + [dma((2, 7)), dma((2, 3))]
        + [dma((ffn[0], 2, dps)), dma((attn[0], 2, dps))]
        + [dma((2, planes)), dma((2, dps)), dma((2, planes))],
        compiler_params=pltpu.CompilerParams(
            collective_id=1, has_side_effects=True, vmem_limit_bytes=36 << 20
        ),
    )(ffn_total, *own, *rest, rows, *flat)
    whole = [o.reshape(-1, o.shape[-1]) for o in outs[:4]]
    return (*whole, outs[4])


def to_rows(values):
    return lax.all_to_all(values, "tensor", split_axis=0, concat_axis=0, tiled=True).reshape(
        -1, values.shape[-1]
    )


def to_places(values):
    blocks = values.reshape(TENSORS, -1, values.shape[-1])
    return lax.all_to_all(blocks, "tensor", split_axis=0, concat_axis=0, tiled=True)


def layer_forward(l, x, seg, attn, ffn, vec, hook):
    xb = x.astype(BF)
    kept = []
    z1 = x + vec["pb"]
    for j in range(TENSORS):
        first, second = attn.blocks[j]
        *saved, z1 = attend_forward(l, vec["cols"], xb, first, second, vec["heads"](j), z1, seg)
        kept.append(saved)
        z1 = hook("attn", j, z1)
    n1, r1 = normal_parts(z1)
    y = n1 * vec["g0"] + vec["s0"]
    yb = y.astype(BF)
    act, slope = [], []
    z2 = y + vec["sb"]
    for j in range(TENSORS):
        first, second = ffn.blocks[j]
        a, b = gelu_parts(mm(yb, first, 1, 0) + vec["eb"](j))
        act.append(a.astype(BF))
        slope.append(b.astype(BF))
        z2 = z2 + mm(act[-1], second, 1, 0)
        z2 = hook("ffn", j, z2)
    n2, r2 = normal_parts(z2)
    out = n2 * vec["g1"] + vec["s1"]
    return out, (xb, kept, n1, r1, yb, act, slope, n2, r2)


def total_rows(values):
    return jnp.sum(values, axis=0)


def ffn_backward(dout, ffn_w, vec, kept, hook):
    xb, saved, n1, r1, yb, act, slope, n2, r2 = kept
    dz2 = normal_back(dout, n2, r2, vec["g1"])
    small = {"g1": total_rows(dout * n2), "s1": total_rows(dout), "sb": total_rows(dz2), "eb": []}
    dz2 = hook("seeded", dz2)
    dzb = dz2.astype(BF)
    dy = dz2
    blocks = []
    for j, (first, second) in enumerate(ffn_w):
        own, rest, sums, dy = ffn_block_backward(dzb, yb, act[j], slope[j], first, second, dy)
        small["eb"].append(sums)
        blocks.append((own, rest))
        if j == 2:
            dzb, dy = hook("three", (dzb, dy))
    return dy, blocks, small


def attn_backward(dy, seg, attn_w, vec, kept, hook):
    xb, saved, n1, r1, yb, act, slope, n2, r2 = kept
    dz1 = normal_back(dy, n1, r1, vec["g0"])
    small = {"g0": total_rows(dy * n1), "s0": total_rows(dy), "pb": total_rows(dz1), "heads": []}
    dz1 = hook("normed", dz1)
    da = dz1.astype(BF)
    dx = dz1
    blocks = []
    for j, (first, second) in enumerate(attn_w):
        dfirst, dsecond, sums, dx = attend_backward(vec["cols"], da, xb, first, second, saved[j], dx, seg)
        small["heads"].append(sums)
        blocks.append((dfirst, dsecond))
        if j == 2:
            da, dx = hook("three", (da, dx))
    return dx, blocks, small


def attn_unpack(first, second):
    cols = first.shape[0] // 2
    heads = jnp.stack([first[:cols], first[cols:], second[:cols]])
    return jnp.swapaxes(heads, 1, 2), second[cols:]


class Reduction:
    def start(self, value, blocks):
        self.blocks = blocks
        value, *self.outgoing = tie(value, *reduce_outgoing(blocks))
        return value

    def swapped(self, value):
        value, self.main_rest, self.main_own, self.across, self.mine = tie(
            value, *reduce_swapped(self.blocks, self.outgoing)
        )
        self.from_rest = send(self.main_rest, MAIN)
        return value

    def crossed(self, value):
        value, self.main_own = tie(value, reduce_across(self.main_own, self.across))
        self.from_own = send(self.main_own, MAIN)
        self.from_peer = send(self.from_rest, SWAP)
        return value

    def summed(self, value):
        value, self.total = tie(value, plus(self.mine, self.from_own, self.from_peer))
        return value


def shards(
    layer_input, skip_tokens, backbone_cotangent, head_cotangent, segment_lengths, pair_index,
    w_heads, heads_bias, w_project, project_bias, norm_gain, norm_shift,
    w_expand, expand_bias, w_shrink, shrink_bias,
):
    side = lax.axis_index("span")
    mine = lax.axis_index("tensor")
    width = layer_input.shape[-1]
    head_cols = w_heads.shape[-1]
    ff_cols = w_expand.shape[-1]

    extra = 16
    bias_rows = jnp.concatenate([heads_bias.reshape(1, 4 * head_cols), expand_bias], axis=0)
    bias_rows = jnp.pad(bias_rows, ((0, extra - bias_rows.shape[0]), (0, 0)))

    def attn_rows(l):
        heads = jnp.swapaxes(w_heads[l], 1, 2)
        first = heads[:2].reshape(2 * head_cols, width)
        return first, jnp.concatenate([heads[2], w_project[l]], axis=0)

    first, second = attn_rows(0)
    first = jnp.concatenate([first, bias_rows], axis=0)
    second = jnp.pad(second, ((0, extra), (0, 0)))
    gather_attn0, gather_ffn0, gather_attn1, gather_ffn1 = (Gathering(side) for _ in range(4))
    x = to_rows(layer_input[0])
    mark = gather_attn0.start(layer_input[0, 0, 0], first, second)
    mark = gather_ffn0.start(mark, w_expand[0], w_shrink[0])
    later = {}

    def during_forward0(kind, j, value):
        if kind == "attn":
            if j == 0:
                value = gather_attn0.arrived(value)
            if j == 1:
                value = gather_attn1.start(value, *attn_rows(1))
            if j == 2:
                value = gather_attn0.crossed(value)
            if j == 3:
                value = gather_ffn0.arrived(value)
                value = gather_ffn1.start(value, w_expand[1], w_shrink[1])
        else:
            if j == 0:
                skip, value = tie(skip_tokens[0], value)
                later["skip"] = to_rows(skip)
            if j == 1:
                value = gather_attn1.arrived(value)
            if j == 2:
                value = gather_ffn0.crossed(value)
        return value

    def during_forward1(kind, j, value):
        if kind == "attn":
            if j == 0:
                head_cot, value = tie(head_cotangent[0], value)
                later["head"] = to_rows(head_cot)
            if j == 1:
                value = gather_attn1.crossed(value)
            if j == 2:
                value, mark = tie(value, later["backbone_out"])
            if j == 3:
                value = gather_ffn1.arrived(value)
        else:
            if j == 0:
                backbone_cot, value = tie(backbone_cotangent[0], value)
                later["backbone"] = to_rows(backbone_cot)
            if j == 2:
                value = gather_ffn1.crossed(value)
        return value

    tokens = x.shape[0]

    def bias_row(j, i):
        first, second = gather_attn0.blocks[j]
        return first[2 * head_cols + i : 2 * head_cols + i + 1].astype(F32)

    def vectors(l):
        return {
            "cols": head_cols, "heads": lambda j: bias_row(j, 0),
            "eb": lambda j: bias_row(j, 1 + l), "pb": project_bias[l].astype(F32),
            "g0": norm_gain[l, 0].astype(F32), "g1": norm_gain[l, 1].astype(F32),
            "s0": norm_shift[l, 0].astype(F32), "s1": norm_shift[l, 1].astype(F32),
            "sb": shrink_bias[l].astype(F32),
        }

    lengths = lax.dynamic_index_in_dim(segment_lengths[0], mine, 0, keepdims=False)
    span_count = lengths.shape[0]
    starts = jnp.cumsum(lengths) - lengths
    row_length = jnp.sum(lengths)
    places = jnp.arange(tokens, dtype=jnp.int32)
    counted = jnp.sum((places[:, None] >= starts[None, :]).astype(jnp.int32), axis=-1) - 1
    segment = jnp.where(places < row_length, counted, span_count)
    seg = (segment[:, None], segment[None, :])
    valid = (places < row_length).astype(F32)[:, None]
    picker = (starts[:, None] == places[None, :]).astype(F32)
    first_place = jnp.sum(picker, axis=0)[:, None] > 0

    vec0, vec1 = vectors(0), vectors(1)
    backbone, kept0 = layer_forward(0, x.astype(F32), seg, gather_attn0, gather_ffn0, vec0, during_forward0)
    attn_w0, ffn_w0 = gather_attn0.blocks, gather_ffn0.blocks
    later["backbone_out"] = to_places((backbone * valid).astype(BF))
    cls = mm(picker.astype(BF), backbone.astype(BF), 1, 0).astype(BF)
    anchors = gather_anchors(cls)
    dp_count = lax.axis_size("dp")
    pair_count = lax.axis_size("span")
    vector_count = dp_count * TENSORS * span_count
    anchors = anchors.reshape(dp_count, pair_count, TENSORS * span_count, width)
    anchors = jnp.swapaxes(anchors, 0, 1).reshape(pair_count, vector_count, width)

    head_in = jnp.where(first_place, backbone, later["skip"].astype(F32))
    head, kept1 = layer_forward(1, head_in, seg, gather_attn1, gather_ffn1, vec1, during_forward1)
    attn_w1, ffn_w1 = gather_attn1.blocks, gather_ffn1.blocks
    head_cot, backbone_cot = later["head"], later["backbone"]
    head_out = to_places((head * valid).astype(BF))

    root = math.sqrt(width)
    logits = mm(anchors[0], anchors[1], 1, 1) / root
    columns = jnp.arange(vector_count, dtype=jnp.int32)
    target = (pair_index[:, None] == columns[None, :]).astype(F32)
    lse_rows = jax.nn.logsumexp(logits, axis=1)
    lse_cols = jax.nn.logsumexp(logits, axis=0)
    dlogits = LOSS_WEIGHT * (
        jnp.exp(logits - lse_rows[:, None]) + jnp.exp(logits - lse_cols[None, :]) - 2.0 * target
    )
    span_loss = (jnp.sum(lse_rows) + jnp.sum(lse_cols) - 2.0 * jnp.sum(target * logits)) / (
        2 * vector_count
    )
    own = (lax.axis_index("dp") * TENSORS + mine) * span_count
    wanted = jnp.where(side == 0, dlogits, dlogits.T)
    wanted = lax.dynamic_slice(wanted, (own, 0), (span_count, vector_count))
    other = lax.dynamic_index_in_dim(anchors, 1 - side, 0, keepdims=False).astype(F32)
    dcls = jnp.dot(wanted, other, precision=HIGHEST) / root

    def plain(name, value):
        return value

    ffn1, attn1, ffn0 = (Reduction() for _ in range(3))

    dy, blocks, small1 = ffn_backward(head_cot.astype(F32) * valid, ffn_w1, vec1, kept1, plain)
    dy, mark = tie(dy, head_out)
    dy = ffn1.start(dy, blocks)

    def during_attn1(name, value):
        if name == "normed":
            return ffn1.swapped(value)
        return ffn1.crossed(value)

    du, blocks, more = attn_backward(dy, seg, attn_w1, vec1, kept1, during_attn1)
    small1.update(more)
    du = attn1.start(du, blocks)
    du = ffn1.summed(du)
    ffn_total1 = lax.psum(ffn1.total, "dp")
    grad_skip = to_places(jnp.where(first_place, 0.0, du).astype(BF))

    seed = backbone_cot.astype(F32) * valid + jnp.where(first_place, du, 0.0)
    seed = seed + jnp.dot(picker.T, dcls, precision=HIGHEST)

    def during_ffn0(name, value):
        if name == "seeded":
            return attn1.swapped(value)
        return attn1.crossed(value)

    dy, blocks, small0 = ffn_backward(seed, ffn_w0, vec0, kept0, during_ffn0)
    dy, mark = tie(dy, grad_skip)
    dy = ffn0.start(dy, blocks)
    dy = attn1.summed(dy)

    dy, ffn_total1, late = tie(dy, ffn_total1, attn1.total)
    attn_total1 = lax.psum(late, "dp")
    finished = {}

    def during_attn0(name, value):
        if name == "normed":
            return ffn0.swapped(value)
        value = ffn0.crossed(value)
        value, finished["attn"] = tie(value, attn_total1)
        return value

    dx, attn_blocks, more = attn_backward(dy, seg, attn_w0, vec0, kept0, during_attn0)
    small0.update(more)
    attn_total1 = finished["attn"]
    grad_input = to_places(dx.astype(BF))

    place = lax.broadcasted_iota(jnp.int32, (2 * CHUNKS_PER_LAYER * ROWS_PER_CHUNK, 1), 0)
    rows = jnp.zeros((place.shape[0], width), F32)
    for l, small in enumerate((small0, small1)):
        base = l * CHUNKS_PER_LAYER * ROWS_PER_CHUNK
        for i, k in enumerate(VECTORS):
            rows = rows + jnp.where(place == base + 2 * ROWS_PER_CHUNK + i, small[k][None], 0.0)
    rows = ffn0.summed(rows.reshape(2 * CHUNKS_PER_LAYER, ROWS_PER_CHUNK, width))
    ffn_total1, attn_total1 = tie(ffn_total1, attn_total1)
    other_ffn1, other_attn1 = send(ffn_total1, SWAP), send(attn_total1, SWAP)
    rows, other_ffn1, other_attn1 = tie(rows, other_ffn1, other_attn1)
    ffn_own, ffn_other, attn_own, attn_other, total = last_sums(
        ffn0.total, attn_blocks, rows, [(small["eb"], small["heads"]) for small in (small0, small1)]
    )

    hb, eb, vector_sums = [], [], []
    for l in range(2):
        base = l * CHUNKS_PER_LAYER
        own = lax.dynamic_slice(total[base : base + 2], (0, mine, 0), (2, 1, width))[:, 0]
        eb.append(own[0])
        hb.append(jnp.stack([own[1, :head_cols], own[1, head_cols : 2 * head_cols]]))
        rows = total[base + 2 : base + CHUNKS_PER_LAYER].reshape(-1, width)
        vector_sums.append({k: rows[i] for i, k in enumerate(VECTORS)})
    sums = vector_sums

    ge1, gs1 = in_order(side, ffn_total1, other_ffn1)
    gh1, gp1 = attn_unpack(*in_order(side, attn_total1, other_attn1))
    ge0, gs0 = in_order(side, ffn_own, ffn_other)
    gh0, gp0 = attn_unpack(*in_order(side, attn_own, attn_other))

    return (
        later["backbone_out"][None],
        head_out[None],
        span_loss,
        grad_input[None],
        grad_skip[None],
        jnp.stack([gh0, gh1]),
        jnp.stack(hb),
        jnp.stack([gp0, gp1]),
        jnp.stack([s["pb"] for s in sums]),
        jnp.stack([jnp.stack([s["g0"], s["g1"]]) for s in sums]),
        jnp.stack([jnp.stack([s["s0"], s["s1"]]) for s in sums]),
        jnp.stack([ge0, ge1]),
        jnp.stack(eb),
        jnp.stack([gs0, gs1]),
        jnp.stack([s["sb"] for s in sums]),
    )


def solution(mesh):
    rows = P("span", "dp", "tensor", None)
    in_specs = (
        rows, rows, rows, rows, P("span", "dp", None), P(),
        P(None, None, None, "tensor"), P(None, None, "tensor"), P(None, "tensor", None),
        P(), P(), P(), P(None, None, "tensor"), P(None, "tensor"), P(None, "tensor", None), P(),
    )
    out_specs = (
        rows, rows, P(), rows, rows,
        P(None, None, None, "tensor"), P(None, None, "tensor"), P(None, "tensor", None),
        P(), P(), P(), P(None, None, "tensor"), P(None, "tensor"), P(None, "tensor", None), P(),
    )
    return jax.shard_map(shards, mesh=mesh, in_specs=in_specs, out_specs=out_specs, check_vma=False)
```

```python
import math

import jax
import jax.numpy as jnp
from jax import lax
from jax.experimental import pallas as pl
from jax.experimental.pallas import tpu as pltpu
from jax.sharding import PartitionSpec as P

HEAD_DIM = 64
EPSILON = 1e-12
LOSS_WEIGHT = 8.0
HIGHEST = lax.Precision.HIGHEST
MASKED = -1e30
BF = jnp.bfloat16
F32 = jnp.float32
PLANE = ("span", "tensor")
MESH = pl.DeviceIdType.MESH
TENSORS = 4
MAIN, DIAG, SWAP = "main", "diag", "swap"


def mm(a, b, ca, cb):
    return lax.dot_general(a, b, (((ca,), (cb,)), ((), ())), preferred_element_type=F32)


def normal_parts(values):
    centred = values - jnp.mean(values, axis=-1, keepdims=True)
    spread = jnp.mean(centred * centred, axis=-1, keepdims=True)
    scale = lax.rsqrt(spread + EPSILON)
    return centred * scale, scale


def normal_back(upward, normed, scale, gain):
    weighted = upward * gain
    first = jnp.mean(weighted, axis=-1, keepdims=True)
    second = jnp.mean(weighted * normed, axis=-1, keepdims=True)
    return (weighted - first - normed * second) * scale


def gelu_parts(hidden):
    phi = 0.5 * (1.0 + lax.erf(hidden * math.sqrt(0.5)))
    slope = phi + hidden * jnp.exp(-0.5 * hidden * hidden) * (1.0 / math.sqrt(2.0 * math.pi))
    return hidden * phi, slope


def plane_pairs(kind):
    pairs = []
    for side in range(2):
        for t in range(TENSORS):
            if kind == SWAP:
                target = (1 - side, t)
            elif kind == MAIN:
                target = (side, t ^ (1 + side))
            else:
                target = (side, t ^ (2 - side))
            pairs.append((side * TENSORS + t, target[0] * TENSORS + target[1]))
    return pairs


def send(values, kind):
    return lax.ppermute(values, PLANE, plane_pairs(kind))


def plus(*terms):
    total = terms[0].astype(F32)
    for term in terms[1:]:
        total = total + term.astype(F32)
    return total.astype(BF)


def pick(side, zero, one):
    return jnp.where(side == 0, zero, one)


def tie(*values):
    return lax.optimization_barrier(values)


class Gathering:
    def __init__(self, side):
        self.side = side

    def start(self, value, first, second):
        value, first, second = tie(value, first, second)
        self.got = (send(first, MAIN), send(second, MAIN))
        self.blocks = [(first, second)]
        return value

    def arrived(self, value):
        value, *got = tie(value, *self.got)
        self.across = send(pick(self.side, *got), DIAG)
        self.blocks += [tuple(got), tuple(send(g, SWAP) for g in got)]
        return value

    def crossed(self, value):
        value, across = tie(value, self.across)
        rest = send(across, SWAP)
        self.blocks.append((pick(self.side, across, rest), pick(self.side, rest, across)))
        return value


def reduce_outgoing(blocks):
    return blocks[2][0], blocks[2][1], blocks[3][1], blocks[0][1]


def reduce_swapped(blocks, outgoing):
    got = [send(o, SWAP) for o in outgoing]
    return (
        plus(blocks[1][1], got[0]), plus(blocks[1][0], got[1]), plus(blocks[3][0], got[2]), plus(blocks[0][0], got[3])
    )


def reduce_across(main_own, across):
    return plus(main_own, send(across, DIAG))


def in_order(side, own, other):
    return pick(side, own, other).astype(F32), pick(side, other, own).astype(F32)


Q_ROWS = 128


def attend_forward_kernel(
    layer, x_ref, first_ref, second_ref, bias_ref, z_ref, down_ref, across_ref,
    q_ref, k_ref, v_ref, o_ref, lse_ref, out_ref
):
    tokens, width = q_ref.shape
    at = 2 * layer * width
    x = x_ref[...]
    q_ref[...] = (mm(x, first_ref[:width, :], 1, 1) + bias_ref[:, at : at + width]).astype(BF)
    k_ref[...] = mm(x, first_ref[width : 2 * width, :], 1, 1).astype(BF)
    v_ref[...] = (mm(x, second_ref[:width, :], 1, 1) + bias_ref[:, at + width : at + 2 * width]).astype(BF)

    def step(i, carry):
        rows = pl.ds(pl.multiple_of(i * Q_ROWS, Q_ROWS), Q_ROWS)
        same = down_ref[rows, :] == across_ref[...]
        for h in range(width // HEAD_DIM):
            head = slice(h * HEAD_DIM, (h + 1) * HEAD_DIM)
            s = mm(q_ref[rows, head], k_ref[:, head], 1, 1) * 0.125
            s = jnp.where(same, s, MASKED)
            top = jnp.max(s, axis=-1, keepdims=True)
            raised = jnp.exp(s - top)
            total = jnp.sum(raised, axis=-1, keepdims=True)
            weights = (raised * (1.0 / total)).astype(BF)
            o_ref[rows, head] = mm(weights, v_ref[:, head], 1, 0).astype(BF)
            lse_ref[rows, h : h + 1] = top + jnp.log(total)
        out_ref[rows, :] = z_ref[rows, :] + mm(o_ref[rows, :], second_ref[width : 2 * width, :], 1, 0)
        return carry

    lax.fori_loop(0, tokens // Q_ROWS, step, 0)


def attend_backward_kernel(
    da_ref, x_ref, first_ref, second_ref, q_ref, k_ref, v_ref, o_ref, lse_ref, dx_ref, down_ref, across_ref,
    own_ref, rest_ref, sums_ref, out_ref, do_ref, dq_ref, dk_ref, dv_ref
):
    tokens, width = q_ref.shape
    da = da_ref[...]
    do_ref[...] = mm(da, second_ref[width : 2 * width, :], 1, 1).astype(BF)
    dk_ref[...] = jnp.zeros_like(dk_ref)
    dv_ref[...] = jnp.zeros_like(dv_ref)

    def step(i, carry):
        rows = pl.ds(pl.multiple_of(i * Q_ROWS, Q_ROWS), Q_ROWS)
        same = down_ref[rows, :] == across_ref[...]
        for h in range(width // HEAD_DIM):
            head = slice(h * HEAD_DIM, (h + 1) * HEAD_DIM)
            q, k, up = q_ref[rows, head], k_ref[:, head], do_ref[rows, head]
            s = mm(q, k, 1, 1) * 0.125
            s = jnp.where(same, s, MASKED)
            pr = jnp.exp(s - lse_ref[rows, h : h + 1])
            dp = mm(up, v_ref[:, head], 1, 1)
            inner = jnp.sum(pr * dp, axis=-1, keepdims=True)
            ds = (pr * (dp - inner)).astype(BF)
            dq_ref[rows, head] = (mm(ds, k, 1, 0) * 0.125).astype(BF)
            dk_ref[:, head] += mm(ds, q, 0, 0)
            dv_ref[:, head] += mm(pr.astype(BF), up, 0, 0)
        return carry

    lax.fori_loop(0, tokens // Q_ROWS, step, 0)
    x = x_ref[...]
    dq = dq_ref[...]
    dk = (dk_ref[...] * 0.125).astype(BF)
    dv = dv_ref[...].astype(BF)
    out_ref[...] = (
        dx_ref[...]
        + mm(dq, first_ref[:width, :], 1, 0)
        + mm(dk, first_ref[width : 2 * width, :], 1, 0)
        + mm(dv, second_ref[:width, :], 1, 0)
    )
    side = lax.axis_index("span")
    store_both(
        side, own_ref, rest_ref, slice(0, width), mm(dq, x, 0, 0).astype(BF), mm(dv, x, 0, 0).astype(BF)
    )
    store_both(
        side, own_ref, rest_ref, slice(width, 2 * width),
        mm(dk, x, 0, 0).astype(BF), mm(o_ref[...], da, 0, 0).astype(BF),
    )
    sums_ref[:, :width] = jnp.sum(dq.astype(F32), axis=0, keepdims=True)
    sums_ref[:, width:] = jnp.sum(dv.astype(F32), axis=0, keepdims=True)


def small_cost():
    return pl.CostEstimate(flops=1 << 20, bytes_accessed=1 << 10, transcendentals=0)


def kernel_params():
    return pltpu.CompilerParams(vmem_limit_bytes=24 << 20)


def store_both(side, own_ref, rest_ref, rows, first, second):
    @pl.when(side == 0)
    def _():
        own_ref[rows, :] = first
        rest_ref[rows, :] = second

    @pl.when(side != 0)
    def _():
        own_ref[rows, :] = second
        rest_ref[rows, :] = first


def ffn_backward_kernel(
    dz_ref, y_ref, act_ref, slope_ref, first_ref, second_ref, dy_ref, own_ref, rest_ref, sums_ref, out_ref, dh_ref
):
    tokens, model = dz_ref.shape
    side = lax.axis_index("span")
    sums_ref[...] = jnp.zeros_like(sums_ref)

    def data(i, carry):
        rows = pl.ds(pl.multiple_of(i * Q_ROWS, Q_ROWS), Q_ROWS)
        dhid = mm(dz_ref[rows, :], second_ref[...], 1, 1) * slope_ref[rows, :].astype(F32)
        sums_ref[...] += jnp.sum(dhid, axis=0, keepdims=True)
        dhb = dhid.astype(BF)
        dh_ref[rows, :] = dhb
        out_ref[rows, :] = dy_ref[rows, :] + mm(dhb, first_ref[...], 1, 1)
        return carry

    def weights(i, carry):
        rows = pl.ds(pl.multiple_of(i * Q_ROWS, Q_ROWS), Q_ROWS)
        first = mm(y_ref[:, rows], dh_ref[...], 0, 0).astype(BF)
        second = mm(act_ref[:, rows], dz_ref[...], 0, 0).astype(BF)
        store_both(side, own_ref, rest_ref, rows, first, second)
        return carry

    lax.fori_loop(0, tokens // Q_ROWS, data, 0)
    lax.fori_loop(0, model // Q_ROWS, weights, 0)


def streamed_blocks(name, body, shared, total, blocks, big, small, scratch):
    count, takes, gives = len(blocks), len(blocks[0]), len(big)
    vmem, anywhere = pl.BlockSpec(memory_space=pltpu.VMEM), pl.BlockSpec(memory_space=pl.ANY)
    dma = pltpu.SemaphoreType.DMA

    def kernel(*refs):
        refs = list(refs)

        def take(n):
            taken = refs[:n]
            del refs[:n]
            return taken

        shared_refs, (total_ref,), ins = take(len(shared)), take(1), take(count * takes)
        (out_ref,), smalls, outs = take(1), take(count), take(count * gives)
        in_bufs, out_bufs, (in_sems, out_sems), extra = take(takes), take(gives), take(2), take(len(scratch))

        def fetch(j):
            return [
                pltpu.make_async_copy(ins[j * takes + i], in_bufs[i].at[j % 2], in_sems.at[j % 2, i])
                for i in range(takes)
            ]

        def put(j):
            return [
                pltpu.make_async_copy(out_bufs[i].at[j % 2], outs[j * gives + i], out_sems.at[j % 2, i])
                for i in range(gives)
            ]

        for copy in fetch(0):
            copy.start()
        for j in range(count):
            if j + 1 < count:
                for copy in fetch(j + 1):
                    copy.start()
            for copy in fetch(j):
                copy.wait()
            if j >= 2:
                for copy in put(j - 2):
                    copy.wait()
            body(
                shared_refs, total_ref if j == 0 else out_ref, [r.at[j % 2] for r in in_bufs],
                [r.at[j % 2] for r in out_bufs], smalls[j], out_ref, extra,
            )
            for copy in put(j):
                copy.start()
        for j in range(max(0, count - 2), count):
            for copy in put(j):
                copy.wait()

    out = pl.pallas_call(
        kernel,
        name=name,
        out_shape=(jax.ShapeDtypeStruct(total.shape, F32),)
        + (jax.ShapeDtypeStruct(small, F32),) * count
        + tuple(jax.ShapeDtypeStruct(shape, BF) for shape in big) * count,
        in_specs=[vmem] * (len(shared) + 1) + [anywhere] * (count * takes),
        out_specs=(vmem,) * (1 + count) + (anywhere,) * (count * gives),
        scratch_shapes=[pltpu.VMEM((2,) + x.shape, x.dtype) for x in blocks[0]]
        + [pltpu.VMEM((2,) + shape, BF) for shape in big]
        + [dma((2, takes)), dma((2, gives))]
        + list(scratch),
        compiler_params=pltpu.CompilerParams(vmem_limit_bytes=28 << 20),
        cost_estimate=small_cost(),
    )(*shared, total, *[x for block in blocks for x in block])
    smalls, bigs = out[1 : 1 + count], out[1 + count :]
    return out[0], smalls, [tuple(bigs[j * gives : (j + 1) * gives]) for j in range(count)]


def ffn_blocks_backward(dzb, yb, dy, blocks):
    def body(shared, total, ins, outs, small, out, extra):
        ffn_backward_kernel(*shared, *ins, total, *outs, small, out, *extra)

    first = blocks[0][2].shape
    act = blocks[0][0].shape
    return streamed_blocks(
        "ffn_backward", body, (dzb, yb), dy, blocks, (first, first), (1, act[1]), [pltpu.VMEM(act, BF)]
    )


def attend_blocks_backward(cols, da, x, dx, blocks, seg):
    tokens, model = x.shape

    def body(shared, total, ins, outs, small, out, extra):
        da_ref, x_ref, down_ref, across_ref = shared
        attend_backward_kernel(
            da_ref, x_ref, *ins, total, down_ref, across_ref, *outs, small, out, *extra
        )

    grad = (2 * cols, model)
    scratch = [pltpu.VMEM((tokens, cols), kind) for kind in (BF, BF, F32, F32)]
    return streamed_blocks(
        "attend_backward", body, (da, x, *seg), dx, blocks, (grad, grad), (1, 2 * cols), scratch
    )


def attend_forward(layer, cols, x, first, second, bias, z, seg):
    tokens, model = x.shape
    narrow = jax.ShapeDtypeStruct((tokens, cols), BF)

    def body(*refs):
        attend_forward_kernel(layer, *refs)

    return pl.pallas_call(
        body,
        name="attend_forward",
        out_shape=(
            narrow, narrow, narrow, narrow,
            jax.ShapeDtypeStruct((tokens, cols // HEAD_DIM), F32),
            jax.ShapeDtypeStruct(z.shape, F32),
        ),
        compiler_params=kernel_params(),
        cost_estimate=small_cost(),
    )(x, first, second, bias, z, *seg)


def anchors_kernel(dps, planes, x_ref, out_ref, near_send, near_recv, far_send, far_recv, own_sem):
    dp = lax.axis_index("dp")
    me = lax.axis_index("span") * TENSORS + lax.axis_index("tensor")

    def near(k):
        peer = lax.rem(me + k, planes)
        return {"span": peer // TENSORS, "tensor": lax.rem(peer, TENSORS)}

    def far(k):
        return {"dp": lax.rem(dp + k, dps)}

    barrier = pltpu.get_barrier_semaphore()
    for k in range(1, planes):
        pl.semaphore_signal(barrier, inc=1, device_id=near(k), device_id_type=MESH)
    for k in range(1, dps):
        pl.semaphore_signal(barrier, inc=1, device_id=far(k), device_id_type=MESH)
    pl.semaphore_wait(barrier, planes + dps - 2)

    own = pltpu.make_async_copy(x_ref, out_ref.at[dp, me], own_sem)
    own.start()

    def near_copy(k):
        return pltpu.make_async_remote_copy(
            src_ref=x_ref, dst_ref=out_ref.at[dp, me], send_sem=near_send.at[k],
            recv_sem=near_recv.at[k], device_id=near(k), device_id_type=MESH,
        )

    def far_copy(k):
        return pltpu.make_async_remote_copy(
            src_ref=out_ref.at[dp], dst_ref=out_ref.at[dp], send_sem=far_send.at[k],
            recv_sem=far_recv.at[k], device_id=far(k), device_id_type=MESH,
        )

    for k in range(1, planes):
        near_copy(k).start()
    own.wait()
    for k in range(1, planes):
        near_copy(k).wait()
    for k in range(1, dps):
        far_copy(k).start()
    for k in range(1, dps):
        far_copy(k).wait()


def gather_anchors(values):
    dps = lax.axis_size("dp")
    planes = lax.axis_size("span") * lax.axis_size("tensor")
    dma = pltpu.SemaphoreType.DMA
    vmem = pl.BlockSpec(memory_space=pltpu.VMEM)

    def body(*refs):
        anchors_kernel(dps, planes, *refs)

    return pl.pallas_call(
        body,
        name="gather_anchors",
        out_shape=jax.ShapeDtypeStruct((dps, planes) + values.shape, values.dtype),
        in_specs=[vmem],
        out_specs=vmem,
        scratch_shapes=[dma((planes,)), dma((planes,)), dma((dps,)), dma((dps,)), dma],
        compiler_params=pltpu.CompilerParams(collective_id=0, has_side_effects=True),
    )(values)


VECTORS = ("pb", "g0", "g1", "s0", "s1", "sb")
ROWS_PER_CHUNK = 4
CHUNKS_PER_LAYER = 4


def block_order(side, tensor):
    flip_one = tensor + 1 - 2 * lax.rem(tensor, 2)
    flip_two = tensor + 2 - 4 * (tensor // 2)
    swing = side * (flip_two - flip_one)
    return tensor, flip_one + swing, flip_two - swing, TENSORS - 1 - tensor


def remote(src, dst, sems, i, device):
    return pltpu.make_async_remote_copy(
        src_ref=src, dst_ref=dst, send_sem=sems.at[0, i], recv_sem=sems.at[1, i],
        device_id=device, device_id_type=MESH,
    )


class Halving:
    def __init__(self, dps, dp, src, result, scratch, sums, sems):
        self.src, self.result, self.scratch, self.sums, self.sems = src, result, scratch, sums, sems
        self.steps = []
        base, size, bit = 0, dps, 1
        while bit < dps:
            size = size // 2
            up = lax.rem(dp // bit, 2)
            self.steps.append((base + (1 - up) * size, base + up * size, size, {"dp": dp + bit * (1 - 2 * up)}))
            base = base + up * size
            bit *= 2

    def current(self, s):
        return self.src if s == 0 else self.sums

    def down(self, s):
        away, kept, size, partner = self.steps[s]
        room = self.scratch.at[pl.ds(self.steps_room(s), size)]
        return remote(self.current(s).at[pl.ds(away, size)], room, self.sems, s, partner)

    def steps_room(self, s):
        return sum(step[2] for step in self.steps[:s])

    def add(self, s):
        self.down(s).wait()
        away, kept, size, partner = self.steps[s]
        came = self.scratch[pl.ds(self.steps_room(s), size)]
        into = self.result if s == len(self.steps) - 1 else self.sums
        into[pl.ds(kept, size)] = plus(self.current(s)[pl.ds(kept, size)], came)

    def up(self, s):
        away, kept, size, partner = self.steps[s]
        part = self.result.at[pl.ds(kept, size)]
        return remote(part, part, self.sems, len(self.steps) + s, partner)


def last_kernel(dps, planes, ffn_ref, own, rest, rows_ref, blocks, outs, scratch):
    ffn_own, ffn_other, attn_own, attn_other, out_ref = outs
    (
        swapped, main_rest, main_own, across, mine, got_rest, got_own, got_across, got_peer, total_ref,
        ffn_room, attn_room, ffn_sums, attn_sums, x_ref, parts, sums,
        swap_sems, plane_sems, ffn_sems, attn_sems, one_sems, two_sems, three_sems,
    ) = scratch
    dp = lax.axis_index("dp")
    side = lax.axis_index("span")
    tensor = lax.axis_index("tensor")
    me = side * TENSORS + tensor
    order = block_order(side, tensor)
    x_ref[...] = rows_ref[...]
    for l in range(2):
        for j in range(TENSORS):
            for k in range(2):
                columns = blocks[l][k][j].shape[1]
                x_ref[l * CHUNKS_PER_LAYER + k, pl.ds(order[j], 1), :columns] = blocks[l][k][j][...]

    def near_peer(k):
        return lax.rem(me + k, planes)

    def near(k):
        peer = near_peer(k)
        return {"span": peer // TENSORS, "tensor": lax.rem(peer, TENSORS)}

    def far_peer(k):
        return lax.rem(dp + k, dps)

    def far(k):
        return {"dp": far_peer(k)}

    peer_core, main_peer, diag_peer = {"span": 1 - side}, {"tensor": order[1]}, {"tensor": order[2]}
    nears, fars = range(1, planes), range(1, dps)

    barrier = pltpu.get_barrier_semaphore()
    for k in nears:
        pl.semaphore_signal(barrier, inc=1, device_id=near(k), device_id_type=MESH)
    for k in fars:
        pl.semaphore_signal(barrier, inc=1, device_id=far(k), device_id_type=MESH)
    pl.semaphore_wait(barrier, planes + dps - 2)

    swaps = [
        remote(src, swapped.at[i], swap_sems, i, peer_core)
        for i, src in enumerate((own[2], rest[2], rest[3], rest[0]))
    ]
    for copy in swaps:
        copy.start()
    ones = [remote(x_ref.at[near_peer(k)], parts.at[k], one_sems, k, near(k)) for k in nears]
    for copy in ones:
        copy.start()
    ffn_chunks = [
        Halving(dps, dp, ffn_ref.at[c], ffn_own.at[c], ffn_room.at[c], ffn_sums.at[c], ffn_sems.at[c])
        for c in range(ffn_ref.shape[0])
    ]
    attn_chunks = [
        Halving(dps, dp, total_ref.at[c], attn_own.at[c], attn_room.at[c], attn_sums.at[c], attn_sems.at[c])
        for c in range(total_ref.shape[0])
    ]
    stages = range(len(ffn_chunks[0].steps))
    last = len(stages) - 1

    def down_from(chunks, s):
        for chunk in chunks:
            chunk.down(s).start()

    def down_to_end(chunks, s):
        for chunk in chunks:
            chunk.add(s)
            (chunk.down(s + 1) if s < last else chunk.up(last)).start()

    def up_next(chunks, s):
        for chunk in chunks:
            chunk.up(s).wait()
            if s > 0:
                chunk.up(s - 1).start()

    down_from(ffn_chunks, 0)

    for copy in swaps:
        copy.wait()
    across[...] = plus(own[3][...], swapped[2])
    main_rest[...] = plus(rest[1][...], swapped[0])
    send_across = remote(across, got_across, plane_sems, 0, diag_peer)
    send_across.start()
    send_rest = remote(main_rest, got_rest, plane_sems, 1, main_peer)
    send_rest.start()
    mine[...] = plus(own[0][...], swapped[3])
    for copy in ones:
        copy.wait()
    total = x_ref[me]
    for k in nears:
        total = total + parts[k]
    sums[dp] = total
    twos = [remote(sums.at[dp], sums.at[dp], two_sems, k, far(k)) for k in fars]
    for copy in twos:
        copy.start()

    down_to_end(ffn_chunks, 0)
    send_across.wait()
    main_own[...] = plus(own[1][...], swapped[1], got_across[...])
    send_own = remote(main_own, got_own, plane_sems, 2, main_peer)
    send_own.start()
    for s in stages[1:]:
        down_to_end(ffn_chunks, s)
    send_rest.wait()
    send_peer = remote(got_rest, got_peer, swap_sems, 4, peer_core)
    send_peer.start()
    send_peer.wait()
    send_own.wait()
    total_ref[...] = plus(mine[...], got_own[...], got_peer[...])
    down_from(attn_chunks, 0)

    for copy in twos:
        copy.wait()
    total = sums[0]
    for k in fars:
        total = total + sums[k]
    out_ref[me] = total
    threes = [remote(out_ref.at[me], out_ref.at[me], three_sems, k, near(k)) for k in nears]
    for copy in threes:
        copy.start()

    for s in reversed(stages[1:]):
        up_next(ffn_chunks, s)
    for s in stages:
        down_to_end(attn_chunks, s)
    up_next(ffn_chunks, 0)
    swap_ffn = remote(ffn_own, ffn_other, swap_sems, 5, peer_core)
    swap_ffn.start()
    for s in reversed(stages):
        up_next(attn_chunks, s)
    swap_attn = remote(attn_own, attn_other, swap_sems, 6, peer_core)
    swap_attn.start()
    for copy in threes:
        copy.wait()
    swap_ffn.wait()
    swap_attn.wait()


def last_sums(ffn_total, attn_blocks, rows, blocks):
    dps = lax.axis_size("dp")
    planes = lax.axis_size("span") * lax.axis_size("tensor")
    flat, tree = jax.tree.flatten(blocks)

    def by_dp(values):
        rows = values.shape[0]
        chunks = 2 if rows % (32 * dps) == 0 else 1
        return values.reshape(chunks, dps, rows // (chunks * dps), values.shape[1])

    ffn_total = by_dp(ffn_total)
    own = [by_dp(o) for o, r in attn_blocks]
    rest = [by_dp(r) for o, r in attn_blocks]
    dma = pltpu.SemaphoreType.DMA
    vmem = pl.BlockSpec(memory_space=pltpu.VMEM)
    attn, ffn = own[0].shape, ffn_total.shape

    def body(ffn_ref, *refs):
        own_refs, rest_refs, rows_ref = refs[:TENSORS], refs[TENSORS : 2 * TENSORS], refs[2 * TENSORS]
        refs = refs[2 * TENSORS + 1 :]
        inputs = jax.tree.unflatten(tree, refs[: len(flat)])
        outs, scratch = refs[len(flat) : len(flat) + 5], refs[len(flat) + 5 :]
        last_kernel(dps, planes, ffn_ref, own_refs, rest_refs, rows_ref, inputs, outs, scratch)

    outs = pl.pallas_call(
        body,
        name="last_sums",
        out_shape=tuple(jax.ShapeDtypeStruct(shape, BF) for shape in (ffn, ffn, attn, attn))
        + (jax.ShapeDtypeStruct(rows.shape, F32),),
        in_specs=[vmem] * (2 + 2 * TENSORS + len(flat)),
        out_specs=(vmem,) * 5,
        scratch_shapes=[pltpu.VMEM((TENSORS,) + attn, BF)]
        + [pltpu.VMEM(attn, BF)] * 9
        + [pltpu.VMEM(ffn, BF), pltpu.VMEM(attn, BF)] * 2
        + [pltpu.VMEM(rows.shape, F32), pltpu.VMEM(rows.shape, F32), pltpu.VMEM((dps,) + rows.shape[1:], F32)]
        + [dma((2, 7)), dma((2, 3))]
        + [dma((ffn[0], 2, dps)), dma((attn[0], 2, dps))]
        + [dma((2, planes)), dma((2, dps)), dma((2, planes))],
        compiler_params=pltpu.CompilerParams(
            collective_id=1, has_side_effects=True, vmem_limit_bytes=36 << 20
        ),
    )(ffn_total, *own, *rest, rows, *flat)
    whole = [o.reshape(-1, o.shape[-1]) for o in outs[:4]]
    return (*whole, outs[4])


def to_rows(values):
    return lax.all_to_all(values, "tensor", split_axis=0, concat_axis=0, tiled=True).reshape(
        -1, values.shape[-1]
    )


def to_places(values):
    blocks = values.reshape(TENSORS, -1, values.shape[-1])
    return lax.all_to_all(blocks, "tensor", split_axis=0, concat_axis=0, tiled=True)


def layer_forward(l, x, seg, attn, ffn, vec, hook):
    xb = x.astype(BF)
    kept = []
    z1 = x + vec["pb"]
    for j in range(TENSORS):
        first, second = attn.blocks[j]
        *saved, z1 = attend_forward(l, vec["cols"], xb, first, second, vec["heads"](j), z1, seg)
        kept.append(saved)
        z1 = hook("attn", j, z1)
    n1, r1 = normal_parts(z1)
    y = n1 * vec["g0"] + vec["s0"]
    yb = y.astype(BF)
    act, slope = [], []
    z2 = y + vec["sb"]
    for j in range(TENSORS):
        first, second = ffn.blocks[j]
        a, b = gelu_parts(mm(yb, first, 1, 0) + vec["eb"](j))
        act.append(a.astype(BF))
        slope.append(b.astype(BF))
        z2 = z2 + mm(act[-1], second, 1, 0)
        z2 = hook("ffn", j, z2)
    n2, r2 = normal_parts(z2)
    out = n2 * vec["g1"] + vec["s1"]
    return out, (xb, kept, n1, r1, yb, act, slope, n2, r2)


def total_rows(values):
    return jnp.sum(values, axis=0)


def ffn_backward(dout, ffn_w, vec, kept, hook, cut):
    xb, saved, n1, r1, yb, act, slope, n2, r2 = kept
    dz2 = normal_back(dout, n2, r2, vec["g1"])
    small = {"g1": total_rows(dout * n2), "s1": total_rows(dout), "sb": total_rows(dz2), "eb": []}
    dz2 = hook("seeded", dz2)
    dzb = dz2.astype(BF)
    dy = dz2
    blocks = []
    for lo, hi in ((0, cut), (cut, TENSORS)):
        if lo == hi:
            continue
        parts = [(act[j], slope[j], *ffn_w[j]) for j in range(lo, hi)]
        dy, sums, grads = ffn_blocks_backward(dzb, yb, dy, parts)
        small["eb"] += sums
        blocks += grads
        if hi < TENSORS:
            dzb, dy = hook("three", (dzb, dy))
    return dy, blocks, small


def attn_backward(dy, seg, attn_w, vec, kept, hook):
    xb, saved, n1, r1, yb, act, slope, n2, r2 = kept
    dz1 = normal_back(dy, n1, r1, vec["g0"])
    small = {"g0": total_rows(dy * n1), "s0": total_rows(dy), "pb": total_rows(dz1), "heads": []}
    dz1 = hook("normed", dz1)
    da = dz1.astype(BF)
    dx = dz1
    blocks = []
    for lo, hi in ((0, TENSORS - 1), (TENSORS - 1, TENSORS)):
        parts = [(*attn_w[j], *saved[j]) for j in range(lo, hi)]
        dx, sums, grads = attend_blocks_backward(vec["cols"], da, xb, dx, parts, seg)
        small["heads"] += sums
        blocks += grads
        if lo == 0:
            da, dx = hook("three", (da, dx))
    return dx, blocks, small


def attn_unpack(first, second):
    cols = first.shape[0] // 2
    heads = jnp.stack([first[:cols], first[cols:], second[:cols]])
    return jnp.swapaxes(heads, 1, 2), second[cols:]


class Reduction:
    def start(self, value, blocks):
        self.blocks = blocks
        value, *self.outgoing = tie(value, *reduce_outgoing(blocks))
        return value

    def swapped(self, value):
        value, self.main_rest, self.main_own, self.across, self.mine = tie(
            value, *reduce_swapped(self.blocks, self.outgoing)
        )
        self.from_rest = send(self.main_rest, MAIN)
        return value

    def crossed(self, value):
        value, self.main_own = tie(value, reduce_across(self.main_own, self.across))
        self.from_own = send(self.main_own, MAIN)
        self.from_peer = send(self.from_rest, SWAP)
        return value

    def summed(self, value):
        value, self.total = tie(value, plus(self.mine, self.from_own, self.from_peer))
        return value


def shards(
    layer_input, skip_tokens, backbone_cotangent, head_cotangent, segment_lengths, pair_index,
    w_heads, heads_bias, w_project, project_bias, norm_gain, norm_shift,
    w_expand, expand_bias, w_shrink, shrink_bias,
):
    side = lax.axis_index("span")
    mine = lax.axis_index("tensor")
    width = layer_input.shape[-1]
    head_cols = w_heads.shape[-1]
    ff_cols = w_expand.shape[-1]

    extra = 16
    bias_rows = jnp.concatenate([heads_bias.reshape(1, 4 * head_cols), expand_bias], axis=0)
    bias_rows = jnp.pad(bias_rows, ((0, extra - bias_rows.shape[0]), (0, 0)))

    def attn_rows(l):
        heads = jnp.swapaxes(w_heads[l], 1, 2)
        first = heads[:2].reshape(2 * head_cols, width)
        return first, jnp.concatenate([heads[2], w_project[l]], axis=0)

    first, second = attn_rows(0)
    first = jnp.concatenate([first, bias_rows], axis=0)
    second = jnp.pad(second, ((0, extra), (0, 0)))
    gather_attn0, gather_ffn0, gather_attn1, gather_ffn1 = (Gathering(side) for _ in range(4))
    x = to_rows(layer_input[0])
    mark = gather_attn0.start(layer_input[0, 0, 0], first, second)
    mark = gather_ffn0.start(mark, w_expand[0], w_shrink[0])
    later = {}

    def during_forward0(kind, j, value):
        if kind == "attn":
            if j == 0:
                value = gather_attn0.arrived(value)
            if j == 1:
                value = gather_attn1.start(value, *attn_rows(1))
            if j == 2:
                value = gather_attn0.crossed(value)
            if j == 3:
                value = gather_ffn0.arrived(value)
                value = gather_ffn1.start(value, w_expand[1], w_shrink[1])
        else:
            if j == 0:
                skip, value = tie(skip_tokens[0], value)
                later["skip"] = to_rows(skip)
            if j == 1:
                value = gather_attn1.arrived(value)
            if j == 2:
                value = gather_ffn0.crossed(value)
        return value

    def during_forward1(kind, j, value):
        if kind == "attn":
            if j == 0:
                head_cot, value = tie(head_cotangent[0], value)
                later["head"] = to_rows(head_cot)
            if j == 1:
                value = gather_attn1.crossed(value)
            if j == 2:
                value, mark = tie(value, later["backbone_out"])
            if j == 3:
                value = gather_ffn1.arrived(value)
        else:
            if j == 0:
                backbone_cot, value = tie(backbone_cotangent[0], value)
                later["backbone"] = to_rows(backbone_cot)
            if j == 2:
                value = gather_ffn1.crossed(value)
        return value

    tokens = x.shape[0]

    def bias_row(j, i):
        first, second = gather_attn0.blocks[j]
        return first[2 * head_cols + i : 2 * head_cols + i + 1].astype(F32)

    def vectors(l):
        return {
            "cols": head_cols, "heads": lambda j: bias_row(j, 0),
            "eb": lambda j: bias_row(j, 1 + l), "pb": project_bias[l].astype(F32),
            "g0": norm_gain[l, 0].astype(F32), "g1": norm_gain[l, 1].astype(F32),
            "s0": norm_shift[l, 0].astype(F32), "s1": norm_shift[l, 1].astype(F32),
            "sb": shrink_bias[l].astype(F32),
        }

    lengths = lax.dynamic_index_in_dim(segment_lengths[0], mine, 0, keepdims=False)
    span_count = lengths.shape[0]
    starts = jnp.cumsum(lengths) - lengths
    row_length = jnp.sum(lengths)
    places = jnp.arange(tokens, dtype=jnp.int32)
    counted = jnp.sum((places[:, None] >= starts[None, :]).astype(jnp.int32), axis=-1) - 1
    segment = jnp.where(places < row_length, counted, span_count)
    seg = (segment[:, None], segment[None, :])
    valid = (places < row_length).astype(F32)[:, None]
    picker = (starts[:, None] == places[None, :]).astype(F32)
    first_place = jnp.sum(picker, axis=0)[:, None] > 0

    vec0, vec1 = vectors(0), vectors(1)
    backbone, kept0 = layer_forward(0, x.astype(F32), seg, gather_attn0, gather_ffn0, vec0, during_forward0)
    attn_w0, ffn_w0 = gather_attn0.blocks, gather_ffn0.blocks
    later["backbone_out"] = to_places((backbone * valid).astype(BF))
    cls = mm(picker.astype(BF), backbone.astype(BF), 1, 0).astype(BF)
    anchors = gather_anchors(cls)
    dp_count = lax.axis_size("dp")
    pair_count = lax.axis_size("span")
    vector_count = dp_count * TENSORS * span_count
    anchors = anchors.reshape(dp_count, pair_count, TENSORS * span_count, width)
    anchors = jnp.swapaxes(anchors, 0, 1).reshape(pair_count, vector_count, width)

    head_in = jnp.where(first_place, backbone, later["skip"].astype(F32))
    head, kept1 = layer_forward(1, head_in, seg, gather_attn1, gather_ffn1, vec1, during_forward1)
    attn_w1, ffn_w1 = gather_attn1.blocks, gather_ffn1.blocks
    head_cot, backbone_cot = later["head"], later["backbone"]
    head_out = to_places((head * valid).astype(BF))

    root = math.sqrt(width)
    logits = mm(anchors[0], anchors[1], 1, 1) / root
    columns = jnp.arange(vector_count, dtype=jnp.int32)
    target = (pair_index[:, None] == columns[None, :]).astype(F32)
    lse_rows = jax.nn.logsumexp(logits, axis=1)
    lse_cols = jax.nn.logsumexp(logits, axis=0)
    dlogits = LOSS_WEIGHT * (
        jnp.exp(logits - lse_rows[:, None]) + jnp.exp(logits - lse_cols[None, :]) - 2.0 * target
    )
    span_loss = (jnp.sum(lse_rows) + jnp.sum(lse_cols) - 2.0 * jnp.sum(target * logits)) / (
        2 * vector_count
    )
    own = (lax.axis_index("dp") * TENSORS + mine) * span_count
    wanted = jnp.where(side == 0, dlogits, dlogits.T)
    wanted = lax.dynamic_slice(wanted, (own, 0), (span_count, vector_count))
    other = lax.dynamic_index_in_dim(anchors, 1 - side, 0, keepdims=False).astype(F32)
    dcls = jnp.dot(wanted, other, precision=HIGHEST) / root

    def plain(name, value):
        return value

    ffn1, attn1, ffn0 = (Reduction() for _ in range(3))

    dy, blocks, small1 = ffn_backward(head_cot.astype(F32) * valid, ffn_w1, vec1, kept1, plain, 0)
    dy, mark = tie(dy, head_out)
    dy = ffn1.start(dy, blocks)

    def during_attn1(name, value):
        if name == "normed":
            return ffn1.swapped(value)
        return ffn1.crossed(value)

    du, blocks, more = attn_backward(dy, seg, attn_w1, vec1, kept1, during_attn1)
    small1.update(more)
    du = attn1.start(du, blocks)
    du = ffn1.summed(du)
    ffn_total1 = lax.psum(ffn1.total, "dp")
    grad_skip = to_places(jnp.where(first_place, 0.0, du).astype(BF))

    seed = backbone_cot.astype(F32) * valid + jnp.where(first_place, du, 0.0)
    seed = seed + jnp.dot(picker.T, dcls, precision=HIGHEST)

    def during_ffn0(name, value):
        if name == "seeded":
            return attn1.swapped(value)
        return attn1.crossed(value)

    dy, blocks, small0 = ffn_backward(seed, ffn_w0, vec0, kept0, during_ffn0, 2)
    dy, mark = tie(dy, grad_skip)
    dy = ffn0.start(dy, blocks)
    dy = attn1.summed(dy)

    dy, ffn_total1, late = tie(dy, ffn_total1, attn1.total)
    attn_total1 = lax.psum(late, "dp")
    finished = {}

    def during_attn0(name, value):
        if name == "normed":
            return ffn0.swapped(value)
        value = ffn0.crossed(value)
        value, finished["attn"] = tie(value, attn_total1)
        return value

    dx, attn_blocks, more = attn_backward(dy, seg, attn_w0, vec0, kept0, during_attn0)
    small0.update(more)
    attn_total1 = finished["attn"]
    grad_input = to_places(dx.astype(BF))

    place = lax.broadcasted_iota(jnp.int32, (2 * CHUNKS_PER_LAYER * ROWS_PER_CHUNK, 1), 0)
    rows = jnp.zeros((place.shape[0], width), F32)
    for l, small in enumerate((small0, small1)):
        base = l * CHUNKS_PER_LAYER * ROWS_PER_CHUNK
        for i, k in enumerate(VECTORS):
            rows = rows + jnp.where(place == base + 2 * ROWS_PER_CHUNK + i, small[k][None], 0.0)
    rows = ffn0.summed(rows.reshape(2 * CHUNKS_PER_LAYER, ROWS_PER_CHUNK, width))
    ffn_total1, attn_total1 = tie(ffn_total1, attn_total1)
    other_ffn1, other_attn1 = send(ffn_total1, SWAP), send(attn_total1, SWAP)
    rows, other_ffn1, other_attn1 = tie(rows, other_ffn1, other_attn1)
    ffn_own, ffn_other, attn_own, attn_other, total = last_sums(
        ffn0.total, attn_blocks, rows, [(small["eb"], small["heads"]) for small in (small0, small1)]
    )

    hb, eb, vector_sums = [], [], []
    for l in range(2):
        base = l * CHUNKS_PER_LAYER
        own = lax.dynamic_slice(total[base : base + 2], (0, mine, 0), (2, 1, width))[:, 0]
        eb.append(own[0])
        hb.append(jnp.stack([own[1, :head_cols], own[1, head_cols : 2 * head_cols]]))
        rows = total[base + 2 : base + CHUNKS_PER_LAYER].reshape(-1, width)
        vector_sums.append({k: rows[i] for i, k in enumerate(VECTORS)})
    sums = vector_sums

    ge1, gs1 = in_order(side, ffn_total1, other_ffn1)
    gh1, gp1 = attn_unpack(*in_order(side, attn_total1, other_attn1))
    ge0, gs0 = in_order(side, ffn_own, ffn_other)
    gh0, gp0 = attn_unpack(*in_order(side, attn_own, attn_other))

    return (
        later["backbone_out"][None],
        head_out[None],
        span_loss,
        grad_input[None],
        grad_skip[None],
        jnp.stack([gh0, gh1]),
        jnp.stack(hb),
        jnp.stack([gp0, gp1]),
        jnp.stack([s["pb"] for s in sums]),
        jnp.stack([jnp.stack([s["g0"], s["g1"]]) for s in sums]),
        jnp.stack([jnp.stack([s["s0"], s["s1"]]) for s in sums]),
        jnp.stack([ge0, ge1]),
        jnp.stack(eb),
        jnp.stack([gs0, gs1]),
        jnp.stack([s["sb"] for s in sums]),
    )


def solution(mesh):
    rows = P("span", "dp", "tensor", None)
    in_specs = (
        rows, rows, rows, rows, P("span", "dp", None), P(),
        P(None, None, None, "tensor"), P(None, None, "tensor"), P(None, "tensor", None),
        P(), P(), P(), P(None, None, "tensor"), P(None, "tensor"), P(None, "tensor", None), P(),
    )
    out_specs = (
        rows, rows, P(), rows, rows,
        P(None, None, None, "tensor"), P(None, None, "tensor"), P(None, "tensor", None),
        P(), P(), P(), P(None, None, "tensor"), P(None, "tensor"), P(None, "tensor", None), P(),
    )
    return jax.shard_map(shards, mesh=mesh, in_specs=in_specs, out_specs=out_specs, check_vma=False)
```

```python
import math

import jax
import jax.numpy as jnp
from jax import lax
from jax.experimental import pallas as pl
from jax.experimental.pallas import tpu as pltpu
from jax.sharding import PartitionSpec as P

HEAD_DIM = 64
EPSILON = 1e-12
LOSS_WEIGHT = 8.0
HIGHEST = lax.Precision.HIGHEST
MASKED = -1e30
BF = jnp.bfloat16
F32 = jnp.float32
PLANE = ("span", "tensor")
MESH = pl.DeviceIdType.MESH
TENSORS = 4
MAIN, DIAG, SWAP = "main", "diag", "swap"


def mm(a, b, ca, cb):
    return lax.dot_general(a, b, (((ca,), (cb,)), ((), ())), preferred_element_type=F32)


def normal_parts(values):
    centred = values - jnp.mean(values, axis=-1, keepdims=True)
    spread = jnp.mean(centred * centred, axis=-1, keepdims=True)
    scale = lax.rsqrt(spread + EPSILON)
    return centred * scale, scale


def normal_back(upward, normed, scale, gain):
    weighted = upward * gain
    first = jnp.mean(weighted, axis=-1, keepdims=True)
    second = jnp.mean(weighted * normed, axis=-1, keepdims=True)
    return (weighted - first - normed * second) * scale


def gelu_parts(hidden):
    phi = 0.5 * (1.0 + lax.erf(hidden * math.sqrt(0.5)))
    slope = phi + hidden * jnp.exp(-0.5 * hidden * hidden) * (1.0 / math.sqrt(2.0 * math.pi))
    return hidden * phi, slope


def plane_pairs(kind):
    pairs = []
    for side in range(2):
        for t in range(TENSORS):
            if kind == SWAP:
                target = (1 - side, t)
            elif kind == MAIN:
                target = (side, t ^ (1 + side))
            else:
                target = (side, t ^ (2 - side))
            pairs.append((side * TENSORS + t, target[0] * TENSORS + target[1]))
    return pairs


def send(values, kind):
    return lax.ppermute(values, PLANE, plane_pairs(kind))


def plus(*terms):
    total = terms[0].astype(F32)
    for term in terms[1:]:
        total = total + term.astype(F32)
    return total.astype(BF)


def pick(side, zero, one):
    return jnp.where(side == 0, zero, one)


def tie(*values):
    return lax.optimization_barrier(values)


class Gathering:
    def __init__(self, side):
        self.side = side

    def start(self, value, first, second):
        value, first, second = tie(value, first, second)
        self.got = (send(first, MAIN), send(second, MAIN))
        self.blocks = [(first, second)]
        return value

    def arrived(self, value):
        value, *got = tie(value, *self.got)
        self.across = send(pick(self.side, *got), DIAG)
        self.blocks += [tuple(got), tuple(send(g, SWAP) for g in got)]
        return value

    def crossed(self, value):
        value, across = tie(value, self.across)
        rest = send(across, SWAP)
        self.blocks.append((pick(self.side, across, rest), pick(self.side, rest, across)))
        return value


def reduce_outgoing(blocks):
    return blocks[2][0], blocks[2][1], blocks[3][1], blocks[0][1]


def reduce_swapped(blocks, outgoing):
    got = [send(o, SWAP) for o in outgoing]
    return (
        plus(blocks[1][1], got[0]), plus(blocks[1][0], got[1]), plus(blocks[3][0], got[2]), plus(blocks[0][0], got[3])
    )


def reduce_across(main_own, across):
    return plus(main_own, send(across, DIAG))


def in_order(side, own, other):
    return pick(side, own, other).astype(F32), pick(side, other, own).astype(F32)


Q_ROWS = 128


def attend_forward_kernel(
    layer, x_ref, first_ref, second_ref, bias_ref, z_ref, down_ref, across_ref,
    q_ref, k_ref, v_ref, o_ref, lse_ref, out_ref
):
    tokens, width = q_ref.shape
    at = 2 * layer * width
    x = x_ref[...]
    q_ref[...] = (mm(x, first_ref[:width, :], 1, 1) + bias_ref[:, at : at + width]).astype(BF)
    k_ref[...] = mm(x, first_ref[width : 2 * width, :], 1, 1).astype(BF)
    v_ref[...] = (mm(x, second_ref[:width, :], 1, 1) + bias_ref[:, at + width : at + 2 * width]).astype(BF)

    def step(i, carry):
        rows = pl.ds(pl.multiple_of(i * Q_ROWS, Q_ROWS), Q_ROWS)
        same = down_ref[rows, :] == across_ref[...]
        for h in range(width // HEAD_DIM):
            head = slice(h * HEAD_DIM, (h + 1) * HEAD_DIM)
            s = mm(q_ref[rows, head], k_ref[:, head], 1, 1) * 0.125
            s = jnp.where(same, s, MASKED)
            top = jnp.max(s, axis=-1, keepdims=True)
            raised = jnp.exp(s - top)
            total = jnp.sum(raised, axis=-1, keepdims=True)
            weights = (raised * (1.0 / total)).astype(BF)
            o_ref[rows, head] = mm(weights, v_ref[:, head], 1, 0).astype(BF)
            lse_ref[rows, h : h + 1] = top + jnp.log(total)
        out_ref[rows, :] = z_ref[rows, :] + mm(o_ref[rows, :], second_ref[width : 2 * width, :], 1, 0)
        return carry

    lax.fori_loop(0, tokens // Q_ROWS, step, 0)


def attend_backward_kernel(
    da_ref, x_ref, first_ref, second_ref, q_ref, k_ref, v_ref, o_ref, lse_ref, dx_ref, down_ref, across_ref,
    own_ref, rest_ref, sums_ref, out_ref, do_ref, dq_ref, dk_ref, dv_ref
):
    tokens, width = q_ref.shape
    da = da_ref[...]
    do_ref[...] = mm(da, second_ref[width : 2 * width, :], 1, 1).astype(BF)
    dk_ref[...] = jnp.zeros_like(dk_ref)
    dv_ref[...] = jnp.zeros_like(dv_ref)

    def step(i, carry):
        rows = pl.ds(pl.multiple_of(i * Q_ROWS, Q_ROWS), Q_ROWS)
        same = down_ref[rows, :] == across_ref[...]
        for h in range(width // HEAD_DIM):
            head = slice(h * HEAD_DIM, (h + 1) * HEAD_DIM)
            q, k, up = q_ref[rows, head], k_ref[:, head], do_ref[rows, head]
            s = mm(q, k, 1, 1) * 0.125
            s = jnp.where(same, s, MASKED)
            pr = jnp.exp(s - lse_ref[rows, h : h + 1])
            dp = mm(up, v_ref[:, head], 1, 1)
            inner = jnp.sum(pr * dp, axis=-1, keepdims=True)
            ds = (pr * (dp - inner)).astype(BF)
            dq_ref[rows, head] = (mm(ds, k, 1, 0) * 0.125).astype(BF)
            dk_ref[:, head] += mm(ds, q, 0, 0)
            dv_ref[:, head] += mm(pr.astype(BF), up, 0, 0)
        return carry

    lax.fori_loop(0, tokens // Q_ROWS, step, 0)
    x = x_ref[...]
    dq = dq_ref[...]
    dk = (dk_ref[...] * 0.125).astype(BF)
    dv = dv_ref[...].astype(BF)
    out_ref[...] = (
        dx_ref[...]
        + mm(dq, first_ref[:width, :], 1, 0)
        + mm(dk, first_ref[width : 2 * width, :], 1, 0)
        + mm(dv, second_ref[:width, :], 1, 0)
    )
    side = lax.axis_index("span")
    store_both(
        side, own_ref, rest_ref, slice(0, width), mm(dq, x, 0, 0).astype(BF), mm(dv, x, 0, 0).astype(BF)
    )
    store_both(
        side, own_ref, rest_ref, slice(width, 2 * width),
        mm(dk, x, 0, 0).astype(BF), mm(o_ref[...], da, 0, 0).astype(BF),
    )
    sums_ref[:, :width] = jnp.sum(dq.astype(F32), axis=0, keepdims=True)
    sums_ref[:, width:] = jnp.sum(dv.astype(F32), axis=0, keepdims=True)


def small_cost():
    return pl.CostEstimate(flops=1 << 20, bytes_accessed=1 << 10, transcendentals=0)


def kernel_params():
    return pltpu.CompilerParams(vmem_limit_bytes=24 << 20)


def store_both(side, own_ref, rest_ref, rows, first, second):
    @pl.when(side == 0)
    def _():
        own_ref[rows, :] = first
        rest_ref[rows, :] = second

    @pl.when(side != 0)
    def _():
        own_ref[rows, :] = second
        rest_ref[rows, :] = first


def ffn_backward_kernel(
    dz_ref, y_ref, act_ref, slope_ref, first_ref, second_ref, dy_ref, own_ref, rest_ref, sums_ref, out_ref, dh_ref
):
    tokens, model = dz_ref.shape
    side = lax.axis_index("span")
    sums_ref[...] = jnp.zeros_like(sums_ref)

    def data(i, carry):
        rows = pl.ds(pl.multiple_of(i * Q_ROWS, Q_ROWS), Q_ROWS)
        dhid = mm(dz_ref[rows, :], second_ref[...], 1, 1) * slope_ref[rows, :].astype(F32)
        sums_ref[...] += jnp.sum(dhid, axis=0, keepdims=True)
        dhb = dhid.astype(BF)
        dh_ref[rows, :] = dhb
        out_ref[rows, :] = dy_ref[rows, :] + mm(dhb, first_ref[...], 1, 1)
        return carry

    def weights(i, carry):
        rows = pl.ds(pl.multiple_of(i * Q_ROWS, Q_ROWS), Q_ROWS)
        first = mm(y_ref[:, rows], dh_ref[...], 0, 0).astype(BF)
        second = mm(act_ref[:, rows], dz_ref[...], 0, 0).astype(BF)
        store_both(side, own_ref, rest_ref, rows, first, second)
        return carry

    lax.fori_loop(0, tokens // Q_ROWS, data, 0)
    lax.fori_loop(0, model // Q_ROWS, weights, 0)


def streamed_blocks(name, body, shared, total, blocks, big, small, scratch):
    count, takes, gives = len(blocks), len(blocks[0]), len(big)
    vmem, anywhere = pl.BlockSpec(memory_space=pltpu.VMEM), pl.BlockSpec(memory_space=pl.ANY)
    dma = pltpu.SemaphoreType.DMA

    def kernel(*refs):
        refs = list(refs)

        def take(n):
            taken = refs[:n]
            del refs[:n]
            return taken

        shared_refs, (total_ref,), ins = take(len(shared)), take(1), take(count * takes)
        (out_ref,), smalls, outs = take(1), take(count), take(count * gives)
        in_bufs, out_bufs, (in_sems, out_sems), extra = take(takes), take(gives), take(2), take(len(scratch))

        def fetch(j):
            return [
                pltpu.make_async_copy(ins[j * takes + i], in_bufs[i].at[j % 2], in_sems.at[j % 2, i])
                for i in range(takes)
            ]

        def put(j):
            return [
                pltpu.make_async_copy(out_bufs[i].at[j % 2], outs[j * gives + i], out_sems.at[j % 2, i])
                for i in range(gives)
            ]

        for copy in fetch(0):
            copy.start()
        for j in range(count):
            if j + 1 < count:
                for copy in fetch(j + 1):
                    copy.start()
            for copy in fetch(j):
                copy.wait()
            if j >= 2:
                for copy in put(j - 2):
                    copy.wait()
            body(
                shared_refs, total_ref if j == 0 else out_ref, [r.at[j % 2] for r in in_bufs],
                [r.at[j % 2] for r in out_bufs], smalls[j], out_ref, extra,
            )
            for copy in put(j):
                copy.start()
        for j in range(max(0, count - 2), count):
            for copy in put(j):
                copy.wait()

    out = pl.pallas_call(
        kernel,
        name=name,
        out_shape=(jax.ShapeDtypeStruct(total.shape, F32),)
        + (jax.ShapeDtypeStruct(small, F32),) * count
        + tuple(jax.ShapeDtypeStruct(shape, BF) for shape in big) * count,
        in_specs=[vmem] * (len(shared) + 1) + [anywhere] * (count * takes),
        out_specs=(vmem,) * (1 + count) + (anywhere,) * (count * gives),
        scratch_shapes=[pltpu.VMEM((2,) + x.shape, x.dtype) for x in blocks[0]]
        + [pltpu.VMEM((2,) + shape, BF) for shape in big]
        + [dma((2, takes)), dma((2, gives))]
        + list(scratch),
        compiler_params=pltpu.CompilerParams(vmem_limit_bytes=63 << 20),
        cost_estimate=small_cost(),
    )(*shared, total, *[x for block in blocks for x in block])
    smalls, bigs = out[1 : 1 + count], out[1 + count :]
    return out[0], smalls, [tuple(bigs[j * gives : (j + 1) * gives]) for j in range(count)]


def ffn_blocks_backward(dzb, yb, dy, blocks):
    def body(shared, total, ins, outs, small, out, extra):
        ffn_backward_kernel(*shared, *ins, total, *outs, small, out, *extra)

    first = blocks[0][2].shape
    act = blocks[0][0].shape
    return streamed_blocks(
        "ffn_backward", body, (dzb, yb), dy, blocks, (first, first), (1, act[1]), [pltpu.VMEM(act, BF)]
    )


def attend_blocks_backward(cols, da, x, dx, blocks, seg):
    tokens, model = x.shape

    def body(shared, total, ins, outs, small, out, extra):
        da_ref, x_ref, down_ref, across_ref = shared
        attend_backward_kernel(
            da_ref, x_ref, *ins, total, down_ref, across_ref, *outs, small, out, *extra
        )

    grad = (2 * cols, model)
    scratch = [pltpu.VMEM((tokens, cols), kind) for kind in (BF, BF, F32, F32)]
    return streamed_blocks(
        "attend_backward", body, (da, x, *seg), dx, blocks, (grad, grad), (1, 2 * cols), scratch
    )


def attend_forward(layer, cols, x, first, second, bias, z, seg):
    tokens, model = x.shape
    narrow = jax.ShapeDtypeStruct((tokens, cols), BF)

    def body(*refs):
        attend_forward_kernel(layer, *refs)

    return pl.pallas_call(
        body,
        name="attend_forward",
        out_shape=(
            narrow, narrow, narrow, narrow,
            jax.ShapeDtypeStruct((tokens, cols // HEAD_DIM), F32),
            jax.ShapeDtypeStruct(z.shape, F32),
        ),
        compiler_params=kernel_params(),
        cost_estimate=small_cost(),
    )(x, first, second, bias, z, *seg)


def anchors_kernel(dps, planes, x_ref, out_ref, near_send, near_recv, far_send, far_recv, own_sem):
    dp = lax.axis_index("dp")
    me = lax.axis_index("span") * TENSORS + lax.axis_index("tensor")

    def near(k):
        peer = lax.rem(me + k, planes)
        return {"span": peer // TENSORS, "tensor": lax.rem(peer, TENSORS)}

    def far(k):
        return {"dp": lax.rem(dp + k, dps)}

    barrier = pltpu.get_barrier_semaphore()
    for k in range(1, planes):
        pl.semaphore_signal(barrier, inc=1, device_id=near(k), device_id_type=MESH)
    for k in range(1, dps):
        pl.semaphore_signal(barrier, inc=1, device_id=far(k), device_id_type=MESH)
    pl.semaphore_wait(barrier, planes + dps - 2)

    own = pltpu.make_async_copy(x_ref, out_ref.at[dp, me], own_sem)
    own.start()

    def near_copy(k):
        return pltpu.make_async_remote_copy(
            src_ref=x_ref, dst_ref=out_ref.at[dp, me], send_sem=near_send.at[k],
            recv_sem=near_recv.at[k], device_id=near(k), device_id_type=MESH,
        )

    def far_copy(k):
        return pltpu.make_async_remote_copy(
            src_ref=out_ref.at[dp], dst_ref=out_ref.at[dp], send_sem=far_send.at[k],
            recv_sem=far_recv.at[k], device_id=far(k), device_id_type=MESH,
        )

    for k in range(1, planes):
        near_copy(k).start()
    own.wait()
    for k in range(1, planes):
        near_copy(k).wait()
    for k in range(1, dps):
        far_copy(k).start()
    for k in range(1, dps):
        far_copy(k).wait()


def gather_anchors(values):
    dps = lax.axis_size("dp")
    planes = lax.axis_size("span") * lax.axis_size("tensor")
    dma = pltpu.SemaphoreType.DMA
    vmem = pl.BlockSpec(memory_space=pltpu.VMEM)

    def body(*refs):
        anchors_kernel(dps, planes, *refs)

    return pl.pallas_call(
        body,
        name="gather_anchors",
        out_shape=jax.ShapeDtypeStruct((dps, planes) + values.shape, values.dtype),
        in_specs=[vmem],
        out_specs=vmem,
        scratch_shapes=[dma((planes,)), dma((planes,)), dma((dps,)), dma((dps,)), dma],
        compiler_params=pltpu.CompilerParams(collective_id=0, has_side_effects=True),
    )(values)


VECTORS = ("pb", "g0", "g1", "s0", "s1", "sb")
ROWS_PER_CHUNK = 4
CHUNKS_PER_LAYER = 4


def block_order(side, tensor):
    flip_one = tensor + 1 - 2 * lax.rem(tensor, 2)
    flip_two = tensor + 2 - 4 * (tensor // 2)
    swing = side * (flip_two - flip_one)
    return tensor, flip_one + swing, flip_two - swing, TENSORS - 1 - tensor


def remote(src, dst, sems, i, device):
    return pltpu.make_async_remote_copy(
        src_ref=src, dst_ref=dst, send_sem=sems.at[0, i], recv_sem=sems.at[1, i],
        device_id=device, device_id_type=MESH,
    )


class Halving:
    def __init__(self, dps, dp, src, result, scratch, sums, sems):
        self.src, self.result, self.scratch, self.sums, self.sems = src, result, scratch, sums, sems
        self.steps = []
        base, size, bit = 0, dps, 1
        while bit < dps:
            size = size // 2
            up = lax.rem(dp // bit, 2)
            self.steps.append((base + (1 - up) * size, base + up * size, size, {"dp": dp + bit * (1 - 2 * up)}))
            base = base + up * size
            bit *= 2

    def current(self, s):
        return self.src if s == 0 else self.sums

    def down(self, s):
        away, kept, size, partner = self.steps[s]
        room = self.scratch.at[pl.ds(self.steps_room(s), size)]
        return remote(self.current(s).at[pl.ds(away, size)], room, self.sems, s, partner)

    def steps_room(self, s):
        return sum(step[2] for step in self.steps[:s])

    def add(self, s):
        self.down(s).wait()
        away, kept, size, partner = self.steps[s]
        came = self.scratch[pl.ds(self.steps_room(s), size)]
        into = self.result if s == len(self.steps) - 1 else self.sums
        into[pl.ds(kept, size)] = plus(self.current(s)[pl.ds(kept, size)], came)

    def up(self, s):
        away, kept, size, partner = self.steps[s]
        part = self.result.at[pl.ds(kept, size)]
        return remote(part, part, self.sems, len(self.steps) + s, partner)


def last_kernel(dps, planes, ffn_ref, own, rest, rows_ref, blocks, outs, scratch):
    ffn_own, ffn_other, attn_own, attn_other, out_ref = outs
    (
        swapped, main_rest, main_own, across, mine, got_rest, got_own, got_across, got_peer, total_ref,
        ffn_room, attn_room, ffn_sums, attn_sums, x_ref, parts, sums,
        swap_sems, plane_sems, ffn_sems, attn_sems, one_sems, two_sems, three_sems,
    ) = scratch
    dp = lax.axis_index("dp")
    side = lax.axis_index("span")
    tensor = lax.axis_index("tensor")
    me = side * TENSORS + tensor
    order = block_order(side, tensor)
    x_ref[...] = rows_ref[...]
    for l in range(2):
        for j in range(TENSORS):
            for k in range(2):
                columns = blocks[l][k][j].shape[1]
                x_ref[l * CHUNKS_PER_LAYER + k, pl.ds(order[j], 1), :columns] = blocks[l][k][j][...]

    def near_peer(k):
        return lax.rem(me + k, planes)

    def near(k):
        peer = near_peer(k)
        return {"span": peer // TENSORS, "tensor": lax.rem(peer, TENSORS)}

    def far_peer(k):
        return lax.rem(dp + k, dps)

    def far(k):
        return {"dp": far_peer(k)}

    peer_core, main_peer, diag_peer = {"span": 1 - side}, {"tensor": order[1]}, {"tensor": order[2]}
    nears, fars = range(1, planes), range(1, dps)

    barrier = pltpu.get_barrier_semaphore()
    for k in nears:
        pl.semaphore_signal(barrier, inc=1, device_id=near(k), device_id_type=MESH)
    for k in fars:
        pl.semaphore_signal(barrier, inc=1, device_id=far(k), device_id_type=MESH)
    pl.semaphore_wait(barrier, planes + dps - 2)

    swaps = [
        remote(src, swapped.at[i], swap_sems, i, peer_core)
        for i, src in enumerate((own[2], rest[2], rest[3], rest[0]))
    ]
    for copy in swaps:
        copy.start()
    ones = [remote(x_ref.at[near_peer(k)], parts.at[k], one_sems, k, near(k)) for k in nears]
    for copy in ones:
        copy.start()
    ffn_chunks = [
        Halving(dps, dp, ffn_ref.at[c], ffn_own.at[c], ffn_room.at[c], ffn_sums.at[c], ffn_sems.at[c])
        for c in range(ffn_ref.shape[0])
    ]
    attn_chunks = [
        Halving(dps, dp, total_ref.at[c], attn_own.at[c], attn_room.at[c], attn_sums.at[c], attn_sems.at[c])
        for c in range(total_ref.shape[0])
    ]
    stages = range(len(ffn_chunks[0].steps))
    last = len(stages) - 1

    def down_from(chunks, s):
        for chunk in chunks:
            chunk.down(s).start()

    def down_to_end(chunks, s):
        for chunk in chunks:
            chunk.add(s)
            (chunk.down(s + 1) if s < last else chunk.up(last)).start()

    def up_next(chunks, s):
        for chunk in chunks:
            chunk.up(s).wait()
            if s > 0:
                chunk.up(s - 1).start()

    down_from(ffn_chunks, 0)

    for copy in swaps:
        copy.wait()
    across[...] = plus(own[3][...], swapped[2])
    main_rest[...] = plus(rest[1][...], swapped[0])
    send_across = remote(across, got_across, plane_sems, 0, diag_peer)
    send_across.start()
    send_rest = remote(main_rest, got_rest, plane_sems, 1, main_peer)
    send_rest.start()
    mine[...] = plus(own[0][...], swapped[3])
    for copy in ones:
        copy.wait()
    total = x_ref[me]
    for k in nears:
        total = total + parts[k]
    sums[dp] = total
    twos = [remote(sums.at[dp], sums.at[dp], two_sems, k, far(k)) for k in fars]
    for copy in twos:
        copy.start()

    down_to_end(ffn_chunks, 0)
    send_across.wait()
    main_own[...] = plus(own[1][...], swapped[1], got_across[...])
    send_own = remote(main_own, got_own, plane_sems, 2, main_peer)
    send_own.start()
    for s in stages[1:]:
        down_to_end(ffn_chunks, s)
    send_rest.wait()
    send_peer = remote(got_rest, got_peer, swap_sems, 4, peer_core)
    send_peer.start()
    send_peer.wait()
    send_own.wait()
    total_ref[...] = plus(mine[...], got_own[...], got_peer[...])
    down_from(attn_chunks, 0)

    for copy in twos:
        copy.wait()
    total = sums[0]
    for k in fars:
        total = total + sums[k]
    out_ref[me] = total
    threes = [remote(out_ref.at[me], out_ref.at[me], three_sems, k, near(k)) for k in nears]
    for copy in threes:
        copy.start()

    for s in reversed(stages[1:]):
        up_next(ffn_chunks, s)
    for s in stages:
        down_to_end(attn_chunks, s)
    up_next(ffn_chunks, 0)
    swap_ffn = remote(ffn_own, ffn_other, swap_sems, 5, peer_core)
    swap_ffn.start()
    for s in reversed(stages):
        up_next(attn_chunks, s)
    swap_attn = remote(attn_own, attn_other, swap_sems, 6, peer_core)
    swap_attn.start()
    for copy in threes:
        copy.wait()
    swap_ffn.wait()
    swap_attn.wait()


def last_sums(ffn_total, attn_blocks, rows, blocks):
    dps = lax.axis_size("dp")
    planes = lax.axis_size("span") * lax.axis_size("tensor")
    flat, tree = jax.tree.flatten(blocks)

    def by_dp(values):
        rows = values.shape[0]
        chunks = 2 if rows % (32 * dps) == 0 else 1
        return values.reshape(chunks, dps, rows // (chunks * dps), values.shape[1])

    ffn_total = by_dp(ffn_total)
    own = [by_dp(o) for o, r in attn_blocks]
    rest = [by_dp(r) for o, r in attn_blocks]
    dma = pltpu.SemaphoreType.DMA
    vmem = pl.BlockSpec(memory_space=pltpu.VMEM)
    attn, ffn = own[0].shape, ffn_total.shape

    def body(ffn_ref, *refs):
        own_refs, rest_refs, rows_ref = refs[:TENSORS], refs[TENSORS : 2 * TENSORS], refs[2 * TENSORS]
        refs = refs[2 * TENSORS + 1 :]
        inputs = jax.tree.unflatten(tree, refs[: len(flat)])
        outs, scratch = refs[len(flat) : len(flat) + 5], refs[len(flat) + 5 :]
        last_kernel(dps, planes, ffn_ref, own_refs, rest_refs, rows_ref, inputs, outs, scratch)

    outs = pl.pallas_call(
        body,
        name="last_sums",
        out_shape=tuple(jax.ShapeDtypeStruct(shape, BF) for shape in (ffn, ffn, attn, attn))
        + (jax.ShapeDtypeStruct(rows.shape, F32),),
        in_specs=[vmem] * (2 + 2 * TENSORS + len(flat)),
        out_specs=(vmem,) * 5,
        scratch_shapes=[pltpu.VMEM((TENSORS,) + attn, BF)]
        + [pltpu.VMEM(attn, BF)] * 9
        + [pltpu.VMEM(ffn, BF), pltpu.VMEM(attn, BF)] * 2
        + [pltpu.VMEM(rows.shape, F32), pltpu.VMEM(rows.shape, F32), pltpu.VMEM((dps,) + rows.shape[1:], F32)]
        + [dma((2, 7)), dma((2, 3))]
        + [dma((ffn[0], 2, dps)), dma((attn[0], 2, dps))]
        + [dma((2, planes)), dma((2, dps)), dma((2, planes))],
        compiler_params=pltpu.CompilerParams(
            collective_id=1, has_side_effects=True, vmem_limit_bytes=36 << 20
        ),
    )(ffn_total, *own, *rest, rows, *flat)
    whole = [o.reshape(-1, o.shape[-1]) for o in outs[:4]]
    return (*whole, outs[4])


def to_rows(values):
    return lax.all_to_all(values, "tensor", split_axis=0, concat_axis=0, tiled=True).reshape(
        -1, values.shape[-1]
    )


def to_places(values):
    blocks = values.reshape(TENSORS, -1, values.shape[-1])
    return lax.all_to_all(blocks, "tensor", split_axis=0, concat_axis=0, tiled=True)


def layer_forward(l, x, seg, attn, ffn, vec, hook):
    xb = x.astype(BF)
    kept = []
    z1 = x + vec["pb"]
    for j in range(TENSORS):
        first, second = attn.blocks[j]
        *saved, z1 = attend_forward(l, vec["cols"], xb, first, second, vec["heads"](j), z1, seg)
        kept.append(saved)
        z1 = hook("attn", j, z1)
    n1, r1 = normal_parts(z1)
    y = n1 * vec["g0"] + vec["s0"]
    yb = y.astype(BF)
    act, slope = [], []
    z2 = y + vec["sb"]
    for j in range(TENSORS):
        first, second = ffn.blocks[j]
        a, b = gelu_parts(mm(yb, first, 1, 0) + vec["eb"](j))
        act.append(a.astype(BF))
        slope.append(b.astype(BF))
        z2 = z2 + mm(act[-1], second, 1, 0)
        z2 = hook("ffn", j, z2)
    n2, r2 = normal_parts(z2)
    out = n2 * vec["g1"] + vec["s1"]
    return out, (xb, kept, n1, r1, yb, act, slope, n2, r2)


def total_rows(values):
    return jnp.sum(values, axis=0)


def ffn_backward(dout, ffn_w, vec, kept, hook, cut):
    xb, saved, n1, r1, yb, act, slope, n2, r2 = kept
    dz2 = normal_back(dout, n2, r2, vec["g1"])
    small = {"g1": total_rows(dout * n2), "s1": total_rows(dout), "sb": total_rows(dz2), "eb": []}
    dz2 = hook("seeded", dz2)
    dzb = dz2.astype(BF)
    dy = dz2
    blocks = []
    for lo, hi in ((0, cut), (cut, TENSORS)):
        if lo == hi:
            continue
        parts = [(act[j], slope[j], *ffn_w[j]) for j in range(lo, hi)]
        dy, sums, grads = ffn_blocks_backward(dzb, yb, dy, parts)
        small["eb"] += sums
        blocks += grads
        if hi < TENSORS:
            dzb, dy = hook("three", (dzb, dy))
    return dy, blocks, small


def attn_backward(dy, seg, attn_w, vec, kept, hook):
    xb, saved, n1, r1, yb, act, slope, n2, r2 = kept
    dz1 = normal_back(dy, n1, r1, vec["g0"])
    small = {"g0": total_rows(dy * n1), "s0": total_rows(dy), "pb": total_rows(dz1), "heads": []}
    dz1 = hook("normed", dz1)
    da = dz1.astype(BF)
    dx = dz1
    blocks = []
    for lo, hi in ((0, TENSORS - 1), (TENSORS - 1, TENSORS)):
        parts = [(*attn_w[j], *saved[j]) for j in range(lo, hi)]
        dx, sums, grads = attend_blocks_backward(vec["cols"], da, xb, dx, parts, seg)
        small["heads"] += sums
        blocks += grads
        if lo == 0:
            da, dx = hook("three", (da, dx))
    return dx, blocks, small


def attn_unpack(first, second):
    cols = first.shape[0] // 2
    heads = jnp.stack([first[:cols], first[cols:], second[:cols]])
    return jnp.swapaxes(heads, 1, 2), second[cols:]


class Reduction:
    def start(self, value, blocks):
        self.blocks = blocks
        value, *self.outgoing = tie(value, *reduce_outgoing(blocks))
        return value

    def swapped(self, value):
        value, self.main_rest, self.main_own, self.across, self.mine = tie(
            value, *reduce_swapped(self.blocks, self.outgoing)
        )
        self.from_rest = send(self.main_rest, MAIN)
        return value

    def crossed(self, value):
        value, self.main_own = tie(value, reduce_across(self.main_own, self.across))
        self.from_own = send(self.main_own, MAIN)
        self.from_peer = send(self.from_rest, SWAP)
        return value

    def summed(self, value):
        value, self.total = tie(value, plus(self.mine, self.from_own, self.from_peer))
        return value


def shards(
    layer_input, skip_tokens, backbone_cotangent, head_cotangent, segment_lengths, pair_index,
    w_heads, heads_bias, w_project, project_bias, norm_gain, norm_shift,
    w_expand, expand_bias, w_shrink, shrink_bias,
):
    side = lax.axis_index("span")
    mine = lax.axis_index("tensor")
    width = layer_input.shape[-1]
    head_cols = w_heads.shape[-1]
    ff_cols = w_expand.shape[-1]

    extra = 16
    bias_rows = jnp.concatenate([heads_bias.reshape(1, 4 * head_cols), expand_bias], axis=0)
    bias_rows = jnp.pad(bias_rows, ((0, extra - bias_rows.shape[0]), (0, 0)))

    def attn_rows(l):
        heads = jnp.swapaxes(w_heads[l], 1, 2)
        first = heads[:2].reshape(2 * head_cols, width)
        return first, jnp.concatenate([heads[2], w_project[l]], axis=0)

    first, second = attn_rows(0)
    first = jnp.concatenate([first, bias_rows], axis=0)
    second = jnp.pad(second, ((0, extra), (0, 0)))
    gather_attn0, gather_ffn0, gather_attn1, gather_ffn1 = (Gathering(side) for _ in range(4))
    x = to_rows(layer_input[0])
    mark = gather_attn0.start(layer_input[0, 0, 0], first, second)
    mark = gather_ffn0.start(mark, w_expand[0], w_shrink[0])
    later = {}

    def during_forward0(kind, j, value):
        if kind == "attn":
            if j == 0:
                value = gather_attn0.arrived(value)
            if j == 1:
                value = gather_attn1.start(value, *attn_rows(1))
            if j == 2:
                value = gather_attn0.crossed(value)
            if j == 3:
                value = gather_ffn0.arrived(value)
                value = gather_ffn1.start(value, w_expand[1], w_shrink[1])
        else:
            if j == 0:
                skip, value = tie(skip_tokens[0], value)
                later["skip"] = to_rows(skip)
            if j == 1:
                value = gather_attn1.arrived(value)
            if j == 2:
                value = gather_ffn0.crossed(value)
        return value

    def during_forward1(kind, j, value):
        if kind == "attn":
            if j == 0:
                head_cot, value = tie(head_cotangent[0], value)
                later["head"] = to_rows(head_cot)
            if j == 1:
                value = gather_attn1.crossed(value)
            if j == 2:
                value, mark = tie(value, later["backbone_out"])
            if j == 3:
                value = gather_ffn1.arrived(value)
        else:
            if j == 0:
                backbone_cot, value = tie(backbone_cotangent[0], value)
                later["backbone"] = to_rows(backbone_cot)
            if j == 2:
                value = gather_ffn1.crossed(value)
        return value

    tokens = x.shape[0]

    def bias_row(j, i):
        first, second = gather_attn0.blocks[j]
        return first[2 * head_cols + i : 2 * head_cols + i + 1].astype(F32)

    def vectors(l):
        return {
            "cols": head_cols, "heads": lambda j: bias_row(j, 0),
            "eb": lambda j: bias_row(j, 1 + l), "pb": project_bias[l].astype(F32),
            "g0": norm_gain[l, 0].astype(F32), "g1": norm_gain[l, 1].astype(F32),
            "s0": norm_shift[l, 0].astype(F32), "s1": norm_shift[l, 1].astype(F32),
            "sb": shrink_bias[l].astype(F32),
        }

    lengths = lax.dynamic_index_in_dim(segment_lengths[0], mine, 0, keepdims=False)
    span_count = lengths.shape[0]
    starts = jnp.cumsum(lengths) - lengths
    row_length = jnp.sum(lengths)
    places = jnp.arange(tokens, dtype=jnp.int32)
    counted = jnp.sum((places[:, None] >= starts[None, :]).astype(jnp.int32), axis=-1) - 1
    segment = jnp.where(places < row_length, counted, span_count)
    seg = (segment[:, None], segment[None, :])
    valid = (places < row_length).astype(F32)[:, None]
    picker = (starts[:, None] == places[None, :]).astype(F32)
    first_place = jnp.sum(picker, axis=0)[:, None] > 0

    vec0, vec1 = vectors(0), vectors(1)
    backbone, kept0 = layer_forward(0, x.astype(F32), seg, gather_attn0, gather_ffn0, vec0, during_forward0)
    attn_w0, ffn_w0 = gather_attn0.blocks, gather_ffn0.blocks
    later["backbone_out"] = to_places((backbone * valid).astype(BF))
    cls = mm(picker.astype(BF), backbone.astype(BF), 1, 0).astype(BF)
    anchors = gather_anchors(cls)
    dp_count = lax.axis_size("dp")
    pair_count = lax.axis_size("span")
    vector_count = dp_count * TENSORS * span_count
    anchors = anchors.reshape(dp_count, pair_count, TENSORS * span_count, width)
    anchors = jnp.swapaxes(anchors, 0, 1).reshape(pair_count, vector_count, width)

    head_in = jnp.where(first_place, backbone, later["skip"].astype(F32))
    head, kept1 = layer_forward(1, head_in, seg, gather_attn1, gather_ffn1, vec1, during_forward1)
    attn_w1, ffn_w1 = gather_attn1.blocks, gather_ffn1.blocks
    head_cot, backbone_cot = later["head"], later["backbone"]
    head_out = to_places((head * valid).astype(BF))

    root = math.sqrt(width)
    logits = mm(anchors[0], anchors[1], 1, 1) / root
    columns = jnp.arange(vector_count, dtype=jnp.int32)
    target = (pair_index[:, None] == columns[None, :]).astype(F32)
    lse_rows = jax.nn.logsumexp(logits, axis=1)
    lse_cols = jax.nn.logsumexp(logits, axis=0)
    dlogits = LOSS_WEIGHT * (
        jnp.exp(logits - lse_rows[:, None]) + jnp.exp(logits - lse_cols[None, :]) - 2.0 * target
    )
    span_loss = (jnp.sum(lse_rows) + jnp.sum(lse_cols) - 2.0 * jnp.sum(target * logits)) / (
        2 * vector_count
    )
    own = (lax.axis_index("dp") * TENSORS + mine) * span_count
    wanted = jnp.where(side == 0, dlogits, dlogits.T)
    wanted = lax.dynamic_slice(wanted, (own, 0), (span_count, vector_count))
    other = lax.dynamic_index_in_dim(anchors, 1 - side, 0, keepdims=False).astype(F32)
    dcls = jnp.dot(wanted, other, precision=HIGHEST) / root

    def plain(name, value):
        return value

    ffn1, attn1, ffn0 = (Reduction() for _ in range(3))

    dy, blocks, small1 = ffn_backward(head_cot.astype(F32) * valid, ffn_w1, vec1, kept1, plain, 0)
    dy, mark = tie(dy, head_out)
    dy = ffn1.start(dy, blocks)

    def during_attn1(name, value):
        if name == "normed":
            return ffn1.swapped(value)
        return ffn1.crossed(value)

    du, blocks, more = attn_backward(dy, seg, attn_w1, vec1, kept1, during_attn1)
    small1.update(more)
    du = attn1.start(du, blocks)
    du = ffn1.summed(du)
    ffn_total1 = lax.psum(ffn1.total, "dp")
    grad_skip = to_places(jnp.where(first_place, 0.0, du).astype(BF))

    seed = backbone_cot.astype(F32) * valid + jnp.where(first_place, du, 0.0)
    seed = seed + jnp.dot(picker.T, dcls, precision=HIGHEST)

    def during_ffn0(name, value):
        if name == "seeded":
            return attn1.swapped(value)
        return attn1.crossed(value)

    dy, blocks, small0 = ffn_backward(seed, ffn_w0, vec0, kept0, during_ffn0, 2)
    dy, mark = tie(dy, grad_skip)
    dy = ffn0.start(dy, blocks)
    dy = attn1.summed(dy)

    dy, ffn_total1, late = tie(dy, ffn_total1, attn1.total)
    attn_total1 = lax.psum(late, "dp")
    finished = {}

    def during_attn0(name, value):
        if name == "normed":
            return ffn0.swapped(value)
        value = ffn0.crossed(value)
        value, finished["attn"] = tie(value, attn_total1)
        return value

    dx, attn_blocks, more = attn_backward(dy, seg, attn_w0, vec0, kept0, during_attn0)
    small0.update(more)
    attn_total1 = finished["attn"]
    grad_input = to_places(dx.astype(BF))

    place = lax.broadcasted_iota(jnp.int32, (2 * CHUNKS_PER_LAYER * ROWS_PER_CHUNK, 1), 0)
    rows = jnp.zeros((place.shape[0], width), F32)
    for l, small in enumerate((small0, small1)):
        base = l * CHUNKS_PER_LAYER * ROWS_PER_CHUNK
        for i, k in enumerate(VECTORS):
            rows = rows + jnp.where(place == base + 2 * ROWS_PER_CHUNK + i, small[k][None], 0.0)
    rows = ffn0.summed(rows.reshape(2 * CHUNKS_PER_LAYER, ROWS_PER_CHUNK, width))
    ffn_total1, attn_total1 = tie(ffn_total1, attn_total1)
    other_ffn1, other_attn1 = send(ffn_total1, SWAP), send(attn_total1, SWAP)
    rows, other_ffn1, other_attn1 = tie(rows, other_ffn1, other_attn1)
    ffn_own, ffn_other, attn_own, attn_other, total = last_sums(
        ffn0.total, attn_blocks, rows, [(small["eb"], small["heads"]) for small in (small0, small1)]
    )

    hb, eb, vector_sums = [], [], []
    for l in range(2):
        base = l * CHUNKS_PER_LAYER
        own = lax.dynamic_slice(total[base : base + 2], (0, mine, 0), (2, 1, width))[:, 0]
        eb.append(own[0])
        hb.append(jnp.stack([own[1, :head_cols], own[1, head_cols : 2 * head_cols]]))
        rows = total[base + 2 : base + CHUNKS_PER_LAYER].reshape(-1, width)
        vector_sums.append({k: rows[i] for i, k in enumerate(VECTORS)})
    sums = vector_sums

    ge1, gs1 = in_order(side, ffn_total1, other_ffn1)
    gh1, gp1 = attn_unpack(*in_order(side, attn_total1, other_attn1))
    ge0, gs0 = in_order(side, ffn_own, ffn_other)
    gh0, gp0 = attn_unpack(*in_order(side, attn_own, attn_other))

    return (
        later["backbone_out"][None],
        head_out[None],
        span_loss,
        grad_input[None],
        grad_skip[None],
        jnp.stack([gh0, gh1]),
        jnp.stack(hb),
        jnp.stack([gp0, gp1]),
        jnp.stack([s["pb"] for s in sums]),
        jnp.stack([jnp.stack([s["g0"], s["g1"]]) for s in sums]),
        jnp.stack([jnp.stack([s["s0"], s["s1"]]) for s in sums]),
        jnp.stack([ge0, ge1]),
        jnp.stack(eb),
        jnp.stack([gs0, gs1]),
        jnp.stack([s["sb"] for s in sums]),
    )


def solution(mesh):
    rows = P("span", "dp", "tensor", None)
    in_specs = (
        rows, rows, rows, rows, P("span", "dp", None), P(),
        P(None, None, None, "tensor"), P(None, None, "tensor"), P(None, "tensor", None),
        P(), P(), P(), P(None, None, "tensor"), P(None, "tensor"), P(None, "tensor", None), P(),
    )
    out_specs = (
        rows, rows, P(), rows, rows,
        P(None, None, None, "tensor"), P(None, None, "tensor"), P(None, "tensor", None),
        P(), P(), P(), P(None, None, "tensor"), P(None, "tensor"), P(None, "tensor", None), P(),
    )
    return jax.shard_map(shards, mesh=mesh, in_specs=in_specs, out_specs=out_specs, check_vma=False)
```

```python
import math

import jax
import jax.numpy as jnp
from jax import lax
from jax.experimental import pallas as pl
from jax.experimental.pallas import tpu as pltpu
from jax.sharding import PartitionSpec as P

HEAD_DIM = 64
EPSILON = 1e-12
LOSS_WEIGHT = 8.0
HIGHEST = lax.Precision.HIGHEST
MASKED = -1e30
BF = jnp.bfloat16
F32 = jnp.float32
PLANE = ("span", "tensor")
MESH = pl.DeviceIdType.MESH
TENSORS = 4
MAIN, DIAG, SWAP = "main", "diag", "swap"


def mm(a, b, ca, cb):
    return lax.dot_general(a, b, (((ca,), (cb,)), ((), ())), preferred_element_type=F32)


def normal_parts(values):
    centred = values - jnp.mean(values, axis=-1, keepdims=True)
    spread = jnp.mean(centred * centred, axis=-1, keepdims=True)
    scale = lax.rsqrt(spread + EPSILON)
    return centred * scale, scale


def normal_back(upward, normed, scale, gain):
    weighted = upward * gain
    first = jnp.mean(weighted, axis=-1, keepdims=True)
    second = jnp.mean(weighted * normed, axis=-1, keepdims=True)
    return (weighted - first - normed * second) * scale


def gelu_parts(hidden):
    phi = 0.5 * (1.0 + lax.erf(hidden * math.sqrt(0.5)))
    slope = phi + hidden * jnp.exp(-0.5 * hidden * hidden) * (1.0 / math.sqrt(2.0 * math.pi))
    return hidden * phi, slope


def plane_pairs(kind):
    pairs = []
    for side in range(2):
        for t in range(TENSORS):
            if kind == SWAP:
                target = (1 - side, t)
            elif kind == MAIN:
                target = (side, t ^ (1 + side))
            else:
                target = (side, t ^ (2 - side))
            pairs.append((side * TENSORS + t, target[0] * TENSORS + target[1]))
    return pairs


def send(values, kind):
    return lax.ppermute(values, PLANE, plane_pairs(kind))


def plus(*terms):
    total = terms[0].astype(F32)
    for term in terms[1:]:
        total = total + term.astype(F32)
    return total.astype(BF)


def pick(side, zero, one):
    return jnp.where(side == 0, zero, one)


def tie(*values):
    return lax.optimization_barrier(values)


class Gathering:
    def __init__(self, side):
        self.side = side

    def start(self, value, first, second):
        value, first, second = tie(value, first, second)
        self.got = (send(first, MAIN), send(second, MAIN))
        self.blocks = [(first, second)]
        return value

    def arrived(self, value):
        value, *got = tie(value, *self.got)
        self.across = send(pick(self.side, *got), DIAG)
        self.blocks += [tuple(got), tuple(send(g, SWAP) for g in got)]
        return value

    def crossed(self, value):
        value, across = tie(value, self.across)
        rest = send(across, SWAP)
        self.blocks.append((pick(self.side, across, rest), pick(self.side, rest, across)))
        return value


def reduce_outgoing(blocks):
    return blocks[2][0], blocks[2][1], blocks[3][1], blocks[0][1]


def reduce_swapped(blocks, outgoing):
    got = [send(o, SWAP) for o in outgoing]
    return (
        plus(blocks[1][1], got[0]), plus(blocks[1][0], got[1]), plus(blocks[3][0], got[2]), plus(blocks[0][0], got[3])
    )


def reduce_across(main_own, across):
    return plus(main_own, send(across, DIAG))


def in_order(side, own, other):
    return pick(side, own, other).astype(F32), pick(side, other, own).astype(F32)


Q_ROWS = 128
DATA_ROWS = 512
GRAD_ROWS = 768


def attend_forward_kernel(
    layer, x_ref, first_ref, second_ref, bias_ref, z_ref, down_ref, across_ref,
    q_ref, k_ref, v_ref, o_ref, lse_ref, out_ref
):
    tokens, width = q_ref.shape
    at = 2 * layer * width
    x = x_ref[...]
    q_ref[...] = (mm(x, first_ref[:width, :], 1, 1) + bias_ref[:, at : at + width]).astype(BF)
    k_ref[...] = mm(x, first_ref[width : 2 * width, :], 1, 1).astype(BF)
    v_ref[...] = (mm(x, second_ref[:width, :], 1, 1) + bias_ref[:, at + width : at + 2 * width]).astype(BF)

    def step(i, carry):
        rows = pl.ds(pl.multiple_of(i * Q_ROWS, Q_ROWS), Q_ROWS)
        same = down_ref[rows, :] == across_ref[...]
        for h in range(width // HEAD_DIM):
            head = slice(h * HEAD_DIM, (h + 1) * HEAD_DIM)
            s = mm(q_ref[rows, head], k_ref[:, head], 1, 1) * 0.125
            s = jnp.where(same, s, MASKED)
            top = jnp.max(s, axis=-1, keepdims=True)
            raised = jnp.exp(s - top)
            total = jnp.sum(raised, axis=-1, keepdims=True)
            weights = (raised * (1.0 / total)).astype(BF)
            o_ref[rows, head] = mm(weights, v_ref[:, head], 1, 0).astype(BF)
            lse_ref[rows, h : h + 1] = top + jnp.log(total)
        out_ref[rows, :] = z_ref[rows, :] + mm(o_ref[rows, :], second_ref[width : 2 * width, :], 1, 0)
        return carry

    lax.fori_loop(0, tokens // Q_ROWS, step, 0)


def attend_backward_kernel(
    da_ref, x_ref, first_ref, second_ref, q_ref, k_ref, v_ref, o_ref, lse_ref, dx_ref, down_ref, across_ref,
    own_ref, rest_ref, sums_ref, out_ref, do_ref, dq_ref, dk_ref, dv_ref
):
    tokens, width = q_ref.shape
    da = da_ref[...]
    do_ref[...] = mm(da, second_ref[width : 2 * width, :], 1, 1).astype(BF)
    dk_ref[...] = jnp.zeros_like(dk_ref)
    dv_ref[...] = jnp.zeros_like(dv_ref)

    def step(i, carry):
        rows = pl.ds(pl.multiple_of(i * Q_ROWS, Q_ROWS), Q_ROWS)
        same = down_ref[rows, :] == across_ref[...]
        for h in range(width // HEAD_DIM):
            head = slice(h * HEAD_DIM, (h + 1) * HEAD_DIM)
            q, k, up = q_ref[rows, head], k_ref[:, head], do_ref[rows, head]
            s = mm(q, k, 1, 1) * 0.125
            s = jnp.where(same, s, MASKED)
            pr = jnp.exp(s - lse_ref[rows, h : h + 1])
            dp = mm(up, v_ref[:, head], 1, 1)
            inner = jnp.sum(pr * dp, axis=-1, keepdims=True)
            ds = (pr * (dp - inner)).astype(BF)
            dq_ref[rows, head] = (mm(ds, k, 1, 0) * 0.125).astype(BF)
            dk_ref[:, head] += mm(ds, q, 0, 0)
            dv_ref[:, head] += mm(pr.astype(BF), up, 0, 0)
        return carry

    lax.fori_loop(0, tokens // Q_ROWS, step, 0)
    x = x_ref[...]
    dq = dq_ref[...]
    dk = (dk_ref[...] * 0.125).astype(BF)
    dv = dv_ref[...].astype(BF)
    out_ref[...] = (
        dx_ref[...]
        + mm(dq, first_ref[:width, :], 1, 0)
        + mm(dk, first_ref[width : 2 * width, :], 1, 0)
        + mm(dv, second_ref[:width, :], 1, 0)
    )
    side = lax.axis_index("span")
    store_both(
        side, own_ref, rest_ref, slice(0, width), mm(dq, x, 0, 0).astype(BF), mm(dv, x, 0, 0).astype(BF)
    )
    store_both(
        side, own_ref, rest_ref, slice(width, 2 * width),
        mm(dk, x, 0, 0).astype(BF), mm(o_ref[...], da, 0, 0).astype(BF),
    )
    sums_ref[:, :width] = jnp.sum(dq.astype(F32), axis=0, keepdims=True)
    sums_ref[:, width:] = jnp.sum(dv.astype(F32), axis=0, keepdims=True)


def small_cost():
    return pl.CostEstimate(flops=1 << 20, bytes_accessed=1 << 10, transcendentals=0)


def kernel_params():
    return pltpu.CompilerParams(vmem_limit_bytes=24 << 20)


def store_both(side, own_ref, rest_ref, rows, first, second):
    @pl.when(side == 0)
    def _():
        own_ref[rows, :] = first
        rest_ref[rows, :] = second

    @pl.when(side != 0)
    def _():
        own_ref[rows, :] = second
        rest_ref[rows, :] = first


def ffn_backward_kernel(
    dz_ref, y_ref, act_ref, slope_ref, first_ref, second_ref, dy_ref, own_ref, rest_ref, sums_ref, out_ref, dh_ref
):
    tokens, model = dz_ref.shape
    side = lax.axis_index("span")
    sums_ref[...] = jnp.zeros_like(sums_ref)

    def data(i, carry):
        rows = pl.ds(pl.multiple_of(i * DATA_ROWS, DATA_ROWS), DATA_ROWS)
        dhid = mm(dz_ref[rows, :], second_ref[...], 1, 1) * slope_ref[rows, :].astype(F32)
        sums_ref[...] += jnp.sum(dhid, axis=0, keepdims=True)
        dhb = dhid.astype(BF)
        dh_ref[rows, :] = dhb
        out_ref[rows, :] = dy_ref[rows, :] + mm(dhb, first_ref[...], 1, 1)
        return carry

    def weights(i, carry):
        rows = pl.ds(pl.multiple_of(i * GRAD_ROWS, GRAD_ROWS), GRAD_ROWS)
        first = mm(y_ref[:, rows], dh_ref[...], 0, 0).astype(BF)
        second = mm(act_ref[:, rows], dz_ref[...], 0, 0).astype(BF)
        store_both(side, own_ref, rest_ref, rows, first, second)
        return carry

    lax.fori_loop(0, tokens // DATA_ROWS, data, 0)
    lax.fori_loop(0, model // GRAD_ROWS, weights, 0)


def streamed_blocks(name, body, shared, total, blocks, big, small, scratch):
    count, takes, gives = len(blocks), len(blocks[0]), len(big)
    vmem, anywhere = pl.BlockSpec(memory_space=pltpu.VMEM), pl.BlockSpec(memory_space=pl.ANY)
    dma = pltpu.SemaphoreType.DMA

    def kernel(*refs):
        refs = list(refs)

        def take(n):
            taken = refs[:n]
            del refs[:n]
            return taken

        shared_refs, (total_ref,), ins = take(len(shared)), take(1), take(count * takes)
        (out_ref,), smalls, outs = take(1), take(count), take(count * gives)
        in_bufs, out_bufs, (in_sems, out_sems), extra = take(takes), take(gives), take(2), take(len(scratch))

        def fetch(j):
            return [
                pltpu.make_async_copy(ins[j * takes + i], in_bufs[i].at[j % 2], in_sems.at[j % 2, i])
                for i in range(takes)
            ]

        def put(j):
            return [
                pltpu.make_async_copy(out_bufs[i].at[j % 2], outs[j * gives + i], out_sems.at[j % 2, i])
                for i in range(gives)
            ]

        for copy in fetch(0):
            copy.start()
        for j in range(count):
            if j + 1 < count:
                for copy in fetch(j + 1):
                    copy.start()
            for copy in fetch(j):
                copy.wait()
            if j >= 2:
                for copy in put(j - 2):
                    copy.wait()
            body(
                shared_refs, total_ref if j == 0 else out_ref, [r.at[j % 2] for r in in_bufs],
                [r.at[j % 2] for r in out_bufs], smalls[j], out_ref, extra,
            )
            for copy in put(j):
                copy.start()
        for j in range(max(0, count - 2), count):
            for copy in put(j):
                copy.wait()

    out = pl.pallas_call(
        kernel,
        name=name,
        out_shape=(jax.ShapeDtypeStruct(total.shape, F32),)
        + (jax.ShapeDtypeStruct(small, F32),) * count
        + tuple(jax.ShapeDtypeStruct(shape, BF) for shape in big) * count,
        in_specs=[vmem] * (len(shared) + 1) + [anywhere] * (count * takes),
        out_specs=(vmem,) * (1 + count) + (anywhere,) * (count * gives),
        scratch_shapes=[pltpu.VMEM((2,) + x.shape, x.dtype) for x in blocks[0]]
        + [pltpu.VMEM((2,) + shape, BF) for shape in big]
        + [dma((2, takes)), dma((2, gives))]
        + list(scratch),
        compiler_params=pltpu.CompilerParams(vmem_limit_bytes=63 << 20),
        cost_estimate=small_cost(),
    )(*shared, total, *[x for block in blocks for x in block])
    smalls, bigs = out[1 : 1 + count], out[1 + count :]
    return out[0], smalls, [tuple(bigs[j * gives : (j + 1) * gives]) for j in range(count)]


def ffn_blocks_backward(dzb, yb, dy, blocks):
    def body(shared, total, ins, outs, small, out, extra):
        ffn_backward_kernel(*shared, *ins, total, *outs, small, out, *extra)

    first = blocks[0][2].shape
    act = blocks[0][0].shape
    return streamed_blocks(
        "ffn_backward", body, (dzb, yb), dy, blocks, (first, first), (1, act[1]), [pltpu.VMEM(act, BF)]
    )


def attend_blocks_backward(cols, da, x, dx, blocks, seg):
    tokens, model = x.shape

    def body(shared, total, ins, outs, small, out, extra):
        da_ref, x_ref, down_ref, across_ref = shared
        attend_backward_kernel(
            da_ref, x_ref, *ins, total, down_ref, across_ref, *outs, small, out, *extra
        )

    grad = (2 * cols, model)
    scratch = [pltpu.VMEM((tokens, cols), kind) for kind in (BF, BF, F32, F32)]
    return streamed_blocks(
        "attend_backward", body, (da, x, *seg), dx, blocks, (grad, grad), (1, 2 * cols), scratch
    )


def attend_forward(layer, cols, x, first, second, bias, z, seg):
    tokens, model = x.shape
    narrow = jax.ShapeDtypeStruct((tokens, cols), BF)

    def body(*refs):
        attend_forward_kernel(layer, *refs)

    return pl.pallas_call(
        body,
        name="attend_forward",
        out_shape=(
            narrow, narrow, narrow, narrow,
            jax.ShapeDtypeStruct((tokens, cols // HEAD_DIM), F32),
            jax.ShapeDtypeStruct(z.shape, F32),
        ),
        compiler_params=kernel_params(),
        cost_estimate=small_cost(),
    )(x, first, second, bias, z, *seg)


def anchors_kernel(dps, planes, x_ref, out_ref, near_send, near_recv, far_send, far_recv, own_sem):
    dp = lax.axis_index("dp")
    me = lax.axis_index("span") * TENSORS + lax.axis_index("tensor")

    def near(k):
        peer = lax.rem(me + k, planes)
        return {"span": peer // TENSORS, "tensor": lax.rem(peer, TENSORS)}

    def far(k):
        return {"dp": lax.rem(dp + k, dps)}

    barrier = pltpu.get_barrier_semaphore()
    for k in range(1, planes):
        pl.semaphore_signal(barrier, inc=1, device_id=near(k), device_id_type=MESH)
    for k in range(1, dps):
        pl.semaphore_signal(barrier, inc=1, device_id=far(k), device_id_type=MESH)
    pl.semaphore_wait(barrier, planes + dps - 2)

    own = pltpu.make_async_copy(x_ref, out_ref.at[dp, me], own_sem)
    own.start()

    def near_copy(k):
        return pltpu.make_async_remote_copy(
            src_ref=x_ref, dst_ref=out_ref.at[dp, me], send_sem=near_send.at[k],
            recv_sem=near_recv.at[k], device_id=near(k), device_id_type=MESH,
        )

    def far_copy(k):
        return pltpu.make_async_remote_copy(
            src_ref=out_ref.at[dp], dst_ref=out_ref.at[dp], send_sem=far_send.at[k],
            recv_sem=far_recv.at[k], device_id=far(k), device_id_type=MESH,
        )

    for k in range(1, planes):
        near_copy(k).start()
    own.wait()
    for k in range(1, planes):
        near_copy(k).wait()
    for k in range(1, dps):
        far_copy(k).start()
    for k in range(1, dps):
        far_copy(k).wait()


def gather_anchors(values):
    dps = lax.axis_size("dp")
    planes = lax.axis_size("span") * lax.axis_size("tensor")
    dma = pltpu.SemaphoreType.DMA
    vmem = pl.BlockSpec(memory_space=pltpu.VMEM)

    def body(*refs):
        anchors_kernel(dps, planes, *refs)

    return pl.pallas_call(
        body,
        name="gather_anchors",
        out_shape=jax.ShapeDtypeStruct((dps, planes) + values.shape, values.dtype),
        in_specs=[vmem],
        out_specs=vmem,
        scratch_shapes=[dma((planes,)), dma((planes,)), dma((dps,)), dma((dps,)), dma],
        compiler_params=pltpu.CompilerParams(collective_id=0, has_side_effects=True),
    )(values)


VECTORS = ("pb", "g0", "g1", "s0", "s1", "sb")
ROWS_PER_CHUNK = 4
CHUNKS_PER_LAYER = 4


def block_order(side, tensor):
    flip_one = tensor + 1 - 2 * lax.rem(tensor, 2)
    flip_two = tensor + 2 - 4 * (tensor // 2)
    swing = side * (flip_two - flip_one)
    return tensor, flip_one + swing, flip_two - swing, TENSORS - 1 - tensor


def remote(src, dst, sems, i, device):
    return pltpu.make_async_remote_copy(
        src_ref=src, dst_ref=dst, send_sem=sems.at[0, i], recv_sem=sems.at[1, i],
        device_id=device, device_id_type=MESH,
    )


class Halving:
    def __init__(self, dps, dp, src, result, scratch, sums, sems):
        self.src, self.result, self.scratch, self.sums, self.sems = src, result, scratch, sums, sems
        self.steps = []
        base, size, bit = 0, dps, 1
        while bit < dps:
            size = size // 2
            up = lax.rem(dp // bit, 2)
            self.steps.append((base + (1 - up) * size, base + up * size, size, {"dp": dp + bit * (1 - 2 * up)}))
            base = base + up * size
            bit *= 2

    def current(self, s):
        return self.src if s == 0 else self.sums

    def down(self, s):
        away, kept, size, partner = self.steps[s]
        room = self.scratch.at[pl.ds(self.steps_room(s), size)]
        return remote(self.current(s).at[pl.ds(away, size)], room, self.sems, s, partner)

    def steps_room(self, s):
        return sum(step[2] for step in self.steps[:s])

    def add(self, s):
        self.down(s).wait()
        away, kept, size, partner = self.steps[s]
        came = self.scratch[pl.ds(self.steps_room(s), size)]
        into = self.result if s == len(self.steps) - 1 else self.sums
        into[pl.ds(kept, size)] = plus(self.current(s)[pl.ds(kept, size)], came)

    def up(self, s):
        away, kept, size, partner = self.steps[s]
        part = self.result.at[pl.ds(kept, size)]
        return remote(part, part, self.sems, len(self.steps) + s, partner)


def last_kernel(dps, planes, ffn_ref, own, rest, rows_ref, blocks, outs, scratch):
    ffn_own, ffn_other, attn_own, attn_other, out_ref = outs
    (
        swapped, main_rest, main_own, across, mine, got_rest, got_own, got_across, got_peer, total_ref,
        ffn_room, attn_room, ffn_sums, attn_sums, x_ref, parts, sums,
        swap_sems, plane_sems, ffn_sems, attn_sems, one_sems, two_sems, three_sems,
    ) = scratch
    dp = lax.axis_index("dp")
    side = lax.axis_index("span")
    tensor = lax.axis_index("tensor")
    me = side * TENSORS + tensor
    order = block_order(side, tensor)
    x_ref[...] = rows_ref[...]
    for l in range(2):
        for j in range(TENSORS):
            for k in range(2):
                columns = blocks[l][k][j].shape[1]
                x_ref[l * CHUNKS_PER_LAYER + k, pl.ds(order[j], 1), :columns] = blocks[l][k][j][...]

    def near_peer(k):
        return lax.rem(me + k, planes)

    def near(k):
        peer = near_peer(k)
        return {"span": peer // TENSORS, "tensor": lax.rem(peer, TENSORS)}

    def far_peer(k):
        return lax.rem(dp + k, dps)

    def far(k):
        return {"dp": far_peer(k)}

    peer_core, main_peer, diag_peer = {"span": 1 - side}, {"tensor": order[1]}, {"tensor": order[2]}
    nears, fars = range(1, planes), range(1, dps)

    barrier = pltpu.get_barrier_semaphore()
    for k in nears:
        pl.semaphore_signal(barrier, inc=1, device_id=near(k), device_id_type=MESH)
    for k in fars:
        pl.semaphore_signal(barrier, inc=1, device_id=far(k), device_id_type=MESH)
    pl.semaphore_wait(barrier, planes + dps - 2)

    swaps = [
        remote(src, swapped.at[i], swap_sems, i, peer_core)
        for i, src in enumerate((own[2], rest[2], rest[3], rest[0]))
    ]
    for copy in swaps:
        copy.start()
    ones = [remote(x_ref.at[near_peer(k)], parts.at[k], one_sems, k, near(k)) for k in nears]
    for copy in ones:
        copy.start()
    ffn_chunks = [
        Halving(dps, dp, ffn_ref.at[c], ffn_own.at[c], ffn_room.at[c], ffn_sums.at[c], ffn_sems.at[c])
        for c in range(ffn_ref.shape[0])
    ]
    attn_chunks = [
        Halving(dps, dp, total_ref.at[c], attn_own.at[c], attn_room.at[c], attn_sums.at[c], attn_sems.at[c])
        for c in range(total_ref.shape[0])
    ]
    stages = range(len(ffn_chunks[0].steps))
    last = len(stages) - 1

    def down_from(chunks, s):
        for chunk in chunks:
            chunk.down(s).start()

    def down_to_end(chunks, s):
        for chunk in chunks:
            chunk.add(s)
            (chunk.down(s + 1) if s < last else chunk.up(last)).start()

    def up_next(chunks, s):
        for chunk in chunks:
            chunk.up(s).wait()
            if s > 0:
                chunk.up(s - 1).start()

    down_from(ffn_chunks, 0)

    for copy in swaps:
        copy.wait()
    across[...] = plus(own[3][...], swapped[2])
    main_rest[...] = plus(rest[1][...], swapped[0])
    send_across = remote(across, got_across, plane_sems, 0, diag_peer)
    send_across.start()
    send_rest = remote(main_rest, got_rest, plane_sems, 1, main_peer)
    send_rest.start()
    mine[...] = plus(own[0][...], swapped[3])
    for copy in ones:
        copy.wait()
    total = x_ref[me]
    for k in nears:
        total = total + parts[k]
    sums[dp] = total
    twos = [remote(sums.at[dp], sums.at[dp], two_sems, k, far(k)) for k in fars]
    for copy in twos:
        copy.start()

    down_to_end(ffn_chunks, 0)
    send_across.wait()
    main_own[...] = plus(own[1][...], swapped[1], got_across[...])
    send_own = remote(main_own, got_own, plane_sems, 2, main_peer)
    send_own.start()
    for s in stages[1:]:
        down_to_end(ffn_chunks, s)
    send_rest.wait()
    send_peer = remote(got_rest, got_peer, swap_sems, 4, peer_core)
    send_peer.start()
    send_peer.wait()
    send_own.wait()
    total_ref[...] = plus(mine[...], got_own[...], got_peer[...])
    down_from(attn_chunks, 0)

    for copy in twos:
        copy.wait()
    total = sums[0]
    for k in fars:
        total = total + sums[k]
    out_ref[me] = total
    threes = [remote(out_ref.at[me], out_ref.at[me], three_sems, k, near(k)) for k in nears]
    for copy in threes:
        copy.start()

    for s in reversed(stages[1:]):
        up_next(ffn_chunks, s)
    for s in stages:
        down_to_end(attn_chunks, s)
    up_next(ffn_chunks, 0)
    swap_ffn = remote(ffn_own, ffn_other, swap_sems, 5, peer_core)
    swap_ffn.start()
    for s in reversed(stages):
        up_next(attn_chunks, s)
    swap_attn = remote(attn_own, attn_other, swap_sems, 6, peer_core)
    swap_attn.start()
    for copy in threes:
        copy.wait()
    swap_ffn.wait()
    swap_attn.wait()


def last_sums(ffn_total, attn_blocks, rows, blocks):
    dps = lax.axis_size("dp")
    planes = lax.axis_size("span") * lax.axis_size("tensor")
    flat, tree = jax.tree.flatten(blocks)

    def by_dp(values):
        rows = values.shape[0]
        chunks = 2 if rows % (32 * dps) == 0 else 1
        return values.reshape(chunks, dps, rows // (chunks * dps), values.shape[1])

    ffn_total = by_dp(ffn_total)
    own = [by_dp(o) for o, r in attn_blocks]
    rest = [by_dp(r) for o, r in attn_blocks]
    dma = pltpu.SemaphoreType.DMA
    vmem = pl.BlockSpec(memory_space=pltpu.VMEM)
    attn, ffn = own[0].shape, ffn_total.shape

    def body(ffn_ref, *refs):
        own_refs, rest_refs, rows_ref = refs[:TENSORS], refs[TENSORS : 2 * TENSORS], refs[2 * TENSORS]
        refs = refs[2 * TENSORS + 1 :]
        inputs = jax.tree.unflatten(tree, refs[: len(flat)])
        outs, scratch = refs[len(flat) : len(flat) + 5], refs[len(flat) + 5 :]
        last_kernel(dps, planes, ffn_ref, own_refs, rest_refs, rows_ref, inputs, outs, scratch)

    outs = pl.pallas_call(
        body,
        name="last_sums",
        out_shape=tuple(jax.ShapeDtypeStruct(shape, BF) for shape in (ffn, ffn, attn, attn))
        + (jax.ShapeDtypeStruct(rows.shape, F32),),
        in_specs=[vmem] * (2 + 2 * TENSORS + len(flat)),
        out_specs=(vmem,) * 5,
        scratch_shapes=[pltpu.VMEM((TENSORS,) + attn, BF)]
        + [pltpu.VMEM(attn, BF)] * 9
        + [pltpu.VMEM(ffn, BF), pltpu.VMEM(attn, BF)] * 2
        + [pltpu.VMEM(rows.shape, F32), pltpu.VMEM(rows.shape, F32), pltpu.VMEM((dps,) + rows.shape[1:], F32)]
        + [dma((2, 7)), dma((2, 3))]
        + [dma((ffn[0], 2, dps)), dma((attn[0], 2, dps))]
        + [dma((2, planes)), dma((2, dps)), dma((2, planes))],
        compiler_params=pltpu.CompilerParams(
            collective_id=1, has_side_effects=True, vmem_limit_bytes=36 << 20
        ),
    )(ffn_total, *own, *rest, rows, *flat)
    whole = [o.reshape(-1, o.shape[-1]) for o in outs[:4]]
    return (*whole, outs[4])


def to_rows(values):
    return lax.all_to_all(values, "tensor", split_axis=0, concat_axis=0, tiled=True).reshape(
        -1, values.shape[-1]
    )


def to_places(values):
    blocks = values.reshape(TENSORS, -1, values.shape[-1])
    return lax.all_to_all(blocks, "tensor", split_axis=0, concat_axis=0, tiled=True)


def layer_forward(l, x, seg, attn, ffn, vec, hook):
    xb = x.astype(BF)
    kept = []
    z1 = x + vec["pb"]
    for j in range(TENSORS):
        first, second = attn.blocks[j]
        *saved, z1 = attend_forward(l, vec["cols"], xb, first, second, vec["heads"](j), z1, seg)
        kept.append(saved)
        z1 = hook("attn", j, z1)
    n1, r1 = normal_parts(z1)
    y = n1 * vec["g0"] + vec["s0"]
    yb = y.astype(BF)
    act, slope = [], []
    z2 = y + vec["sb"]
    for j in range(TENSORS):
        first, second = ffn.blocks[j]
        a, b = gelu_parts(mm(yb, first, 1, 0) + vec["eb"](j))
        act.append(a.astype(BF))
        slope.append(b.astype(BF))
        z2 = z2 + mm(act[-1], second, 1, 0)
        z2 = hook("ffn", j, z2)
    n2, r2 = normal_parts(z2)
    out = n2 * vec["g1"] + vec["s1"]
    return out, (xb, kept, n1, r1, yb, act, slope, n2, r2)


def total_rows(values):
    return jnp.sum(values, axis=0)


def ffn_backward(dout, ffn_w, vec, kept, hook, cut):
    xb, saved, n1, r1, yb, act, slope, n2, r2 = kept
    dz2 = normal_back(dout, n2, r2, vec["g1"])
    small = {"g1": total_rows(dout * n2), "s1": total_rows(dout), "sb": total_rows(dz2), "eb": []}
    dz2 = hook("seeded", dz2)
    dzb = dz2.astype(BF)
    dy = dz2
    blocks = []
    for lo, hi in ((0, cut), (cut, TENSORS)):
        if lo == hi:
            continue
        parts = [(act[j], slope[j], *ffn_w[j]) for j in range(lo, hi)]
        dy, sums, grads = ffn_blocks_backward(dzb, yb, dy, parts)
        small["eb"] += sums
        blocks += grads
        if hi < TENSORS:
            dzb, dy = hook("three", (dzb, dy))
    return dy, blocks, small


def attn_backward(dy, seg, attn_w, vec, kept, hook):
    xb, saved, n1, r1, yb, act, slope, n2, r2 = kept
    dz1 = normal_back(dy, n1, r1, vec["g0"])
    small = {"g0": total_rows(dy * n1), "s0": total_rows(dy), "pb": total_rows(dz1), "heads": []}
    dz1 = hook("normed", dz1)
    da = dz1.astype(BF)
    dx = dz1
    blocks = []
    for lo, hi in ((0, TENSORS - 1), (TENSORS - 1, TENSORS)):
        parts = [(*attn_w[j], *saved[j]) for j in range(lo, hi)]
        dx, sums, grads = attend_blocks_backward(vec["cols"], da, xb, dx, parts, seg)
        small["heads"] += sums
        blocks += grads
        if lo == 0:
            da, dx = hook("three", (da, dx))
    return dx, blocks, small


def attn_unpack(first, second):
    cols = first.shape[0] // 2
    heads = jnp.stack([first[:cols], first[cols:], second[:cols]])
    return jnp.swapaxes(heads, 1, 2), second[cols:]


class Reduction:
    def start(self, value, blocks):
        self.blocks = blocks
        value, *self.outgoing = tie(value, *reduce_outgoing(blocks))
        return value

    def swapped(self, value):
        value, self.main_rest, self.main_own, self.across, self.mine = tie(
            value, *reduce_swapped(self.blocks, self.outgoing)
        )
        self.from_rest = send(self.main_rest, MAIN)
        return value

    def crossed(self, value):
        value, self.main_own = tie(value, reduce_across(self.main_own, self.across))
        self.from_own = send(self.main_own, MAIN)
        self.from_peer = send(self.from_rest, SWAP)
        return value

    def summed(self, value):
        value, self.total = tie(value, plus(self.mine, self.from_own, self.from_peer))
        return value


def shards(
    layer_input, skip_tokens, backbone_cotangent, head_cotangent, segment_lengths, pair_index,
    w_heads, heads_bias, w_project, project_bias, norm_gain, norm_shift,
    w_expand, expand_bias, w_shrink, shrink_bias,
):
    side = lax.axis_index("span")
    mine = lax.axis_index("tensor")
    width = layer_input.shape[-1]
    head_cols = w_heads.shape[-1]
    ff_cols = w_expand.shape[-1]

    extra = 16
    bias_rows = jnp.concatenate([heads_bias.reshape(1, 4 * head_cols), expand_bias], axis=0)
    bias_rows = jnp.pad(bias_rows, ((0, extra - bias_rows.shape[0]), (0, 0)))

    def attn_rows(l):
        heads = jnp.swapaxes(w_heads[l], 1, 2)
        first = heads[:2].reshape(2 * head_cols, width)
        return first, jnp.concatenate([heads[2], w_project[l]], axis=0)

    first, second = attn_rows(0)
    first = jnp.concatenate([first, bias_rows], axis=0)
    second = jnp.pad(second, ((0, extra), (0, 0)))
    gather_attn0, gather_ffn0, gather_attn1, gather_ffn1 = (Gathering(side) for _ in range(4))
    x = to_rows(layer_input[0])
    mark = gather_attn0.start(layer_input[0, 0, 0], first, second)
    mark = gather_ffn0.start(mark, w_expand[0], w_shrink[0])
    later = {}

    def during_forward0(kind, j, value):
        if kind == "attn":
            if j == 0:
                value = gather_attn0.arrived(value)
            if j == 1:
                value = gather_attn1.start(value, *attn_rows(1))
            if j == 2:
                value = gather_attn0.crossed(value)
            if j == 3:
                value = gather_ffn0.arrived(value)
                value = gather_ffn1.start(value, w_expand[1], w_shrink[1])
        else:
            if j == 0:
                skip, value = tie(skip_tokens[0], value)
                later["skip"] = to_rows(skip)
            if j == 1:
                value = gather_attn1.arrived(value)
            if j == 2:
                value = gather_ffn0.crossed(value)
        return value

    def during_forward1(kind, j, value):
        if kind == "attn":
            if j == 0:
                head_cot, value = tie(head_cotangent[0], value)
                later["head"] = to_rows(head_cot)
            if j == 1:
                value = gather_attn1.crossed(value)
            if j == 2:
                value, mark = tie(value, later["backbone_out"])
            if j == 3:
                value = gather_ffn1.arrived(value)
        else:
            if j == 0:
                backbone_cot, value = tie(backbone_cotangent[0], value)
                later["backbone"] = to_rows(backbone_cot)
            if j == 2:
                value = gather_ffn1.crossed(value)
        return value

    tokens = x.shape[0]

    def bias_row(j, i):
        first, second = gather_attn0.blocks[j]
        return first[2 * head_cols + i : 2 * head_cols + i + 1].astype(F32)

    def vectors(l):
        return {
            "cols": head_cols, "heads": lambda j: bias_row(j, 0),
            "eb": lambda j: bias_row(j, 1 + l), "pb": project_bias[l].astype(F32),
            "g0": norm_gain[l, 0].astype(F32), "g1": norm_gain[l, 1].astype(F32),
            "s0": norm_shift[l, 0].astype(F32), "s1": norm_shift[l, 1].astype(F32),
            "sb": shrink_bias[l].astype(F32),
        }

    lengths = lax.dynamic_index_in_dim(segment_lengths[0], mine, 0, keepdims=False)
    span_count = lengths.shape[0]
    starts = jnp.cumsum(lengths) - lengths
    row_length = jnp.sum(lengths)
    places = jnp.arange(tokens, dtype=jnp.int32)
    counted = jnp.sum((places[:, None] >= starts[None, :]).astype(jnp.int32), axis=-1) - 1
    segment = jnp.where(places < row_length, counted, span_count)
    seg = (segment[:, None], segment[None, :])
    valid = (places < row_length).astype(F32)[:, None]
    picker = (starts[:, None] == places[None, :]).astype(F32)
    first_place = jnp.sum(picker, axis=0)[:, None] > 0

    vec0, vec1 = vectors(0), vectors(1)
    backbone, kept0 = layer_forward(0, x.astype(F32), seg, gather_attn0, gather_ffn0, vec0, during_forward0)
    attn_w0, ffn_w0 = gather_attn0.blocks, gather_ffn0.blocks
    later["backbone_out"] = to_places((backbone * valid).astype(BF))
    cls = mm(picker.astype(BF), backbone.astype(BF), 1, 0).astype(BF)
    anchors = gather_anchors(cls)
    dp_count = lax.axis_size("dp")
    pair_count = lax.axis_size("span")
    vector_count = dp_count * TENSORS * span_count
    anchors = anchors.reshape(dp_count, pair_count, TENSORS * span_count, width)
    anchors = jnp.swapaxes(anchors, 0, 1).reshape(pair_count, vector_count, width)

    head_in = jnp.where(first_place, backbone, later["skip"].astype(F32))
    head, kept1 = layer_forward(1, head_in, seg, gather_attn1, gather_ffn1, vec1, during_forward1)
    attn_w1, ffn_w1 = gather_attn1.blocks, gather_ffn1.blocks
    head_cot, backbone_cot = later["head"], later["backbone"]
    head_out = to_places((head * valid).astype(BF))

    root = math.sqrt(width)
    logits = mm(anchors[0], anchors[1], 1, 1) / root
    columns = jnp.arange(vector_count, dtype=jnp.int32)
    target = (pair_index[:, None] == columns[None, :]).astype(F32)
    lse_rows = jax.nn.logsumexp(logits, axis=1)
    lse_cols = jax.nn.logsumexp(logits, axis=0)
    dlogits = LOSS_WEIGHT * (
        jnp.exp(logits - lse_rows[:, None]) + jnp.exp(logits - lse_cols[None, :]) - 2.0 * target
    )
    span_loss = (jnp.sum(lse_rows) + jnp.sum(lse_cols) - 2.0 * jnp.sum(target * logits)) / (
        2 * vector_count
    )
    own = (lax.axis_index("dp") * TENSORS + mine) * span_count
    wanted = jnp.where(side == 0, dlogits, dlogits.T)
    wanted = lax.dynamic_slice(wanted, (own, 0), (span_count, vector_count))
    other = lax.dynamic_index_in_dim(anchors, 1 - side, 0, keepdims=False).astype(F32)
    dcls = jnp.dot(wanted, other, precision=HIGHEST) / root

    def plain(name, value):
        return value

    ffn1, attn1, ffn0 = (Reduction() for _ in range(3))

    dy, blocks, small1 = ffn_backward(head_cot.astype(F32) * valid, ffn_w1, vec1, kept1, plain, 0)
    dy, mark = tie(dy, head_out)
    dy = ffn1.start(dy, blocks)

    def during_attn1(name, value):
        if name == "normed":
            return ffn1.swapped(value)
        return ffn1.crossed(value)

    du, blocks, more = attn_backward(dy, seg, attn_w1, vec1, kept1, during_attn1)
    small1.update(more)
    du = attn1.start(du, blocks)
    du = ffn1.summed(du)
    ffn_total1 = lax.psum(ffn1.total, "dp")
    grad_skip = to_places(jnp.where(first_place, 0.0, du).astype(BF))

    seed = backbone_cot.astype(F32) * valid + jnp.where(first_place, du, 0.0)
    seed = seed + jnp.dot(picker.T, dcls, precision=HIGHEST)

    def during_ffn0(name, value):
        if name == "seeded":
            return attn1.swapped(value)
        return attn1.crossed(value)

    dy, blocks, small0 = ffn_backward(seed, ffn_w0, vec0, kept0, during_ffn0, 2)
    dy, mark = tie(dy, grad_skip)
    dy = ffn0.start(dy, blocks)
    dy = attn1.summed(dy)

    dy, ffn_total1, late = tie(dy, ffn_total1, attn1.total)
    attn_total1 = lax.psum(late, "dp")
    finished = {}

    def during_attn0(name, value):
        if name == "normed":
            return ffn0.swapped(value)
        value = ffn0.crossed(value)
        value, finished["attn"] = tie(value, attn_total1)
        return value

    dx, attn_blocks, more = attn_backward(dy, seg, attn_w0, vec0, kept0, during_attn0)
    small0.update(more)
    attn_total1 = finished["attn"]
    grad_input = to_places(dx.astype(BF))

    place = lax.broadcasted_iota(jnp.int32, (2 * CHUNKS_PER_LAYER * ROWS_PER_CHUNK, 1), 0)
    rows = jnp.zeros((place.shape[0], width), F32)
    for l, small in enumerate((small0, small1)):
        base = l * CHUNKS_PER_LAYER * ROWS_PER_CHUNK
        for i, k in enumerate(VECTORS):
            rows = rows + jnp.where(place == base + 2 * ROWS_PER_CHUNK + i, small[k][None], 0.0)
    rows = ffn0.summed(rows.reshape(2 * CHUNKS_PER_LAYER, ROWS_PER_CHUNK, width))
    ffn_total1, attn_total1 = tie(ffn_total1, attn_total1)
    other_ffn1, other_attn1 = send(ffn_total1, SWAP), send(attn_total1, SWAP)
    rows, other_ffn1, other_attn1 = tie(rows, other_ffn1, other_attn1)
    ffn_own, ffn_other, attn_own, attn_other, total = last_sums(
        ffn0.total, attn_blocks, rows, [(small["eb"], small["heads"]) for small in (small0, small1)]
    )

    hb, eb, vector_sums = [], [], []
    for l in range(2):
        base = l * CHUNKS_PER_LAYER
        own = lax.dynamic_slice(total[base : base + 2], (0, mine, 0), (2, 1, width))[:, 0]
        eb.append(own[0])
        hb.append(jnp.stack([own[1, :head_cols], own[1, head_cols : 2 * head_cols]]))
        rows = total[base + 2 : base + CHUNKS_PER_LAYER].reshape(-1, width)
        vector_sums.append({k: rows[i] for i, k in enumerate(VECTORS)})
    sums = vector_sums

    ge1, gs1 = in_order(side, ffn_total1, other_ffn1)
    gh1, gp1 = attn_unpack(*in_order(side, attn_total1, other_attn1))
    ge0, gs0 = in_order(side, ffn_own, ffn_other)
    gh0, gp0 = attn_unpack(*in_order(side, attn_own, attn_other))

    return (
        later["backbone_out"][None],
        head_out[None],
        span_loss,
        grad_input[None],
        grad_skip[None],
        jnp.stack([gh0, gh1]),
        jnp.stack(hb),
        jnp.stack([gp0, gp1]),
        jnp.stack([s["pb"] for s in sums]),
        jnp.stack([jnp.stack([s["g0"], s["g1"]]) for s in sums]),
        jnp.stack([jnp.stack([s["s0"], s["s1"]]) for s in sums]),
        jnp.stack([ge0, ge1]),
        jnp.stack(eb),
        jnp.stack([gs0, gs1]),
        jnp.stack([s["sb"] for s in sums]),
    )


def solution(mesh):
    rows = P("span", "dp", "tensor", None)
    in_specs = (
        rows, rows, rows, rows, P("span", "dp", None), P(),
        P(None, None, None, "tensor"), P(None, None, "tensor"), P(None, "tensor", None),
        P(), P(), P(), P(None, None, "tensor"), P(None, "tensor"), P(None, "tensor", None), P(),
    )
    out_specs = (
        rows, rows, P(), rows, rows,
        P(None, None, None, "tensor"), P(None, None, "tensor"), P(None, "tensor", None),
        P(), P(), P(), P(None, None, "tensor"), P(None, "tensor"), P(None, "tensor", None), P(),
    )
    return jax.shard_map(shards, mesh=mesh, in_specs=in_specs, out_specs=out_specs, check_vma=False)
```

```python
import math

import jax
import jax.numpy as jnp
from jax import lax
from jax.experimental import pallas as pl
from jax.experimental.pallas import tpu as pltpu
from jax.sharding import PartitionSpec as P

HEAD_DIM = 64
EPSILON = 1e-12
LOSS_WEIGHT = 8.0
HIGHEST = lax.Precision.HIGHEST
MASKED = -1e30
BF = jnp.bfloat16
F32 = jnp.float32
PLANE = ("span", "tensor")
MESH = pl.DeviceIdType.MESH
TENSORS = 4
MAIN, DIAG, SWAP = "main", "diag", "swap"


def mm(a, b, ca, cb):
    return lax.dot_general(a, b, (((ca,), (cb,)), ((), ())), preferred_element_type=F32)


def normal_parts(values):
    centred = values - jnp.mean(values, axis=-1, keepdims=True)
    spread = jnp.mean(centred * centred, axis=-1, keepdims=True)
    scale = lax.rsqrt(spread + EPSILON)
    return centred * scale, scale


def normal_back(upward, normed, scale, gain):
    weighted = upward * gain
    first = jnp.mean(weighted, axis=-1, keepdims=True)
    second = jnp.mean(weighted * normed, axis=-1, keepdims=True)
    return (weighted - first - normed * second) * scale


def gelu_parts(hidden):
    phi = 0.5 * (1.0 + lax.erf(hidden * math.sqrt(0.5)))
    slope = phi + hidden * jnp.exp(-0.5 * hidden * hidden) * (1.0 / math.sqrt(2.0 * math.pi))
    return hidden * phi, slope


def plane_pairs(kind):
    pairs = []
    for side in range(2):
        for t in range(TENSORS):
            if kind == SWAP:
                target = (1 - side, t)
            elif kind == MAIN:
                target = (side, t ^ (1 + side))
            else:
                target = (side, t ^ (2 - side))
            pairs.append((side * TENSORS + t, target[0] * TENSORS + target[1]))
    return pairs


def send(values, kind):
    return lax.ppermute(values, PLANE, plane_pairs(kind))


def plus(*terms):
    total = terms[0].astype(F32)
    for term in terms[1:]:
        total = total + term.astype(F32)
    return total.astype(BF)


def pick(side, zero, one):
    return jnp.where(side == 0, zero, one)


def tie(*values):
    return lax.optimization_barrier(values)


class Gathering:
    def __init__(self, side):
        self.side = side

    def start(self, value, first, second):
        value, first, second = tie(value, first, second)
        self.got = (send(first, MAIN), send(second, MAIN))
        self.blocks = [(first, second)]
        return value

    def arrived(self, value):
        value, *got = tie(value, *self.got)
        self.across = send(pick(self.side, *got), DIAG)
        self.blocks += [tuple(got), tuple(send(g, SWAP) for g in got)]
        return value

    def crossed(self, value):
        value, across = tie(value, self.across)
        rest = send(across, SWAP)
        self.blocks.append((pick(self.side, across, rest), pick(self.side, rest, across)))
        return value


def reduce_outgoing(blocks):
    return blocks[2][0], blocks[2][1], blocks[3][1], blocks[0][1]


def reduce_swapped(blocks, outgoing):
    got = [send(o, SWAP) for o in outgoing]
    return (
        plus(blocks[1][1], got[0]), plus(blocks[1][0], got[1]), plus(blocks[3][0], got[2]), plus(blocks[0][0], got[3])
    )


def reduce_across(main_own, across):
    return plus(main_own, send(across, DIAG))


def in_order(side, own, other):
    return pick(side, own, other).astype(F32), pick(side, other, own).astype(F32)


Q_ROWS = 128
DATA_ROWS = 512
GRAD_ROWS = 768


def attend_forward_kernel(
    layer, x_ref, first_ref, second_ref, bias_ref, z_ref, down_ref, across_ref,
    q_ref, k_ref, v_ref, o_ref, lse_ref, out_ref
):
    tokens, width = q_ref.shape
    at = 2 * layer * width
    x = x_ref[...]
    q_ref[...] = (mm(x, first_ref[:width, :], 1, 1) + bias_ref[:, at : at + width]).astype(BF)
    k_ref[...] = mm(x, first_ref[width : 2 * width, :], 1, 1).astype(BF)
    v_ref[...] = (mm(x, second_ref[:width, :], 1, 1) + bias_ref[:, at + width : at + 2 * width]).astype(BF)

    def step(i, carry):
        rows = pl.ds(pl.multiple_of(i * Q_ROWS, Q_ROWS), Q_ROWS)
        same = down_ref[rows, :] == across_ref[...]
        for h in range(width // HEAD_DIM):
            head = slice(h * HEAD_DIM, (h + 1) * HEAD_DIM)
            s = mm(q_ref[rows, head], k_ref[:, head], 1, 1) * 0.125
            s = jnp.where(same, s, MASKED)
            top = jnp.max(s, axis=-1, keepdims=True)
            raised = jnp.exp(s - top)
            total = jnp.sum(raised, axis=-1, keepdims=True)
            weights = (raised * (1.0 / total)).astype(BF)
            o_ref[rows, head] = mm(weights, v_ref[:, head], 1, 0).astype(BF)
            lse_ref[rows, h : h + 1] = top + jnp.log(total)
        out_ref[rows, :] = z_ref[rows, :] + mm(o_ref[rows, :], second_ref[width : 2 * width, :], 1, 0)
        return carry

    lax.fori_loop(0, tokens // Q_ROWS, step, 0)


def attend_backward_kernel(
    da_ref, x_ref, first_ref, second_ref, q_ref, k_ref, v_ref, o_ref, lse_ref, dx_ref, down_ref, across_ref,
    own_ref, rest_ref, sums_ref, out_ref, do_ref, dq_ref, dk_ref, dv_ref
):
    tokens, width = q_ref.shape
    da = da_ref[...]
    do_ref[...] = mm(da, second_ref[width : 2 * width, :], 1, 1).astype(BF)
    dk_ref[...] = jnp.zeros_like(dk_ref)
    dv_ref[...] = jnp.zeros_like(dv_ref)

    def step(i, carry):
        rows = pl.ds(pl.multiple_of(i * Q_ROWS, Q_ROWS), Q_ROWS)
        same = down_ref[rows, :] == across_ref[...]
        for h in range(width // HEAD_DIM):
            head = slice(h * HEAD_DIM, (h + 1) * HEAD_DIM)
            q, k, up = q_ref[rows, head], k_ref[:, head], do_ref[rows, head]
            s = mm(q, k, 1, 1) * 0.125
            s = jnp.where(same, s, MASKED)
            pr = jnp.exp(s - lse_ref[rows, h : h + 1])
            dp = mm(up, v_ref[:, head], 1, 1)
            inner = jnp.sum(pr * dp, axis=-1, keepdims=True)
            ds = (pr * (dp - inner)).astype(BF)
            dq_ref[rows, head] = (mm(ds, k, 1, 0) * 0.125).astype(BF)
            dk_ref[:, head] += mm(ds, q, 0, 0)
            dv_ref[:, head] += mm(pr.astype(BF), up, 0, 0)
        return carry

    lax.fori_loop(0, tokens // Q_ROWS, step, 0)
    x = x_ref[...]
    dq = dq_ref[...]
    dk = (dk_ref[...] * 0.125).astype(BF)
    dv = dv_ref[...].astype(BF)
    out_ref[...] = (
        dx_ref[...]
        + mm(dq, first_ref[:width, :], 1, 0)
        + mm(dk, first_ref[width : 2 * width, :], 1, 0)
        + mm(dv, second_ref[:width, :], 1, 0)
    )
    side = lax.axis_index("span")
    store_both(
        side, own_ref, rest_ref, slice(0, width), mm(dq, x, 0, 0).astype(BF), mm(dv, x, 0, 0).astype(BF)
    )
    store_both(
        side, own_ref, rest_ref, slice(width, 2 * width),
        mm(dk, x, 0, 0).astype(BF), mm(o_ref[...], da, 0, 0).astype(BF),
    )
    sums_ref[:, :width] = jnp.sum(dq.astype(F32), axis=0, keepdims=True)
    sums_ref[:, width:] = jnp.sum(dv.astype(F32), axis=0, keepdims=True)


def small_cost():
    return pl.CostEstimate(flops=1 << 20, bytes_accessed=1 << 10, transcendentals=0)


def kernel_params():
    return pltpu.CompilerParams(vmem_limit_bytes=24 << 20)


def store_both(side, own_ref, rest_ref, rows, first, second):
    @pl.when(side == 0)
    def _():
        own_ref[rows, :] = first
        rest_ref[rows, :] = second

    @pl.when(side != 0)
    def _():
        own_ref[rows, :] = second
        rest_ref[rows, :] = first


def ffn_backward_kernel(
    dz_ref, y_ref, act_ref, slope_ref, first_ref, second_ref, dy_ref, own_ref, rest_ref, sums_ref, out_ref, dh_ref
):
    tokens, model = dz_ref.shape
    side = lax.axis_index("span")
    sums_ref[...] = jnp.zeros_like(sums_ref)

    def data(i, carry):
        rows = pl.ds(pl.multiple_of(i * DATA_ROWS, DATA_ROWS), DATA_ROWS)
        dhid = mm(dz_ref[rows, :], second_ref[...], 1, 1) * slope_ref[rows, :].astype(F32)
        sums_ref[...] += jnp.sum(dhid, axis=0, keepdims=True)
        dhb = dhid.astype(BF)
        dh_ref[rows, :] = dhb
        out_ref[rows, :] = dy_ref[rows, :] + mm(dhb, first_ref[...], 1, 1)
        return carry

    def weights(i, carry):
        rows = pl.ds(pl.multiple_of(i * GRAD_ROWS, GRAD_ROWS), GRAD_ROWS)
        first = mm(y_ref[:, rows], dh_ref[...], 0, 0).astype(BF)
        second = mm(act_ref[:, rows], dz_ref[...], 0, 0).astype(BF)
        store_both(side, own_ref, rest_ref, rows, first, second)
        return carry

    lax.fori_loop(0, tokens // DATA_ROWS, data, 0)
    lax.fori_loop(0, model // GRAD_ROWS, weights, 0)


def streamed_blocks(name, body, shared, total, blocks, big, small, scratch):
    count, takes, gives = len(blocks), len(blocks[0]), len(big)
    vmem, anywhere = pl.BlockSpec(memory_space=pltpu.VMEM), pl.BlockSpec(memory_space=pl.ANY)
    dma = pltpu.SemaphoreType.DMA

    def kernel(*refs):
        refs = list(refs)

        def take(n):
            taken = refs[:n]
            del refs[:n]
            return taken

        shared_refs, (total_ref,), ins = take(len(shared)), take(1), take(count * takes)
        (out_ref,), smalls, outs = take(1), take(count), take(count * gives)
        in_bufs, out_bufs, (in_sems, out_sems), extra = take(takes), take(gives), take(2), take(len(scratch))

        def fetch(j):
            return [
                pltpu.make_async_copy(ins[j * takes + i], in_bufs[i].at[j % 2], in_sems.at[j % 2, i])
                for i in range(takes)
            ]

        def put(j):
            return [
                pltpu.make_async_copy(out_bufs[i].at[j % 2], outs[j * gives + i], out_sems.at[j % 2, i])
                for i in range(gives)
            ]

        for copy in fetch(0):
            copy.start()
        for j in range(count):
            if j + 1 < count:
                for copy in fetch(j + 1):
                    copy.start()
            for copy in fetch(j):
                copy.wait()
            if j >= 2:
                for copy in put(j - 2):
                    copy.wait()
            body(
                shared_refs, total_ref if j == 0 else out_ref, [r.at[j % 2] for r in in_bufs],
                [r.at[j % 2] for r in out_bufs], smalls[j], out_ref, extra,
            )
            for copy in put(j):
                copy.start()
        for j in range(max(0, count - 2), count):
            for copy in put(j):
                copy.wait()

    out = pl.pallas_call(
        kernel,
        name=name,
        out_shape=(jax.ShapeDtypeStruct(total.shape, F32),)
        + (jax.ShapeDtypeStruct(small, F32),) * count
        + tuple(jax.ShapeDtypeStruct(shape, BF) for shape in big) * count,
        in_specs=[vmem] * (len(shared) + 1) + [anywhere] * (count * takes),
        out_specs=(vmem,) * (1 + count) + (anywhere,) * (count * gives),
        scratch_shapes=[pltpu.VMEM((2,) + x.shape, x.dtype) for x in blocks[0]]
        + [pltpu.VMEM((2,) + shape, BF) for shape in big]
        + [dma((2, takes)), dma((2, gives))]
        + list(scratch),
        compiler_params=pltpu.CompilerParams(vmem_limit_bytes=63 << 20),
        cost_estimate=small_cost(),
    )(*shared, total, *[x for block in blocks for x in block])
    smalls, bigs = out[1 : 1 + count], out[1 + count :]
    return out[0], smalls, [tuple(bigs[j * gives : (j + 1) * gives]) for j in range(count)]


def ffn_blocks_backward(dzb, yb, dy, blocks):
    def body(shared, total, ins, outs, small, out, extra):
        ffn_backward_kernel(*shared, *ins, total, *outs, small, out, *extra)

    first = blocks[0][2].shape
    act = blocks[0][0].shape
    return streamed_blocks(
        "ffn_backward", body, (dzb, yb), dy, blocks, (first, first), (1, act[1]), [pltpu.VMEM(act, BF)]
    )


def attend_blocks_backward(cols, da, x, dx, blocks, seg):
    tokens, model = x.shape

    def body(shared, total, ins, outs, small, out, extra):
        da_ref, x_ref, down_ref, across_ref = shared
        attend_backward_kernel(
            da_ref, x_ref, *ins, total, down_ref, across_ref, *outs, small, out, *extra
        )

    grad = (2 * cols, model)
    scratch = [pltpu.VMEM((tokens, cols), kind) for kind in (BF, BF, F32, F32)]
    return streamed_blocks(
        "attend_backward", body, (da, x, *seg), dx, blocks, (grad, grad), (1, 2 * cols), scratch
    )


def attend_forward(layer, cols, x, first, second, bias, z, seg):
    tokens, model = x.shape
    narrow = jax.ShapeDtypeStruct((tokens, cols), BF)

    def body(*refs):
        attend_forward_kernel(layer, *refs)

    return pl.pallas_call(
        body,
        name="attend_forward",
        out_shape=(
            narrow, narrow, narrow, narrow,
            jax.ShapeDtypeStruct((tokens, cols // HEAD_DIM), F32),
            jax.ShapeDtypeStruct(z.shape, F32),
        ),
        compiler_params=kernel_params(),
        cost_estimate=small_cost(),
    )(x, first, second, bias, z, *seg)


def anchors_kernel(dps, planes, x_ref, out_ref, near_send, near_recv, far_send, far_recv, own_sem):
    dp = lax.axis_index("dp")
    me = lax.axis_index("span") * TENSORS + lax.axis_index("tensor")

    def near(k):
        peer = lax.rem(me + k, planes)
        return {"span": peer // TENSORS, "tensor": lax.rem(peer, TENSORS)}

    def far(k):
        return {"dp": lax.rem(dp + k, dps)}

    barrier = pltpu.get_barrier_semaphore()
    for k in range(1, planes):
        pl.semaphore_signal(barrier, inc=1, device_id=near(k), device_id_type=MESH)
    for k in range(1, dps):
        pl.semaphore_signal(barrier, inc=1, device_id=far(k), device_id_type=MESH)
    pl.semaphore_wait(barrier, planes + dps - 2)

    own = pltpu.make_async_copy(x_ref, out_ref.at[dp, me], own_sem)
    own.start()

    def near_copy(k):
        return pltpu.make_async_remote_copy(
            src_ref=x_ref, dst_ref=out_ref.at[dp, me], send_sem=near_send.at[k],
            recv_sem=near_recv.at[k], device_id=near(k), device_id_type=MESH,
        )

    def far_copy(k):
        return pltpu.make_async_remote_copy(
            src_ref=out_ref.at[dp], dst_ref=out_ref.at[dp], send_sem=far_send.at[k],
            recv_sem=far_recv.at[k], device_id=far(k), device_id_type=MESH,
        )

    for k in range(1, planes):
        near_copy(k).start()
    own.wait()
    for k in range(1, planes):
        near_copy(k).wait()
    for k in range(1, dps):
        far_copy(k).start()
    for k in range(1, dps):
        far_copy(k).wait()


def gather_anchors(values):
    dps = lax.axis_size("dp")
    planes = lax.axis_size("span") * lax.axis_size("tensor")
    dma = pltpu.SemaphoreType.DMA
    vmem = pl.BlockSpec(memory_space=pltpu.VMEM)

    def body(*refs):
        anchors_kernel(dps, planes, *refs)

    return pl.pallas_call(
        body,
        name="gather_anchors",
        out_shape=jax.ShapeDtypeStruct((dps, planes) + values.shape, values.dtype),
        in_specs=[vmem],
        out_specs=vmem,
        scratch_shapes=[dma((planes,)), dma((planes,)), dma((dps,)), dma((dps,)), dma],
        compiler_params=pltpu.CompilerParams(collective_id=0, has_side_effects=True),
    )(values)


VECTORS = ("pb", "g0", "g1", "s0", "s1", "sb")
ROWS_PER_CHUNK = 4
CHUNKS_PER_LAYER = 4


def block_order(side, tensor):
    flip_one = tensor + 1 - 2 * lax.rem(tensor, 2)
    flip_two = tensor + 2 - 4 * (tensor // 2)
    swing = side * (flip_two - flip_one)
    return tensor, flip_one + swing, flip_two - swing, TENSORS - 1 - tensor


def remote(src, dst, sems, i, device):
    return pltpu.make_async_remote_copy(
        src_ref=src, dst_ref=dst, send_sem=sems.at[0, i], recv_sem=sems.at[1, i],
        device_id=device, device_id_type=MESH,
    )


class Halving:
    def __init__(self, dps, dp, src, result, scratch, sums, sems):
        self.src, self.result, self.scratch, self.sums, self.sems = src, result, scratch, sums, sems
        self.steps = []
        base, size, bit = 0, dps, 1
        while bit < dps:
            size = size // 2
            up = lax.rem(dp // bit, 2)
            self.steps.append((base + (1 - up) * size, base + up * size, size, {"dp": dp + bit * (1 - 2 * up)}))
            base = base + up * size
            bit *= 2

    def current(self, s):
        return self.src if s == 0 else self.sums

    def down(self, s):
        away, kept, size, partner = self.steps[s]
        room = self.scratch.at[pl.ds(self.steps_room(s), size)]
        return remote(self.current(s).at[pl.ds(away, size)], room, self.sems, s, partner)

    def steps_room(self, s):
        return sum(step[2] for step in self.steps[:s])

    def add(self, s):
        self.down(s).wait()
        away, kept, size, partner = self.steps[s]
        came = self.scratch[pl.ds(self.steps_room(s), size)]
        into = self.result if s == len(self.steps) - 1 else self.sums
        into[pl.ds(kept, size)] = plus(self.current(s)[pl.ds(kept, size)], came)

    def up(self, s):
        away, kept, size, partner = self.steps[s]
        part = self.result.at[pl.ds(kept, size)]
        return remote(part, part, self.sems, len(self.steps) + s, partner)


def last_kernel(dps, planes, ffn_ref, own, rest, rows_ref, blocks, outs, scratch):
    ffn_own, ffn_other, attn_own, attn_other, out_ref = outs
    (
        swapped, main_rest, main_own, across, mine, got_rest, got_own, got_across, got_peer, total_ref,
        ffn_room, attn_room, ffn_sums, attn_sums, x_ref, parts, sums,
        swap_sems, plane_sems, ffn_sems, attn_sems, one_sems, two_sems, three_sems,
    ) = scratch
    dp = lax.axis_index("dp")
    side = lax.axis_index("span")
    tensor = lax.axis_index("tensor")
    me = side * TENSORS + tensor
    order = block_order(side, tensor)
    x_ref[...] = rows_ref[...]
    for l in range(2):
        for j in range(TENSORS):
            for k in range(2):
                columns = blocks[l][k][j].shape[1]
                x_ref[l * CHUNKS_PER_LAYER + k, pl.ds(order[j], 1), :columns] = blocks[l][k][j][...]

    def near_peer(k):
        return lax.rem(me + k, planes)

    def near(k):
        peer = near_peer(k)
        return {"span": peer // TENSORS, "tensor": lax.rem(peer, TENSORS)}

    def far_peer(k):
        return lax.rem(dp + k, dps)

    def far(k):
        return {"dp": far_peer(k)}

    peer_core, main_peer, diag_peer = {"span": 1 - side}, {"tensor": order[1]}, {"tensor": order[2]}
    nears, fars = range(1, planes), range(1, dps)

    barrier = pltpu.get_barrier_semaphore()
    for k in nears:
        pl.semaphore_signal(barrier, inc=1, device_id=near(k), device_id_type=MESH)
    for k in fars:
        pl.semaphore_signal(barrier, inc=1, device_id=far(k), device_id_type=MESH)
    pl.semaphore_wait(barrier, planes + dps - 2)

    swaps = [
        remote(src, swapped.at[i], swap_sems, i, peer_core)
        for i, src in enumerate((own[2], rest[2], rest[3], rest[0]))
    ]
    for copy in swaps:
        copy.start()
    ones = [remote(x_ref.at[near_peer(k)], parts.at[k], one_sems, k, near(k)) for k in nears]
    for copy in ones:
        copy.start()
    ffn_chunks = [
        Halving(dps, dp, ffn_ref.at[c], ffn_own.at[c], ffn_room.at[c], ffn_sums.at[c], ffn_sems.at[c])
        for c in range(ffn_ref.shape[0])
    ]
    attn_chunks = [
        Halving(dps, dp, total_ref.at[c], attn_own.at[c], attn_room.at[c], attn_sums.at[c], attn_sems.at[c])
        for c in range(total_ref.shape[0])
    ]
    stages = range(len(ffn_chunks[0].steps))
    last = len(stages) - 1

    def down_from(chunks, s):
        for chunk in chunks:
            chunk.down(s).start()

    def down_to_end(chunks, s):
        for chunk in chunks:
            chunk.add(s)
            (chunk.down(s + 1) if s < last else chunk.up(last)).start()

    def up_next(chunks, s):
        for chunk in chunks:
            chunk.up(s).wait()
            if s > 0:
                chunk.up(s - 1).start()

    down_from(ffn_chunks, 0)

    for copy in swaps:
        copy.wait()
    across[...] = plus(own[3][...], swapped[2])
    main_rest[...] = plus(rest[1][...], swapped[0])
    send_across = remote(across, got_across, plane_sems, 0, diag_peer)
    send_across.start()
    send_rest = remote(main_rest, got_rest, plane_sems, 1, main_peer)
    send_rest.start()
    mine[...] = plus(own[0][...], swapped[3])
    for copy in ones:
        copy.wait()
    total = x_ref[me]
    for k in nears:
        total = total + parts[k]
    sums[dp] = total
    twos = [remote(sums.at[dp], sums.at[dp], two_sems, k, far(k)) for k in fars]
    for copy in twos:
        copy.start()

    down_to_end(ffn_chunks, 0)
    send_across.wait()
    main_own[...] = plus(own[1][...], swapped[1], got_across[...])
    send_own = remote(main_own, got_own, plane_sems, 2, main_peer)
    send_own.start()
    for s in stages[1:]:
        down_to_end(ffn_chunks, s)
    send_rest.wait()
    send_peer = remote(got_rest, got_peer, swap_sems, 4, peer_core)
    send_peer.start()
    send_peer.wait()
    send_own.wait()
    total_ref[...] = plus(mine[...], got_own[...], got_peer[...])
    down_from(attn_chunks, 0)

    for copy in twos:
        copy.wait()
    total = sums[0]
    for k in fars:
        total = total + sums[k]
    out_ref[me] = total
    threes = [remote(out_ref.at[me], out_ref.at[me], three_sems, k, near(k)) for k in nears]
    for copy in threes:
        copy.start()

    for s in reversed(stages[1:]):
        up_next(ffn_chunks, s)
    for s in stages:
        down_to_end(attn_chunks, s)
    up_next(ffn_chunks, 0)
    swap_ffn = remote(ffn_own, ffn_other, swap_sems, 5, peer_core)
    swap_ffn.start()
    for s in reversed(stages):
        up_next(attn_chunks, s)
    swap_attn = remote(attn_own, attn_other, swap_sems, 6, peer_core)
    swap_attn.start()
    for copy in threes:
        copy.wait()
    swap_ffn.wait()
    swap_attn.wait()


def last_sums(ffn_total, attn_blocks, rows, blocks):
    dps = lax.axis_size("dp")
    planes = lax.axis_size("span") * lax.axis_size("tensor")
    flat, tree = jax.tree.flatten(blocks)

    def by_dp(values):
        rows = values.shape[0]
        chunks = 2 if rows % (32 * dps) == 0 else 1
        return values.reshape(chunks, dps, rows // (chunks * dps), values.shape[1])

    ffn_total = by_dp(ffn_total)
    own = [by_dp(o) for o, r in attn_blocks]
    rest = [by_dp(r) for o, r in attn_blocks]
    dma = pltpu.SemaphoreType.DMA
    vmem = pl.BlockSpec(memory_space=pltpu.VMEM)
    attn, ffn = own[0].shape, ffn_total.shape

    def body(ffn_ref, *refs):
        own_refs, rest_refs, rows_ref = refs[:TENSORS], refs[TENSORS : 2 * TENSORS], refs[2 * TENSORS]
        refs = refs[2 * TENSORS + 1 :]
        inputs = jax.tree.unflatten(tree, refs[: len(flat)])
        outs, scratch = refs[len(flat) : len(flat) + 5], refs[len(flat) + 5 :]
        last_kernel(dps, planes, ffn_ref, own_refs, rest_refs, rows_ref, inputs, outs, scratch)

    outs = pl.pallas_call(
        body,
        name="last_sums",
        out_shape=tuple(jax.ShapeDtypeStruct(shape, BF) for shape in (ffn, ffn, attn, attn))
        + (jax.ShapeDtypeStruct(rows.shape, F32),),
        in_specs=[vmem] * (2 + 2 * TENSORS + len(flat)),
        out_specs=(vmem,) * 5,
        scratch_shapes=[pltpu.VMEM((TENSORS,) + attn, BF)]
        + [pltpu.VMEM(attn, BF)] * 9
        + [pltpu.VMEM(ffn, BF), pltpu.VMEM(attn, BF)] * 2
        + [pltpu.VMEM(rows.shape, F32), pltpu.VMEM(rows.shape, F32), pltpu.VMEM((dps,) + rows.shape[1:], F32)]
        + [dma((2, 7)), dma((2, 3))]
        + [dma((ffn[0], 2, dps)), dma((attn[0], 2, dps))]
        + [dma((2, planes)), dma((2, dps)), dma((2, planes))],
        compiler_params=pltpu.CompilerParams(
            collective_id=1, has_side_effects=True, vmem_limit_bytes=36 << 20
        ),
    )(ffn_total, *own, *rest, rows, *flat)
    whole = [o.reshape(-1, o.shape[-1]) for o in outs[:4]]
    return (*whole, outs[4])


def to_rows(values):
    return lax.all_to_all(values, "tensor", split_axis=0, concat_axis=0, tiled=True).reshape(
        -1, values.shape[-1]
    )


def to_places(values):
    blocks = values.reshape(TENSORS, -1, values.shape[-1])
    return lax.all_to_all(blocks, "tensor", split_axis=0, concat_axis=0, tiled=True)


def layer_forward(l, x, seg, attn, ffn, vec, hook):
    xb = x.astype(BF)
    kept = []
    z1 = x + vec["pb"]
    for j in range(TENSORS):
        first, second = attn.blocks[j]
        *saved, z1 = attend_forward(l, vec["cols"], xb, first, second, vec["heads"](j), z1, seg)
        kept.append(saved)
        z1 = hook("attn", j, z1)
    n1, r1 = normal_parts(z1)
    y = n1 * vec["g0"] + vec["s0"]
    yb = y.astype(BF)
    act, slope = [], []
    z2 = y + vec["sb"]
    for j in range(TENSORS):
        first, second = ffn.blocks[j]
        a, b = gelu_parts(mm(yb, first, 1, 0) + vec["eb"](j))
        act.append(a.astype(BF))
        slope.append(b.astype(BF))
        z2 = z2 + mm(act[-1], second, 1, 0)
        z2 = hook("ffn", j, z2)
    n2, r2 = normal_parts(z2)
    out = n2 * vec["g1"] + vec["s1"]
    return out, (xb, kept, n1, r1, yb, act, slope, n2, r2)


def total_rows(values):
    return jnp.sum(values, axis=0)


def ffn_backward(dout, ffn_w, vec, kept, hook, cut):
    xb, saved, n1, r1, yb, act, slope, n2, r2 = kept
    dz2 = normal_back(dout, n2, r2, vec["g1"])
    small = {"g1": total_rows(dout * n2), "s1": total_rows(dout), "sb": total_rows(dz2), "eb": []}
    dz2 = hook("seeded", dz2)
    dzb = dz2.astype(BF)
    dy = dz2
    blocks = []
    for lo, hi in ((0, cut), (cut, TENSORS)):
        if lo == hi:
            continue
        parts = [(act[j], slope[j], *ffn_w[j]) for j in range(lo, hi)]
        dy, sums, grads = ffn_blocks_backward(dzb, yb, dy, parts)
        small["eb"] += sums
        blocks += grads
        if hi < TENSORS:
            dzb, dy = hook("three", (dzb, dy))
    return dy, blocks, small


def attn_backward(dy, seg, attn_w, vec, kept, hook, cut):
    xb, saved, n1, r1, yb, act, slope, n2, r2 = kept
    dz1 = normal_back(dy, n1, r1, vec["g0"])
    small = {"g0": total_rows(dy * n1), "s0": total_rows(dy), "pb": total_rows(dz1), "heads": []}
    dz1 = hook("normed", dz1)
    da = dz1.astype(BF)
    dx = dz1
    blocks = []
    for lo, hi in ((0, cut), (cut, TENSORS)):
        if lo == hi:
            continue
        parts = [(*attn_w[j], *saved[j]) for j in range(lo, hi)]
        dx, sums, grads = attend_blocks_backward(vec["cols"], da, xb, dx, parts, seg)
        small["heads"] += sums
        blocks += grads
        if hi < TENSORS:
            da, dx = hook("three", (da, dx))
    return dx, blocks, small


def attn_unpack(first, second):
    cols = first.shape[0] // 2
    heads = jnp.stack([first[:cols], first[cols:], second[:cols]])
    return jnp.swapaxes(heads, 1, 2), second[cols:]


class Reduction:
    def start(self, value, blocks):
        self.blocks = blocks
        value, *self.outgoing = tie(value, *reduce_outgoing(blocks))
        return value

    def swapped(self, value):
        value, self.main_rest, self.main_own, self.across, self.mine = tie(
            value, *reduce_swapped(self.blocks, self.outgoing)
        )
        self.from_rest = send(self.main_rest, MAIN)
        return value

    def crossed(self, value):
        value, self.main_own = tie(value, reduce_across(self.main_own, self.across))
        self.from_own = send(self.main_own, MAIN)
        self.from_peer = send(self.from_rest, SWAP)
        return value

    def summed(self, value):
        value, self.total = tie(value, plus(self.mine, self.from_own, self.from_peer))
        return value


def shards(
    layer_input, skip_tokens, backbone_cotangent, head_cotangent, segment_lengths, pair_index,
    w_heads, heads_bias, w_project, project_bias, norm_gain, norm_shift,
    w_expand, expand_bias, w_shrink, shrink_bias,
):
    side = lax.axis_index("span")
    mine = lax.axis_index("tensor")
    width = layer_input.shape[-1]
    head_cols = w_heads.shape[-1]
    ff_cols = w_expand.shape[-1]

    extra = 16
    bias_rows = jnp.concatenate([heads_bias.reshape(1, 4 * head_cols), expand_bias], axis=0)
    bias_rows = jnp.pad(bias_rows, ((0, extra - bias_rows.shape[0]), (0, 0)))

    def attn_rows(l):
        heads = jnp.swapaxes(w_heads[l], 1, 2)
        first = heads[:2].reshape(2 * head_cols, width)
        return first, jnp.concatenate([heads[2], w_project[l]], axis=0)

    first, second = attn_rows(0)
    first = jnp.concatenate([first, bias_rows], axis=0)
    second = jnp.pad(second, ((0, extra), (0, 0)))
    gather_attn0, gather_ffn0, gather_attn1, gather_ffn1 = (Gathering(side) for _ in range(4))
    x = to_rows(layer_input[0])
    mark = gather_attn0.start(layer_input[0, 0, 0], first, second)
    mark = gather_ffn0.start(mark, w_expand[0], w_shrink[0])
    later = {}

    def during_forward0(kind, j, value):
        if kind == "attn":
            if j == 0:
                value = gather_attn0.arrived(value)
            if j == 1:
                value = gather_attn1.start(value, *attn_rows(1))
            if j == 2:
                value = gather_attn0.crossed(value)
            if j == 3:
                value = gather_ffn0.arrived(value)
                value = gather_ffn1.start(value, w_expand[1], w_shrink[1])
        else:
            if j == 0:
                skip, value = tie(skip_tokens[0], value)
                later["skip"] = to_rows(skip)
            if j == 1:
                value = gather_attn1.arrived(value)
            if j == 2:
                value = gather_ffn0.crossed(value)
        return value

    def during_forward1(kind, j, value):
        if kind == "attn":
            if j == 0:
                head_cot, value = tie(head_cotangent[0], value)
                later["head"] = to_rows(head_cot)
            if j == 1:
                value = gather_attn1.crossed(value)
            if j == 2:
                value, mark = tie(value, later["backbone_out"])
            if j == 3:
                value = gather_ffn1.arrived(value)
        else:
            if j == 0:
                backbone_cot, value = tie(backbone_cotangent[0], value)
                later["backbone"] = to_rows(backbone_cot)
            if j == 2:
                value = gather_ffn1.crossed(value)
        return value

    tokens = x.shape[0]

    def bias_row(j, i):
        first, second = gather_attn0.blocks[j]
        return first[2 * head_cols + i : 2 * head_cols + i + 1].astype(F32)

    def vectors(l):
        return {
            "cols": head_cols, "heads": lambda j: bias_row(j, 0),
            "eb": lambda j: bias_row(j, 1 + l), "pb": project_bias[l].astype(F32),
            "g0": norm_gain[l, 0].astype(F32), "g1": norm_gain[l, 1].astype(F32),
            "s0": norm_shift[l, 0].astype(F32), "s1": norm_shift[l, 1].astype(F32),
            "sb": shrink_bias[l].astype(F32),
        }

    lengths = lax.dynamic_index_in_dim(segment_lengths[0], mine, 0, keepdims=False)
    span_count = lengths.shape[0]
    starts = jnp.cumsum(lengths) - lengths
    row_length = jnp.sum(lengths)
    places = jnp.arange(tokens, dtype=jnp.int32)
    counted = jnp.sum((places[:, None] >= starts[None, :]).astype(jnp.int32), axis=-1) - 1
    segment = jnp.where(places < row_length, counted, span_count)
    seg = (segment[:, None], segment[None, :])
    valid = (places < row_length).astype(F32)[:, None]
    picker = (starts[:, None] == places[None, :]).astype(F32)
    first_place = jnp.sum(picker, axis=0)[:, None] > 0

    vec0, vec1 = vectors(0), vectors(1)
    backbone, kept0 = layer_forward(0, x.astype(F32), seg, gather_attn0, gather_ffn0, vec0, during_forward0)
    attn_w0, ffn_w0 = gather_attn0.blocks, gather_ffn0.blocks
    later["backbone_out"] = to_places((backbone * valid).astype(BF))
    cls = mm(picker.astype(BF), backbone.astype(BF), 1, 0).astype(BF)
    anchors = gather_anchors(cls)
    dp_count = lax.axis_size("dp")
    pair_count = lax.axis_size("span")
    vector_count = dp_count * TENSORS * span_count
    anchors = anchors.reshape(dp_count, pair_count, TENSORS * span_count, width)
    anchors = jnp.swapaxes(anchors, 0, 1).reshape(pair_count, vector_count, width)

    head_in = jnp.where(first_place, backbone, later["skip"].astype(F32))
    head, kept1 = layer_forward(1, head_in, seg, gather_attn1, gather_ffn1, vec1, during_forward1)
    attn_w1, ffn_w1 = gather_attn1.blocks, gather_ffn1.blocks
    head_cot, backbone_cot = later["head"], later["backbone"]
    head_out = to_places((head * valid).astype(BF))

    root = math.sqrt(width)
    logits = mm(anchors[0], anchors[1], 1, 1) / root
    columns = jnp.arange(vector_count, dtype=jnp.int32)
    target = (pair_index[:, None] == columns[None, :]).astype(F32)
    lse_rows = jax.nn.logsumexp(logits, axis=1)
    lse_cols = jax.nn.logsumexp(logits, axis=0)
    dlogits = LOSS_WEIGHT * (
        jnp.exp(logits - lse_rows[:, None]) + jnp.exp(logits - lse_cols[None, :]) - 2.0 * target
    )
    span_loss = (jnp.sum(lse_rows) + jnp.sum(lse_cols) - 2.0 * jnp.sum(target * logits)) / (
        2 * vector_count
    )
    own = (lax.axis_index("dp") * TENSORS + mine) * span_count
    wanted = jnp.where(side == 0, dlogits, dlogits.T)
    wanted = lax.dynamic_slice(wanted, (own, 0), (span_count, vector_count))
    other = lax.dynamic_index_in_dim(anchors, 1 - side, 0, keepdims=False).astype(F32)
    dcls = jnp.dot(wanted, other, precision=HIGHEST) / root

    def plain(name, value):
        return value

    ffn1, attn1, ffn0 = (Reduction() for _ in range(3))

    dy, blocks, small1 = ffn_backward(head_cot.astype(F32) * valid, ffn_w1, vec1, kept1, plain, 0)
    dy, mark = tie(dy, head_out)
    dy = ffn1.start(dy, blocks)

    def during_attn1(name, value):
        if name == "normed":
            return ffn1.swapped(value)
        return ffn1.crossed(value)

    du, blocks, more = attn_backward(dy, seg, attn_w1, vec1, kept1, during_attn1, TENSORS)
    small1.update(more)
    du = ffn1.crossed(du)
    du = attn1.start(du, blocks)
    grad_skip = to_places(jnp.where(first_place, 0.0, du).astype(BF))

    seed = backbone_cot.astype(F32) * valid + jnp.where(first_place, du, 0.0)
    seed = seed + jnp.dot(picker.T, dcls, precision=HIGHEST)

    finished = {}

    def during_ffn0(name, value):
        if name == "seeded":
            value = attn1.swapped(value)
            value = ffn1.summed(value)
            finished["ffn"] = lax.psum(ffn1.total, "dp")
            return value
        return attn1.crossed(value)

    dy, blocks, small0 = ffn_backward(seed, ffn_w0, vec0, kept0, during_ffn0, 2)
    dy, mark = tie(dy, grad_skip)
    dy = ffn0.start(dy, blocks)
    dy = attn1.summed(dy)

    dy, ffn_total1, late = tie(dy, finished["ffn"], attn1.total)
    attn_total1 = lax.psum(late, "dp")

    def during_attn0(name, value):
        if name == "normed":
            return ffn0.swapped(value)
        value = ffn0.crossed(value)
        value, finished["attn"] = tie(value, attn_total1)
        return value

    dx, attn_blocks, more = attn_backward(dy, seg, attn_w0, vec0, kept0, during_attn0, TENSORS - 1)
    small0.update(more)
    attn_total1 = finished["attn"]
    grad_input = to_places(dx.astype(BF))

    place = lax.broadcasted_iota(jnp.int32, (2 * CHUNKS_PER_LAYER * ROWS_PER_CHUNK, 1), 0)
    rows = jnp.zeros((place.shape[0], width), F32)
    for l, small in enumerate((small0, small1)):
        base = l * CHUNKS_PER_LAYER * ROWS_PER_CHUNK
        for i, k in enumerate(VECTORS):
            rows = rows + jnp.where(place == base + 2 * ROWS_PER_CHUNK + i, small[k][None], 0.0)
    rows = ffn0.summed(rows.reshape(2 * CHUNKS_PER_LAYER, ROWS_PER_CHUNK, width))
    ffn_total1, attn_total1 = tie(ffn_total1, attn_total1)
    other_ffn1, other_attn1 = send(ffn_total1, SWAP), send(attn_total1, SWAP)
    rows, other_ffn1, other_attn1 = tie(rows, other_ffn1, other_attn1)
    ffn_own, ffn_other, attn_own, attn_other, total = last_sums(
        ffn0.total, attn_blocks, rows, [(small["eb"], small["heads"]) for small in (small0, small1)]
    )

    hb, eb, vector_sums = [], [], []
    for l in range(2):
        base = l * CHUNKS_PER_LAYER
        own = lax.dynamic_slice(total[base : base + 2], (0, mine, 0), (2, 1, width))[:, 0]
        eb.append(own[0])
        hb.append(jnp.stack([own[1, :head_cols], own[1, head_cols : 2 * head_cols]]))
        rows = total[base + 2 : base + CHUNKS_PER_LAYER].reshape(-1, width)
        vector_sums.append({k: rows[i] for i, k in enumerate(VECTORS)})
    sums = vector_sums

    ge1, gs1 = in_order(side, ffn_total1, other_ffn1)
    gh1, gp1 = attn_unpack(*in_order(side, attn_total1, other_attn1))
    ge0, gs0 = in_order(side, ffn_own, ffn_other)
    gh0, gp0 = attn_unpack(*in_order(side, attn_own, attn_other))

    return (
        later["backbone_out"][None],
        head_out[None],
        span_loss,
        grad_input[None],
        grad_skip[None],
        jnp.stack([gh0, gh1]),
        jnp.stack(hb),
        jnp.stack([gp0, gp1]),
        jnp.stack([s["pb"] for s in sums]),
        jnp.stack([jnp.stack([s["g0"], s["g1"]]) for s in sums]),
        jnp.stack([jnp.stack([s["s0"], s["s1"]]) for s in sums]),
        jnp.stack([ge0, ge1]),
        jnp.stack(eb),
        jnp.stack([gs0, gs1]),
        jnp.stack([s["sb"] for s in sums]),
    )


def solution(mesh):
    rows = P("span", "dp", "tensor", None)
    in_specs = (
        rows, rows, rows, rows, P("span", "dp", None), P(),
        P(None, None, None, "tensor"), P(None, None, "tensor"), P(None, "tensor", None),
        P(), P(), P(), P(None, None, "tensor"), P(None, "tensor"), P(None, "tensor", None), P(),
    )
    out_specs = (
        rows, rows, P(), rows, rows,
        P(None, None, None, "tensor"), P(None, None, "tensor"), P(None, "tensor", None),
        P(), P(), P(), P(None, None, "tensor"), P(None, "tensor"), P(None, "tensor", None), P(),
    )
    return jax.shard_map(shards, mesh=mesh, in_specs=in_specs, out_specs=out_specs, check_vma=False)
```
